32 devices in a mesh: seq: 8 (over z, y), mlp: 4 (over x, core).
Axes of the slice: x: 2, y: 2, z: 4, core: 2. Of those that a mesh axis runs over, the one named last changes fastest.
Arguments:
- inputs: bfloat16 [1024, 2048], P('seq'), may hold values from -6 to 6
- first_gain: float32 [3, 2048], replicated, may hold values from 0.1 to 1.9
- query_weight: bfloat16 [2048, 2048], P(None, 'mlp'), may hold values from -0.1875 to 0.1875
- key_weight: bfloat16 [2048, 2048], P(None, 'mlp'), may hold values from -0.125 to 0.125
- value_weight: bfloat16 [2048, 2048], P(None, 'mlp'), may hold values from -0.125 to 0.125
- output_weight: bfloat16 [2048, 2048], P('mlp'), may hold values from -0.75 to 0.75
- second_gain: float32 [3, 2048], replicated, may hold values from 0.1 to 1.9
- up_weight: bfloat16 [2048, 8192], P(None, 'mlp'), may hold values from -0.125 to 0.125
- down_weight: bfloat16 [8192, 2048], P('mlp'), may hold values from -0.0625 to 0.0625
- frame_sizes: int32 [1, 8], replicated, may hold values from 144 to 576, as said below
- text_counts: int32 [1, 8], replicated, may hold values from 1 to 32
- action_counts: int32 [1, 8], replicated, may hold values from 1 to 2
- cotangent: bfloat16 [1024, 2048], P('seq'), may hold values from -6 to 6
Outputs:
- outputs: bfloat16 [1024, 2048], P('seq')
- input_grad: bfloat16 [1024, 2048], P('seq')
- first_gain_grad: float32 [3, 2048], P(None, 'seq')
- query_grad: float32 [2048, 2048], P('seq', 'mlp')
- key_grad: float32 [2048, 2048], P('seq', 'mlp')
- value_grad: float32 [2048, 2048], P('seq', 'mlp')
- output_grad: float32 [2048, 2048], P('mlp', 'seq')
- second_gain_grad: float32 [3, 2048], P(None, 'seq')
- up_grad: float32 [2048, 8192], P('seq', 'mlp')
- down_grad: float32 [8192, 2048], P('mlp', 'seq')
The draws below stay inside these ranges and needn't reach their ends.
Inputs may be any that keep to these rules, and one draw needn't show every extreme that they name: `frame_sizes`: each entry is 144 or 576; in every clip frame 0 has 576 and frame 1 has 144.
All inputs are finite; a program needn't handle non-finite values.
Results may differ from the reference program's by a relative error of at most 0.024.
Values may be sent and summed in bfloat16 or wider, within the bound.
No kernel may reach another device: no remote copies, remote signals or barrier semaphores. Data moves between devices by JAX's collectives and lax.ppermute only.
A program may use at most 192 MiB of HBM per device.

```python
import math
import jax
import jax.numpy as jnp
from jax import lax

D = 2048
HEADS = 16
HEAD_DIM = 128
FF = 8192
TOK_DEV = 128
CLIPS = 1
TOKENS = 1024
CLIP_LEN = 1024
SHARDS = 8
PIECE = 16
FRAMES = 8


def draw_frame_sizes(key, part):
    picks = jax.random.randint(key, (CLIPS, FRAMES), 0, 2)
    places = jnp.arange(FRAMES, dtype=jnp.int32)[None, :]
    picks = jnp.where(places == 0, 1, jnp.where(places == 1, 0, picks))
    return (144 + 432 * picks).astype(jnp.int32)


def with_ends(values, own_key, least, high):
    index_at = [jax.random.randint(jax.random.fold_in(own_key, axis), (), 0, length) for axis, length in enumerate(values.shape)]
    longest = values.shape.index(max(values.shape))
    next_to = index_at[:longest] + [(index_at[longest] + 1) % values.shape[longest]] + index_at[longest + 1:]
    return values.at[tuple(index_at)].set(least).at[tuple(next_to)].set(high)


def block_levels(rng, dims, shards, low, largest):
    def one(position, blocks):
        draws = jax.random.uniform(jax.random.fold_in(jax.random.fold_in(rng, 6), position), (blocks,), jnp.float32, low / len(shards), largest / len(shards))
        return jnp.repeat(jnp.exp(draws), dims[position] // blocks).reshape((-1,) + (1,) * (len(dims) - position - 1))

    level = one(*shards[0])
    for cut in shards[1:]:
        level = level * one(*cut)
    return level


def noise(own_key, extent, scale, bound, pieces=(), kind=jnp.bfloat16):
    values = jax.random.normal(own_key, extent, jnp.float32) * scale
    if len(pieces) > 0:
        values = block_levels(own_key, extent, pieces, -0.22, 0.18) * values
    return jnp.clip(values, min=-bound, max=bound).astype(kind)


def setup_inputs(seed: int = 0) -> dict:
    splits = jax.random.split(jax.random.key(seed), 14)
    inputs = noise(splits[0], (TOKENS, D), 1.0, 6.0, ((0, 8),))
    first_gain = jnp.clip(1.0 + 0.18 * jax.random.normal(splits[1], (3, D), jnp.float32), 0.1, 1.9)
    query_weight = noise(splits[2], (D, D), (D // 2) ** -0.5, 0.1875, ((1, 4),))
    key_weight = noise(splits[3], (D, D), D ** -0.5, 0.125, ((1, 4),))
    value_weight = noise(splits[4], (D, D), D ** -0.5, 0.125, ((1, 4),))
    output_weight = noise(splits[5], (D, D), (max(2, 32 * D // CLIP_LEN)) ** -0.5, 0.75, ((0, 4),))
    second_gain = jnp.clip(1.0 + 0.18 * jax.random.normal(splits[6], (3, D), jnp.float32), 0.1, 1.9)
    up_weight = noise(splits[7], (D, FF), D ** -0.5, 0.125, ((1, 4),))
    down_weight = noise(splits[8], (FF, D), FF ** -0.5, 0.0625, ((0, 4),))
    frame_sizes = draw_frame_sizes(jax.random.fold_in(splits[13], 71), 0)
    text_counts = with_ends(jax.random.randint(splits[10], (CLIPS, FRAMES), 1, 33), jax.random.fold_in(splits[10], 1), 1, 32).astype(jnp.int32)
    action_counts = with_ends(jax.random.randint(splits[11], (CLIPS, FRAMES), 1, 3), jax.random.fold_in(splits[11], 1), 1, 2).astype(jnp.int32)
    cotangent = noise(splits[12], (TOKENS, D), 1.0, 6.0, ((0, 8),))
    return {"inputs": inputs, "first_gain": first_gain, "query_weight": query_weight, "key_weight": key_weight, "value_weight": value_weight, "output_weight": output_weight, "second_gain": second_gain, "up_weight": up_weight, "down_weight": down_weight, "frame_sizes": frame_sizes, "text_counts": text_counts, "action_counts": action_counts, "cotangent": cotangent}


epsilon = 1e-05
highest = lax.Precision.HIGHEST

@jax.custom_vjp
def low(v):
    return lax.optimization_barrier(v.astype(jnp.bfloat16)).astype(jnp.float32)

@jax.custom_vjp
def low_back(v):
    return v

def low_keep(v):
    return (low(v), None)

def low_pass(kept, grad):
    return (grad,)

def back_keep(v):
    return (v, None)

def back_low(kept, grad):
    return (low(grad),)
low.defvjp(low_keep, low_pass)
low_back.defvjp(back_keep, back_low)

def modality_kinds(frame_sizes, text_counts, action_counts, clip_length):
    lengths = text_counts + action_counts + frame_sizes
    starts = jnp.cumsum(lengths, axis=1) - lengths
    text_end = starts + text_counts
    action_end = text_end + action_counts
    place = jnp.arange(clip_length, dtype=jnp.int32)[None, :, None]
    in_text = lax.optimization_barrier(jnp.sum(((place >= starts[:, None, :]) & (place < text_end[:, None, :])).astype(jnp.int32), axis=2))
    in_action = lax.optimization_barrier(jnp.sum(((place >= text_end[:, None, :]) & (place < action_end[:, None, :])).astype(jnp.int32), axis=2))
    return (in_action + 2 * (1 - in_text - in_action)).reshape(-1)

def sorted_rank(kinds):
    onehot = (kinds[:, None] == jnp.arange(3, dtype=jnp.int32)[None, :]).astype(jnp.int32)
    counts = lax.optimization_barrier(jnp.sum(onehot, axis=0))
    before = jnp.cumsum(counts) - counts
    within = jnp.cumsum(onehot, axis=0) - onehot
    return lax.optimization_barrier(jnp.sum(onehot * (within + before[None, :]), axis=1))

def gain_rows(gain, kinds):
    column = kinds[:, None]
    return jnp.where(column == 0, gain[0][None, :], jnp.where(column == 1, gain[1][None, :], gain[2][None, :]))

def layer_norm(values, gains):
    mean = lax.optimization_barrier(jnp.mean(values, axis=-1, keepdims=True))
    centered = values - mean
    variance = lax.optimization_barrier(jnp.mean(centered * centered, axis=-1, keepdims=True))
    return centered * lax.rsqrt(variance + epsilon) * gains

def attend(query, keys, values):
    scale = 1.0 / math.sqrt(HEAD_DIM)
    block = math.gcd(CLIP_LEN, 512)
    count = CLIP_LEN // block
    starts = jnp.arange(count, dtype=jnp.int32) * block

    def one_clip(item):
        clip_query, clip_keys, clip_values = item

        def one_block(inner):
            rows, start = inner
            raw = jnp.einsum('qhd,khd->hqk', rows, clip_keys, precision=highest) * scale
            scores = low_back(raw)
            here = start + jnp.arange(block, dtype=jnp.int32)
            there = jnp.arange(CLIP_LEN, dtype=jnp.int32)
            allowed = there[None, :] <= here[:, None]
            masked = jnp.where(allowed[None], scores, -jnp.inf)
            weights = jnp.exp(masked - lax.optimization_barrier(jnp.max(masked, axis=2, keepdims=True)))
            prob = low(weights / lax.optimization_barrier(jnp.sum(weights, axis=2, keepdims=True)))
            return jnp.einsum('hqk,khd->qhd', prob, clip_values, precision=highest)
        result = lax.map(jax.checkpoint(one_block), (clip_query.reshape(count, block, HEADS, HEAD_DIM), starts))
        return result.reshape(CLIP_LEN, D)
    shaped = tuple((matrix.reshape(CLIPS, CLIP_LEN, HEADS, HEAD_DIM) for matrix in (query, keys, values)))
    return lax.map(one_clip, shaped).reshape(TOKENS, D)

def layer(rows, first_gain, query_weight, key_weight, value_weight, output_weight, second_gain, up_weight, down_weight, kinds):
    normed = low(layer_norm(rows, gain_rows(first_gain, kinds)))
    query = low(low_back(jnp.dot(normed, query_weight, precision=highest)))
    keys = low(low_back(jnp.dot(normed, key_weight, precision=highest)))
    values = low(low_back(jnp.dot(normed, value_weight, precision=highest)))
    attended = low(low_back(attend(query, keys, values)))
    residual = rows + low_back(jnp.dot(attended, output_weight, precision=highest))
    block = math.gcd(TOKENS, 4096)

    def feed(item):
        block_rows, block_kinds = item
        lifted = low(layer_norm(block_rows, gain_rows(second_gain, block_kinds)))
        hidden = low_back(jnp.dot(lifted, up_weight, precision=highest))
        activated = low(jax.nn.gelu(hidden, approximate=True))
        return block_rows + jnp.dot(activated, down_weight, precision=highest)
    result = lax.map(jax.checkpoint(feed), (residual.reshape(-1, block, D), kinds.reshape(-1, block)))
    return result.reshape(TOKENS, D)

def reference(inputs, first_gain, query_weight, key_weight, value_weight, output_weight, second_gain, up_weight, down_weight, frame_sizes, text_counts, action_counts, cotangent):
    kinds = modality_kinds(frame_sizes, text_counts, action_counts, CLIP_LEN)
    ranks = jax.vmap(sorted_rank)(kinds.reshape(SHARDS, TOK_DEV))
    source = jnp.arange(SHARDS, dtype=jnp.int32)[:, None]
    row_place = (ranks // PIECE * TOK_DEV + ranks % PIECE * SHARDS + source).reshape(TOKENS).astype(jnp.int32)
    ordered_inputs = inputs[row_place].astype(jnp.float32)
    ordered_cotangent = cotangent[row_place].astype(jnp.float32)

    def forward(rows, gain_first, weight_query, weight_key, weight_value, weight_output, gain_second, weight_up, weight_down):
        return layer(rows, gain_first, weight_query, weight_key, weight_value, weight_output, gain_second, weight_up, weight_down, kinds)
    result, pullback = jax.vjp(forward, ordered_inputs, first_gain, query_weight.astype(jnp.float32), key_weight.astype(jnp.float32), value_weight.astype(jnp.float32), output_weight.astype(jnp.float32), second_gain, up_weight.astype(jnp.float32), down_weight.astype(jnp.float32))
    grads = pullback(ordered_cotangent)
    outputs = jnp.zeros((TOKENS, D), jnp.bfloat16).at[row_place].set(result.astype(jnp.bfloat16))
    input_grad = jnp.zeros((TOKENS, D), jnp.bfloat16).at[row_place].set(grads[0].astype(jnp.bfloat16))
    return (outputs, input_grad, grads[1], grads[2], grads[3], grads[4], grads[5], grads[6], grads[7], grads[8])
```

```python
from functools import partial
import math

import jax
import jax.numpy as jnp
from jax import lax
from jax.experimental import pallas as pl
from jax.experimental.pallas import tpu as pltpu
from jax.sharding import PartitionSpec as P

HEAD_DIM = 128
epsilon = 1e-05
bf16 = jnp.bfloat16
f32 = jnp.float32
NEGATIVE = -1e30


def dot(a, b, dims):
    return lax.dot_general(a, b, (dims, ((), ())), preferred_element_type=f32)


NN = ((1,), (0,))
NT = ((1,), (1,))
TN = ((0,), (0,))


def swap(value, axis, bit):
    size = lax.axis_size(axis)
    return lax.ppermute(value, axis, [(i, i ^ bit) for i in range(size)])


def gather_seq(piece):
    size = lax.axis_size("seq")
    inner = 1 << (int(math.log2(size)) // 2)
    pieces = {0: piece}
    for outer in range(inner, size, inner):
        pieces[outer] = swap(piece, "seq", outer)
    for outer in range(0, size, inner):
        for bit in range(1, inner):
            pieces[outer | bit] = swap(pieces[outer], "seq", bit)
    return [pieces[d] for d in range(size)]


def gather_rows(half):
    mine = jnp.concatenate(gather_seq(half), axis=0)
    return jnp.concatenate([mine, swap(mine, "mlp", 1)], axis=0)


def rounded(value):
    return lax.optimization_barrier(value.astype(bf16))


def sum_mlp(partial_sum):
    half = partial_sum.shape[0] // 2
    came = swap(partial_sum[half:].astype(bf16), "mlp", 1)
    total = partial_sum[:half] + came.astype(f32)
    bit = 2
    while bit < lax.axis_size("mlp"):
        low = rounded(total)
        total = low.astype(f32) + swap(low, "mlp", bit).astype(f32)
        bit *= 2
    return total


def modality_kinds(frame_sizes, text_counts, action_counts, clip_length):
    lengths = text_counts + action_counts + frame_sizes
    frames = lengths.shape[1]
    earlier = jnp.arange(frames)[:, None] < jnp.arange(frames)[None, :]
    starts = jnp.sum(jnp.where(earlier[None], lengths[:, :, None], 0), axis=1)
    text_end = starts + text_counts
    action_end = text_end + action_counts
    place = jnp.arange(clip_length, dtype=jnp.int32)[None, :, None]
    in_text = (place >= starts[:, None, :]) & (place < text_end[:, None, :])
    in_action = (place >= text_end[:, None, :]) & (place < action_end[:, None, :])
    lower = jnp.sum(2 * in_text.astype(jnp.int32) + in_action.astype(jnp.int32), axis=2)
    return (2 - lower).reshape(-1)


def places_and_kinds(kinds, core, shard_index, shards, length):
    kinds = kinds.reshape(shards, length)
    order = jnp.arange(length, dtype=jnp.int32)
    mine, other = kinds[:, :, None], kinds[:, None, :]
    before = (other < mine) | ((other == mine) & (order[None, None, :] < order[None, :, None]))
    rank = jnp.sum(before.astype(jnp.int32), axis=2)
    piece = length // shards
    half = piece // 2
    halves = jnp.arange(2, dtype=jnp.int32)[:, None, None]
    offsets = jnp.arange(shards, dtype=jnp.int32)[None, :, None]
    rows = jnp.arange(half, dtype=jnp.int32)[None, None, :]
    wanted = ((shard_index ^ offsets) * piece + (core ^ halves) * half + rows).reshape(-1)
    hit = rank[None] == wanted[:, None, None]
    place = jnp.sum(jnp.where(hit, order[None, None, :], 0), axis=2)
    place = place + jnp.arange(shards, dtype=jnp.int32)[None, :] * length
    kind = jnp.sum(jnp.where(hit, kinds[None], 0), axis=2)
    return place.reshape(-1), kind.reshape(-1)


def gain_rows(gain, kinds):
    column = kinds[:, None]
    return jnp.where(
        column == 0, gain[0][None, :], jnp.where(column == 1, gain[1][None, :], gain[2][None, :])
    )


def normalize(values):
    mean = jnp.mean(values, axis=1, keepdims=True)
    centered = values - mean
    inverse = lax.rsqrt(jnp.mean(centered * centered, axis=1, keepdims=True) + epsilon)
    return (centered * inverse, inverse)


def norm_back(grad, normal, inverse, gains):
    scaled = grad * gains
    return inverse * (
        scaled
        - jnp.mean(scaled, axis=1, keepdims=True)
        - normal * jnp.mean(scaled * normal, axis=1, keepdims=True)
    )


def gelu_parts(value):
    rate = math.sqrt(2 / math.pi)
    square = value * value
    bent = jnp.tanh(rate * value * (1 + 0.044715 * square))
    upper = 0.5 * (1 + bent)
    slope = upper + 0.5 * value * (1 - bent * bent) * rate * (1 + 3 * 0.044715 * square)
    return value * upper, slope


def mask_of(key_place, query_place, clip_length, clips):
    allowed = key_place <= query_place
    if clips > 1:
        allowed = allowed & (key_place // clip_length == query_place // clip_length)
    return allowed


def weights_of(key, query, allowed, scale):
    scores = jnp.where(allowed, dot(key, query, NT) * scale, NEGATIVE)
    top = jnp.max(scores, axis=0, keepdims=True)
    weights = jnp.exp(scores - top)
    return weights * (1.0 / jnp.sum(weights, axis=0, keepdims=True))


def forward_kernel(query, key, value, key_place, query_place, out, *, scale, clip_length, clips):
    allowed = mask_of(key_place[...], query_place[...], clip_length, clips)
    prob = weights_of(key[...], query[...], allowed, scale).astype(bf16)
    out[...] = dot(prob, value[...], TN).astype(bf16)


def attend(query, key, value, key_place, query_place, clip_length, clips):
    rows, width = query.shape
    total = key.shape[0]
    heads = width // HEAD_DIM
    by_head = lambda h: (0, h)
    same = lambda h: (0, 0)
    return pl.pallas_call(
        partial(
            forward_kernel, scale=1.0 / math.sqrt(HEAD_DIM), clip_length=clip_length, clips=clips
        ),
        grid=(heads,),
        in_specs=[
            pl.BlockSpec((rows, HEAD_DIM), by_head),
            pl.BlockSpec((total, HEAD_DIM), by_head),
            pl.BlockSpec((total, HEAD_DIM), by_head),
            pl.BlockSpec((total, 1), same),
            pl.BlockSpec((1, rows), same),
        ],
        out_specs=pl.BlockSpec((rows, HEAD_DIM), by_head),
        out_shape=jax.ShapeDtypeStruct((rows, width), bf16),
        cost_estimate=pl.CostEstimate(
            flops=4 * rows * total * width,
            bytes_accessed=4 * total * width + 4 * rows * width,
            transcendentals=rows * total * heads,
        ),
        name="attend",
    )(query, key, value, key_place, query_place)


def backward_kernel(
    query,
    key,
    value,
    grad,
    key_place,
    query_place,
    attended,
    grad_query,
    grad_key,
    grad_value,
    key_sum,
    value_sum,
    *,
    scale,
    clip_length,
    clips,
):
    step = pl.program_id(1)
    allowed = mask_of(key_place[...], query_place[...], clip_length, clips)
    prob = weights_of(key[...], query[...], allowed, scale)
    low = prob.astype(bf16)
    attended[...] = dot(low, value[...], TN).astype(bf16)
    grad_prob = dot(value[...], grad[...], NT)
    delta = jnp.sum(prob * grad_prob, axis=0, keepdims=True)
    grad_score = (prob * (grad_prob - delta)).astype(bf16)
    grad_query[...] = (dot(grad_score, key[...], TN) * scale).astype(bf16)
    key_term = dot(grad_score, query[...], NN)
    value_term = dot(low, grad[...], NN)

    @pl.when(step == 0)
    def _():
        key_sum[...] = key_term
        value_sum[...] = value_term

    @pl.when(step > 0)
    def _():
        key_sum[...] += key_term
        value_sum[...] += value_term

    @pl.when(step == pl.num_programs(1) - 1)
    def _():
        grad_key[...] = (key_sum[...] * scale).astype(bf16)
        grad_value[...] = value_sum[...].astype(bf16)


def attend_back(query, key, value, grad, key_place, query_place, clip_length, clips):
    total, width = key.shape
    heads = width // HEAD_DIM
    block = min(256, total)
    by_block = lambda h, q: (q, h)
    by_head = lambda h, q: (0, h)
    return pl.pallas_call(
        partial(
            backward_kernel, scale=1.0 / math.sqrt(HEAD_DIM), clip_length=clip_length, clips=clips
        ),
        grid=(heads, total // block),
        in_specs=[
            pl.BlockSpec((block, HEAD_DIM), by_block),
            pl.BlockSpec((total, HEAD_DIM), by_head),
            pl.BlockSpec((total, HEAD_DIM), by_head),
            pl.BlockSpec((block, HEAD_DIM), by_block),
            pl.BlockSpec((total, 1), lambda h, q: (0, 0)),
            pl.BlockSpec((1, block), lambda h, q: (0, q)),
        ],
        out_specs=[
            pl.BlockSpec((block, HEAD_DIM), by_block),
            pl.BlockSpec((block, HEAD_DIM), by_block),
            pl.BlockSpec((total, HEAD_DIM), by_head),
            pl.BlockSpec((total, HEAD_DIM), by_head),
        ],
        out_shape=[jax.ShapeDtypeStruct((total, width), bf16)] * 4,
        scratch_shapes=[pltpu.VMEM((total, HEAD_DIM), f32)] * 2,
        cost_estimate=pl.CostEstimate(
            flops=12 * total * total * width,
            bytes_accessed=16 * total * width,
            transcendentals=total * total * heads,
        ),
        name="attend_back",
    )(query, key, value, grad, key_place, query_place)


def body(
    inputs,
    first_gain,
    query_weight,
    key_weight,
    value_weight,
    output_weight,
    second_gain,
    up_weight,
    down_weight,
    frame_sizes,
    text_counts,
    action_counts,
    cotangent,
):
    shards = lax.axis_size("seq")
    shard_index = lax.axis_index("seq")
    core = lax.axis_index("mlp") % 2
    length, width = inputs.shape
    total = length * shards
    half = length // 2
    clips = frame_sizes.shape[0]
    clip_length = total // clips
    part = width // shards

    def halves(rows):
        mine = lax.dynamic_slice_in_dim(rows, core * half, half, 0)
        other = lax.dynamic_slice_in_dim(rows, (1 - core) * half, half, 0)
        return mine, other

    def restore(mine, other):
        upper = jnp.where(core == 0, mine, other)
        lower = jnp.where(core == 0, other, mine)
        return jnp.concatenate([upper, lower], axis=0)

    def own(rows):
        pieces = rows.reshape(2, shards, half, rows.shape[1])
        return pieces[:, 0].reshape(length, rows.shape[1])

    def columns(rows):
        return lax.dynamic_slice_in_dim(rows, shard_index * part, part, 1)

    kinds_by_place = modality_kinds(frame_sizes, text_counts, action_counts, clip_length)
    place, kind = places_and_kinds(kinds_by_place, core, shard_index, shards, length)
    half_kind = kind[:half]
    place_row = place.reshape(1, total)
    place_column = place.reshape(total, 1)
    own_place_row = own(place_column).reshape(1, length)

    inputs_half, _ = halves(inputs)
    grad_half, grad_other = halves(cotangent)
    inputs_all = gather_rows(inputs_half)
    grad_all = gather_rows(grad_half)
    grad_own = jnp.concatenate([grad_half, grad_other], axis=0)

    normal_all, _ = normalize(inputs_all.astype(f32))
    normed_all = (normal_all * gain_rows(first_gain, kind)).astype(bf16)
    key_all = dot(normed_all, key_weight, NN).astype(bf16)
    value_all = dot(normed_all, value_weight, NN).astype(bf16)
    query_all = dot(normed_all, query_weight, NN).astype(bf16)
    heads_own = attend(
        own(query_all), key_all, value_all, place_column, own_place_row, clip_length, clips
    )
    inputs_wide = inputs_half.astype(f32)
    residual = inputs_wide + sum_mlp(dot(heads_own, output_weight, NN))

    second_rows = gain_rows(second_gain, half_kind)
    second_normal, second_inverse = normalize(residual)
    lifted_half = (second_normal * second_rows).astype(bf16)
    lifted_own = jnp.concatenate([lifted_half, swap(lifted_half, "mlp", 1)], axis=0)
    activated_own, slope_own = gelu_parts(dot(lifted_own, up_weight, NN))
    activated_own = activated_own.astype(bf16)
    hidden_grad_own = (dot(grad_own, down_weight, NT) * slope_own).astype(bf16)
    lifted_grad = sum_mlp(dot(hidden_grad_own, up_weight, NT))
    grad_residual = grad_half.astype(f32) + norm_back(
        lifted_grad, second_normal, second_inverse, second_rows
    )
    mixed_grad_half = grad_residual.astype(bf16)
    mixed_grad_own = jnp.concatenate(
        [mixed_grad_half, swap(mixed_grad_half, "mlp", 1)], axis=0
    )
    heads_grad_own = dot(mixed_grad_own, output_weight, NT).astype(bf16)
    outputs_half = (residual + sum_mlp(dot(activated_own, down_weight, NN))).astype(bf16)
    outputs = restore(outputs_half, swap(outputs_half, "mlp", 1))

    heads_grad_all = jnp.stack(
        [piece.reshape(2, half, -1) for piece in gather_seq(heads_grad_own)], axis=1
    ).reshape(total, -1)
    attended_all, query_low, key_low, value_low = attend_back(
        query_all, key_all, value_all, heads_grad_all, place_column, place_row, clip_length, clips
    )
    normed_term = (
        dot(own(query_low), query_weight, NT)
        + dot(own(key_low), key_weight, NT)
        + dot(own(value_low), value_weight, NT)
    )
    normed_grad = sum_mlp(normed_term)
    first_normal, first_inverse = normalize(inputs_wide)
    first_rows = gain_rows(first_gain, half_kind)
    input_grad_half = (
        grad_residual + norm_back(normed_grad, first_normal, first_inverse, first_rows)
    ).astype(bf16)
    input_grad = restore(input_grad_half, swap(input_grad_half, "mlp", 1))

    normed_part = columns(normed_all)
    query_grad = dot(normed_part, query_low, TN)
    key_grad = dot(normed_part, key_low, TN)
    value_grad = dot(normed_part, value_low, TN)

    came = lax.all_to_all(
        mixed_grad_half.reshape(half, shards, part), "seq", split_axis=1, concat_axis=0, tiled=False
    )
    mixed_part = came[shard_index ^ jnp.arange(shards, dtype=jnp.int32)].reshape(half * shards, part)
    mixed_part = jnp.concatenate([mixed_part, swap(mixed_part, "mlp", 1)], axis=0)
    output_grad = dot(attended_all, mixed_part, TN)

    lifted_all = gather_rows(lifted_half)
    activated_all, slope_all = gelu_parts(dot(lifted_all, up_weight, NN))
    activated_all = activated_all.astype(bf16)
    hidden_grad_all = (dot(grad_all, down_weight, NT) * slope_all).astype(bf16)
    down_grad = dot(activated_all, columns(grad_all), TN)
    lifted_part = columns(lifted_all)
    up_grad = dot(lifted_part, hidden_grad_all, TN)

    def rows_of(weight):
        return lax.dynamic_slice_in_dim(weight, shard_index * part, part, 0)

    gain_part = gain_rows(columns(second_gain), kind)
    lifted_grad_part = dot(hidden_grad_all, rows_of(up_weight), NT)
    normed_grad_part = (
        dot(query_low, rows_of(query_weight), NT)
        + dot(key_low, rows_of(key_weight), NT)
        + dot(value_low, rows_of(value_weight), NT)
    )
    chosen = (kind[None, :] == jnp.arange(3, dtype=jnp.int32)[:, None]).astype(f32)
    second_term = lifted_grad_part * lifted_part.astype(f32) / gain_part
    first_term = normed_grad_part * columns(normal_all)
    gain_grads = lax.dot_general(
        chosen,
        jnp.concatenate([first_term, second_term], axis=1),
        (NN, ((), ())),
        precision=lax.Precision.HIGHEST,
        preferred_element_type=f32,
    )
    bit = 1
    while bit < lax.axis_size("mlp"):
        gain_grads = gain_grads + swap(gain_grads, "mlp", bit)
        bit *= 2

    return (
        outputs,
        input_grad,
        gain_grads[:, :part],
        query_grad,
        key_grad,
        value_grad,
        output_grad,
        gain_grads[:, part:],
        up_grad,
        down_grad,
    )


def solution(mesh):
    return jax.shard_map(
        body,
        mesh=mesh,
        in_specs=(
            P("seq", None),
            P(),
            P(None, "mlp"),
            P(None, "mlp"),
            P(None, "mlp"),
            P("mlp", None),
            P(),
            P(None, "mlp"),
            P("mlp", None),
            P(),
            P(),
            P(),
            P("seq", None),
        ),
        out_specs=(
            P("seq", None),
            P("seq", None),
            P(None, "seq"),
            P("seq", "mlp"),
            P("seq", "mlp"),
            P("seq", "mlp"),
            P("mlp", "seq"),
            P(None, "seq"),
            P("seq", "mlp"),
            P("mlp", "seq"),
        ),
        check_vma=False,
    )
```

```python
from functools import partial
import math

import jax
import jax.numpy as jnp
from jax import lax
from jax.experimental import pallas as pl
from jax.experimental.pallas import tpu as pltpu
from jax.sharding import PartitionSpec as P

HEAD_DIM = 128
epsilon = 1e-05
bf16 = jnp.bfloat16
f32 = jnp.float32
NEGATIVE = -1e30
VMEM_LIMIT = 60 * 1024 * 1024

NN = ((1,), (0,))
NT = ((1,), (1,))
TN = ((0,), (0,))


def dot(a, b, dims):
    return lax.dot_general(a, b, (dims, ((), ())), preferred_element_type=f32)


def params():
    return pltpu.CompilerParams(vmem_limit_bytes=VMEM_LIMIT)


def cost(flops, moved, transcendentals=0):
    return pl.CostEstimate(
        flops=int(flops), bytes_accessed=int(moved), transcendentals=int(transcendentals)
    )


def swap(value, axis, bit):
    size = lax.axis_size(axis)
    return lax.ppermute(value, axis, [(i, i ^ bit) for i in range(size)])


def inner_size():
    return 1 << (int(math.log2(lax.axis_size("seq"))) // 2)


def join_x(quarters):
    place = lax.axis_index("mlp") // 2
    bit = 1
    while 2 * bit < lax.axis_size("mlp"):
        other = swap(quarters, "mlp", 2 * bit)
        first = (place & bit) == 0
        quarters = jnp.concatenate(
            [jnp.where(first, quarters, other), jnp.where(first, other, quarters)], axis=1
        )
        bit *= 2
    return quarters


def own_quarter(half):
    rows = half.shape[0] // (lax.axis_size("mlp") // 2)
    return lax.dynamic_slice_in_dim(half, (lax.axis_index("mlp") // 2) * rows, rows, 0)


def gather_early(half):
    size, inner = lax.axis_size("seq"), inner_size()
    quarter = own_quarter(half)
    pieces = {0: half}
    far = {outer: swap(quarter, "seq", outer) for outer in range(inner, size, inner)}
    for bit in range(1, inner):
        pieces[bit] = swap(half, "seq", bit)
    for outer in range(inner, size, inner):
        pieces[outer] = join_x(far[outer][None])[0]
        for bit in range(1, inner):
            pieces[outer | bit] = swap(pieces[outer], "seq", bit)
    return [pieces[d] for d in range(size)]


def gather_late(half, after=None):
    size, inner = lax.axis_size("seq"), inner_size()
    quarter = own_quarter(half)
    if after is not None:
        quarter, half, _ = lax.optimization_barrier((quarter, half, after))
    far = jnp.stack([swap(quarter, "seq", outer) for outer in range(inner, size, inner)], axis=0)
    near = jnp.concatenate([half, join_x(far).reshape(-1, half.shape[1])], axis=0)
    return jnp.concatenate([near] + [swap(near, "seq", bit) for bit in range(1, inner)], axis=0)


def gather_order(size, inner):
    return [outer | bit for bit in range(inner) for outer in range(0, size, inner)]


def gather_pieces(piece):
    size, inner = lax.axis_size("seq"), inner_size()
    pieces = {0: piece}
    for outer in range(inner, size, inner):
        pieces[outer] = swap(piece, "seq", outer)
    for outer in range(0, size, inner):
        for bit in range(1, inner):
            pieces[outer | bit] = swap(pieces[outer], "seq", bit)
    return [pieces[d] for d in range(size)]


def rounded(value):
    return lax.optimization_barrier(value.astype(bf16))


def sum_mlp(partial_sum):
    half = partial_sum.shape[0] // 2
    came = swap(partial_sum[half:].astype(bf16), "mlp", 1)
    total = partial_sum[:half] + came.astype(f32)
    bit = 2
    while bit < lax.axis_size("mlp"):
        low = rounded(total)
        total = low.astype(f32) + swap(low, "mlp", bit).astype(f32)
        bit *= 2
    return total


def both(half):
    return jnp.concatenate([half, swap(half, "mlp", 1)], axis=0)


def modality_kinds(frame_sizes, text_counts, action_counts, clip_length):
    lengths = text_counts + action_counts + frame_sizes
    frames = lengths.shape[1]
    earlier = jnp.arange(frames)[:, None] < jnp.arange(frames)[None, :]
    starts = jnp.sum(jnp.where(earlier[None], lengths[:, :, None], 0), axis=1)
    text_end = starts + text_counts
    action_end = text_end + action_counts
    place = jnp.arange(clip_length, dtype=jnp.int32)[None, :, None]
    in_text = (place >= starts[:, None, :]) & (place < text_end[:, None, :])
    in_action = (place >= text_end[:, None, :]) & (place < action_end[:, None, :])
    lower = jnp.sum(2 * in_text.astype(jnp.int32) + in_action.astype(jnp.int32), axis=2)
    return (2 - lower).reshape(-1)


def places_and_kinds(kinds, core, shard_index, shards, length):
    kinds = kinds.reshape(shards, length)
    order = jnp.arange(length, dtype=jnp.int32)
    mine, other = kinds[:, :, None], kinds[:, None, :]
    before = (other < mine) | ((other == mine) & (order[None, None, :] < order[None, :, None]))
    rank = jnp.sum(before.astype(jnp.int32), axis=2)
    piece = length // shards
    half = piece // 2
    halves = jnp.arange(2, dtype=jnp.int32)[:, None, None]
    offsets = jnp.arange(shards, dtype=jnp.int32)[None, :, None]
    rows = jnp.arange(half, dtype=jnp.int32)[None, None, :]
    wanted = ((shard_index ^ offsets) * piece + (core ^ halves) * half + rows).reshape(-1)
    hit = rank[None] == wanted[:, None, None]
    packed = order[None, None, :] * 4 + kinds[None]
    found = jnp.sum(jnp.where(hit, packed, 0), axis=2)
    found = found.reshape(2, shards, half, shards).transpose(0, 1, 3, 2)
    kind = found & 3
    place = (found >> 2) + jnp.arange(shards, dtype=jnp.int32)[None, None, :, None] * length
    return place, kind


def gain_rows(gain, column):
    return jnp.where(
        column == 0, gain[0:1, :], jnp.where(column == 1, gain[1:2, :], gain[2:3, :])
    )


def normalize(values):
    mean = jnp.mean(values, axis=1, keepdims=True)
    centered = values - mean
    inverse = lax.rsqrt(jnp.mean(centered * centered, axis=1, keepdims=True) + epsilon)
    return (centered * inverse, inverse)


def norm_back(grad, normal, inverse, gains):
    scaled = grad * gains
    return inverse * (
        scaled
        - jnp.mean(scaled, axis=1, keepdims=True)
        - normal * jnp.mean(scaled * normal, axis=1, keepdims=True)
    )


def norm_kernel(*refs, groups):
    pieces, (gain, kind, out) = refs[:-3], refs[-3:]
    rows, width = pieces[0].shape
    for d, piece in enumerate(pieces):
        normal, _ = normalize(piece[...].astype(f32))
        column = kind[pl.ds(d * rows, rows), :]
        normed = (normal * gain_rows(gain, column)).astype(bf16)
        out[:, d] = normed.reshape(groups, rows // groups, width)


def norm_pieces(pieces, gain, kind, groups):
    rows, width = pieces[0].shape
    count = len(pieces)
    out = pl.pallas_call(
        partial(norm_kernel, groups=groups),
        out_shape=jax.ShapeDtypeStruct((groups, count, rows // groups, width), bf16),
        compiler_params=params(),
        cost_estimate=cost(10 * count * rows * width, 4 * count * rows * width),
        name="norm_pieces",
    )(*pieces, gain, kind)
    return out.reshape(count * rows, width)


def gelu_parts(value):
    rate = math.sqrt(2 / math.pi)
    square = value * value
    bent = jnp.tanh(value * (rate + (rate * 0.044715) * square))
    upper = 0.5 * (1 + bent)
    slope = upper + (0.5 * value) * (1 - bent * bent) * (rate + (rate * 3 * 0.044715) * square)
    return value * upper, slope


def own_kernel(lifted, up, grad_activated, activated, lifted_grad):
    value, slope = gelu_parts(dot(lifted[...], up[...], NN))
    activated[...] = value.astype(bf16)
    hidden_grad = (grad_activated[...] * slope).astype(bf16)
    term = dot(hidden_grad, up[...], NT)

    @pl.when(pl.program_id(0) == 0)
    def _():
        lifted_grad[...] = term

    @pl.when(pl.program_id(0) > 0)
    def _():
        lifted_grad[...] += term


def feed_own(lifted, up, grad_activated):
    rows, width = lifted.shape
    hidden = up.shape[1]
    tile = math.gcd(hidden, 256)
    across = lambda t: (0, t)
    whole = lambda t: (0, 0)
    return pl.pallas_call(
        own_kernel,
        grid=(hidden // tile,),
        in_specs=[
            pl.BlockSpec((rows, width), whole),
            pl.BlockSpec((width, tile), across),
            pl.BlockSpec((rows, tile), across),
        ],
        out_specs=[pl.BlockSpec((rows, tile), across), pl.BlockSpec((rows, width), whole)],
        out_shape=[
            jax.ShapeDtypeStruct((rows, hidden), bf16),
            jax.ShapeDtypeStruct((rows, width), f32),
        ],
        compiler_params=params(),
        cost_estimate=cost(4 * rows * width * hidden, 2 * width * hidden),
        name="feed_own",
    )(lifted, up, grad_activated)


def all_kernel(*refs, first):
    lifted, grad, lifted_part, grad_part, up, down, up_rows = refs[:7]
    up_grad, down_grad, part_grad = refs[-3:]
    value, slope = gelu_parts(dot(lifted[...], up[...], NN))
    activated = value.astype(bf16)
    hidden_grad = (dot(grad[...], down[...], NT) * slope).astype(bf16)
    down_term = dot(activated, grad_part[...], TN)
    up_term = dot(lifted_part[...], hidden_grad, TN)
    part_term = dot(hidden_grad, up_rows[...], NT)
    if not first:
        up_term += refs[7][...]
        down_term += refs[8][...]
    up_grad[...] = up_term
    down_grad[...] = down_term

    @pl.when(pl.program_id(0) == 0)
    def _():
        part_grad[...] = part_term

    @pl.when(pl.program_id(0) > 0)
    def _():
        part_grad[...] += part_term


def feed_all(lifted, grad, lifted_part, grad_part, up, down, up_rows, sums=()):
    rows, width = lifted.shape
    part = lifted_part.shape[1]
    hidden = up.shape[1]
    tile = math.gcd(hidden, 256)
    across = lambda t: (0, t)
    below = lambda t: (t, 0)
    whole = lambda t: (0, 0)
    sum_specs = [pl.BlockSpec((part, tile), across), pl.BlockSpec((tile, part), below)]
    return pl.pallas_call(
        partial(all_kernel, first=not sums),
        grid=(hidden // tile,),
        in_specs=[
            pl.BlockSpec((rows, width), whole),
            pl.BlockSpec((rows, width), whole),
            pl.BlockSpec((rows, part), whole),
            pl.BlockSpec((rows, part), whole),
            pl.BlockSpec((width, tile), across),
            pl.BlockSpec((tile, width), below),
            pl.BlockSpec((part, tile), across),
        ]
        + (sum_specs if sums else []),
        out_specs=sum_specs + [pl.BlockSpec((rows, part), whole)],
        out_shape=[
            jax.ShapeDtypeStruct((part, hidden), f32),
            jax.ShapeDtypeStruct((hidden, part), f32),
            jax.ShapeDtypeStruct((rows, part), f32),
        ],
        compiler_params=params(),
        cost_estimate=cost(
            2 * rows * hidden * (2 * width + 3 * part), 4 * width * hidden + 4 * rows * width
        ),
        name="feed_all",
    )(lifted, grad, lifted_part, grad_part, up, down, up_rows, *sums)


def mask_of(key_place, query_place, clip_length, clips):
    allowed = key_place <= query_place
    if clips > 1:
        allowed = allowed & (key_place // clip_length == query_place // clip_length)
    return allowed


def probabilities(scores, scale):
    top = scores[0].max(axis=0, keepdims=True)
    for block in scores[1:]:
        top = jnp.maximum(top, block.max(axis=0, keepdims=True))
    rate = scale * math.log2(math.e)
    weights = [jnp.exp2((block - top) * rate) for block in scores]
    total = weights[0].sum(axis=0, keepdims=True)
    for block in weights[1:]:
        total = total + block.sum(axis=0, keepdims=True)
    inverse = 1.0 / total
    return [block * inverse for block in weights]


def forward_kernel(query, key_a, key_b, value_a, value_b, place_a, place_b, query_place, out, **opts):
    scale = opts["scale"]
    query_place = query_place[...]
    allowed = [
        mask_of(place[...], query_place, opts["clip_length"], opts["clips"])
        for place in (place_a, place_b)
    ]
    for head in range(query.shape[1] // HEAD_DIM):
        at = pl.ds(head * HEAD_DIM, HEAD_DIM)
        scores = [
            jnp.where(mask, dot(key[:, at], query[:, at], NT), NEGATIVE)
            for mask, key in zip(allowed, (key_a, key_b))
        ]
        prob = [block.astype(bf16) for block in probabilities(scores, scale)]
        result = dot(prob[0], value_a[:, at], TN) + dot(prob[1], value_b[:, at], TN)
        out[:, at] = result.astype(bf16)


def attend(query, keys, values, places, query_place, clip_length, clips):
    rows, width = query.shape
    total = 2 * keys[0].shape[0]
    return pl.pallas_call(
        partial(
            forward_kernel, scale=1.0 / math.sqrt(HEAD_DIM), clip_length=clip_length, clips=clips
        ),
        out_shape=jax.ShapeDtypeStruct((rows, width), bf16),
        compiler_params=params(),
        cost_estimate=cost(
            4 * rows * total * width, 4 * total * width, rows * total * (width // HEAD_DIM)
        ),
        name="attend",
    )(query, *keys, *values, *places, query_place)


def backward_kernel(*refs, count, groups, scale, clip_length, clips):
    grads = refs[:count]
    query_a, query_b, key_a, key_b, value_a, value_b, place_a, place_b, query_place = refs[
        count : count + 9
    ]
    outs = refs[count + 9 : count + 20]
    attended, grad_query, grad_key, grad_value = outs[0:2], outs[2:4], outs[4:6], outs[6:8]
    own_query, own_key, own_value = outs[8:11]
    sums = refs[count + 20 :]
    half = key_a.shape[0]
    rows = half // count
    group_rows = rows // groups
    block = min(128, half)
    blocks = half // block

    def sources(index):
        found = []
        if groups == 1:
            for d in range(index * block // rows, (index + 1) * block // rows):
                found.append((d, 0, rows))
            return found
        each = count * group_rows
        for j in range(index * block // each, (index + 1) * block // each):
            for d in range(count):
                found.append((d, j * group_rows, group_rows))
        return found

    def keep_own(target, values, index):
        for side in range(2):
            at = side * block
            for d, start, size in sources(index):
                if d == 0:
                    target[pl.ds(side * rows + start, size), :] = values[at : at + size]
                at += size

    for ref in sums:
        ref[...] = jnp.zeros_like(ref)
    for index in range(blocks):
        mine = pl.ds(index * block, block)
        reach = (index + 1) * block if groups > 1 else half
        free = index * block if groups > 1 else 0
        query = jnp.concatenate([query_a[mine, :], query_b[mine, :]], axis=0)
        grad = jnp.concatenate(
            [
                grads[d][pl.ds(side * rows + start, size), :]
                for side in range(2)
                for d, start, size in sources(index)
            ],
            axis=0,
        )
        at_place = query_place[:, pl.ds(index * 2 * block, 2 * block)]
        spans = []
        for side in range(2):
            if free:
                spans.append((side, 0, free, False))
            spans.append((side, free, reach, True))
        keys, values, places = (key_a, key_b), (value_a, value_b), (place_a, place_b)
        scores = []
        for side, low, high, masked in spans:
            score = dot(keys[side][pl.ds(low, high - low), :], query, NT)
            if masked:
                place = places[side][pl.ds(low, high - low), :]
                score = jnp.where(mask_of(place, at_place, clip_length, clips), score, NEGATIVE)
            scores.append(score)
        prob = probabilities(scores, scale)
        lows = [part.astype(bf16) for part in prob]
        grad_prob = [
            dot(values[side][pl.ds(low, high - low), :], grad, NT) for side, low, high, _ in spans
        ]
        delta = sum((p * g).sum(axis=0, keepdims=True) for p, g in zip(prob, grad_prob))
        grad_score = [(p * (g - delta)).astype(bf16) for p, g in zip(prob, grad_prob)]
        result = sum(
            dot(part, values[side][pl.ds(low, high - low), :], TN)
            for part, (side, low, high, _) in zip(lows, spans)
        ).astype(bf16)
        back = (
            sum(
                dot(part, keys[side][pl.ds(low, high - low), :], TN)
                for part, (side, low, high, _) in zip(grad_score, spans)
            )
            * scale
        ).astype(bf16)
        for side in range(2):
            attended[side][mine, :] = result[side * block : (side + 1) * block]
            grad_query[side][mine, :] = back[side * block : (side + 1) * block]
        keep_own(own_query, back, index)
        for (side, low, high, _), score, part in zip(spans, grad_score, lows):
            at = pl.ds(low, high - low)
            sums[side][at, :] += dot(score, query, NN)
            sums[2 + side][at, :] += dot(part, grad, NN)
    low_key = [(sums[side][...] * scale).astype(bf16) for side in range(2)]
    low_value = [sums[2 + side][...].astype(bf16) for side in range(2)]
    for side in range(2):
        grad_key[side][...] = low_key[side]
        grad_value[side][...] = low_value[side]
    for index in range(blocks):
        cut = slice(index * block, (index + 1) * block)
        keep_own(own_key, jnp.concatenate([low[cut] for low in low_key], axis=0), index)
        keep_own(own_value, jnp.concatenate([low[cut] for low in low_value], axis=0), index)


def attend_back(grads, queries, keys, values, places, query_place, groups, clip_length, clips):
    half, width = keys[0].shape
    count = len(grads)
    heads = width // HEAD_DIM
    rows = grads[0].shape[0]
    by_head = lambda h: (0, h)
    whole = lambda h: (0, 0)
    tall = pl.BlockSpec((half, HEAD_DIM), by_head)
    short = pl.BlockSpec((rows, HEAD_DIM), by_head)
    outs = pl.pallas_call(
        partial(
            backward_kernel,
            count=count,
            groups=groups,
            scale=1.0 / math.sqrt(HEAD_DIM),
            clip_length=clip_length,
            clips=clips,
        ),
        grid=(heads,),
        in_specs=[short] * count
        + [tall] * 6
        + [pl.BlockSpec((half, 1), whole)] * 2
        + [pl.BlockSpec((1, 2 * half), whole)],
        out_specs=[tall] * 8 + [short] * 3,
        out_shape=[jax.ShapeDtypeStruct((half, width), bf16)] * 8
        + [jax.ShapeDtypeStruct((rows, width), bf16)] * 3,
        scratch_shapes=[pltpu.VMEM((half, HEAD_DIM), f32)] * 4,
        compiler_params=params(),
        cost_estimate=cost(
            12 * 4 * half * half * width, 32 * half * width, 4 * half * half * heads
        ),
        name="attend_back",
    )(*grads, *queries, *keys, *values, *places, query_place)
    return outs[0:2], outs[2:4], outs[4:6], outs[6:8], outs[8:11]


def body(
    inputs,
    first_gain,
    query_weight,
    key_weight,
    value_weight,
    output_weight,
    second_gain,
    up_weight,
    down_weight,
    frame_sizes,
    text_counts,
    action_counts,
    cotangent,
):
    shards = lax.axis_size("seq")
    shard_index = lax.axis_index("seq")
    core = lax.axis_index("mlp") % 2
    length, width = inputs.shape
    total = length * shards
    half = length // 2
    piece = half // shards
    clips = frame_sizes.shape[0]
    clip_length = total // clips
    part = width // shards
    groups = shards if piece % 8 == 0 else 1

    def halves(rows):
        cut = rows.reshape(2, piece, shards, width)
        mine = lax.dynamic_index_in_dim(cut, core, 0, keepdims=False)
        other = lax.dynamic_index_in_dim(cut, 1 - core, 0, keepdims=False)
        return (
            mine.transpose(1, 0, 2).reshape(half, width),
            other.transpose(1, 0, 2).reshape(half, width),
        )

    def restore(mine):
        other = swap(mine, "mlp", 1)
        upper = jnp.where(core == 0, mine, other)
        lower = jnp.where(core == 0, other, mine)
        rows = jnp.stack([upper, lower]).reshape(2, shards, piece, width)
        return rows.transpose(0, 2, 1, 3).reshape(length, width)

    def columns(rows):
        return lax.dynamic_slice_in_dim(rows, shard_index * part, part, 1)

    def rows_of(weight):
        return lax.dynamic_slice_in_dim(weight, shard_index * part, part, 0)

    kinds_by_place = modality_kinds(frame_sizes, text_counts, action_counts, clip_length)
    place, kind = places_and_kinds(kinds_by_place, core, shard_index, shards, length)

    def by_group(table):
        if groups == 1:
            return table.reshape(2, -1)
        return table.transpose(0, 2, 1, 3).reshape(2, -1)

    token_place = by_group(place)
    token_kind = by_group(kind)
    key_places = [token_place[side].reshape(-1, 1) for side in range(2)]
    block = min(128, total // 2)
    query_place = token_place.reshape(2, -1, block).transpose(1, 0, 2).reshape(1, total)
    own_place = place[:, 0].reshape(1, length)
    own_kind = kind[:, 0].reshape(length, 1)
    half_kind = own_kind[:half]
    piece_kind = kind[0].reshape(-1, 1)
    late = jnp.array(gather_order(shards, inner_size()), dtype=jnp.int32)
    late_kind = kind[:, late].reshape(2, -1, 1)

    inputs_half, inputs_other = halves(inputs)
    grad_half, grad_other = halves(cotangent)
    grad_own = jnp.concatenate([grad_half, grad_other], axis=0)
    pieces = gather_early(inputs_half)

    inputs_wide = inputs_half.astype(f32)
    own_normal, own_inverse = normalize(
        jnp.concatenate([inputs_half, inputs_other], axis=0).astype(f32)
    )
    own_normed = (own_normal * gain_rows(first_gain, own_kind)).astype(bf16)
    query_own = dot(own_normed, query_weight, NN).astype(bf16)
    own_activated_grad = dot(grad_own, down_weight, NT)

    normed = [norm_pieces(pieces, first_gain, piece_kind, groups)]
    normed.append(swap(normed[0], "mlp", 1))
    keys = [dot(rows, key_weight, NN).astype(bf16) for rows in normed]
    values = [dot(rows, value_weight, NN).astype(bf16) for rows in normed]
    heads_own = attend(query_own, keys, values, key_places, own_place, clip_length, clips)
    residual = inputs_wide + sum_mlp(dot(heads_own, output_weight, NN))
    queries = [dot(rows, query_weight, NN).astype(bf16) for rows in normed]

    grads = [gather_late(grad_half, after=pieces[-1])]
    grads.append(swap(grads[0], "mlp", 1))

    second_rows = gain_rows(second_gain, half_kind)
    second_normal, second_inverse = normalize(residual)
    lifted_half = (second_normal * second_rows).astype(bf16)
    lifted = [gather_late(lifted_half)]
    lifted.append(swap(lifted[0], "mlp", 1))
    activated_own, lifted_term = feed_own(both(lifted_half), up_weight, own_activated_grad)
    lifted_grad = sum_mlp(lifted_term)
    grad_residual = grad_half.astype(f32) + norm_back(
        lifted_grad, second_normal, second_inverse, second_rows
    )
    mixed_half = grad_residual.astype(bf16)
    heads_grad = dot(both(mixed_half), output_weight, NT).astype(bf16)
    outputs = restore((residual + sum_mlp(dot(activated_own, down_weight, NN))).astype(bf16))

    attended, query_low, key_low, value_low, own_low = attend_back(
        gather_pieces(heads_grad),
        queries,
        keys,
        values,
        key_places,
        query_place,
        groups,
        clip_length,
        clips,
    )
    attention_weights = (query_weight, key_weight, value_weight)
    normed_term = sum(dot(low, weight, NT) for low, weight in zip(own_low, attention_weights))
    normed_grad = sum_mlp(normed_term)
    input_grad = restore(
        (
            grad_residual
            + norm_back(
                normed_grad,
                own_normal[:half],
                own_inverse[:half],
                gain_rows(first_gain, half_kind),
            )
        ).astype(bf16)
    )

    normed_part = [columns(rows) for rows in normed]
    query_grad, key_grad, value_grad = (
        sum(dot(rows, low, TN) for rows, low in zip(normed_part, lows))
        for lows in (query_low, key_low, value_low)
    )

    came = lax.all_to_all(
        mixed_half.reshape(half, shards, part), "seq", split_axis=1, concat_axis=0, tiled=False
    )
    came = came[shard_index ^ jnp.arange(shards, dtype=jnp.int32)]
    if groups > 1:
        came = came.reshape(shards, shards, piece, part).transpose(1, 0, 2, 3)
    mixed_part = [came.reshape(-1, part)]
    mixed_part.append(swap(mixed_part[0], "mlp", 1))
    output_grad = sum(dot(rows, mixed, TN) for rows, mixed in zip(attended, mixed_part))

    up_rows = rows_of(up_weight)
    sums = ()
    lifted_grad_part = []
    lifted_part = [columns(rows) for rows in lifted]
    for side in range(2):
        *sums, part_grad = feed_all(
            lifted[side],
            grads[side],
            lifted_part[side],
            columns(grads[side]),
            up_weight,
            down_weight,
            up_rows,
            sums,
        )
        lifted_grad_part.append(part_grad)
    up_grad, down_grad = sums

    def gain_grad(grads_part, normed_parts, gain, kinds):
        result = 0
        for grad_part, normed_rows, column in zip(grads_part, normed_parts, kinds):
            term = grad_part * normed_rows.astype(f32) / gain_rows(gain, column)
            result = result + jnp.stack(
                [jnp.sum(jnp.where(column == k, term, 0.0), axis=0) for k in range(3)]
            )
        return result

    normed_grad_part = [
        sum(
            dot(lows[side], rows_of(weight), NT)
            for lows, weight in zip((query_low, key_low, value_low), attention_weights)
        )
        for side in range(2)
    ]
    gain_grads = jnp.concatenate(
        [
            gain_grad(
                normed_grad_part,
                normed_part,
                columns(first_gain),
                [token_kind[side].reshape(-1, 1) for side in range(2)],
            ),
            gain_grad(lifted_grad_part, lifted_part, columns(second_gain), late_kind),
        ],
        axis=1,
    )
    bit = 1
    while bit < lax.axis_size("mlp"):
        gain_grads = gain_grads + swap(gain_grads, "mlp", bit)
        bit *= 2

    return (
        outputs,
        input_grad,
        gain_grads[:, :part],
        query_grad,
        key_grad,
        value_grad,
        output_grad,
        gain_grads[:, part:],
        up_grad,
        down_grad,
    )


def solution(mesh):
    return jax.shard_map(
        body,
        mesh=mesh,
        in_specs=(
            P("seq", None),
            P(),
            P(None, "mlp"),
            P(None, "mlp"),
            P(None, "mlp"),
            P("mlp", None),
            P(),
            P(None, "mlp"),
            P("mlp", None),
            P(),
            P(),
            P(),
            P("seq", None),
        ),
        out_specs=(
            P("seq", None),
            P("seq", None),
            P(None, "seq"),
            P("seq", "mlp"),
            P("seq", "mlp"),
            P("seq", "mlp"),
            P("mlp", "seq"),
            P(None, "seq"),
            P("seq", "mlp"),
            P("mlp", "seq"),
        ),
        check_vma=False,
    )
```

```python
from functools import partial
import math

import jax
import jax.numpy as jnp
from jax import lax
from jax.experimental import pallas as pl
from jax.experimental.pallas import tpu as pltpu
from jax.sharding import PartitionSpec as P

HEAD_DIM = 128
epsilon = 1e-05
bf16 = jnp.bfloat16
f32 = jnp.float32
NEGATIVE = -1e30
VMEM_LIMIT = 60 * 1024 * 1024

NN = ((1,), (0,))
NT = ((1,), (1,))
TN = ((0,), (0,))


def dot(a, b, dims):
    return lax.dot_general(a, b, (dims, ((), ())), preferred_element_type=f32)


def params():
    return pltpu.CompilerParams(vmem_limit_bytes=VMEM_LIMIT)


def cost(flops, moved, transcendentals=0):
    return pl.CostEstimate(
        flops=int(flops), bytes_accessed=int(moved), transcendentals=int(transcendentals)
    )


def swap(value, axis, bit):
    size = lax.axis_size(axis)
    return lax.ppermute(value, axis, [(i, i ^ bit) for i in range(size)])


def inner_size():
    return 1 << (int(math.log2(lax.axis_size("seq"))) // 2)


def x_size():
    return lax.axis_size("mlp") // 2


def own_quarter(half):
    rows = half.shape[0] // x_size()
    return lax.dynamic_slice_in_dim(half, (lax.axis_index("mlp") // 2) * rows, rows, 0)


def join_x(quarter):
    bit = 1
    while bit < x_size():
        quarter = jnp.concatenate([quarter, swap(quarter, "mlp", 2 * bit)], axis=0)
        bit *= 2
    return quarter


def gather_early(half):
    size, inner = lax.axis_size("seq"), inner_size()
    quarter = own_quarter(half)
    pieces = {0: half}
    far = {outer: swap(quarter, "seq", outer) for outer in range(inner, size, inner)}
    for bit in range(1, inner):
        pieces[bit] = swap(half, "seq", bit)
    for outer in range(inner, size, inner):
        pieces[outer] = join_x(far[outer])
        for bit in range(1, inner):
            pieces[outer | bit] = swap(pieces[outer], "seq", bit)
    return [pieces[d] for d in range(size)]


def gather_late(half, after=None):
    size, inner = lax.axis_size("seq"), inner_size()
    quarter = own_quarter(half)
    if after is not None:
        quarter, half, _ = lax.optimization_barrier((quarter, half, after))
    far = [swap(quarter, "seq", outer) for outer in range(inner, size, inner)]
    near = jnp.concatenate([half, join_x(jnp.concatenate(far, axis=0))], axis=0)
    rows = [near] + [swap(near, "seq", bit) for bit in range(1, inner)]
    return rows, [swap(array, "mlp", 1) for array in rows]


def gather_pieces(piece):
    size, inner = lax.axis_size("seq"), inner_size()
    pieces = {0: piece}
    for outer in range(inner, size, inner):
        pieces[outer] = swap(piece, "seq", outer)
    for outer in range(0, size, inner):
        for bit in range(1, inner):
            pieces[outer | bit] = swap(pieces[outer], "seq", bit)
    return [pieces[d] for d in range(size)]


def rounded(value):
    return lax.optimization_barrier(value.astype(bf16))


def pair_mlp(partial_sum):
    half = partial_sum.shape[0] // 2
    came = swap(partial_sum[half:].astype(bf16), "mlp", 1)
    total = partial_sum[:half] + came.astype(f32)
    low, other = rounded(total), None
    bit = 2
    while bit < lax.axis_size("mlp"):
        if other is not None:
            low = rounded(low.astype(f32) + other.astype(f32))
        other = swap(low, "mlp", bit)
        bit *= 2
    if other is None:
        other = jnp.zeros_like(low)
    return low, other


def both(half):
    return jnp.concatenate([half, swap(half, "mlp", 1)], axis=0)


def tables_kernel(index, frames, texts, actions, *outs, shards, length, groups, clip_length):
    place_a, place_b, kind_a, kind_b, query_place, own_place, own_kind = outs
    shard_index, core = index[0], index[1]
    shape = (shards, length)
    place = lax.broadcasted_iota(jnp.int32, shape, 0) * length + lax.broadcasted_iota(
        jnp.int32, shape, 1
    )
    kinds = jnp.full(shape, 2, jnp.int32)
    for clip in range(frames.shape[0]):
        start = jnp.int32(clip * clip_length)
        within = (place >= clip * clip_length) & (place < (clip + 1) * clip_length)
        for frame in range(frames.shape[1]):
            text_end = start + texts[clip, frame]
            action_end = text_end + actions[clip, frame]
            kinds = jnp.where(within & (place >= start) & (place < text_end), 0, kinds)
            kinds = jnp.where(within & (place >= text_end) & (place < action_end), 1, kinds)
            start = action_end + frames[clip, frame]
    square = (length, length)
    down = lax.broadcasted_iota(jnp.int32, square, 0)
    across = lax.broadcasted_iota(jnp.int32, square, 1)
    earlier = (down < across).astype(f32).astype(bf16)
    rank = jnp.zeros(shape, f32)
    before = jnp.zeros((shards, 1), f32)
    for kind in range(3):
        chosen = (kinds == kind).astype(f32)
        rank += chosen * (dot(chosen.astype(bf16), earlier, NN) + before)
        before += chosen.sum(axis=1, keepdims=True)
    rank_low, kinds_low = rank.astype(bf16), kinds.astype(f32).astype(bf16)
    piece = length // shards // 2
    lane = lax.broadcasted_iota(jnp.int32, (1, length), 1).astype(f32)

    def find(shard, offset, side, row):
        wanted = (shard_index ^ offset) * (2 * piece) + (core ^ side) * piece + row
        pick = shard == lax.broadcasted_iota(jnp.int32, (length, shards), 1)
        pick = pick.astype(f32).astype(bf16)
        hit = dot(pick, rank_low, NN) == wanted.astype(f32)
        where = jnp.sum(jnp.where(hit, lane, 0.0), axis=1, keepdims=True).astype(jnp.int32)
        kind = jnp.sum(jnp.where(hit, dot(pick, kinds_low, NN), 0.0), axis=1, keepdims=True)
        return where + shard * length, kind.astype(jnp.int32)

    def as_row(column):
        return jnp.sum(jnp.where(down == across, column, 0), axis=0, keepdims=True)

    step = lax.broadcasted_iota(jnp.int32, (length, 1), 0)
    half = length // 2
    for side, (place_out, kind_out) in enumerate(((place_a, kind_a), (place_b, kind_b))):
        for block in range(shards // 2):
            token = step + block * length
            if groups > 1:
                shard, offset = token // (shards * piece), (token // piece) % shards
            else:
                offset, shard = token // half, (token % half) // piece
            where, kind = find(shard, offset, side, token % piece)
            at = pl.ds(block * length, length)
            place_out[at, :] = where
            kind_out[at, :] = kind
            query_place[:, pl.ds((2 * block + side) * length, length)] = as_row(where)
    where, kind = find((step % half) // piece, step * 0, step // half, step % piece)
    own_place[...] = as_row(where)
    own_kind[...] = kind


def tables(frames, texts, actions, shards, length, groups):
    index = jnp.stack([lax.axis_index("seq"), lax.axis_index("mlp") % 2]).astype(jnp.int32)
    total = shards * length
    column = jax.ShapeDtypeStruct((total // 2, 1), jnp.int32)
    return pl.pallas_call(
        partial(
            tables_kernel,
            shards=shards,
            length=length,
            groups=groups,
            clip_length=total // frames.shape[0],
        ),
        in_specs=[pl.BlockSpec(memory_space=pltpu.SMEM)] * 4,
        out_shape=[column] * 4
        + [
            jax.ShapeDtypeStruct((1, total), jnp.int32),
            jax.ShapeDtypeStruct((1, length), jnp.int32),
            jax.ShapeDtypeStruct((length, 1), jnp.int32),
        ],
        cost_estimate=cost(8 * total * length, 8 * 128 * total),
        name="tables",
    )(index, frames, texts, actions)


def gain_rows(gain, column):
    return jnp.where(
        column == 0, gain[0:1, :], jnp.where(column == 1, gain[1:2, :], gain[2:3, :])
    )


def normalize(values):
    mean = jnp.mean(values, axis=1, keepdims=True)
    centered = values - mean
    inverse = lax.rsqrt(jnp.mean(centered * centered, axis=1, keepdims=True) + epsilon)
    return (centered * inverse, inverse)


def norm_back(grad, normal, inverse, gains):
    scaled = grad * gains
    return inverse * (
        scaled
        - jnp.mean(scaled, axis=1, keepdims=True)
        - normal * jnp.mean(scaled * normal, axis=1, keepdims=True)
    )


def norm_kernel(*refs, groups, inner, parts):
    index, gain, kind, out = refs[0], refs[-3], refs[-2], refs[-1]
    pieces = refs[1:-3]
    rows, width = pieces[0].shape
    count = len(pieces)
    step = rows // parts
    for d, piece in enumerate(pieces):
        for part in range(parts):
            normal, _ = normalize(piece[pl.ds(part * step, step), :].astype(f32))
            place = part if d < inner else part ^ index[0]
            if groups > 1:
                each = groups // parts
                at = pl.ds(place * each, each)
                column = kind[at, d].reshape(step, 1)
                normed = (normal * gain_rows(gain, column)).astype(bf16)
                out[at, d] = normed.reshape(each, rows // groups, width)
            else:
                column = kind[d, place]
                out[d, place] = (normal * gain_rows(gain, column)).astype(bf16)


def norm_pieces(pieces, gain, kind, groups):
    rows, width = pieces[0].shape
    count = len(pieces)
    parts = x_size()
    if groups > 1:
        shape = (groups, count, rows // groups)
    else:
        shape = (count, parts, rows // parts)
    memory = [pl.BlockSpec(memory_space=pltpu.SMEM)]
    index = (lax.axis_index("mlp") // 2).astype(jnp.int32).reshape(1)
    out = pl.pallas_call(
        partial(norm_kernel, groups=groups, inner=inner_size(), parts=parts),
        in_specs=memory + [pl.BlockSpec(memory_space=pltpu.VMEM)] * (count + 2),
        out_shape=jax.ShapeDtypeStruct(shape + (width,), bf16),
        compiler_params=params(),
        cost_estimate=cost(10 * count * rows * width, 4 * count * rows * width),
        name="norm_pieces",
    )(index, *pieces, gain, kind.reshape(shape + (1,)))
    return out.reshape(count * rows, width)


def own_norm_kernel(rows, gain, kind, out):
    normal, _ = normalize(rows[...].astype(f32))
    out[...] = (normal * gain_rows(gain, kind[...])).astype(bf16)


def own_norm(rows, gain, kind):
    return pl.pallas_call(
        own_norm_kernel,
        out_shape=jax.ShapeDtypeStruct(rows.shape, bf16),
        compiler_params=params(),
        cost_estimate=cost(10 * rows.size, 4 * rows.size),
        name="own_norm",
    )(rows, gain, kind)


def lift_kernel(rows, low, other, gain, kind, residual, lifted):
    value = rows[...].astype(f32) + (low[...].astype(f32) + other[...].astype(f32))
    residual[...] = value
    normal, _ = normalize(value)
    lifted[...] = (normal * gain_rows(gain, kind[...])).astype(bf16)


def lift(rows, low, other, gain, kind):
    return pl.pallas_call(
        lift_kernel,
        out_shape=[jax.ShapeDtypeStruct(rows.shape, f32), jax.ShapeDtypeStruct(rows.shape, bf16)],
        compiler_params=params(),
        cost_estimate=cost(10 * rows.size, 12 * rows.size),
        name="lift",
    )(rows, low, other, gain, kind)


def kind_sums(term, kind):
    sums = [jnp.sum(jnp.where(kind == k, term, 0.0), axis=0, keepdims=True) for k in range(3)]
    high = [value.astype(bf16) for value in sums]
    low = [(value - part.astype(f32)).astype(bf16) for value, part in zip(sums, high)]
    zero = jnp.zeros((1, term.shape[1]), bf16)
    return jnp.concatenate(high + low + [zero, zero], axis=0)


def middle_kernel(residual, low, other, grad, gain, kind, grad_residual, mixed, sums):
    lifted_grad = low[...].astype(f32) + other[...].astype(f32)
    normal, inverse = normalize(residual[...])
    column = kind[...]
    back = norm_back(lifted_grad, normal, inverse, gain_rows(gain, column))
    value = grad[...].astype(f32) + back
    grad_residual[...] = value
    mixed[...] = value.astype(bf16)
    sums[...] = kind_sums(lifted_grad * normal, column)


def middle(residual, low, other, grad, gain, kind):
    width = residual.shape[1]
    return pl.pallas_call(
        middle_kernel,
        out_shape=[
            jax.ShapeDtypeStruct(residual.shape, f32),
            jax.ShapeDtypeStruct(residual.shape, bf16),
            jax.ShapeDtypeStruct((8, width), bf16),
        ],
        compiler_params=params(),
        cost_estimate=cost(20 * residual.size, 16 * residual.size),
        name="middle",
    )(residual, low, other, grad, gain, kind)


def last_kernel(rows, low, other, grad_residual, gain, kind, out):
    grad = low[...].astype(f32) + other[...].astype(f32)
    normal, inverse = normalize(rows[...].astype(f32))
    back = norm_back(grad, normal, inverse, gain_rows(gain, kind[...]))
    out[...] = (grad_residual[...] + back).astype(bf16)


def last(rows, low, other, grad_residual, gain, kind):
    return pl.pallas_call(
        last_kernel,
        out_shape=jax.ShapeDtypeStruct(rows.shape, bf16),
        compiler_params=params(),
        cost_estimate=cost(20 * rows.size, 12 * rows.size),
        name="last",
    )(rows, low, other, grad_residual, gain, kind)


def gelu_parts(value):
    rate = math.sqrt(2 / math.pi)
    square = value * value
    bent = jnp.tanh(value * (rate + (rate * 0.044715) * square))
    upper = 0.5 * (1 + bent)
    slope = upper + (0.5 * value) * (1 - bent * bent) * (rate + (rate * 3 * 0.044715) * square)
    return value * upper, slope


def own_kernel(lifted, up, grad_activated, activated, lifted_grad):
    value, slope = gelu_parts(dot(lifted[...], up[...], NN))
    activated[...] = value.astype(bf16)
    hidden_grad = (grad_activated[...] * slope).astype(bf16)
    term = dot(hidden_grad, up[...], NT)

    @pl.when(pl.program_id(0) == 0)
    def _():
        lifted_grad[...] = term

    @pl.when(pl.program_id(0) > 0)
    def _():
        lifted_grad[...] += term


def feed_own(lifted, up, grad_activated):
    rows, width = lifted.shape
    hidden = up.shape[1]
    tile = math.gcd(hidden, 512)
    across = lambda t: (0, t)
    whole = lambda t: (0, 0)
    return pl.pallas_call(
        own_kernel,
        grid=(hidden // tile,),
        in_specs=[
            pl.BlockSpec((rows, width), whole),
            pl.BlockSpec((width, tile), across),
            pl.BlockSpec((rows, tile), across),
        ],
        out_specs=[pl.BlockSpec((rows, tile), across), pl.BlockSpec((rows, width), whole)],
        out_shape=[
            jax.ShapeDtypeStruct((rows, hidden), bf16),
            jax.ShapeDtypeStruct((rows, width), f32),
        ],
        compiler_params=params(),
        cost_estimate=cost(4 * rows * width * hidden, 2 * width * hidden),
        name="feed_own",
    )(lifted, up, grad_activated)


def all_kernel(index, *refs, count, first):
    lifted, grad = refs[:count], refs[count : 2 * count]
    lifted_part, grad_part = refs[2 * count : 3 * count], refs[3 * count : 4 * count]
    up, down = refs[4 * count : 4 * count + 2]
    up_grad, down_grad = refs[-2:]
    up_sum = None if first else refs[4 * count + 2][...]
    down_sum = None if first else refs[4 * count + 3][...]
    for k in range(count):
        value, slope = gelu_parts(dot(lifted[k][...], up[...], NN))
        hidden_grad = (dot(grad[k][...], down[...], NT) * slope).astype(bf16)
        down_term = dot(value.astype(bf16), grad_part[k][...], TN)
        up_term = dot(lifted_part[k][...], hidden_grad, TN)
        up_sum = up_term if up_sum is None else up_sum + up_term
        down_sum = down_term if down_sum is None else down_sum + down_term
    up_grad[...] = up_sum
    down_grad[...] = down_sum


def feed_all(lifted, grad, up, down, shards, sums=()):
    rows, width = lifted[0].shape
    count = len(lifted)
    part = width // shards
    hidden = up.shape[1]
    tile = math.gcd(hidden, 256)
    across = lambda t, index: (0, t)
    below = lambda t, index: (t, 0)
    whole = lambda t, index: (0, 0)
    mine = lambda t, index: (0, index[0])
    sum_specs = [pl.BlockSpec((part, tile), across), pl.BlockSpec((tile, part), below)]
    index = lax.axis_index("seq").astype(jnp.int32).reshape(1)
    return pl.pallas_call(
        partial(all_kernel, count=count, first=not sums),
        grid_spec=pltpu.PrefetchScalarGridSpec(
            num_scalar_prefetch=1,
            grid=(hidden // tile,),
            in_specs=[pl.BlockSpec((rows, width), whole)] * (2 * count)
            + [pl.BlockSpec((rows, part), mine)] * (2 * count)
            + [pl.BlockSpec((width, tile), across), pl.BlockSpec((tile, width), below)]
            + (sum_specs if sums else []),
            out_specs=sum_specs,
        ),
        out_shape=[
            jax.ShapeDtypeStruct((part, hidden), f32),
            jax.ShapeDtypeStruct((hidden, part), f32),
        ],
        compiler_params=params(),
        cost_estimate=cost(
            4 * count * rows * hidden * (width + part), 4 * width * hidden + 4 * count * rows * width
        ),
        name="feed_all",
    )(index, *lifted, *grad, *lifted, *grad, up, down, *sums)


def project_kernel(index, *refs):
    normed, lows, weights = refs[0:2], refs[2:8], refs[8:11]
    gain, kinds = refs[11], refs[12:14]
    outs, gain_grad = refs[14:17], refs[17]
    for k in range(3):
        outs[k][...] = sum(dot(normed[side][...], lows[2 * k + side][...], TN) for side in range(2))
    gain_sum = [0.0, 0.0, 0.0]
    for side in range(2):
        column = kinds[side][...]
        term = sum(dot(lows[2 * k + side][...], weights[k][...], NT) for k in range(3))
        term = term * (normed[side][...].astype(f32) / gain_rows(gain, column))
        for k in range(3):
            gain_sum[k] += jnp.sum(jnp.where(column == k, term, 0.0), axis=0, keepdims=True)
    gain_grad[...] = jnp.concatenate(gain_sum, axis=0)


def project(normed, lows, weights, gain, kinds, shards):
    rows, width = normed[0].shape
    across = lows[0][0].shape[1]
    part = width // shards
    whole = lambda t, index: (0, 0)
    mine = lambda t, index: (0, index[0])
    below = lambda t, index: (index[0], 0)
    index = lax.axis_index("seq").astype(jnp.int32).reshape(1)
    return pl.pallas_call(
        project_kernel,
        grid_spec=pltpu.PrefetchScalarGridSpec(
            num_scalar_prefetch=1,
            grid=(1,),
            in_specs=[pl.BlockSpec((rows, part), mine)] * 2
            + [pl.BlockSpec((rows, across), whole)] * 6
            + [pl.BlockSpec((part, across), below)] * 3
            + [pl.BlockSpec((gain.shape[0], part), mine)]
            + [pl.BlockSpec((rows, 1), whole)] * 2,
            out_specs=[pl.BlockSpec((part, across), whole)] * 3
            + [pl.BlockSpec((gain.shape[0], part), whole)],
        ),
        out_shape=[jax.ShapeDtypeStruct((part, across), f32)] * 3
        + [jax.ShapeDtypeStruct((gain.shape[0], part), f32)],
        compiler_params=params(),
        cost_estimate=cost(24 * rows * part * across, 12 * rows * across + 12 * part * across),
        name="project",
    )(index, *normed, *[low for pair in lows for low in pair], *weights, gain, *kinds)


def mask_of(key_place, query_place, clip_length, clips):
    allowed = key_place <= query_place
    if clips > 1:
        allowed = allowed & (key_place // clip_length == query_place // clip_length)
    return allowed


def probabilities(scores, scale):
    top = scores[0].max(axis=0, keepdims=True)
    for block in scores[1:]:
        top = jnp.maximum(top, block.max(axis=0, keepdims=True))
    rate = scale * math.log2(math.e)
    weights = [jnp.exp2((block - top) * rate) for block in scores]
    total = weights[0].sum(axis=0, keepdims=True)
    for block in weights[1:]:
        total = total + block.sum(axis=0, keepdims=True)
    inverse = 1.0 / total
    return [block * inverse for block in weights]


def forward_kernel(query, key_a, key_b, value_a, value_b, place_a, place_b, query_place, out, **opts):
    scale = opts["scale"]
    query_place = query_place[...]
    allowed = [
        mask_of(place[...], query_place, opts["clip_length"], opts["clips"])
        for place in (place_a, place_b)
    ]
    for head in range(query.shape[1] // HEAD_DIM):
        at = pl.ds(head * HEAD_DIM, HEAD_DIM)
        scores = [
            jnp.where(mask, dot(key[:, at], query[:, at], NT), NEGATIVE)
            for mask, key in zip(allowed, (key_a, key_b))
        ]
        prob = [block.astype(bf16) for block in probabilities(scores, scale)]
        result = dot(prob[0], value_a[:, at], TN) + dot(prob[1], value_b[:, at], TN)
        out[:, at] = result.astype(bf16)


def attend(query, keys, values, places, query_place, clip_length, clips):
    rows, width = query.shape
    total = 2 * keys[0].shape[0]
    return pl.pallas_call(
        partial(
            forward_kernel, scale=1.0 / math.sqrt(HEAD_DIM), clip_length=clip_length, clips=clips
        ),
        out_shape=jax.ShapeDtypeStruct((rows, width), bf16),
        compiler_params=params(),
        cost_estimate=cost(
            4 * rows * total * width, 4 * total * width, rows * total * (width // HEAD_DIM)
        ),
        name="attend",
    )(query, *keys, *values, *places, query_place)


def backward_kernel(*refs, count, groups, scale, clip_length, clips):
    grads = refs[:count]
    query_a, query_b, key_a, key_b, value_a, value_b, place_a, place_b, query_place = refs[
        count : count + 9
    ]
    outs = refs[count + 9 : count + 20]
    attended, grad_query, grad_key, grad_value = outs[0:2], outs[2:4], outs[4:6], outs[6:8]
    own_query, own_key, own_value = outs[8:11]
    sums = refs[count + 20 :]
    half = key_a.shape[0]
    rows = half // count
    group_rows = rows // groups
    block = min(128, half)
    blocks = half // block

    def sources(index):
        found = []
        if groups == 1:
            for d in range(index * block // rows, (index + 1) * block // rows):
                found.append((d, 0, rows))
            return found
        each = count * group_rows
        for j in range(index * block // each, (index + 1) * block // each):
            for d in range(count):
                found.append((d, j * group_rows, group_rows))
        return found

    def keep_own(target, values, index):
        for side in range(2):
            at = side * block
            for d, start, size in sources(index):
                if d == 0:
                    target[pl.ds(side * rows + start, size), :] = values[at : at + size]
                at += size

    for ref in sums:
        ref[...] = jnp.zeros_like(ref)
    for index in range(blocks):
        mine = pl.ds(index * block, block)
        reach = (index + 1) * block if groups > 1 else half
        free = index * block if groups > 1 else 0
        query = jnp.concatenate([query_a[mine, :], query_b[mine, :]], axis=0)
        grad = jnp.concatenate(
            [
                grads[d][pl.ds(side * rows + start, size), :]
                for side in range(2)
                for d, start, size in sources(index)
            ],
            axis=0,
        )
        at_place = query_place[:, pl.ds(index * 2 * block, 2 * block)]
        spans = []
        for side in range(2):
            if free:
                spans.append((side, 0, free, False))
            spans.append((side, free, reach, True))
        keys, values, places = (key_a, key_b), (value_a, value_b), (place_a, place_b)
        scores = []
        for side, low, high, masked in spans:
            score = dot(keys[side][pl.ds(low, high - low), :], query, NT)
            if masked:
                place = places[side][pl.ds(low, high - low), :]
                score = jnp.where(mask_of(place, at_place, clip_length, clips), score, NEGATIVE)
            scores.append(score)
        prob = probabilities(scores, scale)
        lows = [part.astype(bf16) for part in prob]
        grad_prob = [
            dot(values[side][pl.ds(low, high - low), :], grad, NT) for side, low, high, _ in spans
        ]
        delta = sum((p * g).sum(axis=0, keepdims=True) for p, g in zip(prob, grad_prob))
        grad_score = [(p * (g - delta)).astype(bf16) for p, g in zip(prob, grad_prob)]
        result = sum(
            dot(part, values[side][pl.ds(low, high - low), :], TN)
            for part, (side, low, high, _) in zip(lows, spans)
        ).astype(bf16)
        back = (
            sum(
                dot(part, keys[side][pl.ds(low, high - low), :], TN)
                for part, (side, low, high, _) in zip(grad_score, spans)
            )
            * scale
        ).astype(bf16)
        for side in range(2):
            attended[side][mine, :] = result[side * block : (side + 1) * block]
            grad_query[side][mine, :] = back[side * block : (side + 1) * block]
        keep_own(own_query, back, index)
        for (side, low, high, _), score, part in zip(spans, grad_score, lows):
            at = pl.ds(low, high - low)
            sums[side][at, :] += dot(score, query, NN)
            sums[2 + side][at, :] += dot(part, grad, NN)
    low_key = [(sums[side][...] * scale).astype(bf16) for side in range(2)]
    low_value = [sums[2 + side][...].astype(bf16) for side in range(2)]
    for side in range(2):
        grad_key[side][...] = low_key[side]
        grad_value[side][...] = low_value[side]
    for index in range(blocks):
        cut = slice(index * block, (index + 1) * block)
        keep_own(own_key, jnp.concatenate([low[cut] for low in low_key], axis=0), index)
        keep_own(own_value, jnp.concatenate([low[cut] for low in low_value], axis=0), index)


def attend_back(grads, queries, keys, values, places, query_place, groups, clip_length, clips):
    half, width = keys[0].shape
    count = len(grads)
    heads = width // HEAD_DIM
    rows = grads[0].shape[0]
    by_head = lambda h: (0, h)
    whole = lambda h: (0, 0)
    tall = pl.BlockSpec((half, HEAD_DIM), by_head)
    short = pl.BlockSpec((rows, HEAD_DIM), by_head)
    outs = pl.pallas_call(
        partial(
            backward_kernel,
            count=count,
            groups=groups,
            scale=1.0 / math.sqrt(HEAD_DIM),
            clip_length=clip_length,
            clips=clips,
        ),
        grid=(heads,),
        in_specs=[short] * count
        + [tall] * 6
        + [pl.BlockSpec((half, 1), whole)] * 2
        + [pl.BlockSpec((1, 2 * half), whole)],
        out_specs=[tall] * 8 + [short] * 3,
        out_shape=[jax.ShapeDtypeStruct((half, width), bf16)] * 8
        + [jax.ShapeDtypeStruct((rows, width), bf16)] * 3,
        scratch_shapes=[pltpu.VMEM((half, HEAD_DIM), f32)] * 4,
        compiler_params=params(),
        cost_estimate=cost(
            12 * 4 * half * half * width, 32 * half * width, 4 * half * half * heads
        ),
        name="attend_back",
    )(*grads, *queries, *keys, *values, *places, query_place)
    return outs[0:2], outs[2:4], outs[4:6], outs[6:8], outs[8:11]


def body(
    inputs,
    first_gain,
    query_weight,
    key_weight,
    value_weight,
    output_weight,
    second_gain,
    up_weight,
    down_weight,
    frame_sizes,
    text_counts,
    action_counts,
    cotangent,
):
    shards = lax.axis_size("seq")
    shard_index = lax.axis_index("seq")
    core = lax.axis_index("mlp") % 2
    length, width = inputs.shape
    total = length * shards
    half = length // 2
    piece = half // shards
    clips = frame_sizes.shape[0]
    clip_length = total // clips
    part = width // shards
    groups = shards if piece % 8 == 0 else 1

    def halves(rows):
        cut = rows.reshape(2, piece, shards, width)
        mine = lax.dynamic_index_in_dim(cut, core, 0, keepdims=False)
        other = lax.dynamic_index_in_dim(cut, 1 - core, 0, keepdims=False)
        return (
            mine.transpose(1, 0, 2).reshape(half, width),
            other.transpose(1, 0, 2).reshape(half, width),
        )

    def restore(mine):
        other = swap(mine, "mlp", 1)
        upper = jnp.where(core == 0, mine, other)
        lower = jnp.where(core == 0, other, mine)
        rows = jnp.stack([upper, lower]).reshape(2, shards, piece, width)
        return rows.transpose(0, 2, 1, 3).reshape(length, width)

    inputs_half, inputs_other = halves(inputs)
    pieces = gather_early(inputs_half)
    grad_half, grad_other = halves(cotangent)
    grad_own = jnp.concatenate([grad_half, grad_other], axis=0)

    place_a, place_b, kind_a, kind_b, query_place, own_place, own_kind = tables(
        frame_sizes, text_counts, action_counts, shards, length, groups
    )
    places, kinds = (place_a, place_b), (kind_a, kind_b)
    half_kind = own_kind[:half]
    own_normed = own_norm(
        jnp.concatenate([inputs_half, inputs_other], axis=0), first_gain, own_kind
    )
    query_own = dot(own_normed, query_weight, NN).astype(bf16)
    own_activated_grad = dot(grad_own, down_weight, NT)

    normed = [norm_pieces(pieces, first_gain, kind_a, groups)]
    normed.append(swap(normed[0], "mlp", 1))
    keys = [dot(rows, key_weight, NN).astype(bf16) for rows in normed]
    values = [dot(rows, value_weight, NN).astype(bf16) for rows in normed]
    heads_own = attend(query_own, keys, values, places, own_place, clip_length, clips)
    low, other = pair_mlp(dot(heads_own, output_weight, NN))
    residual, lifted_half = lift(inputs_half, low, other, second_gain, half_kind)
    queries = [dot(rows, query_weight, NN).astype(bf16) for rows in normed]
    grads = gather_late(grad_half, after=pieces[-1])

    lifted = gather_late(lifted_half)
    activated_own, lifted_term = feed_own(both(lifted_half), up_weight, own_activated_grad)
    low, other = pair_mlp(lifted_term)
    grad_residual, mixed_half, second_sums = middle(
        residual, low, other, grad_half, second_gain, half_kind
    )
    heads_grad = dot(both(mixed_half), output_weight, NT).astype(bf16)
    low, other = pair_mlp(dot(activated_own, down_weight, NN))
    outputs = restore((residual + (low.astype(f32) + other.astype(f32))).astype(bf16))

    attended, query_low, key_low, value_low, own_low = attend_back(
        gather_pieces(heads_grad),
        queries,
        keys,
        values,
        places,
        query_place,
        groups,
        clip_length,
        clips,
    )
    attention_weights = (query_weight, key_weight, value_weight)
    normed_term = sum(dot(low, weight, NT) for low, weight in zip(own_low, attention_weights))
    low, other = pair_mlp(normed_term)
    input_grad = restore(last(inputs_half, low, other, grad_residual, first_gain, half_kind))

    query_grad, key_grad, value_grad, first_gain_grad = project(
        normed, (query_low, key_low, value_low), attention_weights, first_gain, kinds, shards
    )
    bit = 1
    while bit < lax.axis_size("mlp"):
        first_gain_grad = first_gain_grad + swap(first_gain_grad, "mlp", bit)
        bit *= 2

    came = lax.all_to_all(
        jnp.concatenate([mixed_half, second_sums], axis=0).reshape(half + 8, shards, part),
        "seq",
        split_axis=1,
        concat_axis=0,
        tiled=False,
    )
    second_sums = jnp.sum(came[:, half : half + 6].astype(f32), axis=0)
    second_sums = second_sums[:3] + second_sums[3:]
    second_gain_grad = second_sums + swap(second_sums, "mlp", 1)
    came = came[shard_index ^ jnp.arange(shards, dtype=jnp.int32), :half]
    if groups > 1:
        came = came.reshape(shards, shards, piece, part).transpose(1, 0, 2, 3)
    mixed_part = [came.reshape(-1, part)]
    mixed_part.append(swap(mixed_part[0], "mlp", 1))
    output_grad = sum(dot(rows, mixed, TN) for rows, mixed in zip(attended, mixed_part))

    sums = ()
    for side in range(2):
        sums = feed_all(lifted[side], grads[side], up_weight, down_weight, shards, sums)
    up_grad, down_grad = sums

    return (
        outputs,
        input_grad,
        first_gain_grad,
        query_grad,
        key_grad,
        value_grad,
        output_grad,
        second_gain_grad,
        up_grad,
        down_grad,
    )


def solution(mesh):
    return jax.shard_map(
        body,
        mesh=mesh,
        in_specs=(
            P("seq", None),
            P(),
            P(None, "mlp"),
            P(None, "mlp"),
            P(None, "mlp"),
            P("mlp", None),
            P(),
            P(None, "mlp"),
            P("mlp", None),
            P(),
            P(),
            P(),
            P("seq", None),
        ),
        out_specs=(
            P("seq", None),
            P("seq", None),
            P(None, "seq"),
            P("seq", "mlp"),
            P("seq", "mlp"),
            P("seq", "mlp"),
            P("mlp", "seq"),
            P(None, "seq"),
            P("seq", "mlp"),
            P("mlp", "seq"),
        ),
        check_vma=False,
    )
```

```python
from functools import partial
import math

import jax
import jax.numpy as jnp
from jax import lax
from jax.experimental import pallas as pl
from jax.experimental.pallas import tpu as pltpu
from jax.sharding import PartitionSpec as P

HEAD_DIM = 128
epsilon = 1e-05
bf16 = jnp.bfloat16
f32 = jnp.float32
NEGATIVE = -1e30

NN = ((1,), (0,))
NT = ((1,), (1,))
TN = ((0,), (0,))


def dot(a, b, dims):
    return lax.dot_general(a, b, (dims, ((), ())), preferred_element_type=f32)


def params(mebibytes):
    return pltpu.CompilerParams(vmem_limit_bytes=mebibytes * 1024 * 1024)


def cost(flops, moved, transcendentals=0, share=100):
    return pl.CostEstimate(
        flops=int(flops) // share,
        bytes_accessed=int(moved) // share,
        transcendentals=int(transcendentals) // share,
    )


def swap(value, axis, bit):
    size = lax.axis_size(axis)
    return lax.ppermute(value, axis, [(i, i ^ bit) for i in range(size)])


def inner_size():
    return 1 << (int(math.log2(lax.axis_size("seq"))) // 2)


def x_size():
    return lax.axis_size("mlp") // 2


def after(values, *earlier):
    return lax.optimization_barrier((values, earlier))[0]


def in_hbm(array):
    return pltpu.with_memory_space_constraint(array, pltpu.HBM)


def own_quarter(half):
    rows = half.shape[0] // x_size()
    return lax.dynamic_slice_in_dim(half, (lax.axis_index("mlp") // 2) * rows, rows, 0)


def join_x(quarter, *earlier):
    bit = 1
    while bit < x_size():
        came = after(swap(quarter, "mlp", 2 * bit), earlier)
        quarter = jnp.concatenate([quarter, came], axis=0)
        bit *= 2
    return quarter


def gather_early(half):
    size, inner = lax.axis_size("seq"), inner_size()
    quarter = own_quarter(half)
    pieces = {0: half}
    far = {outer: swap(quarter, "seq", outer) for outer in range(inner, size, inner)}
    for bit in range(1, inner):
        pieces[bit] = swap(half, "seq", bit)
    for outer in range(inner, size, inner):
        pieces[outer] = join_x(far[outer])
        for bit in range(1, inner):
            pieces[outer | bit] = swap(pieces[outer], "seq", bit)
    return [pieces[d] for d in range(size)]


def gather_outer(half):
    size, inner = lax.axis_size("seq"), inner_size()
    quarter = own_quarter(half)
    return [swap(quarter, "seq", outer) for outer in range(inner, size, inner)]


def gather_inner(array):
    return [swap(array, "seq", bit) for bit in range(1, inner_size())]


def with_core(arrays):
    return [each for array in arrays for each in (array, swap(array, "mlp", 1))]


def gather_first(piece):
    size, inner = lax.axis_size("seq"), inner_size()
    pieces = {0: piece}
    for bit in range(1, inner):
        pieces[bit] = swap(piece, "seq", bit)
    return pieces, [swap(piece, "seq", outer) for outer in range(inner, size, inner)]


def gather_pieces(pieces, far):
    size, inner = lax.axis_size("seq"), inner_size()
    for outer, came in zip(range(inner, size, inner), far):
        pieces[outer] = came
        for bit in range(1, inner):
            pieces[outer | bit] = swap(came, "seq", bit)
    return [pieces[d] for d in range(size)]


def rounded(value):
    return lax.optimization_barrier(value.astype(bf16))


def pair_mlp(mine, other_half):
    low, other = rounded(mine + swap(other_half, "mlp", 1).astype(f32)), None
    bit = 2
    while bit < lax.axis_size("mlp"):
        if other is not None:
            low = rounded(low.astype(f32) + other.astype(f32))
        other = swap(low, "mlp", bit)
        bit *= 2
    if other is None:
        other = jnp.zeros_like(low)
    return low, other


def both(half):
    return jnp.concatenate([half, swap(half, "mlp", 1)], axis=0)


def tables_kernel(index, frames, texts, actions, *outs, shards, length, groups, clip_length):
    place_a, place_b, kind_a, kind_b, query_place, own_place, own_kind = outs
    shard_index, core = index[0], index[1]
    shape = (shards, length)
    place = lax.broadcasted_iota(jnp.int32, shape, 0) * length + lax.broadcasted_iota(
        jnp.int32, shape, 1
    )
    kinds = jnp.full(shape, 2, jnp.int32)
    for clip in range(frames.shape[0]):
        start = jnp.int32(clip * clip_length)
        within = (place >= clip * clip_length) & (place < (clip + 1) * clip_length)
        for frame in range(frames.shape[1]):
            text_end = start + texts[clip, frame]
            action_end = text_end + actions[clip, frame]
            kinds = jnp.where(within & (place >= start) & (place < text_end), 0, kinds)
            kinds = jnp.where(within & (place >= text_end) & (place < action_end), 1, kinds)
            start = action_end + frames[clip, frame]
    square = (length, length)
    down = lax.broadcasted_iota(jnp.int32, square, 0)
    across = lax.broadcasted_iota(jnp.int32, square, 1)
    earlier = (down < across).astype(f32).astype(bf16)
    rank = jnp.zeros(shape, f32)
    before = jnp.zeros((shards, 1), f32)
    for kind in range(3):
        chosen = (kinds == kind).astype(f32)
        rank += chosen * (dot(chosen.astype(bf16), earlier, NN) + before)
        before += chosen.sum(axis=1, keepdims=True)
    rank_low, kinds_low = rank.astype(bf16), kinds.astype(f32).astype(bf16)
    piece = length // shards // 2
    lane = lax.broadcasted_iota(jnp.int32, (1, length), 1).astype(f32)

    def find(shard, offset, side, row):
        wanted = (shard_index ^ offset) * (2 * piece) + (core ^ side) * piece + row
        pick = shard == lax.broadcasted_iota(jnp.int32, (length, shards), 1)
        pick = pick.astype(f32).astype(bf16)
        hit = dot(pick, rank_low, NN) == wanted.astype(f32)
        where = jnp.sum(jnp.where(hit, lane, 0.0), axis=1, keepdims=True).astype(jnp.int32)
        kind = jnp.sum(jnp.where(hit, dot(pick, kinds_low, NN), 0.0), axis=1, keepdims=True)
        return where + shard * length, kind.astype(jnp.int32)

    def as_row(column):
        return jnp.sum(jnp.where(down == across, column, 0), axis=0, keepdims=True)

    step = lax.broadcasted_iota(jnp.int32, (length, 1), 0)
    half = length // 2
    for side, (place_out, kind_out) in enumerate(((place_a, kind_a), (place_b, kind_b))):
        for block in range(shards // 2):
            token = step + block * length
            if groups > 1:
                shard, offset = token // (shards * piece), (token // piece) % shards
            else:
                offset, shard = token // half, (token % half) // piece
            where, kind = find(shard, offset, side, token % piece)
            at = pl.ds(block * length, length)
            place_out[at, :] = where
            kind_out[at, :] = kind
            query_place[:, pl.ds((2 * block + side) * length, length)] = as_row(where)
    where, kind = find((step % half) // piece, step * 0, step // half, step % piece)
    own_place[...] = as_row(where)
    own_kind[...] = kind


def tables(frames, texts, actions, shards, length, groups):
    index = jnp.stack([lax.axis_index("seq"), lax.axis_index("mlp") % 2]).astype(jnp.int32)
    total = shards * length
    column = jax.ShapeDtypeStruct((total // 2, 1), jnp.int32)
    return pl.pallas_call(
        partial(
            tables_kernel,
            shards=shards,
            length=length,
            groups=groups,
            clip_length=total // frames.shape[0],
        ),
        in_specs=[pl.BlockSpec(memory_space=pltpu.SMEM)] * 4,
        out_shape=[column] * 4
        + [
            jax.ShapeDtypeStruct((1, total), jnp.int32),
            jax.ShapeDtypeStruct((1, length), jnp.int32),
            jax.ShapeDtypeStruct((length, 1), jnp.int32),
        ],
        cost_estimate=cost(8 * total * length, 8 * 128 * total),
        name="tables",
    )(index, frames, texts, actions)


def rows_kernel(*refs, count):
    rows, weights, outs = refs[0], refs[1 : 1 + count], refs[1 + count :]
    for weight, out in zip(weights, outs):
        out[...] = dot(rows[...], weight[...], NN).astype(bf16)


def project_rows(rows, *weights):
    across = weights[0].shape[1]
    return pl.pallas_call(
        partial(rows_kernel, count=len(weights)),
        out_shape=[jax.ShapeDtypeStruct((rows.shape[0], across), bf16)] * len(weights),
        compiler_params=params(16),
        cost_estimate=cost(2 * rows.size * across * len(weights), 2 * rows.size),
        name="project_rows",
    )(rows, *weights)


def one_kernel(rows, weight, out):
    out[...] = dot(rows[...], weight[...], NT).astype(bf16)


def product_back(rows, weight):
    return pl.pallas_call(
        one_kernel,
        out_shape=jax.ShapeDtypeStruct((rows.shape[0], weight.shape[0]), bf16),
        compiler_params=params(10),
        cost_estimate=cost(2 * rows.size * weight.shape[0], 2 * weight.size),
        name="product_back",
    )(rows, weight)


def halves_kernel(*refs, count, dims):
    mine, other = refs[-2:]
    half = mine.shape[0]
    total = sum(dot(refs[k][...], refs[count + k][...], dims) for k in range(count))
    mine[...] = total[:half]
    other[...] = total[half:].astype(bf16)


def product_halves(rows, weights, dims):
    count = len(rows)
    half = rows[0].shape[0] // 2
    across = weights[0].shape[1 - dims[1][0]]
    shape = (half, across)
    return pl.pallas_call(
        partial(halves_kernel, count=count, dims=dims),
        out_shape=[jax.ShapeDtypeStruct(shape, f32), jax.ShapeDtypeStruct(shape, bf16)],
        compiler_params=params(16),
        cost_estimate=cost(2 * count * rows[0].size * across, 2 * count * weights[0].size),
        name="product_halves",
    )(*rows, *weights)


def down_own_kernel(rows, weight, mine, other, total):
    term = dot(rows[...], weight[...], NN)

    @pl.when(pl.program_id(0) == 0)
    def _():
        total[...] = term

    @pl.when(pl.program_id(0) > 0)
    def _():
        total[...] += term

    @pl.when(pl.program_id(0) == pl.num_programs(0) - 1)
    def _():
        half = mine.shape[0]
        mine[...] = total[:half]
        other[...] = total[half:].astype(bf16)


def down_own(rows, weight):
    count, deep = rows.shape
    across = weight.shape[1]
    tile = math.gcd(deep, 512)
    shape = (count // 2, across)
    whole = pl.BlockSpec(shape, lambda t: (0, 0))
    return pl.pallas_call(
        down_own_kernel,
        grid=(deep // tile,),
        in_specs=[
            pl.BlockSpec((count, tile), lambda t: (0, t)),
            pl.BlockSpec((tile, across), lambda t: (t, 0)),
        ],
        out_specs=[whole, whole],
        out_shape=[jax.ShapeDtypeStruct(shape, f32), jax.ShapeDtypeStruct(shape, bf16)],
        scratch_shapes=[pltpu.VMEM((count, across), f32)],
        compiler_params=params(12),
        cost_estimate=cost(2 * rows.size * across, 2 * weight.size),
        name="down_own",
    )(rows, in_hbm(weight))


def gain_rows(gain, column):
    return jnp.where(
        column == 0, gain[0:1, :], jnp.where(column == 1, gain[1:2, :], gain[2:3, :])
    )


def normalize(values):
    mean = jnp.mean(values, axis=1, keepdims=True)
    centered = values - mean
    inverse = lax.rsqrt(jnp.mean(centered * centered, axis=1, keepdims=True) + epsilon)
    return (centered * inverse, inverse)


def norm_back(grad, normal, inverse, gains):
    scaled = grad * gains
    return inverse * (
        scaled
        - jnp.mean(scaled, axis=1, keepdims=True)
        - normal * jnp.mean(scaled * normal, axis=1, keepdims=True)
    )


def norm_kernel(*refs, groups, inner, parts):
    index, gain, kind, out = refs[0], refs[-3], refs[-2], refs[-1]
    pieces = refs[1:-3]
    rows, width = pieces[0].shape
    count = len(pieces)
    step = rows // parts
    for d, piece in enumerate(pieces):
        for part in range(parts):
            normal, _ = normalize(piece[pl.ds(part * step, step), :].astype(f32))
            place = part if d < inner else part ^ index[0]
            if groups > 1:
                each = groups // parts
                at = pl.ds(place * each, each)
                column = kind[at, d].reshape(step, 1)
                normed = (normal * gain_rows(gain, column)).astype(bf16)
                out[at, d] = normed.reshape(each, rows // groups, width)
            else:
                column = kind[d, place]
                out[d, place] = (normal * gain_rows(gain, column)).astype(bf16)


def norm_pieces(pieces, gain, kind, groups):
    rows, width = pieces[0].shape
    count = len(pieces)
    parts = x_size()
    if groups > 1:
        shape = (groups, count, rows // groups)
    else:
        shape = (count, parts, rows // parts)
    memory = [pl.BlockSpec(memory_space=pltpu.SMEM)]
    index = (lax.axis_index("mlp") // 2).astype(jnp.int32).reshape(1)
    out = pl.pallas_call(
        partial(norm_kernel, groups=groups, inner=inner_size(), parts=parts),
        in_specs=memory + [pl.BlockSpec(memory_space=pltpu.VMEM)] * (count + 2),
        out_shape=jax.ShapeDtypeStruct(shape + (width,), bf16),
        compiler_params=params(20),
        cost_estimate=cost(10 * count * rows * width, 4 * count * rows * width),
        name="norm_pieces",
    )(index, *pieces, gain, kind.reshape(shape + (1,)))
    return out.reshape(count * rows, width)


def own_norm_kernel(rows, gain, kind, out):
    normal, _ = normalize(rows[...].astype(f32))
    out[...] = (normal * gain_rows(gain, kind[...])).astype(bf16)


def own_norm(rows, gain, kind):
    return pl.pallas_call(
        own_norm_kernel,
        out_shape=jax.ShapeDtypeStruct(rows.shape, bf16),
        compiler_params=params(8),
        cost_estimate=cost(10 * rows.size, 4 * rows.size),
        name="own_norm",
    )(rows, gain, kind)


def lift_kernel(rows, low, other, gain, kind, residual, lifted):
    value = rows[...].astype(f32) + (low[...].astype(f32) + other[...].astype(f32))
    residual[...] = value
    normal, _ = normalize(value)
    lifted[...] = (normal * gain_rows(gain, kind[...])).astype(bf16)


def lift(rows, low, other, gain, kind):
    return pl.pallas_call(
        lift_kernel,
        out_shape=[jax.ShapeDtypeStruct(rows.shape, f32), jax.ShapeDtypeStruct(rows.shape, bf16)],
        compiler_params=params(8),
        cost_estimate=cost(10 * rows.size, 12 * rows.size),
        name="lift",
    )(rows, low, other, gain, kind)


def kind_sums(term, kind):
    sums = [jnp.sum(jnp.where(kind == k, term, 0.0), axis=0, keepdims=True) for k in range(3)]
    high = [value.astype(bf16) for value in sums]
    low = [(value - part.astype(f32)).astype(bf16) for value, part in zip(sums, high)]
    zero = jnp.zeros((1, term.shape[1]), bf16)
    return jnp.concatenate(high + low + [zero, zero], axis=0)


def middle_kernel(residual, low, other, grad, gain, kind, grad_residual, mixed, sums):
    lifted_grad = low[...].astype(f32) + other[...].astype(f32)
    normal, inverse = normalize(residual[...])
    column = kind[...]
    back = norm_back(lifted_grad, normal, inverse, gain_rows(gain, column))
    value = grad[...].astype(f32) + back
    grad_residual[...] = value
    mixed[...] = value.astype(bf16)
    sums[...] = kind_sums(lifted_grad * normal, column)


def middle(residual, low, other, grad, gain, kind):
    width = residual.shape[1]
    return pl.pallas_call(
        middle_kernel,
        out_shape=[
            jax.ShapeDtypeStruct(residual.shape, f32),
            jax.ShapeDtypeStruct(residual.shape, bf16),
            jax.ShapeDtypeStruct((8, width), bf16),
        ],
        compiler_params=params(10),
        cost_estimate=cost(20 * residual.size, 16 * residual.size),
        name="middle",
    )(residual, low, other, grad, gain, kind)


def last_kernel(rows, low, other, grad_residual, gain, kind, out):
    grad = low[...].astype(f32) + other[...].astype(f32)
    normal, inverse = normalize(rows[...].astype(f32))
    back = norm_back(grad, normal, inverse, gain_rows(gain, kind[...]))
    out[...] = (grad_residual[...] + back).astype(bf16)


def last(rows, low, other, grad_residual, gain, kind):
    return pl.pallas_call(
        last_kernel,
        out_shape=jax.ShapeDtypeStruct(rows.shape, bf16),
        compiler_params=params(8),
        cost_estimate=cost(20 * rows.size, 12 * rows.size),
        name="last",
    )(rows, low, other, grad_residual, gain, kind)


def gelu_parts(value):
    rate = math.sqrt(2 / math.pi)
    square = value * value
    bent = jnp.tanh(value * (rate + (rate * 0.044715) * square))
    upper = 0.5 * (1 + bent)
    slope = upper + (0.5 * value) * (1 - bent * bent) * (rate + (rate * 3 * 0.044715) * square)
    return value * upper, slope


def own_kernel(lifted, up, grad_activated, activated, mine, other, lifted_grad):
    value, slope = gelu_parts(dot(lifted[...], up[...], NN))
    activated[...] = value.astype(bf16)
    hidden_grad = (grad_activated[...] * slope).astype(bf16)
    term = dot(hidden_grad, up[...], NT)

    @pl.when(pl.program_id(0) == 0)
    def _():
        lifted_grad[...] = term

    @pl.when(pl.program_id(0) > 0)
    def _():
        lifted_grad[...] += term

    @pl.when(pl.program_id(0) == pl.num_programs(0) - 1)
    def _():
        half = mine.shape[0]
        mine[...] = lifted_grad[:half]
        other[...] = lifted_grad[half:].astype(bf16)


def feed_own(lifted, up, grad_activated):
    rows, width = lifted.shape
    hidden = up.shape[1]
    tile = math.gcd(hidden, 512)
    across = lambda t: (0, t)
    whole = lambda t: (0, 0)
    return pl.pallas_call(
        own_kernel,
        grid=(hidden // tile,),
        in_specs=[
            pl.BlockSpec((rows, width), whole),
            pl.BlockSpec((width, tile), across),
            pl.BlockSpec((rows, tile), across),
        ],
        out_specs=[pl.BlockSpec((rows, tile), across)]
        + [pl.BlockSpec((rows // 2, width), whole)] * 2,
        out_shape=[
            jax.ShapeDtypeStruct((rows, hidden), bf16),
            jax.ShapeDtypeStruct((rows // 2, width), f32),
            jax.ShapeDtypeStruct((rows // 2, width), bf16),
        ],
        scratch_shapes=[pltpu.VMEM((rows, width), f32)],
        compiler_params=params(16),
        cost_estimate=cost(4 * rows * width * hidden, 2 * width * hidden),
        name="feed_own",
    )(lifted, up, grad_activated)


def down_kernel(grad, down, out):
    out[...] = dot(grad[...], down[...], NT)


def grad_activated(grad, down):
    rows, width = grad.shape
    hidden = down.shape[0]
    tile = math.gcd(hidden, 512)
    return pl.pallas_call(
        down_kernel,
        grid=(hidden // tile,),
        in_specs=[
            pl.BlockSpec((rows, width), lambda t: (0, 0)),
            pl.BlockSpec((tile, width), lambda t: (t, 0)),
        ],
        out_specs=pl.BlockSpec((rows, tile), lambda t: (0, t)),
        out_shape=jax.ShapeDtypeStruct((rows, hidden), f32),
        compiler_params=params(12),
        cost_estimate=cost(2 * rows * width * hidden, 2 * width * hidden),
        name="grad_activated",
    )(grad, down)


def all_kernel(index, *refs, counts, add):
    count = len(counts)
    lifted_parts, grad_parts = refs[:count], refs[count : 2 * count]
    up, down = refs[2 * count : 2 * count + 2]
    up_grad, down_grad, lifted, grad, sems = refs[-5:]

    @pl.when(pl.program_id(0) == 0)
    def _():
        copies = []
        for k, (source, target) in enumerate(((lifted_parts, lifted), (grad_parts, grad))):
            start = 0
            for j, rows in enumerate(counts):
                here = target.at[pl.ds(start, rows)]
                copies.append(pltpu.make_async_copy(source[j], here, sems.at[k * count + j]))
                start += rows
        for copy in copies:
            copy.start()
        for copy in copies:
            copy.wait()

    part = up_grad.shape[0]
    mine = pl.ds(pl.multiple_of(index[0] * part, part), part)
    value, slope = gelu_parts(dot(lifted[...], up[...], NN))
    hidden_grad = (dot(grad[...], down[...], NT) * slope).astype(bf16)
    down_term = dot(value.astype(bf16), grad[:, mine], TN)
    up_term = dot(lifted[:, mine], hidden_grad, TN)
    if add:
        up_term += refs[2 * count + 2][...]
        down_term += refs[2 * count + 3][...]
    up_grad[...] = up_term
    down_grad[...] = down_term


def feed_all(lifted, grad, up, down, shards, place, places, sums, add):
    counts = [array.shape[0] for array in lifted]
    rows, width = sum(counts), lifted[0].shape[1]
    count = len(counts)
    part = width // shards
    hidden = up.shape[1]
    tile = math.gcd(hidden // places, 256)
    steps = hidden // places // tile
    first = place * steps
    across = lambda t, index: (0, first + t)
    below = lambda t, index: (first + t, 0)
    anywhere = pl.BlockSpec(memory_space=pl.ANY)
    sum_specs = [pl.BlockSpec((part, tile), across), pl.BlockSpec((tile, part), below)]
    index = lax.axis_index("seq").astype(jnp.int32).reshape(1)
    at = 1 + 2 * count + 2
    return pl.pallas_call(
        partial(all_kernel, counts=counts, add=add),
        grid_spec=pltpu.PrefetchScalarGridSpec(
            num_scalar_prefetch=1,
            grid=(steps,),
            in_specs=[anywhere] * (2 * count)
            + [pl.BlockSpec((width, tile), across), pl.BlockSpec((tile, width), below)]
            + ((sum_specs if add else [anywhere] * 2) if sums else []),
            out_specs=sum_specs,
            scratch_shapes=[pltpu.VMEM((rows, width), bf16)] * 2
            + [pltpu.SemaphoreType.DMA((2 * count,))],
        ),
        out_shape=[
            jax.ShapeDtypeStruct((part, hidden), f32),
            jax.ShapeDtypeStruct((hidden, part), f32),
        ],
        input_output_aliases={at: 0, at + 1: 1} if sums else {},
        compiler_params=params(10 + 20 * rows // 640),
        cost_estimate=cost(
            4 * rows * hidden // places * (width + part),
            4 * width * hidden // places + 4 * rows * width,
            share=4,
        ),
        name="feed_all",
    )(index, *lifted, *grad, in_hbm(up), in_hbm(down), *sums)


def project_kernel(index, *refs):
    normed, lows, weights = refs[0:2], refs[2:8], refs[8:11]
    gain, kinds = refs[11], refs[12:14]
    outs, gain_grad = refs[14:17], refs[17]
    for k in range(3):
        outs[k][...] = sum(dot(normed[side][...], lows[2 * k + side][...], TN) for side in range(2))
    gain_sum = [0.0, 0.0, 0.0]
    for side in range(2):
        column = kinds[side][...]
        term = sum(dot(lows[2 * k + side][...], weights[k][...], NT) for k in range(3))
        term = term * (normed[side][...].astype(f32) / gain_rows(gain, column))
        for k in range(3):
            gain_sum[k] += jnp.sum(jnp.where(column == k, term, 0.0), axis=0, keepdims=True)
    gain_grad[...] = jnp.concatenate(gain_sum, axis=0)


def project(normed, lows, weights, gain, kinds, shards):
    rows, width = normed[0].shape
    across = lows[0][0].shape[1]
    part = width // shards
    whole = lambda t, index: (0, 0)
    mine = lambda t, index: (0, index[0])
    below = lambda t, index: (index[0], 0)
    index = lax.axis_index("seq").astype(jnp.int32).reshape(1)
    return pl.pallas_call(
        project_kernel,
        grid_spec=pltpu.PrefetchScalarGridSpec(
            num_scalar_prefetch=1,
            grid=(1,),
            in_specs=[pl.BlockSpec((rows, part), mine)] * 2
            + [pl.BlockSpec((rows, across), whole)] * 6
            + [pl.BlockSpec((part, across), below)] * 3
            + [pl.BlockSpec((gain.shape[0], part), mine)]
            + [pl.BlockSpec((rows, 1), whole)] * 2,
            out_specs=[pl.BlockSpec((part, across), whole)] * 3
            + [pl.BlockSpec((gain.shape[0], part), whole)],
        ),
        out_shape=[jax.ShapeDtypeStruct((part, across), f32)] * 3
        + [jax.ShapeDtypeStruct((gain.shape[0], part), f32)],
        compiler_params=params(20),
        cost_estimate=cost(24 * rows * part * across, 12 * rows * across + 12 * part * across),
        name="project",
    )(index, *normed, *[low for pair in lows for low in pair], *weights, gain, *kinds)


def output_kernel(index, attended_a, attended_b, mixed_a, mixed_b, out, *, groups):
    total = 0.0
    shards, half, part = mixed_a.shape
    each = half // groups
    for attended, mixed in ((attended_a, mixed_a), (attended_b, mixed_b)):
        rows = [
            mixed[index[0] ^ d, pl.ds(group * each, each), :]
            for group in range(groups)
            for d in range(shards)
        ]
        total += dot(attended[...], jnp.concatenate(rows, axis=0), TN)
    out[...] = total


def output_part(attended, mixed, groups):
    index = lax.axis_index("seq").astype(jnp.int32).reshape(1)
    across, part = attended[0].shape[1], mixed[0].shape[2]
    return pl.pallas_call(
        partial(output_kernel, groups=groups),
        in_specs=[pl.BlockSpec(memory_space=pltpu.SMEM)]
        + [pl.BlockSpec(memory_space=pltpu.VMEM)] * 4,
        out_shape=jax.ShapeDtypeStruct((across, part), f32),
        compiler_params=params(10),
        cost_estimate=cost(
            4 * attended[0].shape[0] * across * part, 4 * attended[0].shape[0] * (across + part)
        ),
        name="output_part",
    )(index, *attended, *mixed)


def mask_of(key_place, query_place, clip_length, clips):
    allowed = key_place <= query_place
    if clips > 1:
        allowed = allowed & (key_place // clip_length == query_place // clip_length)
    return allowed


def probabilities(scores, scale):
    top = scores[0].max(axis=0, keepdims=True)
    for block in scores[1:]:
        top = jnp.maximum(top, block.max(axis=0, keepdims=True))
    rate = scale * math.log2(math.e)
    weights = [jnp.exp2((block - top) * rate) for block in scores]
    total = weights[0].sum(axis=0, keepdims=True)
    for block in weights[1:]:
        total = total + block.sum(axis=0, keepdims=True)
    inverse = 1.0 / total
    return [block * inverse for block in weights]


def forward_kernel(query, key_a, key_b, value_a, value_b, place_a, place_b, query_place, out, **opts):
    scale = opts["scale"]
    query_place = query_place[...]
    allowed = [
        mask_of(place[...], query_place, opts["clip_length"], opts["clips"])
        for place in (place_a, place_b)
    ]
    for head in range(query.shape[1] // HEAD_DIM):
        at = pl.ds(head * HEAD_DIM, HEAD_DIM)
        scores = [
            jnp.where(mask, dot(key[:, at], query[:, at], NT), NEGATIVE)
            for mask, key in zip(allowed, (key_a, key_b))
        ]
        prob = [block.astype(bf16) for block in probabilities(scores, scale)]
        result = dot(prob[0], value_a[:, at], TN) + dot(prob[1], value_b[:, at], TN)
        out[:, at] = result.astype(bf16)


def attend(query, keys, values, places, query_place, clip_length, clips):
    rows, width = query.shape
    total = 2 * keys[0].shape[0]
    return pl.pallas_call(
        partial(
            forward_kernel, scale=1.0 / math.sqrt(HEAD_DIM), clip_length=clip_length, clips=clips
        ),
        out_shape=jax.ShapeDtypeStruct((rows, width), bf16),
        compiler_params=params(16),
        cost_estimate=cost(
            4 * rows * total * width, 4 * total * width, rows * total * (width // HEAD_DIM)
        ),
        name="attend",
    )(query, *keys, *values, *places, query_place)


def backward_kernel(*refs, count, groups, scale, clip_length, clips):
    grads = refs[:count]
    query_a, query_b, key_a, key_b, value_a, value_b, place_a, place_b, query_place = refs[
        count : count + 9
    ]
    outs = refs[count + 9 : count + 20]
    attended, grad_query, grad_key, grad_value = outs[0:2], outs[2:4], outs[4:6], outs[6:8]
    own_query, own_key, own_value = outs[8:11]
    sums = refs[count + 20 :]
    half = key_a.shape[0]
    rows = half // count
    group_rows = rows // groups
    block = min(128, half)
    blocks = half // block

    def sources(index):
        found = []
        if groups == 1:
            for d in range(index * block // rows, (index + 1) * block // rows):
                found.append((d, 0, rows))
            return found
        each = count * group_rows
        for j in range(index * block // each, (index + 1) * block // each):
            for d in range(count):
                found.append((d, j * group_rows, group_rows))
        return found

    def keep_own(target, values, index):
        for side in range(2):
            at = side * block
            for d, start, size in sources(index):
                if d == 0:
                    target[pl.ds(side * rows + start, size), :] = values[at : at + size]
                at += size

    for ref in sums:
        ref[...] = jnp.zeros_like(ref)
    for index in range(blocks):
        mine = pl.ds(index * block, block)
        reach = (index + 1) * block if groups > 1 else half
        free = index * block if groups > 1 else 0
        query = jnp.concatenate([query_a[mine, :], query_b[mine, :]], axis=0)
        grad = jnp.concatenate(
            [
                grads[d][pl.ds(side * rows + start, size), :]
                for side in range(2)
                for d, start, size in sources(index)
            ],
            axis=0,
        )
        at_place = query_place[:, pl.ds(index * 2 * block, 2 * block)]
        spans = []
        for side in range(2):
            if free:
                spans.append((side, 0, free, False))
            spans.append((side, free, reach, True))
        keys, values, places = (key_a, key_b), (value_a, value_b), (place_a, place_b)
        scores = []
        for side, low, high, masked in spans:
            score = dot(keys[side][pl.ds(low, high - low), :], query, NT)
            if masked:
                place = places[side][pl.ds(low, high - low), :]
                score = jnp.where(mask_of(place, at_place, clip_length, clips), score, NEGATIVE)
            scores.append(score)
        prob = probabilities(scores, scale)
        lows = [part.astype(bf16) for part in prob]
        grad_prob = [
            dot(values[side][pl.ds(low, high - low), :], grad, NT) for side, low, high, _ in spans
        ]
        delta = sum((p * g).sum(axis=0, keepdims=True) for p, g in zip(prob, grad_prob))
        grad_score = [(p * (g - delta)).astype(bf16) for p, g in zip(prob, grad_prob)]
        result = sum(
            dot(part, values[side][pl.ds(low, high - low), :], TN)
            for part, (side, low, high, _) in zip(lows, spans)
        ).astype(bf16)
        back = (
            sum(
                dot(part, keys[side][pl.ds(low, high - low), :], TN)
                for part, (side, low, high, _) in zip(grad_score, spans)
            )
            * scale
        ).astype(bf16)
        for side in range(2):
            attended[side][mine, :] = result[side * block : (side + 1) * block]
            grad_query[side][mine, :] = back[side * block : (side + 1) * block]
        keep_own(own_query, back, index)
        for (side, low, high, _), score, part in zip(spans, grad_score, lows):
            at = pl.ds(low, high - low)
            sums[side][at, :] += dot(score, query, NN)
            sums[2 + side][at, :] += dot(part, grad, NN)
    low_key = [(sums[side][...] * scale).astype(bf16) for side in range(2)]
    low_value = [sums[2 + side][...].astype(bf16) for side in range(2)]
    for side in range(2):
        grad_key[side][...] = low_key[side]
        grad_value[side][...] = low_value[side]
    for index in range(blocks):
        cut = slice(index * block, (index + 1) * block)
        keep_own(own_key, jnp.concatenate([low[cut] for low in low_key], axis=0), index)
        keep_own(own_value, jnp.concatenate([low[cut] for low in low_value], axis=0), index)


def attend_back(grads, queries, keys, values, places, query_place, groups, clip_length, clips):
    half, width = keys[0].shape
    count = len(grads)
    heads = width // HEAD_DIM
    rows = grads[0].shape[0]
    by_head = lambda h: (0, h)
    whole = lambda h: (0, 0)
    tall = pl.BlockSpec((half, HEAD_DIM), by_head)
    short = pl.BlockSpec((rows, HEAD_DIM), by_head)
    outs = pl.pallas_call(
        partial(
            backward_kernel,
            count=count,
            groups=groups,
            scale=1.0 / math.sqrt(HEAD_DIM),
            clip_length=clip_length,
            clips=clips,
        ),
        grid=(heads,),
        in_specs=[short] * count
        + [tall] * 6
        + [pl.BlockSpec((half, 1), whole)] * 2
        + [pl.BlockSpec((1, 2 * half), whole)],
        out_specs=[tall] * 8 + [short] * 3,
        out_shape=[jax.ShapeDtypeStruct((half, width), bf16)] * 8
        + [jax.ShapeDtypeStruct((rows, width), bf16)] * 3,
        scratch_shapes=[pltpu.VMEM((half, HEAD_DIM), f32)] * 4,
        compiler_params=params(32),
        cost_estimate=cost(
            12 * 4 * half * half * width, 32 * half * width, 4 * half * half * heads
        ),
        name="attend_back",
    )(*[in_hbm(grad) for grad in grads], *queries, *keys, *values, *places, query_place)
    return outs[0:2], outs[2:4], outs[4:6], outs[6:8], outs[8:11]


def body(
    inputs,
    first_gain,
    query_weight,
    key_weight,
    value_weight,
    output_weight,
    second_gain,
    up_weight,
    down_weight,
    frame_sizes,
    text_counts,
    action_counts,
    cotangent,
):
    shards = lax.axis_size("seq")
    shard_index = lax.axis_index("seq")
    core = lax.axis_index("mlp") % 2
    length, width = inputs.shape
    total = length * shards
    half = length // 2
    piece = half // shards
    clips = frame_sizes.shape[0]
    clip_length = total // clips
    part = width // shards
    groups = shards if piece % 8 == 0 else 1

    def halves(rows):
        cut = rows.reshape(2, piece, shards, width)
        mine = lax.dynamic_index_in_dim(cut, core, 0, keepdims=False)
        other = lax.dynamic_index_in_dim(cut, 1 - core, 0, keepdims=False)
        return (
            mine.transpose(1, 0, 2).reshape(half, width),
            other.transpose(1, 0, 2).reshape(half, width),
        )

    def restore(mine):
        other = swap(mine, "mlp", 1)
        upper = jnp.where(core == 0, mine, other)
        lower = jnp.where(core == 0, other, mine)
        rows = jnp.stack([upper, lower]).reshape(2, shards, piece, width)
        return rows.transpose(0, 2, 1, 3).reshape(length, width)

    inputs_half, inputs_other = halves(inputs)
    pieces = gather_early(inputs_half)
    arrived = pieces[inner_size() :: inner_size()]

    place_a, place_b, kind_a, kind_b, query_place, own_place, own_kind = tables(
        frame_sizes, text_counts, action_counts, shards, length, groups
    )
    places, kinds = (place_a, place_b), (kind_a, kind_b)
    half_kind = own_kind[:half]
    own_normed = own_norm(
        jnp.concatenate([inputs_half, inputs_other], axis=0), first_gain, own_kind
    )
    grad_half, grad_other = halves(cotangent)
    grad_own = jnp.concatenate([grad_half, grad_other], axis=0)
    (query_own,) = project_rows(after(own_normed, arrived), query_weight)
    own_activated_grad = grad_activated(after(grad_own, query_own), down_weight)
    grad_far = gather_outer(after(grad_half, arrived))
    pieces, grad_far = after((pieces, grad_far), own_activated_grad)

    normed = [norm_pieces(pieces, first_gain, kind_a, groups)]
    normed.append(swap(normed[0], "mlp", 1))
    keys, values = zip(*[project_rows(rows, key_weight, value_weight) for rows in normed])
    heads_own = attend(query_own, keys, values, places, own_place, clip_length, clips)
    grad_far = join_x(jnp.concatenate(after(grad_far, normed[0]), axis=0), heads_own)
    mine, other = product_halves([heads_own], [output_weight], NN)
    other, grad_far = after((other, grad_far), other)
    grad_inner = gather_inner(grad_half) + gather_inner(grad_far)
    low, other = pair_mlp(mine, other)
    queries = [project_rows(rows, query_weight)[0] for rows in after(normed, low)]
    other = after(other, queries)
    residual, lifted_half = lift(inputs_half, low, other, second_gain, half_kind)

    lifted_own = both(lifted_half)
    activated_own, mine, other = feed_own(lifted_own, up_weight, own_activated_grad)
    lifted_far = gather_outer(after(lifted_half, other))
    other, grad_inner = after((other, grad_inner), other)
    low, other = pair_mlp(mine, other)
    down_mine, down_other = down_own(after(activated_own, low), down_weight)
    other, lifted_far = after((other, lifted_far), down_other)
    grad_residual, mixed_half, second_sums = middle(
        residual, low, other, grad_half, second_gain, half_kind
    )
    heads_grad = product_back(both(mixed_half), output_weight)

    places_up = 2
    sums = ()

    def feed(lifted, grads, place, add, *earlier):
        return feed_all(
            after(lifted, earlier), grads, up_weight, down_weight, shards, place, places_up, sums, add
        )

    heads_first = gather_first(heads_grad)
    lifted_far = join_x(jnp.concatenate(lifted_far, axis=0), heads_first)
    heads_grads = gather_pieces(*heads_first)
    first_lifted = [lifted_own] + with_core([lifted_far])
    first_grads = [grad_own] + with_core([grad_far])
    sums = feed(first_lifted, first_grads, 0, False, heads_grads[inner_size() + 1])
    sums = feed(first_lifted, first_grads, 1, False)
    down_low, down_other = pair_mlp(down_mine, after(down_other, heads_grad))
    heads_grads, down_low = after((heads_grads, down_low), sums)
    lifted_inner = gather_inner(after(lifted_half, heads_grads))
    lifted_inner += gather_inner(after(lifted_far, heads_grads))

    attended, query_low, key_low, value_low, own_low = attend_back(
        heads_grads,
        queries,
        keys,
        values,
        places,
        query_place,
        groups,
        clip_length,
        clips,
    )
    own_low, lifted_inner, down_other = after((own_low, lifted_inner, down_other), own_low)
    rest_lifted, rest_grads = with_core(lifted_inner), with_core(grad_inner)
    attention_weights = (query_weight, key_weight, value_weight)
    low, other = pair_mlp(*product_halves(own_low, attention_weights, NT))
    sums = feed(rest_lifted, rest_grads, 0, True, low)
    other = after(other, sums)
    input_grad_half = last(inputs_half, low, other, grad_residual, first_gain, half_kind)
    input_grad = restore(input_grad_half)

    mixed_part = lax.all_to_all(
        after(jnp.concatenate([mixed_half, second_sums], axis=0), other).reshape(
            half + 8, shards, part
        ),
        "seq",
        split_axis=1,
        concat_axis=0,
        tiled=False,
    )
    down_total = down_low.astype(f32) + after(down_other, input_grad_half).astype(f32)
    outputs = restore((residual + down_total).astype(bf16))

    query_grad, key_grad, value_grad, first_gain_grad = project(
        normed,
        after((query_low, key_low, value_low), other),
        attention_weights,
        first_gain,
        kinds,
        shards,
    )
    bit = 1
    while bit < lax.axis_size("mlp"):
        first_gain_grad = first_gain_grad + swap(first_gain_grad, "mlp", bit)
        bit *= 2
    up_grad, down_grad = feed(rest_lifted, rest_grads, 1, True, query_grad)

    second_sums = jnp.sum(mixed_part[:, half : half + 6].astype(f32), axis=0)
    second_sums = second_sums[:3] + second_sums[3:]
    second_gain_grad = second_sums + swap(second_sums, "mlp", 1)
    mixed_part = after(mixed_part[:, :half], up_grad)
    output_grad = output_part(attended, (mixed_part, swap(mixed_part, "mlp", 1)), groups)

    return (
        outputs,
        input_grad,
        first_gain_grad,
        query_grad,
        key_grad,
        value_grad,
        output_grad,
        second_gain_grad,
        up_grad,
        down_grad,
    )


def solution(mesh):
    return jax.shard_map(
        body,
        mesh=mesh,
        in_specs=(
            P("seq", None),
            P(),
            P(None, "mlp"),
            P(None, "mlp"),
            P(None, "mlp"),
            P("mlp", None),
            P(),
            P(None, "mlp"),
            P("mlp", None),
            P(),
            P(),
            P(),
            P("seq", None),
        ),
        out_specs=(
            P("seq", None),
            P("seq", None),
            P(None, "seq"),
            P("seq", "mlp"),
            P("seq", "mlp"),
            P("seq", "mlp"),
            P("mlp", "seq"),
            P(None, "seq"),
            P("seq", "mlp"),
            P("mlp", "seq"),
        ),
        check_vma=False,
    )
```

```python
from functools import partial
import math

import jax
import jax.numpy as jnp
from jax import lax
from jax.experimental import pallas as pl
from jax.experimental.pallas import tpu as pltpu
from jax.sharding import PartitionSpec as P

HEAD_DIM = 128
epsilon = 1e-05
bf16 = jnp.bfloat16
f32 = jnp.float32
NEGATIVE = -1e30

NN = ((1,), (0,))
NT = ((1,), (1,))
TN = ((0,), (0,))


def dot(a, b, dims):
    return lax.dot_general(a, b, (dims, ((), ())), preferred_element_type=f32)


def params(mebibytes):
    return pltpu.CompilerParams(vmem_limit_bytes=mebibytes * 1024 * 1024)


def cost(flops, moved, transcendentals=0, share=100):
    return pl.CostEstimate(
        flops=int(flops) // share,
        bytes_accessed=int(moved) // share,
        transcendentals=int(transcendentals) // share,
    )


def swap(value, axis, bit):
    size = lax.axis_size(axis)
    return lax.ppermute(value, axis, [(i, i ^ bit) for i in range(size)])


def inner_size():
    return 1 << (int(math.log2(lax.axis_size("seq"))) // 2)


def x_size():
    return lax.axis_size("mlp") // 2


def after(values, *earlier):
    return lax.optimization_barrier((values, earlier))[0]


def in_hbm(array):
    return pltpu.with_memory_space_constraint(array, pltpu.HBM)


def own_quarter(half):
    rows = half.shape[0] // x_size()
    return lax.dynamic_slice_in_dim(half, (lax.axis_index("mlp") // 2) * rows, rows, 0)


def join_x(quarter, *earlier):
    bit = 1
    while bit < x_size():
        came = after(swap(quarter, "mlp", 2 * bit), earlier)
        quarter = jnp.concatenate([quarter, came], axis=0)
        bit *= 2
    return quarter


def gather_early(half):
    size, inner = lax.axis_size("seq"), inner_size()
    quarter = own_quarter(half)
    pieces = {0: half}
    far = {outer: swap(quarter, "seq", outer) for outer in range(inner, size, inner)}
    for bit in range(1, inner):
        pieces[bit] = swap(half, "seq", bit)
    for outer in range(inner, size, inner):
        pieces[outer] = join_x(far[outer])
        for bit in range(1, inner):
            pieces[outer | bit] = swap(pieces[outer], "seq", bit)
    return [pieces[d] for d in range(size)]


def gather_outer(half):
    size, inner = lax.axis_size("seq"), inner_size()
    quarter = own_quarter(half)
    return [swap(quarter, "seq", outer) for outer in range(inner, size, inner)]


def gather_inner(array):
    return [swap(array, "seq", bit) for bit in range(1, inner_size())]


def with_core(arrays):
    return [each for array in arrays for each in (array, swap(array, "mlp", 1))]


def gather_first(piece):
    size, inner = lax.axis_size("seq"), inner_size()
    pieces = {0: piece}
    for bit in range(1, inner):
        pieces[bit] = swap(piece, "seq", bit)
    return pieces, [swap(piece, "seq", outer) for outer in range(inner, size, inner)]


def gather_pieces(pieces, far):
    size, inner = lax.axis_size("seq"), inner_size()
    for outer, came in zip(range(inner, size, inner), far):
        pieces[outer] = came
        for bit in range(1, inner):
            pieces[outer | bit] = swap(came, "seq", bit)
    return [pieces[d] for d in range(size)]


def rounded(value):
    return lax.optimization_barrier(value.astype(bf16))


def pair_mlp(mine, other_half):
    low, other = rounded(mine + swap(other_half, "mlp", 1).astype(f32)), None
    bit = 2
    while bit < lax.axis_size("mlp"):
        if other is not None:
            low = rounded(low.astype(f32) + other.astype(f32))
        other = swap(low, "mlp", bit)
        bit *= 2
    if other is None:
        other = jnp.zeros_like(low)
    return low, other


def both(half):
    return jnp.concatenate([half, swap(half, "mlp", 1)], axis=0)


def tables_kernel(index, frames, texts, actions, *outs, shards, length, groups, clip_length):
    place_a, place_b, kind_a, kind_b, query_place, own_place, own_kind = outs
    shard_index, core = index[0], index[1]
    shape = (shards, length)
    place = lax.broadcasted_iota(jnp.int32, shape, 0) * length + lax.broadcasted_iota(
        jnp.int32, shape, 1
    )
    kinds = jnp.full(shape, 2, jnp.int32)
    for clip in range(frames.shape[0]):
        start = jnp.int32(clip * clip_length)
        within = (place >= clip * clip_length) & (place < (clip + 1) * clip_length)
        for frame in range(frames.shape[1]):
            text_end = start + texts[clip, frame]
            action_end = text_end + actions[clip, frame]
            kinds = jnp.where(within & (place >= start) & (place < text_end), 0, kinds)
            kinds = jnp.where(within & (place >= text_end) & (place < action_end), 1, kinds)
            start = action_end + frames[clip, frame]
    square = (length, length)
    down = lax.broadcasted_iota(jnp.int32, square, 0)
    across = lax.broadcasted_iota(jnp.int32, square, 1)
    earlier = (down < across).astype(f32).astype(bf16)
    rank = jnp.zeros(shape, f32)
    before = jnp.zeros((shards, 1), f32)
    for kind in range(3):
        chosen = (kinds == kind).astype(f32)
        rank += chosen * (dot(chosen.astype(bf16), earlier, NN) + before)
        before += chosen.sum(axis=1, keepdims=True)
    rank_low, kinds_low = rank.astype(bf16), kinds.astype(f32).astype(bf16)
    piece = length // shards // 2
    lane = lax.broadcasted_iota(jnp.int32, (1, length), 1).astype(f32)

    def find(shard, offset, side, row):
        wanted = (shard_index ^ offset) * (2 * piece) + (core ^ side) * piece + row
        pick = shard == lax.broadcasted_iota(jnp.int32, (length, shards), 1)
        pick = pick.astype(f32).astype(bf16)
        hit = dot(pick, rank_low, NN) == wanted.astype(f32)
        where = jnp.sum(jnp.where(hit, lane, 0.0), axis=1, keepdims=True).astype(jnp.int32)
        kind = jnp.sum(jnp.where(hit, dot(pick, kinds_low, NN), 0.0), axis=1, keepdims=True)
        return where + shard * length, kind.astype(jnp.int32)

    def as_row(column):
        return jnp.sum(jnp.where(down == across, column, 0), axis=0, keepdims=True)

    step = lax.broadcasted_iota(jnp.int32, (length, 1), 0)
    half = length // 2
    for side, (place_out, kind_out) in enumerate(((place_a, kind_a), (place_b, kind_b))):
        for block in range(shards // 2):
            token = step + block * length
            if groups > 1:
                shard, offset = token // (shards * piece), (token // piece) % shards
            else:
                offset, shard = token // half, (token % half) // piece
            where, kind = find(shard, offset, side, token % piece)
            at = pl.ds(block * length, length)
            place_out[at, :] = where
            kind_out[at, :] = kind
            query_place[:, pl.ds((2 * block + side) * length, length)] = as_row(where)
    where, kind = find((step % half) // piece, step * 0, step // half, step % piece)
    own_place[...] = as_row(where)
    own_kind[...] = kind


def tables(frames, texts, actions, shards, length, groups):
    index = jnp.stack([lax.axis_index("seq"), lax.axis_index("mlp") % 2]).astype(jnp.int32)
    total = shards * length
    column = jax.ShapeDtypeStruct((total // 2, 1), jnp.int32)
    return pl.pallas_call(
        partial(
            tables_kernel,
            shards=shards,
            length=length,
            groups=groups,
            clip_length=total // frames.shape[0],
        ),
        in_specs=[pl.BlockSpec(memory_space=pltpu.SMEM)] * 4,
        out_shape=[column] * 4
        + [
            jax.ShapeDtypeStruct((1, total), jnp.int32),
            jax.ShapeDtypeStruct((1, length), jnp.int32),
            jax.ShapeDtypeStruct((length, 1), jnp.int32),
        ],
        cost_estimate=cost(8 * total * length, 8 * 128 * total),
        name="tables",
    )(index, frames, texts, actions)


def rows_kernel(*refs, count):
    rows, weights, outs = refs[0], refs[1 : 1 + count], refs[1 + count :]
    for weight, out in zip(weights, outs):
        out[...] = dot(rows[...], weight[...], NN).astype(bf16)


def project_rows(rows, *weights):
    across = weights[0].shape[1]
    return pl.pallas_call(
        partial(rows_kernel, count=len(weights)),
        out_shape=[jax.ShapeDtypeStruct((rows.shape[0], across), bf16)] * len(weights),
        compiler_params=params(10),
        cost_estimate=cost(2 * rows.size * across * len(weights), 2 * rows.size),
        name="project_rows",
    )(rows, *weights)


def one_kernel(rows, weight, out):
    out[...] = dot(rows[...], weight[...], NT).astype(bf16)


def product_back(rows, weight):
    return pl.pallas_call(
        one_kernel,
        out_shape=jax.ShapeDtypeStruct((rows.shape[0], weight.shape[0]), bf16),
        compiler_params=params(6),
        cost_estimate=cost(2 * rows.size * weight.shape[0], 2 * weight.size),
        name="product_back",
    )(rows, weight)


def halves_kernel(*refs, count, dims):
    mine, other = refs[-2:]
    half = mine.shape[0]
    total = sum(dot(refs[k][...], refs[count + k][...], dims) for k in range(count))
    mine[...] = total[:half]
    other[...] = total[half:].astype(bf16)


def product_halves(rows, weights, dims):
    count = len(rows)
    half = rows[0].shape[0] // 2
    across = weights[0].shape[1 - dims[1][0]]
    shape = (half, across)
    return pl.pallas_call(
        partial(halves_kernel, count=count, dims=dims),
        out_shape=[jax.ShapeDtypeStruct(shape, f32), jax.ShapeDtypeStruct(shape, bf16)],
        compiler_params=params(10),
        cost_estimate=cost(2 * count * rows[0].size * across, 2 * count * weights[0].size),
        name="product_halves",
    )(*rows, *weights)


def down_own_kernel(rows, weight, mine, other, total):
    total[...] = jnp.zeros_like(total)

    def step(at):
        total[...] += dot(rows[:, at], weight[at, :], NN)

    tiles_of(weight.shape[0], math.gcd(weight.shape[0], 512), step)
    half = mine.shape[0]
    mine[...] = total[:half]
    other[...] = total[half:].astype(bf16)


def down_own(rows, weight):
    count, deep = rows.shape
    across = weight.shape[1]
    shape = (count // 2, across)
    return pl.pallas_call(
        down_own_kernel,
        in_specs=[WHOLE] * 2,
        out_specs=[WHOLE] * 2,
        out_shape=[jax.ShapeDtypeStruct(shape, f32), jax.ShapeDtypeStruct(shape, bf16)],
        scratch_shapes=[pltpu.VMEM((count, across), f32)],
        compiler_params=params(6),
        cost_estimate=cost(2 * rows.size * across, 2 * weight.size),
        name="down_own",
    )(rows, weight)


def gain_rows(gain, column):
    return jnp.where(
        column == 0, gain[0:1, :], jnp.where(column == 1, gain[1:2, :], gain[2:3, :])
    )


def normalize(values):
    mean = jnp.mean(values, axis=1, keepdims=True)
    centered = values - mean
    inverse = lax.rsqrt(jnp.mean(centered * centered, axis=1, keepdims=True) + epsilon)
    return (centered * inverse, inverse)


def norm_back(grad, normal, inverse, gains):
    scaled = grad * gains
    return inverse * (
        scaled
        - jnp.mean(scaled, axis=1, keepdims=True)
        - normal * jnp.mean(scaled * normal, axis=1, keepdims=True)
    )


def norm_kernel(*refs, groups, inner, parts):
    index, gain, kind, out = refs[0], refs[-3], refs[-2], refs[-1]
    pieces = refs[1:-3]
    rows, width = pieces[0].shape
    count = len(pieces)
    step = rows // parts
    for d, piece in enumerate(pieces):
        for part in range(parts):
            normal, _ = normalize(piece[pl.ds(part * step, step), :].astype(f32))
            place = part if d < inner else part ^ index[0]
            if groups > 1:
                each = groups // parts
                at = pl.ds(place * each, each)
                column = kind[at, d].reshape(step, 1)
                normed = (normal * gain_rows(gain, column)).astype(bf16)
                out[at, d] = normed.reshape(each, rows // groups, width)
            else:
                column = kind[d, place]
                out[d, place] = (normal * gain_rows(gain, column)).astype(bf16)


def norm_pieces(pieces, gain, kind, groups):
    rows, width = pieces[0].shape
    count = len(pieces)
    parts = x_size()
    if groups > 1:
        shape = (groups, count, rows // groups)
    else:
        shape = (count, parts, rows // parts)
    memory = [pl.BlockSpec(memory_space=pltpu.SMEM)]
    index = (lax.axis_index("mlp") // 2).astype(jnp.int32).reshape(1)
    out = pl.pallas_call(
        partial(norm_kernel, groups=groups, inner=inner_size(), parts=parts),
        in_specs=memory + [pl.BlockSpec(memory_space=pltpu.VMEM)] * (count + 2),
        out_shape=jax.ShapeDtypeStruct(shape + (width,), bf16),
        compiler_params=params(4 + count),
        cost_estimate=cost(10 * count * rows * width, 4 * count * rows * width),
        name="norm_pieces",
    )(index, *pieces, gain, kind.reshape(shape + (1,)))
    return out.reshape(count * rows, width)


def own_norm_kernel(rows, gain, kind, out):
    normal, _ = normalize(rows[...].astype(f32))
    out[...] = (normal * gain_rows(gain, kind[...])).astype(bf16)


def own_norm(rows, gain, kind):
    return pl.pallas_call(
        own_norm_kernel,
        out_shape=jax.ShapeDtypeStruct(rows.shape, bf16),
        compiler_params=params(4),
        cost_estimate=cost(10 * rows.size, 4 * rows.size),
        name="own_norm",
    )(rows, gain, kind)


def lift_kernel(rows, low, other, gain, kind, residual, lifted):
    value = rows[...].astype(f32) + (low[...].astype(f32) + other[...].astype(f32))
    residual[...] = value
    normal, _ = normalize(value)
    lifted[...] = (normal * gain_rows(gain, kind[...])).astype(bf16)


def lift(rows, low, other, gain, kind):
    return pl.pallas_call(
        lift_kernel,
        out_shape=[jax.ShapeDtypeStruct(rows.shape, f32), jax.ShapeDtypeStruct(rows.shape, bf16)],
        compiler_params=params(4),
        cost_estimate=cost(10 * rows.size, 12 * rows.size),
        name="lift",
    )(rows, low, other, gain, kind)


def kind_sums(term, kind):
    sums = [jnp.sum(jnp.where(kind == k, term, 0.0), axis=0, keepdims=True) for k in range(3)]
    high = [value.astype(bf16) for value in sums]
    low = [(value - part.astype(f32)).astype(bf16) for value, part in zip(sums, high)]
    zero = jnp.zeros((1, term.shape[1]), bf16)
    return jnp.concatenate(high + low + [zero, zero], axis=0)


def middle_kernel(residual, low, other, grad, gain, kind, grad_residual, mixed, parts):
    lifted_grad = low[...].astype(f32) + other[...].astype(f32)
    normal, inverse = normalize(residual[...])
    column = kind[...]
    back = norm_back(lifted_grad, normal, inverse, gain_rows(gain, column))
    value = grad[...].astype(f32) + back
    grad_residual[...] = value
    rounded_value = value.astype(bf16)
    mixed[...] = rounded_value
    sums = kind_sums(lifted_grad * normal, column)
    shards, rows, part = parts.shape
    for k in range(shards):
        parts[k, pl.ds(0, rows - 8), :] = rounded_value[:, k * part : (k + 1) * part]
        parts[k, pl.ds(rows - 8, 8), :] = sums[:, k * part : (k + 1) * part]


def middle(residual, low, other, grad, gain, kind, shards):
    rows, width = residual.shape
    return pl.pallas_call(
        middle_kernel,
        out_shape=[
            jax.ShapeDtypeStruct(residual.shape, f32),
            jax.ShapeDtypeStruct(residual.shape, bf16),
            jax.ShapeDtypeStruct((shards, rows + 8, width // shards), bf16),
        ],
        compiler_params=params(6),
        cost_estimate=cost(20 * residual.size, 16 * residual.size),
        name="middle",
    )(residual, low, other, grad, gain, kind)


def reordered(values, shards):
    count = values.shape[0]
    piece = count // shards
    to = lax.broadcasted_iota(jnp.int32, (count, count), 0)
    source = lax.broadcasted_iota(jnp.int32, (count, count), 1)
    pick = (source == (to % shards) * piece + to // shards).astype(f32).astype(bf16)
    return dot(pick, values, NN).astype(bf16)


def finish_kernel(residual, low, other, out, *, shards):
    value = residual[...] + (low[...].astype(f32) + other[...].astype(f32))
    out[...] = reordered(value.astype(bf16), shards)


def finish(residual, low, other, shards):
    return pl.pallas_call(
        partial(finish_kernel, shards=shards),
        out_shape=jax.ShapeDtypeStruct(residual.shape, bf16),
        compiler_params=params(4),
        cost_estimate=cost(2 * residual.size, 10 * residual.size),
        name="finish",
    )(residual, low, other)


def place_kernel(index, mine, other, out):
    half = mine.shape[0]
    out[pl.ds(pl.multiple_of(index[0] * half, half), half), :] = mine[...]
    out[pl.ds(pl.multiple_of((1 - index[0]) * half, half), half), :] = other[...]


def place_halves(mine):
    half, width = mine.shape
    index = (lax.axis_index("mlp") % 2).astype(jnp.int32).reshape(1)
    return pl.pallas_call(
        place_kernel,
        in_specs=[pl.BlockSpec(memory_space=pltpu.SMEM)]
        + [pl.BlockSpec(memory_space=pltpu.VMEM)] * 2,
        out_shape=jax.ShapeDtypeStruct((2 * half, width), bf16),
        compiler_params=params(4),
        cost_estimate=cost(mine.size, 8 * mine.size),
        name="place_halves",
    )(index, mine, swap(mine, "mlp", 1))


def last_kernel(rows, low, other, grad_residual, gain, kind, out, *, shards):
    grad = low[...].astype(f32) + other[...].astype(f32)
    normal, inverse = normalize(rows[...].astype(f32))
    back = norm_back(grad, normal, inverse, gain_rows(gain, kind[...]))
    out[...] = reordered((grad_residual[...] + back).astype(bf16), shards)


def last(rows, low, other, grad_residual, gain, kind, shards):
    return pl.pallas_call(
        partial(last_kernel, shards=shards),
        out_shape=jax.ShapeDtypeStruct(rows.shape, bf16),
        compiler_params=params(6),
        cost_estimate=cost(20 * rows.size, 12 * rows.size),
        name="last",
    )(rows, low, other, grad_residual, gain, kind)


def gelu_parts(value):
    rate = math.sqrt(2 / math.pi)
    square = value * value
    bent = jnp.tanh(value * (rate + (rate * 0.044715) * square))
    upper = 0.5 * (1 + bent)
    slope = upper + (0.5 * value) * (1 - bent * bent) * (rate + (rate * 3 * 0.044715) * square)
    return value * upper, slope


WHOLE = pl.BlockSpec(memory_space=pltpu.VMEM)


def tiles_of(extent, tile, step):
    def at(t, _):
        step(pl.ds(pl.multiple_of(t * tile, tile), tile))
        return 0

    lax.fori_loop(0, extent // tile, at, 0)


def own_kernel(lifted, up, grad_activated, activated, hidden_grads, mine, other, total):
    total[...] = jnp.zeros_like(total)

    def step(at):
        value, slope = gelu_parts(dot(lifted[...], up[:, at], NN))
        activated[:, at] = value.astype(bf16)
        hidden_grad = (grad_activated[:, at] * slope).astype(bf16)
        hidden_grads[:, at] = hidden_grad
        total[...] += dot(hidden_grad, up[:, at], NT)

    tiles_of(up.shape[1], math.gcd(up.shape[1], 512), step)
    half = mine.shape[0]
    mine[...] = total[:half]
    other[...] = total[half:].astype(bf16)


def feed_own(lifted, up, grad_activated):
    rows, width = lifted.shape
    hidden = up.shape[1]
    return pl.pallas_call(
        own_kernel,
        in_specs=[WHOLE] * 3,
        out_specs=[WHOLE] * 4,
        out_shape=[jax.ShapeDtypeStruct((rows, hidden), bf16)] * 2
        + [
            jax.ShapeDtypeStruct((rows // 2, width), f32),
            jax.ShapeDtypeStruct((rows // 2, width), bf16),
        ],
        scratch_shapes=[pltpu.VMEM((rows, width), f32)],
        compiler_params=params(8),
        cost_estimate=cost(4 * rows * width * hidden, 2 * width * hidden),
        name="feed_own",
    )(lifted, up, grad_activated)


def down_kernel(grad, down, out):
    def step(at):
        out[:, at] = dot(grad[...], down[at, :], NT)

    tiles_of(down.shape[0], math.gcd(down.shape[0], 512), step)


def grad_activated(grad, down):
    rows, width = grad.shape
    hidden = down.shape[0]
    return pl.pallas_call(
        down_kernel,
        in_specs=[WHOLE] * 2,
        out_specs=WHOLE,
        out_shape=jax.ShapeDtypeStruct((rows, hidden), f32),
        compiler_params=params(6),
        cost_estimate=cost(2 * rows * width * hidden, 2 * width * hidden),
        name="grad_activated",
    )(grad, down)


def all_kernel(index, *refs, counts):
    count = len(counts)
    lifted_parts, grad_parts = refs[:count], refs[count : 2 * count]
    up, down = refs[2 * count : 2 * count + 2]
    before = refs[2 * count + 2 : -8]
    up_grad, down_grad, lifted, grad, lifted_across, hidden_kept, grad_kept, sems = refs[-8:]
    part = up_grad.shape[0]
    mine = pl.ds(pl.multiple_of(index[0] * part, part), part)

    @pl.when(pl.program_id(0) == 0)
    def _():
        copies = []
        for k, (source, target) in enumerate(((lifted_parts, lifted), (grad_parts, grad))):
            start = 0
            for j, rows in enumerate(counts):
                here = target.at[pl.ds(start, rows)]
                copies.append(pltpu.make_async_copy(source[j], here, sems.at[k * count + j]))
                start += rows
        for copy in copies:
            copy.start()
        for copy in copies:
            copy.wait()
        lifted_across[...] = lifted[:, mine].T

    first = pl.program_id(0) == 0
    last_step = pl.num_programs(0) - 1

    def products():
        return dot(lifted[...], up[...], NN), dot(grad[...], down[...], NT)

    def finish_tile(hidden_value, activated_grad):
        value, slope = gelu_parts(hidden_value)
        hidden_grad = (activated_grad * slope).astype(bf16)
        down_term = dot(value.astype(bf16), grad[:, mine], TN)
        up_term = dot(lifted_across[...], hidden_grad, NN)
        if len(before) == 2:
            up_term += before[0][...]
            down_term += before[1][...]
        else:
            lifted_own, grad_own, activated, hidden_own = before
            up_term += dot(lifted_own[...], hidden_own[...], TN)
            down_term += dot(activated[...], grad_own[...], TN)
        up_grad[...] = up_term
        down_grad[...] = down_term

    @pl.when(first)
    def _():
        hidden_kept[...], grad_kept[...] = products()

    @pl.when((pl.program_id(0) > 0) & (pl.program_id(0) < last_step))
    def _():
        kept = hidden_kept[...], grad_kept[...]
        fresh = products()
        finish_tile(*kept)
        hidden_kept[...], grad_kept[...] = fresh

    @pl.when(pl.program_id(0) == last_step)
    def _():
        finish_tile(hidden_kept[...], grad_kept[...])


def feed_all(lifted, grad, up, down, shards, sums=(), own=()):
    counts = [array.shape[0] for array in lifted]
    rows, width = sum(counts), lifted[0].shape[1]
    count = len(counts)
    part = width // shards
    hidden = up.shape[1]
    tile = math.gcd(hidden, 256)
    steps = hidden // tile
    wide = lambda t, index: (0, jnp.minimum(t, steps - 1))
    deep = lambda t, index: (jnp.minimum(t, steps - 1), 0)
    across = lambda t, index: (0, jnp.maximum(t - 1, 0))
    below = lambda t, index: (jnp.maximum(t - 1, 0), 0)
    mine = lambda t, index: (0, index[0])
    anywhere = pl.BlockSpec(memory_space=pl.ANY)
    sum_specs = [pl.BlockSpec((part, tile), across), pl.BlockSpec((tile, part), below)]
    if own:
        own_rows = own[0].shape[0]
        more = [pl.BlockSpec((own_rows, part), mine)] * 2
        more += [pl.BlockSpec((own_rows, tile), across)] * 2
    else:
        more = sum_specs
    index = lax.axis_index("seq").astype(jnp.int32).reshape(1)
    return pl.pallas_call(
        partial(all_kernel, counts=counts),
        grid_spec=pltpu.PrefetchScalarGridSpec(
            num_scalar_prefetch=1,
            grid=(steps + 1,),
            in_specs=[anywhere] * (2 * count)
            + [pl.BlockSpec((width, tile), wide), pl.BlockSpec((tile, width), deep)]
            + more,
            out_specs=sum_specs,
            scratch_shapes=[pltpu.VMEM((rows, width), bf16)] * 2
            + [pltpu.VMEM((part, rows), bf16)]
            + [pltpu.VMEM((rows, tile), f32)] * 2
            + [pltpu.SemaphoreType.DMA((2 * count,))],
        ),
        out_shape=[pltpu.HBM((part, hidden), f32), pltpu.HBM((hidden, part), f32)],
        compiler_params=params(8 + 15 * rows // 640),
        cost_estimate=cost(
            4 * rows * hidden * (width + part),
            4 * width * hidden + 4 * rows * width,
        ),
        name="feed_all",
    )(
        index,
        *lifted,
        *grad,
        in_hbm(up),
        in_hbm(down),
        *(own or [in_hbm(array) for array in sums]),
    )


def project_kernel(index, *refs):
    normed, lows, weights = refs[0:2], refs[2:8], refs[8:11]
    gain, kinds = refs[11], refs[12:14]
    outs, gain_grad = refs[14:17], refs[17]
    for k in range(3):
        outs[k][...] = sum(dot(normed[side][...], lows[2 * k + side][...], TN) for side in range(2))
    gain_sum = [0.0, 0.0, 0.0]
    for side in range(2):
        column = kinds[side][...]
        term = sum(dot(lows[2 * k + side][...], weights[k][...], NT) for k in range(3))
        term = term * (normed[side][...].astype(f32) / gain_rows(gain, column))
        for k in range(3):
            gain_sum[k] += jnp.sum(jnp.where(column == k, term, 0.0), axis=0, keepdims=True)
    gain_grad[...] = jnp.concatenate(gain_sum, axis=0)


def project(normed, lows, weights, gain, kinds, shards):
    rows, width = normed[0].shape
    across = lows[0][0].shape[1]
    part = width // shards
    whole = lambda t, index: (0, 0)
    mine = lambda t, index: (0, index[0])
    below = lambda t, index: (index[0], 0)
    index = lax.axis_index("seq").astype(jnp.int32).reshape(1)
    return pl.pallas_call(
        project_kernel,
        grid_spec=pltpu.PrefetchScalarGridSpec(
            num_scalar_prefetch=1,
            grid=(1,),
            in_specs=[pl.BlockSpec((rows, part), mine)] * 2
            + [pl.BlockSpec((rows, across), whole)] * 6
            + [pl.BlockSpec((part, across), below)] * 3
            + [pl.BlockSpec((gain.shape[0], part), mine)]
            + [pl.BlockSpec((rows, 1), whole)] * 2,
            out_specs=[pl.BlockSpec((part, across), whole)] * 3
            + [pl.BlockSpec((gain.shape[0], part), whole)],
        ),
        out_shape=[jax.ShapeDtypeStruct((part, across), f32)] * 3
        + [jax.ShapeDtypeStruct((gain.shape[0], part), f32)],
        compiler_params=params(14),
        cost_estimate=cost(24 * rows * part * across, 12 * rows * across + 12 * part * across),
        name="project",
    )(index, *normed, *[low for pair in lows for low in pair], *weights, gain, *kinds)


def output_kernel(index, attended_a, attended_b, came_a, came_b, out, gain_grad, *, groups):
    total, sums = 0.0, 0.0
    shards, rows, part = came_a.shape
    half = rows - 8
    each = half // groups
    for attended, came in ((attended_a, came_a), (attended_b, came_b)):
        mixed = [
            came[index[0] ^ d, pl.ds(group * each, each), :]
            for group in range(groups)
            for d in range(shards)
        ]
        total += dot(attended[...], jnp.concatenate(mixed, axis=0), TN)
        own_sums = 0.0
        for k in range(shards):
            own_sums += came[k, pl.ds(half, 8), :].astype(f32)
        sums += own_sums
    out[...] = total
    gain_grad[...] = sums[0:3, :] + sums[3:6, :]


def output_part(attended, came, groups):
    index = lax.axis_index("seq").astype(jnp.int32).reshape(1)
    across, part = attended[0].shape[1], came[0].shape[2]
    return pl.pallas_call(
        partial(output_kernel, groups=groups),
        in_specs=[pl.BlockSpec(memory_space=pltpu.SMEM)]
        + [pl.BlockSpec(memory_space=pltpu.VMEM)] * 4,
        out_shape=[
            jax.ShapeDtypeStruct((across, part), f32),
            jax.ShapeDtypeStruct((3, part), f32),
        ],
        compiler_params=params(6),
        cost_estimate=cost(
            4 * attended[0].shape[0] * across * part, 4 * attended[0].shape[0] * (across + part)
        ),
        name="output_part",
    )(index, *attended, *came)


def mask_of(key_place, query_place, clip_length, clips):
    allowed = key_place <= query_place
    if clips > 1:
        allowed = allowed & (key_place // clip_length == query_place // clip_length)
    return allowed


def probabilities(scores, scale):
    top = scores[0].max(axis=0, keepdims=True)
    for block in scores[1:]:
        top = jnp.maximum(top, block.max(axis=0, keepdims=True))
    rate = scale * math.log2(math.e)
    weights = [jnp.exp2((block - top) * rate) for block in scores]
    total = weights[0].sum(axis=0, keepdims=True)
    for block in weights[1:]:
        total = total + block.sum(axis=0, keepdims=True)
    inverse = 1.0 / total
    return [block * inverse for block in weights]


def forward_kernel(query, key_a, key_b, value_a, value_b, place_a, place_b, query_place, out, **opts):
    scale = opts["scale"]
    query_place = query_place[...]
    allowed = [
        mask_of(place[...], query_place, opts["clip_length"], opts["clips"])
        for place in (place_a, place_b)
    ]
    for head in range(query.shape[1] // HEAD_DIM):
        at = pl.ds(head * HEAD_DIM, HEAD_DIM)
        scores = [
            jnp.where(mask, dot(key[:, at], query[:, at], NT), NEGATIVE)
            for mask, key in zip(allowed, (key_a, key_b))
        ]
        prob = [block.astype(bf16) for block in probabilities(scores, scale)]
        result = dot(value_a[:, at], prob[0], TN) + dot(value_b[:, at], prob[1], TN)
        out[:, at] = result.T.astype(bf16)


def attend(query, keys, values, places, query_place, clip_length, clips):
    rows, width = query.shape
    total = 2 * keys[0].shape[0]
    return pl.pallas_call(
        partial(
            forward_kernel, scale=1.0 / math.sqrt(HEAD_DIM), clip_length=clip_length, clips=clips
        ),
        out_shape=jax.ShapeDtypeStruct((rows, width), bf16),
        compiler_params=params(8),
        cost_estimate=cost(
            4 * rows * total * width, 4 * total * width, rows * total * (width // HEAD_DIM)
        ),
        name="attend",
    )(query, *keys, *values, *places, query_place)


def block_of(half):
    return min(128, half)


def reaches(half, groups):
    blocks = half // block_of(half)
    found, start = [], 0
    for index in range(blocks):
        seen, free = (index + 1, index) if groups > 1 else (blocks, 0)
        found.append((seen, free, start))
        start += seen
    return found, start


def take(first, second, low, high, at):
    block = block_of(first.shape[0])
    rows = [side[pl.ds(k * block, block), at] for k in range(low, high) for side in (first, second)]
    return jnp.concatenate(rows, axis=0)


def columns_of(head):
    return pl.ds(pl.multiple_of(head * HEAD_DIM, HEAD_DIM), HEAD_DIM)


def all_forward_kernel(*refs, groups, scale, clip_length, clips):
    query_a, query_b, key_a, key_b, value_a, value_b, place_a, place_b, query_place = refs[:9]
    attended_a, attended_b, stored = refs[9:]
    half, width = key_a.shape
    block = block_of(half)
    pair = 2 * block
    everything = slice(None)

    def one_head(head, _):
        cut = columns_of(head)
        values_across = take(value_a, value_b, 0, half // block, cut).T
        for index, (seen, free, start) in enumerate(reaches(half, groups)[0]):
            mine = pl.ds(index * block, block)
            query = take(query_a, query_b, index, index + 1, cut)
            at_place = query_place[:, pl.ds(index * pair, pair)]
            place = take(place_a, place_b, free, seen, everything)
            mask = mask_of(place, at_place, clip_length, clips)
            score = dot(take(key_a, key_b, free, seen, cut), query, NT)
            scores = [jnp.where(mask, score, NEGATIVE)]
            if free:
                scores.insert(0, dot(take(key_a, key_b, 0, free, cut), query, NT))
            result, at = 0.0, 0
            for prob in probabilities(scores, scale):
                kept = prob.astype(bf16)
                rows = kept.shape[0]
                stored[head, pl.ds(start * pair + at, rows), :] = kept
                result += dot(values_across[:, at : at + rows], kept, NN)
                at += rows
            result = result.T.astype(bf16)
            attended_a[mine, cut] = result[:block]
            attended_b[mine, cut] = result[block:]
        return 0

    lax.fori_loop(0, width // HEAD_DIM, one_head, 0)


def attend_all(queries, keys, values, places, query_place, groups, clip_length, clips):
    half, width = keys[0].shape
    heads = width // HEAD_DIM
    pair = 2 * block_of(half)
    deep = reaches(half, groups)[1] * pair
    outs = pl.pallas_call(
        partial(
            all_forward_kernel,
            groups=groups,
            scale=1.0 / math.sqrt(HEAD_DIM),
            clip_length=clip_length,
            clips=clips,
        ),
        in_specs=[pl.BlockSpec(memory_space=pltpu.VMEM)] * 9,
        out_specs=[pl.BlockSpec(memory_space=pltpu.VMEM)] * 3,
        out_shape=[jax.ShapeDtypeStruct((half, width), bf16)] * 2
        + [jax.ShapeDtypeStruct((heads, deep, pair), bf16)],
        compiler_params=params(max(8, half * half // 2**15)),
        cost_estimate=cost(16 * half * half * width, 16 * half * width, 4 * half * half * heads),
        name="attend_all",
    )(*queries, *keys, *values, *places, query_place)
    return outs[:2], outs[2]


def backward_kernel(*refs, count, groups, scale):
    grad_pieces = refs[:count]
    query_a, query_b, key_a, key_b, value_a, value_b, attended_a, attended_b, stored = refs[
        count : count + 9
    ]
    outs = refs[count + 9 : count + 18]
    grad_query, grad_key, grad_value = outs[0:2], outs[2:4], outs[4:6]
    own_query, own_key, own_value = outs[6:9]
    (scores,) = refs[count + 18 :]
    half, width = key_a.shape
    rows = half // count
    group_rows = rows // groups
    block = block_of(half)
    blocks = half // block
    pair = 2 * block
    reach = reaches(half, groups)[0]

    def sources(index):
        found = []
        if groups == 1:
            for d in range(index * block // rows, (index + 1) * block // rows):
                found.append((d, 0, rows))
            return found
        each = count * group_rows
        for j in range(index * block // each, (index + 1) * block // each):
            for d in range(count):
                found.append((d, j * group_rows, group_rows))
        return found

    def one_head(head, _):
        cut = columns_of(head)

        def keep(targets, own, values, index):
            for side in range(2):
                at = side * block
                targets[side][pl.ds(index * block, block), cut] = values[at : at + block]
                for d, start, size in sources(index):
                    if d == 0:
                        own[pl.ds(side * rows + start, size), cut] = values[at : at + size]
                    at += size

        def take_grads(index):
            return jnp.concatenate(
                [
                    grad_pieces[d][pl.ds(side * rows + start, size), cut]
                    for side in range(2)
                    for d, start, size in sources(index)
                ],
                axis=0,
            )

        keys_across = take(key_a, key_b, 0, blocks, cut).T
        ones = jnp.ones((8, HEAD_DIM), f32)
        for index, (seen, _, start) in enumerate(reach):
            result = take(attended_a, attended_b, index, index + 1, cut)
            grad = take_grads(index)
            delta = lax.dot_general(
                ones,
                grad.astype(f32) * result.astype(f32),
                (NT, ((), ())),
                precision=lax.Precision.HIGHEST,
                preferred_element_type=f32,
            )[0:1, :]
            at = pl.ds(start * pair, seen * pair)
            grad_prob = dot(take(value_a, value_b, 0, seen, cut), grad, NT)
            score = (stored[head, at, :].astype(f32) * (grad_prob - delta)).astype(bf16)
            scores[at, :] = score
            back = dot(keys_across[:, : seen * pair], score, NN)
            keep(grad_query, own_query, (back * scale).T.astype(bf16), index)
        for index in range(blocks):
            key_sum, value_sum = 0.0, 0.0
            for other, (seen, _, start) in enumerate(reach):
                if index < seen:
                    at = pl.ds((start + index) * pair, pair)
                    query = take(query_a, query_b, other, other + 1, cut)
                    key_sum += dot(scores[at, :], query, NN)
                    value_sum += dot(stored[head, at, :], take_grads(other), NN)
            keep(grad_key, own_key, (key_sum * scale).astype(bf16), index)
            keep(grad_value, own_value, value_sum.astype(bf16), index)
        return 0

    lax.fori_loop(0, width // HEAD_DIM, one_head, 0)


def attend_back(grads, queries, keys, values, attended, stored, groups):
    half, width = keys[0].shape
    count = len(grads)
    rows = grads[0].shape[0]
    outs = pl.pallas_call(
        partial(
            backward_kernel,
            count=count,
            groups=groups,
            scale=1.0 / math.sqrt(HEAD_DIM),
        ),
        in_specs=[pl.BlockSpec(memory_space=pltpu.VMEM)] * (count + 9),
        out_specs=[pl.BlockSpec(memory_space=pltpu.VMEM)] * 9,
        out_shape=[jax.ShapeDtypeStruct((half, width), bf16)] * 6
        + [jax.ShapeDtypeStruct((rows, width), bf16)] * 3,
        scratch_shapes=[pltpu.VMEM(stored.shape[1:], bf16)],
        compiler_params=params(8 + 2 * stored.shape[1] * stored.shape[2] // 2**20),
        cost_estimate=cost(8 * 4 * half * half * width, 32 * half * width + 2 * stored.size),
        name="attend_back",
    )(*grads, *queries, *keys, *values, *attended, stored)
    return outs[0:2], outs[2:4], outs[4:6], outs[6:9]


def body(
    inputs,
    first_gain,
    query_weight,
    key_weight,
    value_weight,
    output_weight,
    second_gain,
    up_weight,
    down_weight,
    frame_sizes,
    text_counts,
    action_counts,
    cotangent,
):
    shards = lax.axis_size("seq")
    shard_index = lax.axis_index("seq")
    core = lax.axis_index("mlp") % 2
    length, width = inputs.shape
    total = length * shards
    half = length // 2
    piece = half // shards
    clips = frame_sizes.shape[0]
    clip_length = total // clips
    part = width // shards
    groups = shards if piece % 8 == 0 else 1

    def halves(rows):
        cut = rows.reshape(2, piece, shards, width)
        mine = lax.dynamic_index_in_dim(cut, core, 0, keepdims=False)
        other = lax.dynamic_index_in_dim(cut, 1 - core, 0, keepdims=False)
        return (
            mine.transpose(1, 0, 2).reshape(half, width),
            other.transpose(1, 0, 2).reshape(half, width),
        )

    inputs_half, inputs_other = halves(inputs)
    pieces = gather_early(inputs_half)
    arrived = pieces[inner_size() :: inner_size()]

    place_a, place_b, kind_a, kind_b, query_place, own_place, own_kind = tables(
        frame_sizes, text_counts, action_counts, shards, length, groups
    )
    places, kinds = (place_a, place_b), (kind_a, kind_b)
    half_kind = own_kind[:half]
    own_normed = own_norm(
        jnp.concatenate([inputs_half, inputs_other], axis=0), first_gain, own_kind
    )
    grad_half, grad_other = halves(cotangent)
    grad_own = jnp.concatenate([grad_half, grad_other], axis=0)
    (query_own,) = project_rows(after(own_normed, arrived), query_weight)
    grad_far = gather_outer(after(grad_half, arrived, pieces[inner_size() + 1]))
    pieces = after(pieces, query_own)

    normed = [norm_pieces(pieces, first_gain, kind_a, groups)]
    normed[0], grad_far = after((normed[0], grad_far), normed[0])
    normed.append(swap(normed[0], "mlp", 1))
    keys, values = zip(*[project_rows(rows, key_weight, value_weight) for rows in normed])
    heads_own = attend(query_own, keys, values, places, own_place, clip_length, clips)
    grad_inner = gather_inner(after(grad_half, normed[0]))
    heads_own, grad_inner = after((heads_own, grad_inner), heads_own)
    grad_far = join_x(jnp.concatenate(grad_far, axis=0), heads_own)
    mine, other = product_halves([heads_own], [output_weight], NN)
    other, grad_far = after((other, grad_far), other)
    grad_inner += gather_inner(grad_far)
    low, other = pair_mlp(mine, other)
    own_activated_grad = grad_activated(after(grad_own, low), down_weight)
    other = after(other, own_activated_grad)
    residual, lifted_half = lift(inputs_half, low, other, second_gain, half_kind)

    lifted_own = both(lifted_half)
    activated_own, hidden_own, mine, other = feed_own(lifted_own, up_weight, own_activated_grad)
    lifted_far = gather_outer(after(lifted_half, other))
    other, grad_inner = after((other, grad_inner), other)
    low, other = pair_mlp(mine, other)
    down_mine, down_other = down_own(after(activated_own, low), down_weight)
    other, lifted_far = after((other, lifted_far), down_other)
    grad_residual, mixed_half, mixed_columns = middle(
        residual, low, other, grad_half, second_gain, half_kind, shards
    )
    heads_grad = product_back(both(mixed_half), output_weight)

    heads_first = gather_first(heads_grad)
    queries = [project_rows(rows, query_weight)[0] for rows in after(normed, heads_grad)]
    attended, stored = attend_all(
        queries, keys, values, places, query_place, groups, clip_length, clips
    )
    lifted_far = jnp.concatenate(lifted_far, axis=0)
    lifted_inner = gather_inner(after(lifted_half, heads_grad))
    lifted_inner_far = gather_inner(lifted_far)
    lifted_far = join_x(lifted_far, heads_first, attended)
    heads_grads = gather_pieces(*heads_first)
    first_lifted, first_grads = with_core([lifted_far]), with_core([grad_far])
    own = (lifted_own, grad_own, activated_own, hidden_own)
    sums = feed_all(first_lifted, first_grads, up_weight, down_weight, shards, own=own)
    down_low, down_other = pair_mlp(down_mine, after(down_other, heads_grad))
    heads_grads, down_low, down_other, lifted_inner, lifted_inner_far = after(
        (heads_grads, down_low, down_other, lifted_inner, lifted_inner_far), sums
    )

    query_low, key_low, value_low, own_low = attend_back(
        heads_grads, queries, keys, values, attended, stored, groups
    )
    attention_weights = (query_weight, key_weight, value_weight)
    lifted_inner += [join_x(far, own_low) for far in lifted_inner_far]
    own_low, lifted_inner = after((own_low, lifted_inner), own_low)
    low, other = pair_mlp(*product_halves(own_low, attention_weights, NT))

    query_grad, key_grad, value_grad, first_gain_grad = project(
        normed,
        after((query_low, key_low, value_low), low),
        attention_weights,
        first_gain,
        kinds,
        shards,
    )
    mixed_part = lax.all_to_all(
        after(mixed_columns, query_grad), "seq", split_axis=0, concat_axis=0, tiled=True
    )
    first_gain_grad = first_gain_grad + swap(first_gain_grad, "mlp", 1)
    other, first_gain_grad = after((other, first_gain_grad), query_grad)
    input_half = last(inputs_half, low, other, grad_residual, first_gain, half_kind, shards)
    outputs_half = finish(residual, down_low, after(down_other, input_half), shards)
    rest_lifted = with_core(after(lifted_inner, other))
    rest_grads = with_core(after(grad_inner, other))
    up_grad, down_grad = feed_all(
        after(rest_lifted, outputs_half), rest_grads, up_weight, down_weight, shards, sums
    )
    bit = 2
    while bit < lax.axis_size("mlp"):
        came = after(swap(first_gain_grad, "mlp", bit), up_grad)
        first_gain_grad = first_gain_grad + came
        bit *= 2
    input_grad = place_halves(input_half)
    outputs = place_halves(outputs_half)
    mixed_part = after(mixed_part, up_grad)
    output_grad, second_gain_grad = output_part(
        attended, (mixed_part, swap(mixed_part, "mlp", 1)), groups
    )

    return (
        outputs,
        input_grad,
        first_gain_grad,
        query_grad,
        key_grad,
        value_grad,
        output_grad,
        second_gain_grad,
        up_grad,
        down_grad,
    )


def solution(mesh):
    return jax.shard_map(
        body,
        mesh=mesh,
        in_specs=(
            P("seq", None),
            P(),
            P(None, "mlp"),
            P(None, "mlp"),
            P(None, "mlp"),
            P("mlp", None),
            P(),
            P(None, "mlp"),
            P("mlp", None),
            P(),
            P(),
            P(),
            P("seq", None),
        ),
        out_specs=(
            P("seq", None),
            P("seq", None),
            P(None, "seq"),
            P("seq", "mlp"),
            P("seq", "mlp"),
            P("seq", "mlp"),
            P("mlp", "seq"),
            P(None, "seq"),
            P("seq", "mlp"),
            P("mlp", "seq"),
        ),
        check_vma=False,
    )
```

```python
from functools import partial
import math

import jax
import jax.numpy as jnp
from jax import lax
from jax.experimental import pallas as pl
from jax.experimental.pallas import tpu as pltpu
from jax.sharding import PartitionSpec as P

HEAD_DIM = 128
epsilon = 1e-05
bf16 = jnp.bfloat16
f32 = jnp.float32
NEGATIVE = -1e30

NN = ((1,), (0,))
NT = ((1,), (1,))
TN = ((0,), (0,))


def dot(a, b, dims):
    return lax.dot_general(a, b, (dims, ((), ())), preferred_element_type=f32)


def params(mebibytes):
    return pltpu.CompilerParams(vmem_limit_bytes=mebibytes * 1024 * 1024)


def cost(flops, moved, transcendentals=0, share=100):
    return pl.CostEstimate(
        flops=int(flops) // share,
        bytes_accessed=int(moved) // share,
        transcendentals=int(transcendentals) // share,
    )


def swap(value, axis, bit):
    size = lax.axis_size(axis)
    return lax.ppermute(value, axis, [(i, i ^ bit) for i in range(size)])


def inner_size():
    return 1 << (int(math.log2(lax.axis_size("seq"))) // 2)


def x_size():
    return lax.axis_size("mlp") // 2


def after(values, *earlier):
    return lax.optimization_barrier((values, earlier))[0]


def in_hbm(array):
    return pltpu.with_memory_space_constraint(array, pltpu.HBM)


def own_quarter(half):
    rows = half.shape[0] // x_size()
    return lax.dynamic_slice_in_dim(half, (lax.axis_index("mlp") // 2) * rows, rows, 0)


def join_x(quarter, *earlier):
    bit = 1
    while bit < x_size():
        came = after(swap(quarter, "mlp", 2 * bit), earlier)
        quarter = jnp.concatenate([quarter, came], axis=0)
        bit *= 2
    return quarter


def gather_early(half):
    size, inner = lax.axis_size("seq"), inner_size()
    quarter = own_quarter(half)
    pieces = {0: half}
    far = {outer: swap(quarter, "seq", outer) for outer in range(inner, size, inner)}
    for bit in range(1, inner):
        pieces[bit] = swap(half, "seq", bit)
    for outer in range(inner, size, inner):
        pieces[outer] = join_x(far[outer])
        for bit in range(1, inner):
            pieces[outer | bit] = swap(pieces[outer], "seq", bit)
    return [pieces[d] for d in range(size)]


def gather_outer(half):
    size, inner = lax.axis_size("seq"), inner_size()
    quarter = own_quarter(half)
    return [swap(quarter, "seq", outer) for outer in range(inner, size, inner)]


def gather_inner(array):
    return [swap(array, "seq", bit) for bit in range(1, inner_size())]


def with_core(arrays):
    return [each for array in arrays for each in (array, swap(array, "mlp", 1))]


def gather_first(piece):
    size, inner = lax.axis_size("seq"), inner_size()
    pieces = {0: piece}
    for bit in range(1, inner):
        pieces[bit] = swap(piece, "seq", bit)
    return pieces, [swap(piece, "seq", outer) for outer in range(inner, size, inner)]


def gather_pieces(pieces, far):
    size, inner = lax.axis_size("seq"), inner_size()
    for outer, came in zip(range(inner, size, inner), far):
        pieces[outer] = came
        for bit in range(1, inner):
            pieces[outer | bit] = swap(came, "seq", bit)
    return [pieces[d] for d in range(size)]


def rounded(value):
    return lax.optimization_barrier(value.astype(bf16))


def pair_mlp(mine, other_half):
    low, other = rounded(mine + swap(other_half, "mlp", 1).astype(f32)), None
    bit = 2
    while bit < lax.axis_size("mlp"):
        if other is not None:
            low = rounded(low.astype(f32) + other.astype(f32))
        other = swap(low, "mlp", bit)
        bit *= 2
    if other is None:
        other = jnp.zeros_like(low)
    return low, other


def both(half):
    return jnp.concatenate([half, swap(half, "mlp", 1)], axis=0)


def tables_kernel(index, frames, texts, actions, *outs, shards, length, groups, clip_length):
    place_a, place_b, kind_a, kind_b, query_place, own_place, own_kind = outs
    shard_index, core = index[0], index[1]
    shape = (shards, length)
    place = lax.broadcasted_iota(jnp.int32, shape, 0) * length + lax.broadcasted_iota(
        jnp.int32, shape, 1
    )
    kinds = jnp.full(shape, 2, jnp.int32)
    for clip in range(frames.shape[0]):
        start = jnp.int32(clip * clip_length)
        within = (place >= clip * clip_length) & (place < (clip + 1) * clip_length)
        for frame in range(frames.shape[1]):
            text_end = start + texts[clip, frame]
            action_end = text_end + actions[clip, frame]
            kinds = jnp.where(within & (place >= start) & (place < text_end), 0, kinds)
            kinds = jnp.where(within & (place >= text_end) & (place < action_end), 1, kinds)
            start = action_end + frames[clip, frame]
    square = (length, length)
    down = lax.broadcasted_iota(jnp.int32, square, 0)
    across = lax.broadcasted_iota(jnp.int32, square, 1)
    earlier = (down < across).astype(f32).astype(bf16)
    rank = jnp.zeros(shape, f32)
    before = jnp.zeros((shards, 1), f32)
    for kind in range(3):
        chosen = (kinds == kind).astype(f32)
        rank += chosen * (dot(chosen.astype(bf16), earlier, NN) + before)
        before += chosen.sum(axis=1, keepdims=True)
    rank_low, kinds_low = rank.astype(bf16), kinds.astype(f32).astype(bf16)
    piece = length // shards // 2
    lane = lax.broadcasted_iota(jnp.int32, (1, length), 1).astype(f32)

    def find(shard, offset, side, row):
        wanted = (shard_index ^ offset) * (2 * piece) + (core ^ side) * piece + row
        pick = shard == lax.broadcasted_iota(jnp.int32, (length, shards), 1)
        pick = pick.astype(f32).astype(bf16)
        hit = dot(pick, rank_low, NN) == wanted.astype(f32)
        where = jnp.sum(jnp.where(hit, lane, 0.0), axis=1, keepdims=True).astype(jnp.int32)
        kind = jnp.sum(jnp.where(hit, dot(pick, kinds_low, NN), 0.0), axis=1, keepdims=True)
        return where + shard * length, kind.astype(jnp.int32)

    def as_row(column):
        return jnp.sum(jnp.where(down == across, column, 0), axis=0, keepdims=True)

    step = lax.broadcasted_iota(jnp.int32, (length, 1), 0)
    half = length // 2
    for side, (place_out, kind_out) in enumerate(((place_a, kind_a), (place_b, kind_b))):
        for block in range(shards // 2):
            token = step + block * length
            if groups > 1:
                shard, offset = token // (shards * piece), (token // piece) % shards
            else:
                offset, shard = token // half, (token % half) // piece
            where, kind = find(shard, offset, side, token % piece)
            at = pl.ds(block * length, length)
            place_out[at, :] = where
            kind_out[at, :] = kind
            query_place[:, pl.ds((2 * block + side) * length, length)] = as_row(where)
    where, kind = find((step % half) // piece, step * 0, step // half, step % piece)
    own_place[...] = as_row(where)
    own_kind[...] = kind


def tables(frames, texts, actions, shards, length, groups):
    index = jnp.stack([lax.axis_index("seq"), lax.axis_index("mlp") % 2]).astype(jnp.int32)
    total = shards * length
    column = jax.ShapeDtypeStruct((total // 2, 1), jnp.int32)
    return pl.pallas_call(
        partial(
            tables_kernel,
            shards=shards,
            length=length,
            groups=groups,
            clip_length=total // frames.shape[0],
        ),
        in_specs=[pl.BlockSpec(memory_space=pltpu.SMEM)] * 4,
        out_shape=[column] * 4
        + [
            jax.ShapeDtypeStruct((1, total), jnp.int32),
            jax.ShapeDtypeStruct((1, length), jnp.int32),
            jax.ShapeDtypeStruct((length, 1), jnp.int32),
        ],
        cost_estimate=cost(8 * total * length, 8 * 128 * total),
        name="tables",
    )(index, frames, texts, actions)


def rows_kernel(*refs, count):
    rows, weights, outs = refs[0], refs[1 : 1 + count], refs[1 + count :]
    for weight, out in zip(weights, outs):
        out[...] = dot(rows[...], weight[...], NN).astype(bf16)


def project_rows(rows, *weights):
    across = weights[0].shape[1]
    return pl.pallas_call(
        partial(rows_kernel, count=len(weights)),
        out_shape=[jax.ShapeDtypeStruct((rows.shape[0], across), bf16)] * len(weights),
        compiler_params=params(10),
        cost_estimate=cost(2 * rows.size * across * len(weights), 2 * rows.size),
        name="project_rows",
    )(rows, *weights)


def one_kernel(rows, weight, out):
    out[...] = dot(rows[...], weight[...], NT).astype(bf16)


def product_back(rows, weight):
    return pl.pallas_call(
        one_kernel,
        out_shape=jax.ShapeDtypeStruct((rows.shape[0], weight.shape[0]), bf16),
        compiler_params=params(6),
        cost_estimate=cost(2 * rows.size * weight.shape[0], 2 * weight.size),
        name="product_back",
    )(rows, weight)


def halves_kernel(*refs, count, dims):
    mine, other = refs[-2:]
    half = mine.shape[0]
    total = sum(dot(refs[k][...], refs[count + k][...], dims) for k in range(count))
    mine[...] = total[:half]
    other[...] = total[half:].astype(bf16)


def product_halves(rows, weights, dims):
    count = len(rows)
    half = rows[0].shape[0] // 2
    across = weights[0].shape[1 - dims[1][0]]
    shape = (half, across)
    return pl.pallas_call(
        partial(halves_kernel, count=count, dims=dims),
        out_shape=[jax.ShapeDtypeStruct(shape, f32), jax.ShapeDtypeStruct(shape, bf16)],
        compiler_params=params(10),
        cost_estimate=cost(2 * count * rows[0].size * across, 2 * count * weights[0].size),
        name="product_halves",
    )(*rows, *weights)


def down_own_kernel(rows, weight, mine, other, total):
    total[...] = jnp.zeros_like(total)

    def step(at):
        total[...] += dot(rows[:, at], weight[at, :], NN)

    tiles_of(weight.shape[0], math.gcd(weight.shape[0], 512), step)
    half = mine.shape[0]
    mine[...] = total[:half]
    other[...] = total[half:].astype(bf16)


def down_own(rows, weight):
    count, deep = rows.shape
    across = weight.shape[1]
    shape = (count // 2, across)
    return pl.pallas_call(
        down_own_kernel,
        in_specs=[WHOLE] * 2,
        out_specs=[WHOLE] * 2,
        out_shape=[jax.ShapeDtypeStruct(shape, f32), jax.ShapeDtypeStruct(shape, bf16)],
        scratch_shapes=[pltpu.VMEM((count, across), f32)],
        compiler_params=params(6),
        cost_estimate=cost(2 * rows.size * across, 2 * weight.size),
        name="down_own",
    )(rows, weight)


def gain_rows(gain, column):
    return jnp.where(
        column == 0, gain[0:1, :], jnp.where(column == 1, gain[1:2, :], gain[2:3, :])
    )


def normalize(values):
    mean = jnp.mean(values, axis=1, keepdims=True)
    centered = values - mean
    inverse = lax.rsqrt(jnp.mean(centered * centered, axis=1, keepdims=True) + epsilon)
    return (centered * inverse, inverse)


def norm_back(grad, normal, inverse, gains):
    scaled = grad * gains
    return inverse * (
        scaled
        - jnp.mean(scaled, axis=1, keepdims=True)
        - normal * jnp.mean(scaled * normal, axis=1, keepdims=True)
    )


def norm_kernel(*refs, groups, inner, parts):
    index, gain, kind, out = refs[0], refs[-3], refs[-2], refs[-1]
    pieces = refs[1:-3]
    rows, width = pieces[0].shape
    count = len(pieces)
    step = rows // parts
    for d, piece in enumerate(pieces):
        for part in range(parts):
            normal, _ = normalize(piece[pl.ds(part * step, step), :].astype(f32))
            place = part if d < inner else part ^ index[0]
            if groups > 1:
                each = groups // parts
                at = pl.ds(place * each, each)
                column = kind[at, d].reshape(step, 1)
                normed = (normal * gain_rows(gain, column)).astype(bf16)
                out[at, d] = normed.reshape(each, rows // groups, width)
            else:
                column = kind[d, place]
                out[d, place] = (normal * gain_rows(gain, column)).astype(bf16)


def norm_pieces(pieces, gain, kind, groups):
    rows, width = pieces[0].shape
    count = len(pieces)
    parts = x_size()
    if groups > 1:
        shape = (groups, count, rows // groups)
    else:
        shape = (count, parts, rows // parts)
    memory = [pl.BlockSpec(memory_space=pltpu.SMEM)]
    index = (lax.axis_index("mlp") // 2).astype(jnp.int32).reshape(1)
    out = pl.pallas_call(
        partial(norm_kernel, groups=groups, inner=inner_size(), parts=parts),
        in_specs=memory + [pl.BlockSpec(memory_space=pltpu.VMEM)] * (count + 2),
        out_shape=jax.ShapeDtypeStruct(shape + (width,), bf16),
        compiler_params=params(4 + count),
        cost_estimate=cost(10 * count * rows * width, 4 * count * rows * width),
        name="norm_pieces",
    )(index, *pieces, gain, kind.reshape(shape + (1,)))
    return out.reshape(count * rows, width)


def own_norm_kernel(rows, gain, kind, out):
    normal, _ = normalize(rows[...].astype(f32))
    out[...] = (normal * gain_rows(gain, kind[...])).astype(bf16)


def own_norm(rows, gain, kind):
    return pl.pallas_call(
        own_norm_kernel,
        out_shape=jax.ShapeDtypeStruct(rows.shape, bf16),
        compiler_params=params(4),
        cost_estimate=cost(10 * rows.size, 4 * rows.size),
        name="own_norm",
    )(rows, gain, kind)


def lift_kernel(rows, low, other, gain, kind, residual, lifted):
    value = rows[...].astype(f32) + (low[...].astype(f32) + other[...].astype(f32))
    residual[...] = value
    normal, _ = normalize(value)
    lifted[...] = (normal * gain_rows(gain, kind[...])).astype(bf16)


def lift(rows, low, other, gain, kind):
    return pl.pallas_call(
        lift_kernel,
        out_shape=[jax.ShapeDtypeStruct(rows.shape, f32), jax.ShapeDtypeStruct(rows.shape, bf16)],
        compiler_params=params(4),
        cost_estimate=cost(10 * rows.size, 12 * rows.size),
        name="lift",
    )(rows, low, other, gain, kind)


def kind_sums(term, kind):
    sums = [jnp.sum(jnp.where(kind == k, term, 0.0), axis=0, keepdims=True) for k in range(3)]
    high = [value.astype(bf16) for value in sums]
    low = [(value - part.astype(f32)).astype(bf16) for value, part in zip(sums, high)]
    zero = jnp.zeros((1, term.shape[1]), bf16)
    return jnp.concatenate(high + low + [zero, zero], axis=0)


def middle_kernel(residual, low, other, grad, gain, kind, grad_residual, mixed, parts):
    lifted_grad = low[...].astype(f32) + other[...].astype(f32)
    normal, inverse = normalize(residual[...])
    column = kind[...]
    back = norm_back(lifted_grad, normal, inverse, gain_rows(gain, column))
    value = grad[...].astype(f32) + back
    grad_residual[...] = value
    rounded_value = value.astype(bf16)
    mixed[...] = rounded_value
    sums = kind_sums(lifted_grad * normal, column)
    shards, rows, part = parts.shape
    for k in range(shards):
        parts[k, pl.ds(0, rows - 8), :] = rounded_value[:, k * part : (k + 1) * part]
        parts[k, pl.ds(rows - 8, 8), :] = sums[:, k * part : (k + 1) * part]


def middle(residual, low, other, grad, gain, kind, shards):
    rows, width = residual.shape
    return pl.pallas_call(
        middle_kernel,
        out_shape=[
            jax.ShapeDtypeStruct(residual.shape, f32),
            jax.ShapeDtypeStruct(residual.shape, bf16),
            jax.ShapeDtypeStruct((shards, rows + 8, width // shards), bf16),
        ],
        compiler_params=params(6),
        cost_estimate=cost(20 * residual.size, 16 * residual.size),
        name="middle",
    )(residual, low, other, grad, gain, kind)


def reordered(values, shards):
    count = values.shape[0]
    piece = count // shards
    to = lax.broadcasted_iota(jnp.int32, (count, count), 0)
    source = lax.broadcasted_iota(jnp.int32, (count, count), 1)
    pick = (source == (to % shards) * piece + to // shards).astype(f32).astype(bf16)
    return dot(pick, values, NN).astype(bf16)


def finish_kernel(residual, low, other, out, *, shards):
    value = residual[...] + (low[...].astype(f32) + other[...].astype(f32))
    out[...] = reordered(value.astype(bf16), shards)


def finish(residual, low, other, shards):
    return pl.pallas_call(
        partial(finish_kernel, shards=shards),
        out_shape=jax.ShapeDtypeStruct(residual.shape, bf16),
        compiler_params=params(4),
        cost_estimate=cost(2 * residual.size, 10 * residual.size),
        name="finish",
    )(residual, low, other)


def place_kernel(index, mine, other, out):
    half = mine.shape[0]
    out[pl.ds(pl.multiple_of(index[0] * half, half), half), :] = mine[...]
    out[pl.ds(pl.multiple_of((1 - index[0]) * half, half), half), :] = other[...]


def place_halves(mine):
    half, width = mine.shape
    index = (lax.axis_index("mlp") % 2).astype(jnp.int32).reshape(1)
    return pl.pallas_call(
        place_kernel,
        in_specs=[pl.BlockSpec(memory_space=pltpu.SMEM)]
        + [pl.BlockSpec(memory_space=pltpu.VMEM)] * 2,
        out_shape=jax.ShapeDtypeStruct((2 * half, width), bf16),
        compiler_params=params(4),
        cost_estimate=cost(mine.size, 8 * mine.size),
        name="place_halves",
    )(index, mine, swap(mine, "mlp", 1))


def last_kernel(rows, low, other, grad_residual, gain, kind, out, *, shards):
    grad = low[...].astype(f32) + other[...].astype(f32)
    normal, inverse = normalize(rows[...].astype(f32))
    back = norm_back(grad, normal, inverse, gain_rows(gain, kind[...]))
    out[...] = reordered((grad_residual[...] + back).astype(bf16), shards)


def last(rows, low, other, grad_residual, gain, kind, shards):
    return pl.pallas_call(
        partial(last_kernel, shards=shards),
        out_shape=jax.ShapeDtypeStruct(rows.shape, bf16),
        compiler_params=params(6),
        cost_estimate=cost(20 * rows.size, 12 * rows.size),
        name="last",
    )(rows, low, other, grad_residual, gain, kind)


def gelu_parts(value):
    rate = math.sqrt(2 / math.pi)
    square = value * value
    bent = jnp.tanh(value * (rate + (rate * 0.044715) * square))
    upper = 0.5 * (1 + bent)
    slope = upper + (0.5 * value) * (1 - bent * bent) * (rate + (rate * 3 * 0.044715) * square)
    return value * upper, slope


WHOLE = pl.BlockSpec(memory_space=pltpu.VMEM)


def tiles_of(extent, tile, step):
    def at(t, _):
        step(pl.ds(pl.multiple_of(t * tile, tile), tile))
        return 0

    lax.fori_loop(0, extent // tile, at, 0)


def own_kernel(lifted, up, grad_activated, activated, hidden_grads, mine, other, total):
    total[...] = jnp.zeros_like(total)

    def step(at):
        value, slope = gelu_parts(dot(lifted[...], up[:, at], NN))
        activated[:, at] = value.astype(bf16)
        hidden_grad = (grad_activated[:, at] * slope).astype(bf16)
        hidden_grads[:, at] = hidden_grad
        total[...] += dot(hidden_grad, up[:, at], NT)

    tiles_of(up.shape[1], math.gcd(up.shape[1], 512), step)
    half = mine.shape[0]
    mine[...] = total[:half]
    other[...] = total[half:].astype(bf16)


def feed_own(lifted, up, grad_activated):
    rows, width = lifted.shape
    hidden = up.shape[1]
    return pl.pallas_call(
        own_kernel,
        in_specs=[WHOLE] * 3,
        out_specs=[WHOLE] * 4,
        out_shape=[jax.ShapeDtypeStruct((rows, hidden), bf16)] * 2
        + [
            jax.ShapeDtypeStruct((rows // 2, width), f32),
            jax.ShapeDtypeStruct((rows // 2, width), bf16),
        ],
        scratch_shapes=[pltpu.VMEM((rows, width), f32)],
        compiler_params=params(8),
        cost_estimate=cost(4 * rows * width * hidden, 2 * width * hidden),
        name="feed_own",
    )(lifted, up, grad_activated)


def down_kernel(grad, down, out):
    def step(at):
        out[:, at] = dot(grad[...], down[at, :], NT)

    tiles_of(down.shape[0], math.gcd(down.shape[0], 512), step)


def grad_activated(grad, down):
    rows, width = grad.shape
    hidden = down.shape[0]
    return pl.pallas_call(
        down_kernel,
        in_specs=[WHOLE] * 2,
        out_specs=WHOLE,
        out_shape=jax.ShapeDtypeStruct((rows, hidden), f32),
        compiler_params=params(6),
        cost_estimate=cost(2 * rows * width * hidden, 2 * width * hidden),
        name="grad_activated",
    )(grad, down)


def all_kernel(index, *refs, counts):
    count = len(counts)
    lifted_parts, grad_parts = refs[:count], refs[count : 2 * count]
    up, down = refs[2 * count : 2 * count + 2]
    before = refs[2 * count + 2 : -8]
    up_grad, down_grad, lifted, grad, lifted_across, hidden_kept, grad_kept, sems = refs[-8:]
    part = up_grad.shape[0]
    mine = pl.ds(pl.multiple_of(index[0] * part, part), part)

    @pl.when(pl.program_id(0) == 0)
    def _():
        copies = []
        for k, (source, target) in enumerate(((lifted_parts, lifted), (grad_parts, grad))):
            start = 0
            for j, rows in enumerate(counts):
                here = target.at[pl.ds(start, rows)]
                copies.append(pltpu.make_async_copy(source[j], here, sems.at[k * count + j]))
                start += rows
        for copy in copies:
            copy.start()
        for copy in copies:
            copy.wait()
        lifted_across[...] = lifted[:, mine].T

    first = pl.program_id(0) == 0
    last_step = pl.num_programs(0) - 1

    tile = hidden_kept.shape[1]
    at = jnp.minimum(pl.program_id(0), last_step - 1) if up.shape[1] > tile else 0
    here = pl.ds(pl.multiple_of(at * tile, tile), tile)

    def products():
        return dot(lifted[...], up[:, here], NN), dot(grad[...], down[here, :], NT)

    def finish_tile(hidden_value, activated_grad):
        value, slope = gelu_parts(hidden_value)
        hidden_grad = (activated_grad * slope).astype(bf16)
        down_term = dot(value.astype(bf16), grad[:, mine], TN)
        up_term = dot(lifted_across[...], hidden_grad, NN)
        if len(before) == 2:
            up_term += before[0][...]
            down_term += before[1][...]
        else:
            lifted_own, grad_own, activated, hidden_own = before
            up_term += dot(lifted_own[...], hidden_own[...], TN)
            down_term += dot(activated[...], grad_own[...], TN)
        up_grad[...] = up_term
        down_grad[...] = down_term

    @pl.when(first)
    def _():
        hidden_kept[...], grad_kept[...] = products()

    @pl.when((pl.program_id(0) > 0) & (pl.program_id(0) < last_step))
    def _():
        kept = hidden_kept[...], grad_kept[...]
        fresh = products()
        finish_tile(*kept)
        hidden_kept[...], grad_kept[...] = fresh

    @pl.when(pl.program_id(0) == last_step)
    def _():
        finish_tile(hidden_kept[...], grad_kept[...])


def feed_all(lifted, grad, up, down, shards, sums=(), own=()):
    counts = [array.shape[0] for array in lifted]
    rows, width = sum(counts), lifted[0].shape[1]
    count = len(counts)
    part = width // shards
    hidden = up.shape[1]
    tile = math.gcd(hidden, 256)
    steps = hidden // tile
    wide = lambda t, index: (0, jnp.minimum(t, steps - 1))
    deep = lambda t, index: (jnp.minimum(t, steps - 1), 0)
    across = lambda t, index: (0, jnp.maximum(t - 1, 0))
    below = lambda t, index: (jnp.maximum(t - 1, 0), 0)
    mine = lambda t, index: (0, index[0])
    anywhere = pl.BlockSpec(memory_space=pl.ANY)
    sum_specs = [pl.BlockSpec((part, tile), across), pl.BlockSpec((tile, part), below)]
    if own:
        own_rows = own[0].shape[0]
        more = [pl.BlockSpec((own_rows, part), mine)] * 2
        more += [pl.BlockSpec((own_rows, tile), across)] * 2
    else:
        more = sum_specs
    index = lax.axis_index("seq").astype(jnp.int32).reshape(1)
    return pl.pallas_call(
        partial(all_kernel, counts=counts),
        grid_spec=pltpu.PrefetchScalarGridSpec(
            num_scalar_prefetch=1,
            grid=(steps + 1,),
            in_specs=[anywhere] * (2 * count)
            + (
                [WHOLE] * 2
                if own
                else [pl.BlockSpec((width, tile), wide), pl.BlockSpec((tile, width), deep)]
            )
            + more,
            out_specs=sum_specs,
            scratch_shapes=[pltpu.VMEM((rows, width), bf16)] * 2
            + [pltpu.VMEM((part, rows), bf16)]
            + [pltpu.VMEM((rows, tile), f32)] * 2
            + [pltpu.SemaphoreType.DMA((2 * count,))],
        ),
        out_shape=[pltpu.HBM((part, hidden), f32), pltpu.HBM((hidden, part), f32)],
        compiler_params=params((6 if own else 8) + 8 * rows // 512),
        cost_estimate=cost(
            4 * rows * hidden * (width + part),
            4 * width * hidden + 4 * rows * width,
        ),
        name="feed_all",
    )(
        index,
        *lifted,
        *grad,
        *((up, down) if own else (in_hbm(up), in_hbm(down))),
        *(own or [in_hbm(array) for array in sums]),
    )


def project_kernel(index, *refs):
    normed, lows, weights = refs[0:2], refs[2:8], refs[8:11]
    gain, kinds = refs[11], refs[12:14]
    outs, gain_grad = refs[14:17], refs[17]
    for k in range(3):
        outs[k][...] = sum(dot(normed[side][...], lows[2 * k + side][...], TN) for side in range(2))
    gain_sum = [0.0, 0.0, 0.0]
    for side in range(2):
        column = kinds[side][...]
        term = sum(dot(lows[2 * k + side][...], weights[k][...], NT) for k in range(3))
        term = term * (normed[side][...].astype(f32) / gain_rows(gain, column))
        for k in range(3):
            gain_sum[k] += jnp.sum(jnp.where(column == k, term, 0.0), axis=0, keepdims=True)
    gain_grad[...] = jnp.concatenate(gain_sum, axis=0)


def project(normed, lows, weights, gain, kinds, shards):
    rows, width = normed[0].shape
    across = lows[0][0].shape[1]
    part = width // shards
    whole = lambda t, index: (0, 0)
    mine = lambda t, index: (0, index[0])
    below = lambda t, index: (index[0], 0)
    index = lax.axis_index("seq").astype(jnp.int32).reshape(1)
    return pl.pallas_call(
        project_kernel,
        grid_spec=pltpu.PrefetchScalarGridSpec(
            num_scalar_prefetch=1,
            grid=(1,),
            in_specs=[pl.BlockSpec((rows, part), mine)] * 2
            + [pl.BlockSpec((rows, across), whole)] * 6
            + [pl.BlockSpec((part, across), below)] * 3
            + [pl.BlockSpec((gain.shape[0], part), mine)]
            + [pl.BlockSpec((rows, 1), whole)] * 2,
            out_specs=[pl.BlockSpec((part, across), whole)] * 3
            + [pl.BlockSpec((gain.shape[0], part), whole)],
        ),
        out_shape=[jax.ShapeDtypeStruct((part, across), f32)] * 3
        + [jax.ShapeDtypeStruct((gain.shape[0], part), f32)],
        compiler_params=params(14),
        cost_estimate=cost(24 * rows * part * across, 12 * rows * across + 12 * part * across),
        name="project",
    )(index, *normed, *[low for pair in lows for low in pair], *weights, gain, *kinds)


def output_kernel(index, attended_a, attended_b, came_a, came_b, out, gain_grad, *, groups):
    total, sums = 0.0, 0.0
    shards, rows, part = came_a.shape
    half = rows - 8
    each = half // groups
    for attended, came in ((attended_a, came_a), (attended_b, came_b)):
        mixed = [
            came[index[0] ^ d, pl.ds(group * each, each), :]
            for group in range(groups)
            for d in range(shards)
        ]
        total += dot(attended[...], jnp.concatenate(mixed, axis=0), TN)
        own_sums = 0.0
        for k in range(shards):
            own_sums += came[k, pl.ds(half, 8), :].astype(f32)
        sums += own_sums
    out[...] = total
    gain_grad[...] = sums[0:3, :] + sums[3:6, :]


def output_part(attended, came, groups):
    index = lax.axis_index("seq").astype(jnp.int32).reshape(1)
    across, part = attended[0].shape[1], came[0].shape[2]
    return pl.pallas_call(
        partial(output_kernel, groups=groups),
        in_specs=[pl.BlockSpec(memory_space=pltpu.SMEM)]
        + [pl.BlockSpec(memory_space=pltpu.VMEM)] * 4,
        out_shape=[
            jax.ShapeDtypeStruct((across, part), f32),
            jax.ShapeDtypeStruct((3, part), f32),
        ],
        compiler_params=params(6),
        cost_estimate=cost(
            4 * attended[0].shape[0] * across * part, 4 * attended[0].shape[0] * (across + part)
        ),
        name="output_part",
    )(index, *attended, *came)


def mask_of(key_place, query_place, clip_length, clips):
    allowed = key_place <= query_place
    if clips > 1:
        allowed = allowed & (key_place // clip_length == query_place // clip_length)
    return allowed


def probabilities(scores, scale):
    top = scores[0].max(axis=0, keepdims=True)
    for block in scores[1:]:
        top = jnp.maximum(top, block.max(axis=0, keepdims=True))
    rate = scale * math.log2(math.e)
    weights = [jnp.exp2((block - top) * rate) for block in scores]
    total = weights[0].sum(axis=0, keepdims=True)
    for block in weights[1:]:
        total = total + block.sum(axis=0, keepdims=True)
    inverse = 1.0 / total
    return [block * inverse for block in weights]


def forward_kernel(query, key_a, key_b, value_a, value_b, place_a, place_b, query_place, out, **opts):
    scale = opts["scale"]
    query_place = query_place[...]
    allowed = [
        mask_of(place[...], query_place, opts["clip_length"], opts["clips"])
        for place in (place_a, place_b)
    ]
    for head in range(query.shape[1] // HEAD_DIM):
        at = pl.ds(head * HEAD_DIM, HEAD_DIM)
        scores = [
            jnp.where(mask, dot(key[:, at], query[:, at], NT), NEGATIVE)
            for mask, key in zip(allowed, (key_a, key_b))
        ]
        prob = [block.astype(bf16) for block in probabilities(scores, scale)]
        result = dot(value_a[:, at], prob[0], TN) + dot(value_b[:, at], prob[1], TN)
        out[:, at] = result.T.astype(bf16)


def attend(query, keys, values, places, query_place, clip_length, clips):
    rows, width = query.shape
    total = 2 * keys[0].shape[0]
    return pl.pallas_call(
        partial(
            forward_kernel, scale=1.0 / math.sqrt(HEAD_DIM), clip_length=clip_length, clips=clips
        ),
        out_shape=jax.ShapeDtypeStruct((rows, width), bf16),
        compiler_params=params(8),
        cost_estimate=cost(
            4 * rows * total * width, 4 * total * width, rows * total * (width // HEAD_DIM)
        ),
        name="attend",
    )(query, *keys, *values, *places, query_place)


def block_of(half):
    return min(128, half)


def reaches(half, groups):
    blocks = half // block_of(half)
    found, start = [], 0
    for index in range(blocks):
        seen, free = (index + 1, index) if groups > 1 else (blocks, 0)
        found.append((seen, free, start))
        start += seen
    return found, start


def take(first, second, low, high, at):
    block = block_of(first.shape[0])
    rows = [side[pl.ds(k * block, block), at] for k in range(low, high) for side in (first, second)]
    return jnp.concatenate(rows, axis=0)


def columns_of(head):
    return pl.ds(pl.multiple_of(head * HEAD_DIM, HEAD_DIM), HEAD_DIM)


def all_forward_kernel(*refs, groups, scale, clip_length, clips):
    query_a, query_b, key_a, key_b, value_a, value_b, place_a, place_b, query_place = refs[:9]
    attended_a, attended_b, stored, kept_probs, sems = refs[9:]
    half, width = key_a.shape
    heads = width // HEAD_DIM
    block = block_of(half)
    pair = 2 * block
    everything = slice(None)

    def copy_of(head):
        slot = head % 2
        return pltpu.make_async_copy(kept_probs.at[slot], stored.at[head], sems.at[slot])

    def one_head(head, _):
        cut = columns_of(head)
        slot = head % 2

        @pl.when(head >= 2)
        def _():
            copy_of(head - 2).wait()

        values_across = take(value_a, value_b, 0, half // block, cut).T
        for index, (seen, free, start) in enumerate(reaches(half, groups)[0]):
            mine = pl.ds(index * block, block)
            query = take(query_a, query_b, index, index + 1, cut)
            at_place = query_place[:, pl.ds(index * pair, pair)]
            place = take(place_a, place_b, free, seen, everything)
            mask = mask_of(place, at_place, clip_length, clips)
            score = dot(take(key_a, key_b, free, seen, cut), query, NT)
            scores = [jnp.where(mask, score, NEGATIVE)]
            if free:
                scores.insert(0, dot(take(key_a, key_b, 0, free, cut), query, NT))
            result, at = 0.0, 0
            for prob in probabilities(scores, scale):
                kept = prob.astype(bf16)
                rows = kept.shape[0]
                kept_probs[slot, pl.ds(start * pair + at, rows), :] = kept
                result += dot(values_across[:, at : at + rows], kept, NN)
                at += rows
            result = result.T.astype(bf16)
            attended_a[mine, cut] = result[:block]
            attended_b[mine, cut] = result[block:]
        copy_of(head).start()
        return 0

    lax.fori_loop(0, heads, one_head, 0)
    for head in range(max(0, heads - 2), heads):
        copy_of(head).wait()


def attend_all(queries, keys, values, places, query_place, groups, clip_length, clips):
    half, width = keys[0].shape
    heads = width // HEAD_DIM
    pair = 2 * block_of(half)
    deep = reaches(half, groups)[1] * pair
    outs = pl.pallas_call(
        partial(
            all_forward_kernel,
            groups=groups,
            scale=1.0 / math.sqrt(HEAD_DIM),
            clip_length=clip_length,
            clips=clips,
        ),
        in_specs=[pl.BlockSpec(memory_space=pltpu.VMEM)] * 9,
        out_specs=[pl.BlockSpec(memory_space=pltpu.VMEM)] * 2
        + [pl.BlockSpec(memory_space=pl.ANY)],
        out_shape=[jax.ShapeDtypeStruct((half, width), bf16)] * 2
        + [pltpu.HBM((heads, deep, pair), bf16)],
        scratch_shapes=[
            pltpu.VMEM((2, deep, pair), bf16),
            pltpu.SemaphoreType.DMA((2,)),
        ],
        compiler_params=params(max(10, half * half // 2**14)),
        cost_estimate=cost(16 * half * half * width, 16 * half * width, 4 * half * half * heads),
        name="attend_all",
    )(*queries, *keys, *values, *places, query_place)
    return outs[:2], outs[2]


def backward_kernel(*refs, count, groups, scale):
    grad_pieces = refs[:count]
    query_a, query_b, key_a, key_b, value_a, value_b, attended_a, attended_b, stored = refs[
        count : count + 9
    ]
    outs = refs[count + 9 : count + 18]
    grad_query, grad_key, grad_value = outs[0:2], outs[2:4], outs[4:6]
    own_query, own_key, own_value = outs[6:9]
    (scores,) = refs[count + 18 :]
    half, width = key_a.shape
    rows = half // count
    group_rows = rows // groups
    block = block_of(half)
    blocks = half // block
    pair = 2 * block
    reach = reaches(half, groups)[0]

    def sources(index):
        found = []
        if groups == 1:
            for d in range(index * block // rows, (index + 1) * block // rows):
                found.append((d, 0, rows))
            return found
        each = count * group_rows
        for j in range(index * block // each, (index + 1) * block // each):
            for d in range(count):
                found.append((d, j * group_rows, group_rows))
        return found

    def one_head(head, _):
        cut = columns_of(head)

        def keep(targets, own, values, index):
            for side in range(2):
                at = side * block
                targets[side][pl.ds(index * block, block), cut] = values[at : at + block]
                for d, start, size in sources(index):
                    if d == 0:
                        own[pl.ds(side * rows + start, size), cut] = values[at : at + size]
                    at += size

        def take_grads(index):
            return jnp.concatenate(
                [
                    grad_pieces[d][pl.ds(side * rows + start, size), cut]
                    for side in range(2)
                    for d, start, size in sources(index)
                ],
                axis=0,
            )

        keys_across = take(key_a, key_b, 0, blocks, cut).T
        ones = jnp.ones((8, HEAD_DIM), f32)
        for index, (seen, _, start) in enumerate(reach):
            result = take(attended_a, attended_b, index, index + 1, cut)
            grad = take_grads(index)
            delta = lax.dot_general(
                ones,
                grad.astype(f32) * result.astype(f32),
                (NT, ((), ())),
                precision=lax.Precision.HIGHEST,
                preferred_element_type=f32,
            )[0:1, :]
            at = pl.ds(start * pair, seen * pair)
            grad_prob = dot(take(value_a, value_b, 0, seen, cut), grad, NT)
            score = (stored[head, at, :].astype(f32) * (grad_prob - delta)).astype(bf16)
            scores[at, :] = score
            back = dot(keys_across[:, : seen * pair], score, NN)
            keep(grad_query, own_query, (back * scale).T.astype(bf16), index)
        for index in range(blocks):
            key_sum, value_sum = 0.0, 0.0
            for other, (seen, _, start) in enumerate(reach):
                if index < seen:
                    at = pl.ds((start + index) * pair, pair)
                    query = take(query_a, query_b, other, other + 1, cut)
                    key_sum += dot(scores[at, :], query, NN)
                    value_sum += dot(stored[head, at, :], take_grads(other), NN)
            keep(grad_key, own_key, (key_sum * scale).astype(bf16), index)
            keep(grad_value, own_value, value_sum.astype(bf16), index)
        return 0

    lax.fori_loop(0, width // HEAD_DIM, one_head, 0)


def attend_back(grads, queries, keys, values, attended, stored, groups):
    half, width = keys[0].shape
    count = len(grads)
    rows = grads[0].shape[0]
    outs = pl.pallas_call(
        partial(
            backward_kernel,
            count=count,
            groups=groups,
            scale=1.0 / math.sqrt(HEAD_DIM),
        ),
        in_specs=[pl.BlockSpec(memory_space=pltpu.VMEM)] * (count + 9),
        out_specs=[pl.BlockSpec(memory_space=pltpu.VMEM)] * 9,
        out_shape=[jax.ShapeDtypeStruct((half, width), bf16)] * 6
        + [jax.ShapeDtypeStruct((rows, width), bf16)] * 3,
        scratch_shapes=[pltpu.VMEM(stored.shape[1:], bf16)],
        compiler_params=params(8 + 2 * stored.shape[1] * stored.shape[2] // 2**20),
        cost_estimate=cost(8 * 4 * half * half * width, 32 * half * width + 2 * stored.size),
        name="attend_back",
    )(*grads, *queries, *keys, *values, *attended, stored)
    return outs[0:2], outs[2:4], outs[4:6], outs[6:9]


def body(
    inputs,
    first_gain,
    query_weight,
    key_weight,
    value_weight,
    output_weight,
    second_gain,
    up_weight,
    down_weight,
    frame_sizes,
    text_counts,
    action_counts,
    cotangent,
):
    shards = lax.axis_size("seq")
    shard_index = lax.axis_index("seq")
    core = lax.axis_index("mlp") % 2
    length, width = inputs.shape
    total = length * shards
    half = length // 2
    piece = half // shards
    clips = frame_sizes.shape[0]
    clip_length = total // clips
    part = width // shards
    groups = shards if piece % 8 == 0 else 1

    def halves(rows):
        cut = rows.reshape(2, piece, shards, width)
        mine = lax.dynamic_index_in_dim(cut, core, 0, keepdims=False)
        other = lax.dynamic_index_in_dim(cut, 1 - core, 0, keepdims=False)
        return (
            mine.transpose(1, 0, 2).reshape(half, width),
            other.transpose(1, 0, 2).reshape(half, width),
        )

    inputs_half, inputs_other = halves(inputs)
    pieces = gather_early(inputs_half)
    arrived = pieces[inner_size() :: inner_size()]

    place_a, place_b, kind_a, kind_b, query_place, own_place, own_kind = tables(
        frame_sizes, text_counts, action_counts, shards, length, groups
    )
    places, kinds = (place_a, place_b), (kind_a, kind_b)
    half_kind = own_kind[:half]
    own_normed = own_norm(
        jnp.concatenate([inputs_half, inputs_other], axis=0), first_gain, own_kind
    )
    grad_half, grad_other = halves(cotangent)
    grad_own = jnp.concatenate([grad_half, grad_other], axis=0)
    (query_own,) = project_rows(after(own_normed, arrived), query_weight)
    grad_far = gather_outer(after(grad_half, arrived, pieces[inner_size() + 1]))
    pieces = after(pieces, query_own)

    normed = [norm_pieces(pieces, first_gain, kind_a, groups)]
    normed[0], grad_far = after((normed[0], grad_far), normed[0])
    normed.append(swap(normed[0], "mlp", 1))
    keys, values = zip(*[project_rows(rows, key_weight, value_weight) for rows in normed])
    heads_own = attend(query_own, keys, values, places, own_place, clip_length, clips)
    grad_inner = gather_inner(after(grad_half, normed[0]))
    heads_own, grad_inner = after((heads_own, grad_inner), heads_own)
    grad_far = join_x(jnp.concatenate(grad_far, axis=0), heads_own)
    mine, other = product_halves([heads_own], [output_weight], NN)
    other, grad_far = after((other, grad_far), other)
    grad_inner += gather_inner(grad_far)
    low, other = pair_mlp(mine, other)
    own_activated_grad = grad_activated(after(grad_own, low), down_weight)
    queries = [
        project_rows(rows, query_weight)[0] for rows in after(normed, own_activated_grad)
    ]
    other = after(other, queries)
    residual, lifted_half = lift(inputs_half, low, other, second_gain, half_kind)

    lifted_own = both(lifted_half)
    activated_own, hidden_own, mine, other = feed_own(lifted_own, up_weight, own_activated_grad)
    lifted_far = gather_outer(after(lifted_half, other))
    other, grad_inner = after((other, grad_inner), other)
    low, other = pair_mlp(mine, other)
    attended, stored = attend_all(
        after(queries, low),
        keys,
        values,
        places,
        query_place,
        groups,
        clip_length,
        clips,
    )
    other, lifted_far = after((other, lifted_far), attended)
    grad_residual, mixed_half, mixed_columns = middle(
        residual, low, other, grad_half, second_gain, half_kind, shards
    )
    heads_grad = product_back(both(mixed_half), output_weight)

    heads_first = gather_first(heads_grad)
    lifted_far = jnp.concatenate(lifted_far, axis=0)
    lifted_inner_far = gather_inner(lifted_far)
    down_mine, down_other = down_own(after(activated_own, heads_grad), down_weight)
    lifted_far = join_x(lifted_far, heads_first[1], down_other, lifted_inner_far)
    heads_grads = gather_pieces(*heads_first)
    first_lifted, first_grads = with_core([lifted_far]), with_core([grad_far])
    first_lifted = after(first_lifted, heads_grads[inner_size() + 1])
    own = (lifted_own, grad_own, activated_own, hidden_own)
    sums = feed_all(first_lifted, first_grads, up_weight, down_weight, shards, own=own)
    down_low, down_other = pair_mlp(down_mine, down_other)
    heads_grads, down_low, down_other = after((heads_grads, down_low, down_other), sums)
    lifted_inner = gather_inner(after(lifted_half, down_other))

    query_low, key_low, value_low, own_low = attend_back(
        heads_grads, queries, keys, values, attended, stored, groups
    )
    attention_weights = (query_weight, key_weight, value_weight)
    lifted_inner += [join_x(far, own_low) for far in lifted_inner_far]
    own_low, lifted_inner = after((own_low, lifted_inner), own_low)
    low, other = pair_mlp(*product_halves(own_low, attention_weights, NT))

    query_grad, key_grad, value_grad, first_gain_grad = project(
        normed,
        after((query_low, key_low, value_low), low),
        attention_weights,
        first_gain,
        kinds,
        shards,
    )
    mixed_part = lax.all_to_all(
        after(mixed_columns, query_grad), "seq", split_axis=0, concat_axis=0, tiled=True
    )
    first_gain_grad = first_gain_grad + swap(first_gain_grad, "mlp", 1)
    other, first_gain_grad = after((other, first_gain_grad), query_grad)
    input_half = last(inputs_half, low, other, grad_residual, first_gain, half_kind, shards)
    outputs_half = finish(residual, down_low, after(down_other, input_half), shards)
    rest_lifted = with_core(after(lifted_inner, other))
    rest_grads = with_core(after(grad_inner, other))
    up_grad, down_grad = feed_all(
        after(rest_lifted, outputs_half), rest_grads, up_weight, down_weight, shards, sums
    )
    bit = 2
    while bit < lax.axis_size("mlp"):
        came = after(swap(first_gain_grad, "mlp", bit), up_grad)
        first_gain_grad = first_gain_grad + came
        bit *= 2
    input_grad = place_halves(input_half)
    outputs = place_halves(outputs_half)
    mixed_part = after(mixed_part, up_grad)
    output_grad, second_gain_grad = output_part(
        attended, (mixed_part, swap(mixed_part, "mlp", 1)), groups
    )

    return (
        outputs,
        input_grad,
        first_gain_grad,
        query_grad,
        key_grad,
        value_grad,
        output_grad,
        second_gain_grad,
        up_grad,
        down_grad,
    )


def solution(mesh):
    return jax.shard_map(
        body,
        mesh=mesh,
        in_specs=(
            P("seq", None),
            P(),
            P(None, "mlp"),
            P(None, "mlp"),
            P(None, "mlp"),
            P("mlp", None),
            P(),
            P(None, "mlp"),
            P("mlp", None),
            P(),
            P(),
            P(),
            P("seq", None),
        ),
        out_specs=(
            P("seq", None),
            P("seq", None),
            P(None, "seq"),
            P("seq", "mlp"),
            P("seq", "mlp"),
            P("seq", "mlp"),
            P("mlp", "seq"),
            P(None, "seq"),
            P("seq", "mlp"),
            P("mlp", "seq"),
        ),
        check_vma=False,
    )
```

```python
from functools import partial
import math

import jax
import jax.numpy as jnp
from jax import lax
from jax.experimental import pallas as pl
from jax.experimental.pallas import tpu as pltpu
from jax.sharding import PartitionSpec as P

HEAD_DIM = 128
epsilon = 1e-05
bf16 = jnp.bfloat16
f32 = jnp.float32
NEGATIVE = -1e30

WHOLE = pl.BlockSpec(memory_space=pltpu.VMEM)
NN = ((1,), (0,))
NT = ((1,), (1,))
TN = ((0,), (0,))


def dot(a, b, dims):
    return lax.dot_general(a, b, (dims, ((), ())), preferred_element_type=f32)


def params(mebibytes):
    return pltpu.CompilerParams(vmem_limit_bytes=mebibytes * 1024 * 1024)


def cost(flops, moved, transcendentals=0, share=100):
    return pl.CostEstimate(
        flops=int(flops) // share,
        bytes_accessed=int(moved) // share,
        transcendentals=int(transcendentals) // share,
    )


def swap(value, axis, bit):
    size = lax.axis_size(axis)
    return lax.ppermute(value, axis, [(i, i ^ bit) for i in range(size)])


def inner_size():
    return 1 << (int(math.log2(lax.axis_size("seq"))) // 2)


def x_size():
    return lax.axis_size("mlp") // 2


def after(values, *earlier):
    return lax.optimization_barrier((values, earlier))[0]


def in_hbm(array):
    return pltpu.with_memory_space_constraint(array, pltpu.HBM)


def own_quarter(half):
    rows = half.shape[0] // x_size()
    return lax.dynamic_slice_in_dim(half, (lax.axis_index("mlp") // 2) * rows, rows, 0)


def join_x(quarter, *earlier):
    bit = 1
    while bit < x_size():
        came = after(swap(quarter, "mlp", 2 * bit), earlier)
        quarter = jnp.concatenate([quarter, came], axis=0)
        bit *= 2
    return quarter


def gather_early(half):
    size, inner = lax.axis_size("seq"), inner_size()
    quarter = own_quarter(half)
    pieces = {0: half}
    far = {outer: swap(quarter, "seq", outer) for outer in range(inner, size, inner)}
    for bit in range(1, inner):
        pieces[bit] = swap(half, "seq", bit)
    for outer in range(inner, size, inner):
        pieces[outer] = join_x(far[outer])
        for bit in range(1, inner):
            pieces[outer | bit] = swap(pieces[outer], "seq", bit)
    return [pieces[d] for d in range(size)]


def gather_outer(half):
    size, inner = lax.axis_size("seq"), inner_size()
    quarter = own_quarter(half)
    return [swap(quarter, "seq", outer) for outer in range(inner, size, inner)]


def gather_inner(array):
    return [swap(array, "seq", bit) for bit in range(1, inner_size())]


def with_core(arrays):
    return [each for array in arrays for each in (array, swap(array, "mlp", 1))]


def gather_first(piece):
    size, inner = lax.axis_size("seq"), inner_size()
    pieces = {0: piece}
    for bit in range(1, inner):
        pieces[bit] = swap(piece, "seq", bit)
    return pieces, [swap(piece, "seq", outer) for outer in range(inner, size, inner)]


def gather_pieces(pieces, far):
    size, inner = lax.axis_size("seq"), inner_size()
    for outer, came in zip(range(inner, size, inner), far):
        pieces[outer] = came
        for bit in range(1, inner):
            pieces[outer | bit] = swap(came, "seq", bit)
    return [pieces[d] for d in range(size)]


def rounded(value):
    return lax.optimization_barrier(value.astype(bf16))


def pair_mlp(mine, other_half):
    low, other = rounded(mine + swap(other_half, "mlp", 1).astype(f32)), None
    bit = 2
    while bit < lax.axis_size("mlp"):
        if other is not None:
            low = rounded(low.astype(f32) + other.astype(f32))
        other = swap(low, "mlp", bit)
        bit *= 2
    if other is None:
        other = jnp.zeros_like(low)
    return low, other


def both(half):
    return jnp.concatenate([half, swap(half, "mlp", 1)], axis=0)


def tables_kernel(index, frames, texts, actions, *outs, shards, length, groups, clip_length):
    place_a, place_b, kind_a, kind_b, query_place, own_place, own_kind = outs
    shard_index, core = index[0], index[1]
    shape = (shards, length)
    place = lax.broadcasted_iota(jnp.int32, shape, 0) * length + lax.broadcasted_iota(
        jnp.int32, shape, 1
    )
    kinds = jnp.full(shape, 2, jnp.int32)
    for clip in range(frames.shape[0]):
        start = jnp.int32(clip * clip_length)
        within = (place >= clip * clip_length) & (place < (clip + 1) * clip_length)
        for frame in range(frames.shape[1]):
            text_end = start + texts[clip, frame]
            action_end = text_end + actions[clip, frame]
            kinds = jnp.where(within & (place >= start) & (place < text_end), 0, kinds)
            kinds = jnp.where(within & (place >= text_end) & (place < action_end), 1, kinds)
            start = action_end + frames[clip, frame]
    square = (length, length)
    down = lax.broadcasted_iota(jnp.int32, square, 0)
    across = lax.broadcasted_iota(jnp.int32, square, 1)
    earlier = (down < across).astype(f32).astype(bf16)
    rank = jnp.zeros(shape, f32)
    before = jnp.zeros((shards, 1), f32)
    for kind in range(3):
        chosen = (kinds == kind).astype(f32)
        rank += chosen * (dot(chosen.astype(bf16), earlier, NN) + before)
        before += chosen.sum(axis=1, keepdims=True)
    rank_low, kinds_low = rank.astype(bf16), kinds.astype(f32).astype(bf16)
    piece = length // shards // 2
    lane = lax.broadcasted_iota(jnp.int32, (1, length), 1).astype(f32)

    def find(shard, offset, side, row):
        wanted = (shard_index ^ offset) * (2 * piece) + (core ^ side) * piece + row
        pick = shard == lax.broadcasted_iota(jnp.int32, (length, shards), 1)
        pick = pick.astype(f32).astype(bf16)
        hit = dot(pick, rank_low, NN) == wanted.astype(f32)
        where = jnp.sum(jnp.where(hit, lane, 0.0), axis=1, keepdims=True).astype(jnp.int32)
        kind = jnp.sum(jnp.where(hit, dot(pick, kinds_low, NN), 0.0), axis=1, keepdims=True)
        return where + shard * length, kind.astype(jnp.int32)

    def as_row(column):
        return jnp.sum(jnp.where(down == across, column, 0), axis=0, keepdims=True)

    step = lax.broadcasted_iota(jnp.int32, (length, 1), 0)
    half = length // 2
    for side, (place_out, kind_out) in enumerate(((place_a, kind_a), (place_b, kind_b))):
        for block in range(shards // 2):
            token = step + block * length
            if groups > 1:
                shard, offset = token // (shards * piece), (token // piece) % shards
            else:
                offset, shard = token // half, (token % half) // piece
            where, kind = find(shard, offset, side, token % piece)
            at = pl.ds(block * length, length)
            place_out[at, :] = where
            kind_out[at, :] = kind
            query_place[:, pl.ds((2 * block + side) * length, length)] = as_row(where)
    where, kind = find((step % half) // piece, step * 0, step // half, step % piece)
    own_place[...] = as_row(where)
    own_kind[...] = kind


def tables(frames, texts, actions, shards, length, groups):
    index = jnp.stack([lax.axis_index("seq"), lax.axis_index("mlp") % 2]).astype(jnp.int32)
    total = shards * length
    column = jax.ShapeDtypeStruct((total // 2, 1), jnp.int32)
    return pl.pallas_call(
        partial(
            tables_kernel,
            shards=shards,
            length=length,
            groups=groups,
            clip_length=total // frames.shape[0],
        ),
        in_specs=[pl.BlockSpec(memory_space=pltpu.SMEM)] * 4,
        out_shape=[column] * 4
        + [
            jax.ShapeDtypeStruct((1, total), jnp.int32),
            jax.ShapeDtypeStruct((1, length), jnp.int32),
            jax.ShapeDtypeStruct((length, 1), jnp.int32),
        ],
        cost_estimate=cost(8 * total * length, 8 * 128 * total),
        name="tables",
    )(index, frames, texts, actions)


def rows_kernel(*refs, count):
    rows, weights, outs = refs[0], refs[1 : 1 + count], refs[1 + count :]
    for weight, out in zip(weights, outs):
        out[...] = dot(rows[...], weight[...], NN).astype(bf16)


def project_rows(rows, *weights):
    across = weights[0].shape[1]
    return pl.pallas_call(
        partial(rows_kernel, count=len(weights)),
        out_shape=[jax.ShapeDtypeStruct((rows.shape[0], across), bf16)] * len(weights),
        compiler_params=params(8),
        cost_estimate=cost(2 * rows.size * across * len(weights), 2 * rows.size),
        name="project_rows",
    )(rows, *weights)


def one_kernel(rows, weight, out):
    out[...] = dot(rows[...], weight[...], NT).astype(bf16)


def product_back(rows, weight):
    return pl.pallas_call(
        one_kernel,
        out_shape=jax.ShapeDtypeStruct((rows.shape[0], weight.shape[0]), bf16),
        compiler_params=params(6),
        cost_estimate=cost(2 * rows.size * weight.shape[0], 2 * weight.size),
        name="product_back",
    )(rows, weight)


def halves_kernel(*refs, count, dims):
    mine, other = refs[-2:]
    half = mine.shape[0]
    total = sum(dot(refs[k][...], refs[count + k][...], dims) for k in range(count))
    mine[...] = total[:half]
    other[...] = total[half:].astype(bf16)


def product_halves(rows, weights, dims):
    count = len(rows)
    half = rows[0].shape[0] // 2
    across = weights[0].shape[1 - dims[1][0]]
    shape = (half, across)
    return pl.pallas_call(
        partial(halves_kernel, count=count, dims=dims),
        out_shape=[jax.ShapeDtypeStruct(shape, f32), jax.ShapeDtypeStruct(shape, bf16)],
        compiler_params=params(6),
        cost_estimate=cost(2 * count * rows[0].size * across, 2 * count * weights[0].size),
        name="product_halves",
    )(*rows, *weights)


def down_own_kernel(rows, weight, mine, other, total):
    total[...] = jnp.zeros_like(total)

    def step(at):
        total[...] += dot(rows[:, at], weight[at, :], NN)

    tiles_of(weight.shape[0], math.gcd(weight.shape[0], 512), step)
    half = mine.shape[0]
    mine[...] = total[:half]
    other[...] = total[half:].astype(bf16)


def down_own(rows, weight):
    count, deep = rows.shape
    across = weight.shape[1]
    shape = (count // 2, across)
    return pl.pallas_call(
        down_own_kernel,
        in_specs=[WHOLE] * 2,
        out_specs=[WHOLE] * 2,
        out_shape=[jax.ShapeDtypeStruct(shape, f32), jax.ShapeDtypeStruct(shape, bf16)],
        scratch_shapes=[pltpu.VMEM((count, across), f32)],
        compiler_params=params(6),
        cost_estimate=cost(2 * rows.size * across, 2 * weight.size),
        name="down_own",
    )(rows, weight)


def gain_rows(gain, column):
    return jnp.where(
        column == 0, gain[0:1, :], jnp.where(column == 1, gain[1:2, :], gain[2:3, :])
    )


def normalize(values):
    mean = jnp.mean(values, axis=1, keepdims=True)
    centered = values - mean
    inverse = lax.rsqrt(jnp.mean(centered * centered, axis=1, keepdims=True) + epsilon)
    return (centered * inverse, inverse)


def norm_back(grad, normal, inverse, gains):
    scaled = grad * gains
    return inverse * (
        scaled
        - jnp.mean(scaled, axis=1, keepdims=True)
        - normal * jnp.mean(scaled * normal, axis=1, keepdims=True)
    )


def norm_kernel(*refs, groups, inner, parts):
    index, gain, kind, out = refs[0], refs[-3], refs[-2], refs[-1]
    pieces = refs[1:-3]
    rows, width = pieces[0].shape
    count = len(pieces)
    step = rows // parts
    for d, piece in enumerate(pieces):
        for part in range(parts):
            normal, _ = normalize(piece[pl.ds(part * step, step), :].astype(f32))
            place = part if d < inner else part ^ index[0]
            if groups > 1:
                each = groups // parts
                at = pl.ds(place * each, each)
                column = kind[at, d].reshape(step, 1)
                normed = (normal * gain_rows(gain, column)).astype(bf16)
                out[at, d] = normed.reshape(each, rows // groups, width)
            else:
                column = kind[d, place]
                out[d, place] = (normal * gain_rows(gain, column)).astype(bf16)


def norm_pieces(pieces, gain, kind, groups):
    rows, width = pieces[0].shape
    count = len(pieces)
    parts = x_size()
    if groups > 1:
        shape = (groups, count, rows // groups)
    else:
        shape = (count, parts, rows // parts)
    memory = [pl.BlockSpec(memory_space=pltpu.SMEM)]
    index = (lax.axis_index("mlp") // 2).astype(jnp.int32).reshape(1)
    out = pl.pallas_call(
        partial(norm_kernel, groups=groups, inner=inner_size(), parts=parts),
        in_specs=memory + [pl.BlockSpec(memory_space=pltpu.VMEM)] * (count + 2),
        out_shape=jax.ShapeDtypeStruct(shape + (width,), bf16),
        compiler_params=params(4 + count),
        cost_estimate=cost(10 * count * rows * width, 4 * count * rows * width),
        name="norm_pieces",
    )(index, *pieces, gain, kind.reshape(shape + (1,)))
    return out.reshape(count * rows, width)


def own_norm_kernel(rows, gain, kind, out):
    normal, _ = normalize(rows[...].astype(f32))
    out[...] = (normal * gain_rows(gain, kind[...])).astype(bf16)


def own_norm(rows, gain, kind):
    return pl.pallas_call(
        own_norm_kernel,
        out_shape=jax.ShapeDtypeStruct(rows.shape, bf16),
        compiler_params=params(4),
        cost_estimate=cost(10 * rows.size, 4 * rows.size),
        name="own_norm",
    )(rows, gain, kind)


def lift_kernel(rows, low, other, gain, kind, residual, lifted):
    value = rows[...].astype(f32) + (low[...].astype(f32) + other[...].astype(f32))
    residual[...] = value
    normal, _ = normalize(value)
    lifted[...] = (normal * gain_rows(gain, kind[...])).astype(bf16)


def lift(rows, low, other, gain, kind):
    return pl.pallas_call(
        lift_kernel,
        in_specs=[WHOLE] * 5,
        out_specs=[WHOLE] * 2,
        out_shape=[jax.ShapeDtypeStruct(rows.shape, f32), jax.ShapeDtypeStruct(rows.shape, bf16)],
        compiler_params=params(4),
        cost_estimate=cost(10 * rows.size, 12 * rows.size),
        name="lift",
    )(rows, low, other, gain, kind)


def kind_sums(term, kind):
    sums = [jnp.sum(jnp.where(kind == k, term, 0.0), axis=0, keepdims=True) for k in range(3)]
    high = [value.astype(bf16) for value in sums]
    low = [(value - part.astype(f32)).astype(bf16) for value, part in zip(sums, high)]
    zero = jnp.zeros((1, term.shape[1]), bf16)
    return jnp.concatenate(high + low + [zero, zero], axis=0)


def middle_kernel(residual, low, other, grad, gain, kind, grad_residual, mixed, parts):
    lifted_grad = low[...].astype(f32) + other[...].astype(f32)
    normal, inverse = normalize(residual[...])
    column = kind[...]
    back = norm_back(lifted_grad, normal, inverse, gain_rows(gain, column))
    value = grad[...].astype(f32) + back
    grad_residual[...] = value
    rounded_value = value.astype(bf16)
    mixed[...] = rounded_value
    sums = kind_sums(lifted_grad * normal, column)
    shards, rows, part = parts.shape
    for k in range(shards):
        parts[k, pl.ds(0, rows - 8), :] = rounded_value[:, k * part : (k + 1) * part]
        parts[k, pl.ds(rows - 8, 8), :] = sums[:, k * part : (k + 1) * part]


def middle(residual, low, other, grad, gain, kind, shards):
    rows, width = residual.shape
    return pl.pallas_call(
        middle_kernel,
        in_specs=[WHOLE] * 6,
        out_specs=[WHOLE] * 3,
        out_shape=[
            jax.ShapeDtypeStruct(residual.shape, f32),
            jax.ShapeDtypeStruct(residual.shape, bf16),
            jax.ShapeDtypeStruct((shards, rows + 8, width // shards), bf16),
        ],
        compiler_params=params(6),
        cost_estimate=cost(20 * residual.size, 16 * residual.size),
        name="middle",
    )(residual, low, other, grad, gain, kind)


def reordered(values, shards):
    count = values.shape[0]
    piece = count // shards
    to = lax.broadcasted_iota(jnp.int32, (count, count), 0)
    source = lax.broadcasted_iota(jnp.int32, (count, count), 1)
    pick = (source == (to % shards) * piece + to // shards).astype(f32).astype(bf16)
    return dot(pick, values, NN).astype(bf16)


def finish_kernel(residual, low, other, out, *, shards):
    value = residual[...] + (low[...].astype(f32) + other[...].astype(f32))
    out[...] = reordered(value.astype(bf16), shards)


def finish(residual, low, other, shards):
    return pl.pallas_call(
        partial(finish_kernel, shards=shards),
        in_specs=[WHOLE] * 3,
        out_specs=WHOLE,
        out_shape=jax.ShapeDtypeStruct(residual.shape, bf16),
        compiler_params=params(4),
        cost_estimate=cost(2 * residual.size, 10 * residual.size),
        name="finish",
    )(residual, low, other)


def place_kernel(index, mine, other, out):
    half = mine.shape[0]
    out[pl.ds(pl.multiple_of(index[0] * half, half), half), :] = mine[...]
    out[pl.ds(pl.multiple_of((1 - index[0]) * half, half), half), :] = other[...]


def place_halves(mine):
    half, width = mine.shape
    index = (lax.axis_index("mlp") % 2).astype(jnp.int32).reshape(1)
    return pl.pallas_call(
        place_kernel,
        in_specs=[pl.BlockSpec(memory_space=pltpu.SMEM)]
        + [pl.BlockSpec(memory_space=pltpu.VMEM)] * 2,
        out_shape=jax.ShapeDtypeStruct((2 * half, width), bf16),
        compiler_params=params(4),
        cost_estimate=cost(mine.size, 8 * mine.size),
        name="place_halves",
    )(index, mine, swap(mine, "mlp", 1))


def last_kernel(rows, low, other, grad_residual, gain, kind, out, *, shards):
    grad = low[...].astype(f32) + other[...].astype(f32)
    normal, inverse = normalize(rows[...].astype(f32))
    back = norm_back(grad, normal, inverse, gain_rows(gain, kind[...]))
    out[...] = reordered((grad_residual[...] + back).astype(bf16), shards)


def last(rows, low, other, grad_residual, gain, kind, shards):
    return pl.pallas_call(
        partial(last_kernel, shards=shards),
        in_specs=[WHOLE] * 6,
        out_specs=WHOLE,
        out_shape=jax.ShapeDtypeStruct(rows.shape, bf16),
        compiler_params=params(6),
        cost_estimate=cost(20 * rows.size, 12 * rows.size),
        name="last",
    )(rows, low, other, grad_residual, gain, kind)


def gelu_parts(value):
    rate = math.sqrt(2 / math.pi)
    square = value * value
    bent = jnp.tanh(value * (rate + (rate * 0.044715) * square))
    upper = 0.5 * (1 + bent)
    slope = upper + (0.5 * value) * (1 - bent * bent) * (rate + (rate * 3 * 0.044715) * square)
    return value * upper, slope


def tiles_of(extent, tile, step):
    def at(t, _):
        step(pl.ds(pl.multiple_of(t * tile, tile), tile))
        return 0

    lax.fori_loop(0, extent // tile, at, 0)


def own_kernel(lifted, up, grad_activated, activated, hidden_grads, mine, other, total):
    total[...] = jnp.zeros_like(total)

    def step(at):
        value, slope = gelu_parts(dot(lifted[...], up[:, at], NN))
        activated[:, at] = value.astype(bf16)
        hidden_grad = (grad_activated[:, at] * slope).astype(bf16)
        hidden_grads[:, at] = hidden_grad
        total[...] += dot(hidden_grad, up[:, at], NT)

    tiles_of(up.shape[1], math.gcd(up.shape[1], 512), step)
    half = mine.shape[0]
    mine[...] = total[:half]
    other[...] = total[half:].astype(bf16)


def feed_own(lifted, up, grad_activated):
    rows, width = lifted.shape
    hidden = up.shape[1]
    return pl.pallas_call(
        own_kernel,
        in_specs=[WHOLE] * 3,
        out_specs=[WHOLE] * 4,
        out_shape=[jax.ShapeDtypeStruct((rows, hidden), bf16)] * 2
        + [
            jax.ShapeDtypeStruct((rows // 2, width), f32),
            jax.ShapeDtypeStruct((rows // 2, width), bf16),
        ],
        scratch_shapes=[pltpu.VMEM((rows, width), f32)],
        compiler_params=params(8),
        cost_estimate=cost(4 * rows * width * hidden, 2 * width * hidden),
        name="feed_own",
    )(lifted, up, grad_activated)


def down_kernel(grad, down, out):
    def step(at):
        out[:, at] = dot(grad[...], down[at, :], NT)

    tiles_of(down.shape[0], math.gcd(down.shape[0], 512), step)


def grad_activated(grad, down):
    rows, width = grad.shape
    hidden = down.shape[0]
    return pl.pallas_call(
        down_kernel,
        in_specs=[WHOLE] * 2,
        out_specs=WHOLE,
        out_shape=jax.ShapeDtypeStruct((rows, hidden), f32),
        compiler_params=params(6),
        cost_estimate=cost(2 * rows * width * hidden, 2 * width * hidden),
        name="grad_activated",
    )(grad, down)


def all_kernel(index, *refs, counts):
    count = len(counts)
    lifted_parts, grad_parts = refs[:count], refs[count : 2 * count]
    up, down = refs[2 * count : 2 * count + 2]
    before = refs[2 * count + 2 : -8]
    up_grad, down_grad, lifted, grad, lifted_across, hidden_kept, grad_kept, sems = refs[-8:]
    part = up_grad.shape[0]
    mine = pl.ds(pl.multiple_of(index[0] * part, part), part)

    @pl.when(pl.program_id(0) == 0)
    def _():
        copies = []
        for k, (source, target) in enumerate(((lifted_parts, lifted), (grad_parts, grad))):
            start = 0
            for j, rows in enumerate(counts):
                here = target.at[pl.ds(start, rows)]
                copies.append(pltpu.make_async_copy(source[j], here, sems.at[k * count + j]))
                start += rows
        for copy in copies:
            copy.start()
        for copy in copies:
            copy.wait()
        lifted_across[...] = lifted[:, mine].T

    first = pl.program_id(0) == 0
    last_step = pl.num_programs(0) - 1

    tile = hidden_kept.shape[1]
    at = jnp.minimum(pl.program_id(0), last_step - 1) if up.shape[1] > tile else 0
    here = pl.ds(pl.multiple_of(at * tile, tile), tile)

    def products():
        return dot(lifted[...], up[:, here], NN), dot(grad[...], down[here, :], NT)

    def finish_tile(hidden_value, activated_grad):
        value, slope = gelu_parts(hidden_value)
        hidden_grad = (activated_grad * slope).astype(bf16)
        down_term = dot(value.astype(bf16), grad[:, mine], TN)
        up_term = dot(lifted_across[...], hidden_grad, NN)
        if len(before) == 2:
            up_term += before[0][...].astype(f32)
            down_term += before[1][...].astype(f32)
        else:
            lifted_own, grad_own, activated, hidden_own = before
            up_term += dot(lifted_own[...], hidden_own[...], TN)
            down_term += dot(activated[...], grad_own[...], TN)
        up_grad[...] = up_term.astype(up_grad.dtype)
        down_grad[...] = down_term.astype(down_grad.dtype)

    @pl.when(first)
    def _():
        hidden_kept[...], grad_kept[...] = products()

    @pl.when((pl.program_id(0) > 0) & (pl.program_id(0) < last_step))
    def _():
        kept = hidden_kept[...], grad_kept[...]
        fresh = products()
        finish_tile(*kept)
        hidden_kept[...], grad_kept[...] = fresh

    @pl.when(pl.program_id(0) == last_step)
    def _():
        finish_tile(hidden_kept[...], grad_kept[...])


def feed_all(lifted, grad, up, down, shards, sums=(), own=()):
    counts = [array.shape[0] for array in lifted]
    rows, width = sum(counts), lifted[0].shape[1]
    count = len(counts)
    part = width // shards
    hidden = up.shape[1]
    tile = math.gcd(hidden, 256)
    steps = hidden // tile
    wide = lambda t, index: (0, jnp.minimum(t, steps - 1))
    deep = lambda t, index: (jnp.minimum(t, steps - 1), 0)
    across = lambda t, index: (0, jnp.maximum(t - 1, 0))
    below = lambda t, index: (jnp.maximum(t - 1, 0), 0)
    mine = lambda t, index: (0, index[0])
    anywhere = pl.BlockSpec(memory_space=pl.ANY)
    sum_specs = [pl.BlockSpec((part, tile), across), pl.BlockSpec((tile, part), below)]
    if own:
        own_rows = own[0].shape[0]
        more = [pl.BlockSpec((own_rows, part), mine)] * 2
        more += [pl.BlockSpec((own_rows, tile), across)] * 2
    else:
        more = sum_specs
    index = lax.axis_index("seq").astype(jnp.int32).reshape(1)
    return pl.pallas_call(
        partial(all_kernel, counts=counts),
        grid_spec=pltpu.PrefetchScalarGridSpec(
            num_scalar_prefetch=1,
            grid=(steps + 1,),
            in_specs=[anywhere] * (2 * count)
            + (
                [WHOLE] * 2
                if own
                else [pl.BlockSpec((width, tile), wide), pl.BlockSpec((tile, width), deep)]
            )
            + more,
            out_specs=sum_specs,
            scratch_shapes=[pltpu.VMEM((rows, width), bf16)] * 2
            + [pltpu.VMEM((part, rows), bf16)]
            + [pltpu.VMEM((rows, tile), f32)] * 2
            + [pltpu.SemaphoreType.DMA((2 * count,))],
        ),
        out_shape=[
            pltpu.HBM((part, hidden), bf16 if own else f32),
            pltpu.HBM((hidden, part), bf16 if own else f32),
        ],
        compiler_params=params((6 if own else 8) + 8 * rows // 512),
        cost_estimate=cost(
            4 * rows * hidden * (width + part),
            4 * width * hidden + 4 * rows * width,
        ),
        name="feed_all",
    )(
        index,
        *lifted,
        *grad,
        *((up, down) if own else (in_hbm(up), in_hbm(down))),
        *(own or [in_hbm(array) for array in sums]),
    )


def project_kernel(index, *refs):
    normed, lows, weights = refs[0:2], refs[2:8], refs[8:11]
    gain, kinds = refs[11], refs[12:14]
    outs, gain_grad = refs[14:17], refs[17]
    for k in range(3):
        outs[k][...] = sum(dot(normed[side][...], lows[2 * k + side][...], TN) for side in range(2))
    gain_sum = [0.0, 0.0, 0.0]
    for side in range(2):
        column = kinds[side][...]
        term = sum(dot(lows[2 * k + side][...], weights[k][...], NT) for k in range(3))
        term = term * (normed[side][...].astype(f32) / gain_rows(gain, column))
        for k in range(3):
            gain_sum[k] += jnp.sum(jnp.where(column == k, term, 0.0), axis=0, keepdims=True)
    gain_grad[...] = jnp.concatenate(gain_sum, axis=0)


def project(normed, lows, weights, gain, kinds, shards):
    rows, width = normed[0].shape
    across = lows[0][0].shape[1]
    part = width // shards
    whole = lambda t, index: (0, 0)
    mine = lambda t, index: (0, index[0])
    below = lambda t, index: (index[0], 0)
    index = lax.axis_index("seq").astype(jnp.int32).reshape(1)
    return pl.pallas_call(
        project_kernel,
        grid_spec=pltpu.PrefetchScalarGridSpec(
            num_scalar_prefetch=1,
            grid=(1,),
            in_specs=[pl.BlockSpec((rows, part), mine)] * 2
            + [pl.BlockSpec((rows, across), whole)] * 6
            + [pl.BlockSpec((part, across), below)] * 3
            + [pl.BlockSpec((gain.shape[0], part), mine)]
            + [pl.BlockSpec((rows, 1), whole)] * 2,
            out_specs=[pl.BlockSpec((part, across), whole)] * 3
            + [pl.BlockSpec((gain.shape[0], part), whole)],
        ),
        out_shape=[jax.ShapeDtypeStruct((part, across), f32)] * 3
        + [jax.ShapeDtypeStruct((gain.shape[0], part), f32)],
        compiler_params=params(8),
        cost_estimate=cost(24 * rows * part * across, 12 * rows * across + 12 * part * across),
        name="project",
    )(index, *normed, *[low for pair in lows for low in pair], *weights, gain, *kinds)


def output_kernel(index, attended_a, attended_b, came_a, came_b, out, gain_grad, *, groups):
    total, sums = 0.0, 0.0
    shards, rows, part = came_a.shape
    half = rows - 8
    each = half // groups
    for attended, came in ((attended_a, came_a), (attended_b, came_b)):
        mixed = [
            came[index[0] ^ d, pl.ds(group * each, each), :]
            for group in range(groups)
            for d in range(shards)
        ]
        total += dot(attended[...], jnp.concatenate(mixed, axis=0), TN)
        own_sums = 0.0
        for k in range(shards):
            own_sums += came[k, pl.ds(half, 8), :].astype(f32)
        sums += own_sums
    out[...] = total
    gain_grad[...] = sums[0:3, :] + sums[3:6, :]


def output_part(attended, came, groups):
    index = lax.axis_index("seq").astype(jnp.int32).reshape(1)
    across, part = attended[0].shape[1], came[0].shape[2]
    return pl.pallas_call(
        partial(output_kernel, groups=groups),
        in_specs=[pl.BlockSpec(memory_space=pltpu.SMEM)]
        + [pl.BlockSpec(memory_space=pltpu.VMEM)] * 4,
        out_shape=[
            jax.ShapeDtypeStruct((across, part), f32),
            jax.ShapeDtypeStruct((3, part), f32),
        ],
        compiler_params=params(6),
        cost_estimate=cost(
            4 * attended[0].shape[0] * across * part, 4 * attended[0].shape[0] * (across + part)
        ),
        name="output_part",
    )(index, *attended, *came)


def mask_of(key_place, query_place, clip_length, clips):
    allowed = key_place <= query_place
    if clips > 1:
        allowed = allowed & (key_place // clip_length == query_place // clip_length)
    return allowed


def probabilities(scores, scale):
    top = scores[0].max(axis=0, keepdims=True)
    for block in scores[1:]:
        top = jnp.maximum(top, block.max(axis=0, keepdims=True))
    rate = scale * math.log2(math.e)
    weights = [jnp.exp2((block - top) * rate) for block in scores]
    total = weights[0].sum(axis=0, keepdims=True)
    for block in weights[1:]:
        total = total + block.sum(axis=0, keepdims=True)
    inverse = 1.0 / total
    return [block * inverse for block in weights]


def forward_kernel(query, key_a, key_b, value_a, value_b, place_a, place_b, query_place, out, **opts):
    scale = opts["scale"]
    query_place = query_place[...]
    allowed = [
        mask_of(place[...], query_place, opts["clip_length"], opts["clips"])
        for place in (place_a, place_b)
    ]
    for head in range(query.shape[1] // HEAD_DIM):
        at = pl.ds(head * HEAD_DIM, HEAD_DIM)
        scores = [
            jnp.where(mask, dot(key[:, at], query[:, at], NT), NEGATIVE)
            for mask, key in zip(allowed, (key_a, key_b))
        ]
        prob = [block.astype(bf16) for block in probabilities(scores, scale)]
        result = dot(value_a[:, at], prob[0], TN) + dot(value_b[:, at], prob[1], TN)
        out[:, at] = result.T.astype(bf16)


def attend(query, keys, values, places, query_place, clip_length, clips):
    rows, width = query.shape
    total = 2 * keys[0].shape[0]
    return pl.pallas_call(
        partial(
            forward_kernel, scale=1.0 / math.sqrt(HEAD_DIM), clip_length=clip_length, clips=clips
        ),
        out_shape=jax.ShapeDtypeStruct((rows, width), bf16),
        compiler_params=params(8),
        cost_estimate=cost(
            4 * rows * total * width, 4 * total * width, rows * total * (width // HEAD_DIM)
        ),
        name="attend",
    )(query, *keys, *values, *places, query_place)


def block_of(half):
    return min(128, half)


def reaches(half, groups):
    blocks = half // block_of(half)
    found, start = [], 0
    for index in range(blocks):
        seen, free = (index + 1, index) if groups > 1 else (blocks, 0)
        found.append((seen, free, start))
        start += seen
    return found, start


def take(first, second, low, high, at):
    block = block_of(first.shape[0])
    rows = [side[pl.ds(k * block, block), at] for k in range(low, high) for side in (first, second)]
    return jnp.concatenate(rows, axis=0)


def columns_of(head):
    return pl.ds(pl.multiple_of(head * HEAD_DIM, HEAD_DIM), HEAD_DIM)


def all_forward_kernel(*refs, groups, scale, clip_length, clips):
    query_a, query_b, key_a, key_b, value_a, value_b, place_a, place_b, query_place = refs[:9]
    attended_a, attended_b, stored, kept_probs, sems = refs[9:]
    half, width = key_a.shape
    heads = width // HEAD_DIM
    block = block_of(half)
    pair = 2 * block
    everything = slice(None)

    def copy_of(head):
        slot = head % 2
        return pltpu.make_async_copy(kept_probs.at[slot], stored.at[head], sems.at[slot])

    def one_head(head, _):
        cut = columns_of(head)
        slot = head % 2

        @pl.when(head >= 2)
        def _():
            copy_of(head - 2).wait()

        values_across = take(value_a, value_b, 0, half // block, cut).T
        for index, (seen, free, start) in enumerate(reaches(half, groups)[0]):
            mine = pl.ds(index * block, block)
            query = take(query_a, query_b, index, index + 1, cut)
            at_place = query_place[:, pl.ds(index * pair, pair)]
            place = take(place_a, place_b, free, seen, everything)
            mask = mask_of(place, at_place, clip_length, clips)
            score = dot(take(key_a, key_b, free, seen, cut), query, NT)
            scores = [jnp.where(mask, score, NEGATIVE)]
            if free:
                scores.insert(0, dot(take(key_a, key_b, 0, free, cut), query, NT))
            result, at = 0.0, 0
            for prob in probabilities(scores, scale):
                kept = prob.astype(bf16)
                rows = kept.shape[0]
                kept_probs[slot, pl.ds(start * pair + at, rows), :] = kept
                result += dot(values_across[:, at : at + rows], kept, NN)
                at += rows
            result = result.T.astype(bf16)
            attended_a[mine, cut] = result[:block]
            attended_b[mine, cut] = result[block:]
        copy_of(head).start()
        return 0

    lax.fori_loop(0, heads, one_head, 0)
    for head in range(max(0, heads - 2), heads):
        copy_of(head).wait()


def attend_all(queries, keys, values, places, query_place, groups, clip_length, clips):
    half, width = keys[0].shape
    heads = width // HEAD_DIM
    pair = 2 * block_of(half)
    deep = reaches(half, groups)[1] * pair
    outs = pl.pallas_call(
        partial(
            all_forward_kernel,
            groups=groups,
            scale=1.0 / math.sqrt(HEAD_DIM),
            clip_length=clip_length,
            clips=clips,
        ),
        in_specs=[pl.BlockSpec(memory_space=pltpu.VMEM)] * 9,
        out_specs=[pl.BlockSpec(memory_space=pltpu.VMEM)] * 2
        + [pl.BlockSpec(memory_space=pl.ANY)],
        out_shape=[jax.ShapeDtypeStruct((half, width), bf16)] * 2
        + [pltpu.HBM((heads, deep, pair), bf16)],
        scratch_shapes=[
            pltpu.VMEM((2, deep, pair), bf16),
            pltpu.SemaphoreType.DMA((2,)),
        ],
        compiler_params=params(max(10, half * half // 2**14)),
        cost_estimate=cost(16 * half * half * width, 16 * half * width, 4 * half * half * heads),
        name="attend_all",
    )(*queries, *keys, *values, *places, query_place)
    return outs[:2], outs[2]


def backward_kernel(*refs, count, groups, scale):
    grad_pieces = refs[:count]
    query_a, query_b, key_a, key_b, value_a, value_b, attended_a, attended_b, stored = refs[
        count : count + 9
    ]
    outs = refs[count + 9 : count + 18]
    grad_query, grad_key, grad_value = outs[0:2], outs[2:4], outs[4:6]
    own_query, own_key, own_value = outs[6:9]
    (scores,) = refs[count + 18 :]
    half, width = key_a.shape
    rows = half // count
    group_rows = rows // groups
    block = block_of(half)
    blocks = half // block
    pair = 2 * block
    reach = reaches(half, groups)[0]

    def sources(index):
        found = []
        if groups == 1:
            for d in range(index * block // rows, (index + 1) * block // rows):
                found.append((d, 0, rows))
            return found
        each = count * group_rows
        for j in range(index * block // each, (index + 1) * block // each):
            for d in range(count):
                found.append((d, j * group_rows, group_rows))
        return found

    def one_head(head, _):
        cut = columns_of(head)

        def keep(targets, own, values, index):
            for side in range(2):
                at = side * block
                targets[side][pl.ds(index * block, block), cut] = values[at : at + block]
                for d, start, size in sources(index):
                    if d == 0:
                        own[pl.ds(side * rows + start, size), cut] = values[at : at + size]
                    at += size

        def take_grads(index):
            return jnp.concatenate(
                [
                    grad_pieces[d][pl.ds(side * rows + start, size), cut]
                    for side in range(2)
                    for d, start, size in sources(index)
                ],
                axis=0,
            )

        keys_across = take(key_a, key_b, 0, blocks, cut).T
        ones = jnp.ones((8, HEAD_DIM), f32)
        for index, (seen, _, start) in enumerate(reach):
            result = take(attended_a, attended_b, index, index + 1, cut)
            grad = take_grads(index)
            delta = lax.dot_general(
                ones,
                grad.astype(f32) * result.astype(f32),
                (NT, ((), ())),
                precision=lax.Precision.HIGHEST,
                preferred_element_type=f32,
            )[0:1, :]
            at = pl.ds(start * pair, seen * pair)
            grad_prob = dot(take(value_a, value_b, 0, seen, cut), grad, NT)
            score = (stored[head, at, :].astype(f32) * (grad_prob - delta)).astype(bf16)
            scores[at, :] = score
            back = dot(keys_across[:, : seen * pair], score, NN)
            keep(grad_query, own_query, (back * scale).T.astype(bf16), index)
        for index in range(blocks):
            key_sum, value_sum = 0.0, 0.0
            for other, (seen, _, start) in enumerate(reach):
                if index < seen:
                    at = pl.ds((start + index) * pair, pair)
                    query = take(query_a, query_b, other, other + 1, cut)
                    key_sum += dot(scores[at, :], query, NN)
                    value_sum += dot(stored[head, at, :], take_grads(other), NN)
            keep(grad_key, own_key, (key_sum * scale).astype(bf16), index)
            keep(grad_value, own_value, value_sum.astype(bf16), index)
        return 0

    lax.fori_loop(0, width // HEAD_DIM, one_head, 0)


def attend_back(grads, queries, keys, values, attended, stored, groups):
    half, width = keys[0].shape
    count = len(grads)
    rows = grads[0].shape[0]
    outs = pl.pallas_call(
        partial(
            backward_kernel,
            count=count,
            groups=groups,
            scale=1.0 / math.sqrt(HEAD_DIM),
        ),
        in_specs=[pl.BlockSpec(memory_space=pltpu.VMEM)] * (count + 9),
        out_specs=[pl.BlockSpec(memory_space=pltpu.VMEM)] * 9,
        out_shape=[jax.ShapeDtypeStruct((half, width), bf16)] * 6
        + [jax.ShapeDtypeStruct((rows, width), bf16)] * 3,
        scratch_shapes=[pltpu.VMEM(stored.shape[1:], bf16)],
        compiler_params=params(8 + 2 * stored.shape[1] * stored.shape[2] // 2**20),
        cost_estimate=cost(8 * 4 * half * half * width, 32 * half * width + 2 * stored.size),
        name="attend_back",
    )(*grads, *queries, *keys, *values, *attended, stored)
    return outs[0:2], outs[2:4], outs[4:6], outs[6:9]


def body(
    inputs,
    first_gain,
    query_weight,
    key_weight,
    value_weight,
    output_weight,
    second_gain,
    up_weight,
    down_weight,
    frame_sizes,
    text_counts,
    action_counts,
    cotangent,
):
    shards = lax.axis_size("seq")
    shard_index = lax.axis_index("seq")
    core = lax.axis_index("mlp") % 2
    length, width = inputs.shape
    total = length * shards
    half = length // 2
    piece = half // shards
    clips = frame_sizes.shape[0]
    clip_length = total // clips
    part = width // shards
    groups = shards if piece % 8 == 0 else 1

    def halves(rows):
        cut = rows.reshape(2, piece, shards, width)
        mine = lax.dynamic_index_in_dim(cut, core, 0, keepdims=False)
        other = lax.dynamic_index_in_dim(cut, 1 - core, 0, keepdims=False)
        return (
            mine.transpose(1, 0, 2).reshape(half, width),
            other.transpose(1, 0, 2).reshape(half, width),
        )

    inputs_half, inputs_other = halves(inputs)
    pieces = gather_early(inputs_half)
    arrived = pieces[inner_size() :: inner_size()]

    place_a, place_b, kind_a, kind_b, query_place, own_place, own_kind = tables(
        frame_sizes, text_counts, action_counts, shards, length, groups
    )
    places, kinds = (place_a, place_b), (kind_a, kind_b)
    half_kind = own_kind[:half]
    own_normed = own_norm(
        jnp.concatenate([inputs_half, inputs_other], axis=0), first_gain, own_kind
    )
    grad_half, grad_other = halves(cotangent)
    grad_own = jnp.concatenate([grad_half, grad_other], axis=0)
    (query_own,) = project_rows(after(own_normed, arrived), query_weight)
    grad_far = gather_outer(after(grad_half, arrived, pieces[inner_size() + 1]))
    pieces = after(pieces, query_own)

    normed = [norm_pieces(pieces, first_gain, kind_a, groups)]
    normed[0], grad_far = after((normed[0], grad_far), normed[0])
    normed.append(swap(normed[0], "mlp", 1))
    keys, values = zip(*[project_rows(rows, key_weight, value_weight) for rows in normed])
    heads_own = attend(query_own, keys, values, places, own_place, clip_length, clips)
    grad_inner = gather_inner(after(grad_half, normed[0]))
    heads_own, grad_inner = after((heads_own, grad_inner), heads_own)
    grad_far = join_x(jnp.concatenate(grad_far, axis=0), heads_own)
    mine, other = product_halves([heads_own], [output_weight], NN)
    other, grad_far = after((other, grad_far), other)
    grad_inner += gather_inner(grad_far)
    low, other = pair_mlp(mine, other)
    own_activated_grad = grad_activated(after(grad_own, low), down_weight)
    queries = [
        project_rows(rows, query_weight)[0] for rows in after(normed, own_activated_grad)
    ]
    other = after(other, queries)
    residual, lifted_half = lift(inputs_half, low, other, second_gain, half_kind)

    lifted_own = both(lifted_half)
    activated_own, hidden_own, mine, other = feed_own(lifted_own, up_weight, own_activated_grad)
    lifted_far = gather_outer(after(lifted_half, other))
    other, grad_inner = after((other, grad_inner), other)
    low, other = pair_mlp(mine, other)
    attended, stored = attend_all(
        after(queries, low),
        keys,
        values,
        places,
        query_place,
        groups,
        clip_length,
        clips,
    )
    other, lifted_far = after((other, lifted_far), attended)
    grad_residual, mixed_half, mixed_columns = middle(
        residual, low, other, grad_half, second_gain, half_kind, shards
    )
    heads_grad = product_back(both(mixed_half), output_weight)

    heads_first = gather_first(heads_grad)
    lifted_far = jnp.concatenate(lifted_far, axis=0)
    lifted_inner_far = gather_inner(lifted_far)
    down_mine, down_other = down_own(after(activated_own, heads_grad), down_weight)
    lifted_far = join_x(lifted_far, heads_first[1], down_other, lifted_inner_far)
    heads_grads = gather_pieces(*heads_first)
    first_lifted, first_grads = with_core([lifted_far]), with_core([grad_far])
    first_lifted = after(first_lifted, heads_grads[inner_size() + 1])
    own = (lifted_own, grad_own, activated_own, hidden_own)
    sums = feed_all(first_lifted, first_grads, up_weight, down_weight, shards, own=own)
    down_low, down_other = pair_mlp(down_mine, down_other)
    heads_grads, down_low, down_other = after((heads_grads, down_low, down_other), sums)
    lifted_inner = gather_inner(after(lifted_half, down_other))

    query_low, key_low, value_low, own_low = attend_back(
        heads_grads, queries, keys, values, attended, stored, groups
    )
    attention_weights = (query_weight, key_weight, value_weight)
    lifted_inner += [join_x(far, own_low) for far in lifted_inner_far]
    own_low, lifted_inner = after((own_low, lifted_inner), own_low)
    low, other = pair_mlp(*product_halves(own_low, attention_weights, NT))

    query_grad, key_grad, value_grad, first_gain_grad = project(
        normed,
        after((query_low, key_low, value_low), low),
        attention_weights,
        first_gain,
        kinds,
        shards,
    )
    first_gain_grad = first_gain_grad + swap(first_gain_grad, "mlp", 1)
    other, first_gain_grad = after((other, first_gain_grad), query_grad)
    input_half = last(inputs_half, low, other, grad_residual, first_gain, half_kind, shards)
    outputs_half = finish(residual, down_low, after(down_other, input_half), shards)
    mixed_part = lax.all_to_all(
        after(mixed_columns, outputs_half), "seq", split_axis=0, concat_axis=0, tiled=True
    )
    rest_lifted = with_core(after(lifted_inner, other))
    rest_grads = with_core(after(grad_inner, other))
    up_grad, down_grad = feed_all(
        after(rest_lifted, outputs_half), rest_grads, up_weight, down_weight, shards, sums
    )
    bit = 2
    while bit < lax.axis_size("mlp"):
        came = after(swap(first_gain_grad, "mlp", bit), up_grad)
        first_gain_grad = first_gain_grad + came
        bit *= 2
    input_grad = place_halves(input_half)
    outputs = place_halves(outputs_half)
    mixed_part = after(mixed_part, up_grad)
    output_grad, second_gain_grad = output_part(
        attended, (mixed_part, swap(mixed_part, "mlp", 1)), groups
    )

    return (
        outputs,
        input_grad,
        first_gain_grad,
        query_grad,
        key_grad,
        value_grad,
        output_grad,
        second_gain_grad,
        up_grad,
        down_grad,
    )


def solution(mesh):
    return jax.shard_map(
        body,
        mesh=mesh,
        in_specs=(
            P("seq", None),
            P(),
            P(None, "mlp"),
            P(None, "mlp"),
            P(None, "mlp"),
            P("mlp", None),
            P(),
            P(None, "mlp"),
            P("mlp", None),
            P(),
            P(),
            P(),
            P("seq", None),
        ),
        out_specs=(
            P("seq", None),
            P("seq", None),
            P(None, "seq"),
            P("seq", "mlp"),
            P("seq", "mlp"),
            P("seq", "mlp"),
            P("mlp", "seq"),
            P(None, "seq"),
            P("seq", "mlp"),
            P("mlp", "seq"),
        ),
        check_vma=False,
    )
```

```python
from functools import partial
import math

import jax
import jax.numpy as jnp
from jax import lax
from jax.experimental import pallas as pl
from jax.experimental.pallas import tpu as pltpu
from jax.sharding import PartitionSpec as P

HEAD_DIM = 128
epsilon = 1e-05
bf16 = jnp.bfloat16
f32 = jnp.float32
NEGATIVE = -1e30

WHOLE = pl.BlockSpec(memory_space=pltpu.VMEM)
NN = ((1,), (0,))
NT = ((1,), (1,))
TN = ((0,), (0,))


def dot(a, b, dims):
    return lax.dot_general(a, b, (dims, ((), ())), preferred_element_type=f32)


def params(mebibytes):
    return pltpu.CompilerParams(vmem_limit_bytes=mebibytes * 1024 * 1024)


def cost(flops, moved, transcendentals=0, share=100):
    return pl.CostEstimate(
        flops=int(flops) // share,
        bytes_accessed=int(moved) // share,
        transcendentals=int(transcendentals) // share,
    )


def swap(value, axis, bit):
    size = lax.axis_size(axis)
    return lax.ppermute(value, axis, [(i, i ^ bit) for i in range(size)])


def inner_size():
    return 1 << (int(math.log2(lax.axis_size("seq"))) // 2)


def x_size():
    return lax.axis_size("mlp") // 2


def after(values, *earlier):
    return lax.optimization_barrier((values, earlier))[0]


def in_hbm(array):
    return pltpu.with_memory_space_constraint(array, pltpu.HBM)


def own_quarter(half):
    rows = half.shape[0] // x_size()
    return lax.dynamic_slice_in_dim(half, (lax.axis_index("mlp") // 2) * rows, rows, 0)


def join_x(quarter, *earlier):
    bit = 1
    while bit < x_size():
        came = after(swap(quarter, "mlp", 2 * bit), earlier)
        quarter = jnp.concatenate([quarter, came], axis=0)
        bit *= 2
    return quarter


def gather_early(half):
    size, inner = lax.axis_size("seq"), inner_size()
    quarter = own_quarter(half)
    pieces = {0: half}
    far = {outer: swap(quarter, "seq", outer) for outer in range(inner, size, inner)}
    for bit in range(1, inner):
        pieces[bit] = swap(half, "seq", bit)
    for outer in range(inner, size, inner):
        pieces[outer] = join_x(far[outer])
        for bit in range(1, inner):
            pieces[outer | bit] = swap(pieces[outer], "seq", bit)
    return [pieces[d] for d in range(size)]


def gather_outer(half):
    size, inner = lax.axis_size("seq"), inner_size()
    quarter = own_quarter(half)
    return [swap(quarter, "seq", outer) for outer in range(inner, size, inner)]


def gather_inner(array):
    return [swap(array, "seq", bit) for bit in range(1, inner_size())]


def with_core(arrays):
    return [each for array in arrays for each in (array, swap(array, "mlp", 1))]


def gather_first(piece):
    size, inner = lax.axis_size("seq"), inner_size()
    pieces = {0: piece}
    for bit in range(1, inner):
        pieces[bit] = swap(piece, "seq", bit)
    return pieces, [swap(piece, "seq", outer) for outer in range(inner, size, inner)]


def gather_pieces(pieces, far):
    size, inner = lax.axis_size("seq"), inner_size()
    for outer, came in zip(range(inner, size, inner), far):
        pieces[outer] = came
        for bit in range(1, inner):
            pieces[outer | bit] = swap(came, "seq", bit)
    return [pieces[d] for d in range(size)]


def rounded(value):
    return lax.optimization_barrier(value.astype(bf16))


def pair_mlp(mine, other_half):
    low, other = rounded(mine + swap(other_half, "mlp", 1).astype(f32)), None
    bit = 2
    while bit < lax.axis_size("mlp"):
        if other is not None:
            low = rounded(low.astype(f32) + other.astype(f32))
        other = swap(low, "mlp", bit)
        bit *= 2
    if other is None:
        other = jnp.zeros_like(low)
    return low, other


def both(half):
    return jnp.concatenate([half, swap(half, "mlp", 1)], axis=0)


def tables_kernel(index, frames, texts, actions, *outs, shards, length, groups, clip_length):
    place_a, place_b, kind_a, kind_b, query_place, own_place, own_kind = outs
    shard_index, core = index[0], index[1]
    shape = (shards, length)
    place = lax.broadcasted_iota(jnp.int32, shape, 0) * length + lax.broadcasted_iota(
        jnp.int32, shape, 1
    )
    kinds = jnp.full(shape, 2, jnp.int32)
    for clip in range(frames.shape[0]):
        start = jnp.int32(clip * clip_length)
        within = (place >= clip * clip_length) & (place < (clip + 1) * clip_length)
        for frame in range(frames.shape[1]):
            text_end = start + texts[clip, frame]
            action_end = text_end + actions[clip, frame]
            kinds = jnp.where(within & (place >= start) & (place < text_end), 0, kinds)
            kinds = jnp.where(within & (place >= text_end) & (place < action_end), 1, kinds)
            start = action_end + frames[clip, frame]
    square = (length, length)
    down = lax.broadcasted_iota(jnp.int32, square, 0)
    across = lax.broadcasted_iota(jnp.int32, square, 1)
    earlier = (down < across).astype(f32).astype(bf16)
    rank = jnp.zeros(shape, f32)
    before = jnp.zeros((shards, 1), f32)
    for kind in range(3):
        chosen = (kinds == kind).astype(f32)
        rank += chosen * (dot(chosen.astype(bf16), earlier, NN) + before)
        before += chosen.sum(axis=1, keepdims=True)
    rank_low, kinds_low = rank.astype(bf16), kinds.astype(f32).astype(bf16)
    piece = length // shards // 2
    lane = lax.broadcasted_iota(jnp.int32, (1, length), 1).astype(f32)

    def find(shard, offset, side, row):
        wanted = (shard_index ^ offset) * (2 * piece) + (core ^ side) * piece + row
        pick = shard == lax.broadcasted_iota(jnp.int32, (length, shards), 1)
        pick = pick.astype(f32).astype(bf16)
        hit = dot(pick, rank_low, NN) == wanted.astype(f32)
        where = jnp.sum(jnp.where(hit, lane, 0.0), axis=1, keepdims=True).astype(jnp.int32)
        kind = jnp.sum(jnp.where(hit, dot(pick, kinds_low, NN), 0.0), axis=1, keepdims=True)
        return where + shard * length, kind.astype(jnp.int32)

    def as_row(column):
        return jnp.sum(jnp.where(down == across, column, 0), axis=0, keepdims=True)

    step = lax.broadcasted_iota(jnp.int32, (length, 1), 0)
    half = length // 2
    for side, (place_out, kind_out) in enumerate(((place_a, kind_a), (place_b, kind_b))):
        for block in range(shards // 2):
            token = step + block * length
            if groups > 1:
                shard, offset = token // (shards * piece), (token // piece) % shards
            else:
                offset, shard = token // half, (token % half) // piece
            where, kind = find(shard, offset, side, token % piece)
            at = pl.ds(block * length, length)
            place_out[at, :] = where
            kind_out[at, :] = kind
            query_place[:, pl.ds((2 * block + side) * length, length)] = as_row(where)
    where, kind = find((step % half) // piece, step * 0, step // half, step % piece)
    own_place[...] = as_row(where)
    own_kind[...] = kind


def tables(frames, texts, actions, shards, length, groups):
    index = jnp.stack([lax.axis_index("seq"), lax.axis_index("mlp") % 2]).astype(jnp.int32)
    total = shards * length
    column = jax.ShapeDtypeStruct((total // 2, 1), jnp.int32)
    return pl.pallas_call(
        partial(
            tables_kernel,
            shards=shards,
            length=length,
            groups=groups,
            clip_length=total // frames.shape[0],
        ),
        in_specs=[pl.BlockSpec(memory_space=pltpu.SMEM)] * 4,
        out_shape=[column] * 4
        + [
            jax.ShapeDtypeStruct((1, total), jnp.int32),
            jax.ShapeDtypeStruct((1, length), jnp.int32),
            jax.ShapeDtypeStruct((length, 1), jnp.int32),
        ],
        cost_estimate=cost(8 * total * length, 8 * 128 * total),
        name="tables",
    )(index, frames, texts, actions)


def rows_kernel(*refs, count):
    rows, weights, outs = refs[0], refs[1 : 1 + count], refs[1 + count :]
    for weight, out in zip(weights, outs):
        out[...] = dot(rows[...], weight[...], NN).astype(bf16)


def project_rows(rows, *weights):
    across = weights[0].shape[1]
    return pl.pallas_call(
        partial(rows_kernel, count=len(weights)),
        out_shape=[jax.ShapeDtypeStruct((rows.shape[0], across), bf16)] * len(weights),
        compiler_params=params(8),
        cost_estimate=cost(2 * rows.size * across * len(weights), 2 * rows.size),
        name="project_rows",
    )(rows, *weights)


def one_kernel(rows, weight, out):
    out[...] = dot(rows[...], weight[...], NT).astype(bf16)


def product_back(rows, weight):
    return pl.pallas_call(
        one_kernel,
        out_shape=jax.ShapeDtypeStruct((rows.shape[0], weight.shape[0]), bf16),
        compiler_params=params(6),
        cost_estimate=cost(2 * rows.size * weight.shape[0], 2 * weight.size),
        name="product_back",
    )(rows, weight)


def halves_kernel(*refs, count, dims):
    mine, other = refs[-2:]
    half = mine.shape[0]
    total = sum(dot(refs[k][...], refs[count + k][...], dims) for k in range(count))
    mine[...] = total[:half]
    other[...] = total[half:].astype(bf16)


def product_halves(rows, weights, dims):
    count = len(rows)
    half = rows[0].shape[0] // 2
    across = weights[0].shape[1 - dims[1][0]]
    shape = (half, across)
    return pl.pallas_call(
        partial(halves_kernel, count=count, dims=dims),
        out_shape=[jax.ShapeDtypeStruct(shape, f32), jax.ShapeDtypeStruct(shape, bf16)],
        compiler_params=params(6),
        cost_estimate=cost(2 * count * rows[0].size * across, 2 * count * weights[0].size),
        name="product_halves",
    )(*rows, *weights)


def down_own_kernel(rows, weight, mine, other, total):
    total[...] = jnp.zeros_like(total)

    def step(at):
        total[...] += dot(rows[:, at], weight[at, :], NN)

    tiles_of(weight.shape[0], math.gcd(weight.shape[0], 512), step)
    half = mine.shape[0]
    mine[...] = total[:half]
    other[...] = total[half:].astype(bf16)


def down_own(rows, weight):
    count, deep = rows.shape
    across = weight.shape[1]
    shape = (count // 2, across)
    return pl.pallas_call(
        down_own_kernel,
        in_specs=[WHOLE] * 2,
        out_specs=[WHOLE] * 2,
        out_shape=[jax.ShapeDtypeStruct(shape, f32), jax.ShapeDtypeStruct(shape, bf16)],
        scratch_shapes=[pltpu.VMEM((count, across), f32)],
        compiler_params=params(6),
        cost_estimate=cost(2 * rows.size * across, 2 * weight.size),
        name="down_own",
    )(rows, weight)


def gain_rows(gain, column):
    return jnp.where(
        column == 0, gain[0:1, :], jnp.where(column == 1, gain[1:2, :], gain[2:3, :])
    )


def normalize(values):
    mean = jnp.mean(values, axis=1, keepdims=True)
    centered = values - mean
    inverse = lax.rsqrt(jnp.mean(centered * centered, axis=1, keepdims=True) + epsilon)
    return (centered * inverse, inverse)


def norm_back(grad, normal, inverse, gains):
    scaled = grad * gains
    return inverse * (
        scaled
        - jnp.mean(scaled, axis=1, keepdims=True)
        - normal * jnp.mean(scaled * normal, axis=1, keepdims=True)
    )


def norm_kernel(*refs, groups, inner, parts):
    index, gain, kind, out = refs[0], refs[-3], refs[-2], refs[-1]
    pieces = refs[1:-3]
    rows, width = pieces[0].shape
    count = len(pieces)
    step = rows // parts
    for d, piece in enumerate(pieces):
        for part in range(parts):
            normal, _ = normalize(piece[pl.ds(part * step, step), :].astype(f32))
            place = part if d < inner else part ^ index[0]
            if groups > 1:
                each = groups // parts
                at = pl.ds(place * each, each)
                column = kind[at, d].reshape(step, 1)
                normed = (normal * gain_rows(gain, column)).astype(bf16)
                out[at, d] = normed.reshape(each, rows // groups, width)
            else:
                column = kind[d, place]
                out[d, place] = (normal * gain_rows(gain, column)).astype(bf16)


def norm_pieces(pieces, gain, kind, groups):
    rows, width = pieces[0].shape
    count = len(pieces)
    parts = x_size()
    if groups > 1:
        shape = (groups, count, rows // groups)
    else:
        shape = (count, parts, rows // parts)
    memory = [pl.BlockSpec(memory_space=pltpu.SMEM)]
    index = (lax.axis_index("mlp") // 2).astype(jnp.int32).reshape(1)
    out = pl.pallas_call(
        partial(norm_kernel, groups=groups, inner=inner_size(), parts=parts),
        in_specs=memory + [pl.BlockSpec(memory_space=pltpu.VMEM)] * (count + 2),
        out_shape=jax.ShapeDtypeStruct(shape + (width,), bf16),
        compiler_params=params(4 + count),
        cost_estimate=cost(10 * count * rows * width, 4 * count * rows * width),
        name="norm_pieces",
    )(index, *pieces, gain, kind.reshape(shape + (1,)))
    return out.reshape(count * rows, width)


def own_norm_kernel(rows, gain, kind, out):
    normal, _ = normalize(rows[...].astype(f32))
    out[...] = (normal * gain_rows(gain, kind[...])).astype(bf16)


def own_norm(rows, gain, kind):
    return pl.pallas_call(
        own_norm_kernel,
        out_shape=jax.ShapeDtypeStruct(rows.shape, bf16),
        compiler_params=params(4),
        cost_estimate=cost(10 * rows.size, 4 * rows.size),
        name="own_norm",
    )(rows, gain, kind)


def lift_kernel(rows, low, other, gain, kind, residual, lifted):
    value = rows[...].astype(f32) + (low[...].astype(f32) + other[...].astype(f32))
    residual[...] = value
    normal, _ = normalize(value)
    lifted[...] = (normal * gain_rows(gain, kind[...])).astype(bf16)


def lift(rows, low, other, gain, kind):
    return pl.pallas_call(
        lift_kernel,
        in_specs=[WHOLE] * 5,
        out_specs=[WHOLE] * 2,
        out_shape=[jax.ShapeDtypeStruct(rows.shape, f32), jax.ShapeDtypeStruct(rows.shape, bf16)],
        compiler_params=params(4),
        cost_estimate=cost(10 * rows.size, 12 * rows.size),
        name="lift",
    )(rows, low, other, gain, kind)


def kind_sums(term, kind):
    sums = [jnp.sum(jnp.where(kind == k, term, 0.0), axis=0, keepdims=True) for k in range(3)]
    high = [value.astype(bf16) for value in sums]
    low = [(value - part.astype(f32)).astype(bf16) for value, part in zip(sums, high)]
    zero = jnp.zeros((1, term.shape[1]), bf16)
    return jnp.concatenate(high + low + [zero, zero], axis=0)


def middle_kernel(residual, low, other, grad, gain, kind, grad_residual, mixed, parts):
    lifted_grad = low[...].astype(f32) + other[...].astype(f32)
    normal, inverse = normalize(residual[...])
    column = kind[...]
    back = norm_back(lifted_grad, normal, inverse, gain_rows(gain, column))
    value = grad[...].astype(f32) + back
    grad_residual[...] = value
    rounded_value = value.astype(bf16)
    mixed[...] = rounded_value
    sums = kind_sums(lifted_grad * normal, column)
    shards, rows, part = parts.shape
    for k in range(shards):
        parts[k, pl.ds(0, rows - 8), :] = rounded_value[:, k * part : (k + 1) * part]
        parts[k, pl.ds(rows - 8, 8), :] = sums[:, k * part : (k + 1) * part]


def middle(residual, low, other, grad, gain, kind, shards):
    rows, width = residual.shape
    return pl.pallas_call(
        middle_kernel,
        in_specs=[WHOLE] * 6,
        out_specs=[WHOLE] * 3,
        out_shape=[
            jax.ShapeDtypeStruct(residual.shape, f32),
            jax.ShapeDtypeStruct(residual.shape, bf16),
            jax.ShapeDtypeStruct((shards, rows + 8, width // shards), bf16),
        ],
        compiler_params=params(6),
        cost_estimate=cost(20 * residual.size, 16 * residual.size),
        name="middle",
    )(residual, low, other, grad, gain, kind)


def reordered(values, shards):
    count = values.shape[0]
    piece = count // shards
    to = lax.broadcasted_iota(jnp.int32, (count, count), 0)
    source = lax.broadcasted_iota(jnp.int32, (count, count), 1)
    pick = (source == (to % shards) * piece + to // shards).astype(f32).astype(bf16)
    return dot(pick, values, NN).astype(bf16)


def finish_kernel(residual, low, other, out, *, shards):
    value = residual[...] + (low[...].astype(f32) + other[...].astype(f32))
    out[...] = reordered(value.astype(bf16), shards)


def finish(residual, low, other, shards):
    return pl.pallas_call(
        partial(finish_kernel, shards=shards),
        in_specs=[WHOLE] * 3,
        out_specs=WHOLE,
        out_shape=jax.ShapeDtypeStruct(residual.shape, bf16),
        compiler_params=params(4),
        cost_estimate=cost(2 * residual.size, 10 * residual.size),
        name="finish",
    )(residual, low, other)


def place_kernel(index, *refs):
    count = len(refs) // 3
    for mine, other, out in zip(refs[:count], refs[count : 2 * count], refs[2 * count :]):
        half = mine.shape[0]
        out[pl.ds(pl.multiple_of(index[0] * half, half), half), :] = mine[...]
        out[pl.ds(pl.multiple_of((1 - index[0]) * half, half), half), :] = other[...]


def place_halves(arrays, others):
    half, width = arrays[0].shape
    index = (lax.axis_index("mlp") % 2).astype(jnp.int32).reshape(1)
    return pl.pallas_call(
        place_kernel,
        in_specs=[pl.BlockSpec(memory_space=pltpu.SMEM)] + [WHOLE] * (2 * len(arrays)),
        out_shape=[jax.ShapeDtypeStruct((2 * half, width), bf16)] * len(arrays),
        compiler_params=params(6),
        cost_estimate=cost(half * width, 16 * half * width),
        name="place_halves",
    )(index, *arrays, *others)


def last_kernel(rows, low, other, grad_residual, gain, kind, out, *, shards):
    grad = low[...].astype(f32) + other[...].astype(f32)
    normal, inverse = normalize(rows[...].astype(f32))
    back = norm_back(grad, normal, inverse, gain_rows(gain, kind[...]))
    out[...] = reordered((grad_residual[...] + back).astype(bf16), shards)


def last(rows, low, other, grad_residual, gain, kind, shards):
    return pl.pallas_call(
        partial(last_kernel, shards=shards),
        in_specs=[WHOLE] * 6,
        out_specs=WHOLE,
        out_shape=jax.ShapeDtypeStruct(rows.shape, bf16),
        compiler_params=params(6),
        cost_estimate=cost(20 * rows.size, 12 * rows.size),
        name="last",
    )(rows, low, other, grad_residual, gain, kind)


def gelu_parts(value):
    rate = math.sqrt(2 / math.pi)
    square = value * value
    bent = jnp.tanh(value * (rate + (rate * 0.044715) * square))
    upper = 0.5 * (1 + bent)
    slope = upper + (0.5 * value) * (1 - bent * bent) * (rate + (rate * 3 * 0.044715) * square)
    return value * upper, slope


def tiles_of(extent, tile, step):
    def at(t, _):
        step(pl.ds(pl.multiple_of(t * tile, tile), tile))
        return 0

    lax.fori_loop(0, extent // tile, at, 0)


def own_kernel(lifted, up, grad_activated, activated, hidden_grads, mine, other, total):
    total[...] = jnp.zeros_like(total)

    def step(at):
        value, slope = gelu_parts(dot(lifted[...], up[:, at], NN))
        activated[:, at] = value.astype(bf16)
        hidden_grad = (grad_activated[:, at] * slope).astype(bf16)
        hidden_grads[:, at] = hidden_grad
        total[...] += dot(hidden_grad, up[:, at], NT)

    tiles_of(up.shape[1], math.gcd(up.shape[1], 512), step)
    half = mine.shape[0]
    mine[...] = total[:half]
    other[...] = total[half:].astype(bf16)


def feed_own(lifted, up, grad_activated):
    rows, width = lifted.shape
    hidden = up.shape[1]
    return pl.pallas_call(
        own_kernel,
        in_specs=[WHOLE] * 3,
        out_specs=[WHOLE] * 4,
        out_shape=[jax.ShapeDtypeStruct((rows, hidden), bf16)] * 2
        + [
            jax.ShapeDtypeStruct((rows // 2, width), f32),
            jax.ShapeDtypeStruct((rows // 2, width), bf16),
        ],
        scratch_shapes=[pltpu.VMEM((rows, width), f32)],
        compiler_params=params(8),
        cost_estimate=cost(4 * rows * width * hidden, 2 * width * hidden),
        name="feed_own",
    )(lifted, up, grad_activated)


def down_kernel(grad, down, out):
    def step(at):
        out[:, at] = dot(grad[...], down[at, :], NT)

    tiles_of(down.shape[0], math.gcd(down.shape[0], 512), step)


def grad_activated(grad, down):
    rows, width = grad.shape
    hidden = down.shape[0]
    return pl.pallas_call(
        down_kernel,
        in_specs=[WHOLE] * 2,
        out_specs=WHOLE,
        out_shape=jax.ShapeDtypeStruct((rows, hidden), f32),
        compiler_params=params(6),
        cost_estimate=cost(2 * rows * width * hidden, 2 * width * hidden),
        name="grad_activated",
    )(grad, down)


def all_kernel(index, *refs, count):
    lifted_parts, grad_parts = refs[:count], refs[count : 2 * count]
    up, down = refs[2 * count : 2 * count + 2]
    before = refs[2 * count + 2 : -5]
    up_grad, down_grad, lifted_across, hidden_kept, grad_kept = refs[-5:]
    part = up_grad.shape[0]
    mine = pl.ds(pl.multiple_of(index[0] * part, part), part)

    def rows_of(parts, at):
        return jnp.concatenate([ref[:, at] for ref in parts], axis=0)

    @pl.when(pl.program_id(0) == 0)
    def _():
        lifted_across[...] = rows_of(lifted_parts, mine).T

    first = pl.program_id(0) == 0
    last_step = pl.num_programs(0) - 1

    tile = hidden_kept.shape[1]
    at = jnp.minimum(pl.program_id(0), last_step - 1) if up.shape[1] > tile else 0
    here = pl.ds(pl.multiple_of(at * tile, tile), tile)

    def products():
        everything = slice(None)
        return (
            dot(rows_of(lifted_parts, everything), up[:, here], NN),
            dot(rows_of(grad_parts, everything), down[here, :], NT),
        )

    def finish_tile(hidden_value, activated_grad):
        value, slope = gelu_parts(hidden_value)
        hidden_grad = (activated_grad * slope).astype(bf16)
        down_term = dot(value.astype(bf16), rows_of(grad_parts, mine), TN)
        up_term = dot(lifted_across[...], hidden_grad, NN)
        if len(before) == 2:
            up_term += before[0][...].astype(f32)
            down_term += before[1][...].astype(f32)
        else:
            lifted_own, grad_own, activated, hidden_own = before
            up_term += dot(lifted_own[...], hidden_own[...], TN)
            down_term += dot(activated[...], grad_own[...], TN)
        up_grad[...] = up_term.astype(up_grad.dtype)
        down_grad[...] = down_term.astype(down_grad.dtype)

    @pl.when(first)
    def _():
        hidden_kept[...], grad_kept[...] = products()

    @pl.when((pl.program_id(0) > 0) & (pl.program_id(0) < last_step))
    def _():
        kept = hidden_kept[...], grad_kept[...]
        fresh = products()
        finish_tile(*kept)
        hidden_kept[...], grad_kept[...] = fresh

    @pl.when(pl.program_id(0) == last_step)
    def _():
        finish_tile(hidden_kept[...], grad_kept[...])


def feed_all(lifted, grad, up, down, shards, sums=(), own=()):
    counts = [array.shape[0] for array in lifted]
    rows, width = sum(counts), lifted[0].shape[1]
    count = len(counts)
    part = width // shards
    hidden = up.shape[1]
    tile = math.gcd(hidden, 256)
    steps = hidden // tile
    wide = lambda t, index: (0, jnp.minimum(t, steps - 1))
    deep = lambda t, index: (jnp.minimum(t, steps - 1), 0)
    across = lambda t, index: (0, jnp.maximum(t - 1, 0))
    below = lambda t, index: (jnp.maximum(t - 1, 0), 0)
    mine = lambda t, index: (0, index[0])
    sum_specs = [pl.BlockSpec((part, tile), across), pl.BlockSpec((tile, part), below)]
    if own:
        own_rows = own[0].shape[0]
        more = [pl.BlockSpec((own_rows, part), mine)] * 2
        more += [pl.BlockSpec((own_rows, tile), across)] * 2
    else:
        more = sum_specs
    index = lax.axis_index("seq").astype(jnp.int32).reshape(1)
    return pl.pallas_call(
        partial(all_kernel, count=count),
        grid_spec=pltpu.PrefetchScalarGridSpec(
            num_scalar_prefetch=1,
            grid=(steps + 1,),
            in_specs=[WHOLE] * (2 * count)
            + (
                [WHOLE] * 2
                if own
                else [pl.BlockSpec((width, tile), wide), pl.BlockSpec((tile, width), deep)]
            )
            + more,
            out_specs=sum_specs,
            scratch_shapes=[pltpu.VMEM((part, rows), bf16)]
            + [pltpu.VMEM((rows, tile), f32)] * 2,
        ),
        out_shape=[
            pltpu.HBM((part, hidden), bf16 if own else f32),
            pltpu.HBM((hidden, part), bf16 if own else f32),
        ],
        compiler_params=params((6 if own else 8) + 8 * rows // 512),
        cost_estimate=cost(
            4 * rows * hidden * (width + part),
            4 * width * hidden + 4 * rows * width,
        ),
        name="feed_all",
    )(
        index,
        *lifted,
        *grad,
        *((up, down) if own else (in_hbm(up), in_hbm(down))),
        *(own or [in_hbm(array) for array in sums]),
    )


def project_kernel(index, *refs):
    normed, lows, weights = refs[0:2], refs[2:8], refs[8:11]
    gain, kinds = refs[11], refs[12:14]
    outs, gain_grad = refs[14:17], refs[17]
    for k in range(3):
        outs[k][...] = sum(dot(normed[side][...], lows[2 * k + side][...], TN) for side in range(2))
    gain_sum = [0.0, 0.0, 0.0]
    for side in range(2):
        column = kinds[side][...]
        term = sum(dot(lows[2 * k + side][...], weights[k][...], NT) for k in range(3))
        term = term * (normed[side][...].astype(f32) / gain_rows(gain, column))
        for k in range(3):
            gain_sum[k] += jnp.sum(jnp.where(column == k, term, 0.0), axis=0, keepdims=True)
    gain_grad[...] = jnp.concatenate(gain_sum, axis=0)


def project(normed, lows, weights, gain, kinds, shards):
    rows, width = normed[0].shape
    across = lows[0][0].shape[1]
    part = width // shards
    whole = lambda t, index: (0, 0)
    mine = lambda t, index: (0, index[0])
    below = lambda t, index: (index[0], 0)
    index = lax.axis_index("seq").astype(jnp.int32).reshape(1)
    return pl.pallas_call(
        project_kernel,
        grid_spec=pltpu.PrefetchScalarGridSpec(
            num_scalar_prefetch=1,
            grid=(1,),
            in_specs=[pl.BlockSpec((rows, part), mine)] * 2
            + [pl.BlockSpec((rows, across), whole)] * 6
            + [pl.BlockSpec((part, across), below)] * 3
            + [pl.BlockSpec((gain.shape[0], part), mine)]
            + [pl.BlockSpec((rows, 1), whole)] * 2,
            out_specs=[pl.BlockSpec((part, across), whole)] * 3
            + [pl.BlockSpec((gain.shape[0], part), whole)],
        ),
        out_shape=[jax.ShapeDtypeStruct((part, across), f32)] * 3
        + [jax.ShapeDtypeStruct((gain.shape[0], part), f32)],
        compiler_params=params(8),
        cost_estimate=cost(24 * rows * part * across, 12 * rows * across + 12 * part * across),
        name="project",
    )(index, *normed, *[low for pair in lows for low in pair], *weights, gain, *kinds)


def output_kernel(index, attended_a, attended_b, came_a, came_b, out, gain_grad, *, groups):
    total, sums = 0.0, 0.0
    shards, rows, part = came_a.shape
    half = rows - 8
    each = half // groups
    for attended, came in ((attended_a, came_a), (attended_b, came_b)):
        mixed = [
            came[index[0] ^ d, pl.ds(group * each, each), :]
            for group in range(groups)
            for d in range(shards)
        ]
        total += dot(attended[...], jnp.concatenate(mixed, axis=0), TN)
        own_sums = 0.0
        for k in range(shards):
            own_sums += came[k, pl.ds(half, 8), :].astype(f32)
        sums += own_sums
    out[...] = total
    gain_grad[...] = sums[0:3, :] + sums[3:6, :]


def output_part(attended, came, groups):
    index = lax.axis_index("seq").astype(jnp.int32).reshape(1)
    across, part = attended[0].shape[1], came[0].shape[2]
    return pl.pallas_call(
        partial(output_kernel, groups=groups),
        in_specs=[pl.BlockSpec(memory_space=pltpu.SMEM)]
        + [pl.BlockSpec(memory_space=pltpu.VMEM)] * 4,
        out_shape=[
            jax.ShapeDtypeStruct((across, part), f32),
            jax.ShapeDtypeStruct((3, part), f32),
        ],
        compiler_params=params(6),
        cost_estimate=cost(
            4 * attended[0].shape[0] * across * part, 4 * attended[0].shape[0] * (across + part)
        ),
        name="output_part",
    )(index, *attended, *came)


def mask_of(key_place, query_place, clip_length, clips):
    allowed = key_place <= query_place
    if clips > 1:
        allowed = allowed & (key_place // clip_length == query_place // clip_length)
    return allowed


def probabilities(scores, scale):
    top = scores[0].max(axis=0, keepdims=True)
    for block in scores[1:]:
        top = jnp.maximum(top, block.max(axis=0, keepdims=True))
    rate = scale * math.log2(math.e)
    weights = [jnp.exp2((block - top) * rate) for block in scores]
    total = weights[0].sum(axis=0, keepdims=True)
    for block in weights[1:]:
        total = total + block.sum(axis=0, keepdims=True)
    inverse = 1.0 / total
    return [block * inverse for block in weights]


def forward_kernel(query, key_a, key_b, value_a, value_b, place_a, place_b, query_place, out, **opts):
    scale = opts["scale"]
    query_place = query_place[...]
    allowed = [
        mask_of(place[...], query_place, opts["clip_length"], opts["clips"])
        for place in (place_a, place_b)
    ]
    for head in range(query.shape[1] // HEAD_DIM):
        at = pl.ds(head * HEAD_DIM, HEAD_DIM)
        scores = [
            jnp.where(mask, dot(key[:, at], query[:, at], NT), NEGATIVE)
            for mask, key in zip(allowed, (key_a, key_b))
        ]
        prob = [block.astype(bf16) for block in probabilities(scores, scale)]
        result = dot(value_a[:, at], prob[0], TN) + dot(value_b[:, at], prob[1], TN)
        out[:, at] = result.T.astype(bf16)


def attend(query, keys, values, places, query_place, clip_length, clips):
    rows, width = query.shape
    total = 2 * keys[0].shape[0]
    return pl.pallas_call(
        partial(
            forward_kernel, scale=1.0 / math.sqrt(HEAD_DIM), clip_length=clip_length, clips=clips
        ),
        out_shape=jax.ShapeDtypeStruct((rows, width), bf16),
        compiler_params=params(8),
        cost_estimate=cost(
            4 * rows * total * width, 4 * total * width, rows * total * (width // HEAD_DIM)
        ),
        name="attend",
    )(query, *keys, *values, *places, query_place)


def block_of(half):
    return min(128, half)


def reaches(half, groups):
    blocks = half // block_of(half)
    found, start = [], 0
    for index in range(blocks):
        seen, free = (index + 1, index) if groups > 1 else (blocks, 0)
        found.append((seen, free, start))
        start += seen
    return found, start


def take(first, second, low, high, at):
    block = block_of(first.shape[0])
    rows = [side[pl.ds(k * block, block), at] for k in range(low, high) for side in (first, second)]
    return jnp.concatenate(rows, axis=0)


def columns_of(head):
    return pl.ds(pl.multiple_of(head * HEAD_DIM, HEAD_DIM), HEAD_DIM)


def all_forward_kernel(*refs, groups, scale, clip_length, clips):
    query_a, query_b, key_a, key_b, value_a, value_b, place_a, place_b, query_place = refs[:9]
    attended_a, attended_b, stored, kept_probs, sems = refs[9:]
    half, width = key_a.shape
    heads = width // HEAD_DIM
    block = block_of(half)
    pair = 2 * block
    everything = slice(None)

    def copy_of(head):
        slot = head % 2
        return pltpu.make_async_copy(kept_probs.at[slot], stored.at[head], sems.at[slot])

    def one_head(head, _):
        cut = columns_of(head)
        slot = head % 2

        @pl.when(head >= 2)
        def _():
            copy_of(head - 2).wait()

        values_across = take(value_a, value_b, 0, half // block, cut).T
        for index, (seen, free, start) in enumerate(reaches(half, groups)[0]):
            mine = pl.ds(index * block, block)
            query = take(query_a, query_b, index, index + 1, cut)
            at_place = query_place[:, pl.ds(index * pair, pair)]
            place = take(place_a, place_b, free, seen, everything)
            mask = mask_of(place, at_place, clip_length, clips)
            score = dot(take(key_a, key_b, free, seen, cut), query, NT)
            scores = [jnp.where(mask, score, NEGATIVE)]
            if free:
                scores.insert(0, dot(take(key_a, key_b, 0, free, cut), query, NT))
            result, at = 0.0, 0
            for prob in probabilities(scores, scale):
                kept = prob.astype(bf16)
                rows = kept.shape[0]
                kept_probs[slot, pl.ds(start * pair + at, rows), :] = kept
                result += dot(values_across[:, at : at + rows], kept, NN)
                at += rows
            result = result.T.astype(bf16)
            attended_a[mine, cut] = result[:block]
            attended_b[mine, cut] = result[block:]
        copy_of(head).start()
        return 0

    lax.fori_loop(0, heads, one_head, 0)
    for head in range(max(0, heads - 2), heads):
        copy_of(head).wait()


def attend_all(queries, keys, values, places, query_place, groups, clip_length, clips):
    half, width = keys[0].shape
    heads = width // HEAD_DIM
    pair = 2 * block_of(half)
    deep = reaches(half, groups)[1] * pair
    outs = pl.pallas_call(
        partial(
            all_forward_kernel,
            groups=groups,
            scale=1.0 / math.sqrt(HEAD_DIM),
            clip_length=clip_length,
            clips=clips,
        ),
        in_specs=[pl.BlockSpec(memory_space=pltpu.VMEM)] * 9,
        out_specs=[pl.BlockSpec(memory_space=pltpu.VMEM)] * 2
        + [pl.BlockSpec(memory_space=pl.ANY)],
        out_shape=[jax.ShapeDtypeStruct((half, width), bf16)] * 2
        + [pltpu.HBM((heads, deep, pair), bf16)],
        scratch_shapes=[
            pltpu.VMEM((2, deep, pair), bf16),
            pltpu.SemaphoreType.DMA((2,)),
        ],
        compiler_params=params(max(10, half * half // 2**14)),
        cost_estimate=cost(16 * half * half * width, 16 * half * width, 4 * half * half * heads),
        name="attend_all",
    )(*queries, *keys, *values, *places, query_place)
    return outs[:2], outs[2]


STEP = 2


def backward_kernel(*refs, count, groups, scale):
    grad_pieces = refs[:count]
    query_a, query_b, key_a, key_b, value_a, value_b, attended_a, attended_b, stored = refs[
        count : count + 9
    ]
    outs = refs[count + 9 : count + 18]
    grad_query, grad_key, grad_value = outs[0:2], outs[2:4], outs[4:6]
    own_query, own_key, own_value = outs[6:9]
    (scores,) = refs[count + 18 :]
    half, width = key_a.shape
    rows = half // count
    group_rows = rows // groups
    block = block_of(half)
    blocks = half // block
    pair = 2 * block
    reach = reaches(half, groups)[0]

    def sources(index):
        found = []
        if groups == 1:
            for d in range(index * block // rows, (index + 1) * block // rows):
                found.append((d, 0, rows))
            return found
        each = count * group_rows
        for j in range(index * block // each, (index + 1) * block // each):
            for d in range(count):
                found.append((d, j * group_rows, group_rows))
        return found

    def one_head(head, _):
        cut = columns_of(head)

        def keep(targets, own, values, index):
            for side in range(2):
                at = side * block
                targets[side][pl.ds(index * block, block), cut] = values[at : at + block]
                for d, start, size in sources(index):
                    if d == 0:
                        own[pl.ds(side * rows + start, size), cut] = values[at : at + size]
                    at += size

        def take_grads(index):
            return jnp.concatenate(
                [
                    grad_pieces[d][pl.ds(side * rows + start, size), cut]
                    for side in range(2)
                    for d, start, size in sources(index)
                ],
                axis=0,
            )

        keys_across = take(key_a, key_b, 0, blocks, cut).T
        ones = jnp.ones((8, HEAD_DIM), bf16)
        for index, (seen, _, start) in enumerate(reach):
            result = take(attended_a, attended_b, index, index + 1, cut)
            grad = take_grads(index)
            product = grad.astype(f32) * result.astype(f32)
            high = product.astype(bf16)
            low = (product - high.astype(f32)).astype(bf16)
            delta = (dot(ones, high, NT) + dot(ones, low, NT))[0:1, :]
            back = 0.0
            for low_block in range(0, seen, STEP):
                high_block = min(low_block + STEP, seen)
                at = pl.ds((start + low_block) * pair, (high_block - low_block) * pair)
                values = take(value_a, value_b, low_block, high_block, cut)
                score = stored[head, at, :].astype(f32) * (dot(values, grad, NT) - delta)
                score = score.astype(bf16)
                scores[at, :] = score
                back += dot(keys_across[:, low_block * pair : high_block * pair], score, NN)
            keep(grad_query, own_query, (back * scale).T.astype(bf16), index)
        for index in range(blocks):
            key_sum, value_sum = 0.0, 0.0
            for other, (seen, _, start) in enumerate(reach):
                if index < seen:
                    at = pl.ds((start + index) * pair, pair)
                    query = take(query_a, query_b, other, other + 1, cut)
                    key_sum += dot(scores[at, :], query, NN)
                    value_sum += dot(stored[head, at, :], take_grads(other), NN)
            keep(grad_key, own_key, (key_sum * scale).astype(bf16), index)
            keep(grad_value, own_value, value_sum.astype(bf16), index)
        return 0

    lax.fori_loop(0, width // HEAD_DIM, one_head, 0)


def attend_back(grads, queries, keys, values, attended, stored, groups):
    half, width = keys[0].shape
    count = len(grads)
    rows = grads[0].shape[0]
    outs = pl.pallas_call(
        partial(
            backward_kernel,
            count=count,
            groups=groups,
            scale=1.0 / math.sqrt(HEAD_DIM),
        ),
        in_specs=[pl.BlockSpec(memory_space=pltpu.VMEM)] * (count + 9),
        out_specs=[pl.BlockSpec(memory_space=pltpu.VMEM)] * 9,
        out_shape=[jax.ShapeDtypeStruct((half, width), bf16)] * 6
        + [jax.ShapeDtypeStruct((rows, width), bf16)] * 3,
        scratch_shapes=[pltpu.VMEM(stored.shape[1:], bf16)],
        compiler_params=params(8 + 2 * stored.shape[1] * stored.shape[2] // 2**20),
        cost_estimate=cost(8 * 4 * half * half * width, 32 * half * width + 2 * stored.size),
        name="attend_back",
    )(*grads, *queries, *keys, *values, *attended, stored)
    return outs[0:2], outs[2:4], outs[4:6], outs[6:9]


def body(
    inputs,
    first_gain,
    query_weight,
    key_weight,
    value_weight,
    output_weight,
    second_gain,
    up_weight,
    down_weight,
    frame_sizes,
    text_counts,
    action_counts,
    cotangent,
):
    shards = lax.axis_size("seq")
    shard_index = lax.axis_index("seq")
    core = lax.axis_index("mlp") % 2
    length, width = inputs.shape
    total = length * shards
    half = length // 2
    piece = half // shards
    clips = frame_sizes.shape[0]
    clip_length = total // clips
    part = width // shards
    groups = shards if piece % 8 == 0 else 1

    def halves(rows):
        cut = rows.reshape(2, piece, shards, width)
        mine = lax.dynamic_index_in_dim(cut, core, 0, keepdims=False)
        other = lax.dynamic_index_in_dim(cut, 1 - core, 0, keepdims=False)
        return (
            mine.transpose(1, 0, 2).reshape(half, width),
            other.transpose(1, 0, 2).reshape(half, width),
        )

    inputs_half, inputs_other = halves(inputs)
    pieces = gather_early(inputs_half)
    arrived = pieces[inner_size() :: inner_size()]

    place_a, place_b, kind_a, kind_b, query_place, own_place, own_kind = tables(
        frame_sizes, text_counts, action_counts, shards, length, groups
    )
    places, kinds = (place_a, place_b), (kind_a, kind_b)
    half_kind = own_kind[:half]
    own_normed = own_norm(
        jnp.concatenate([inputs_half, inputs_other], axis=0), first_gain, own_kind
    )
    grad_half, grad_other = halves(cotangent)
    grad_own = jnp.concatenate([grad_half, grad_other], axis=0)
    (query_own,) = project_rows(after(own_normed, arrived), query_weight)
    grad_far = gather_outer(after(grad_half, arrived, pieces[inner_size() + 1]))
    pieces = after(pieces, query_own)

    normed = [norm_pieces(pieces, first_gain, kind_a, groups)]
    normed[0], grad_far = after((normed[0], grad_far), normed[0])
    normed.append(swap(normed[0], "mlp", 1))
    keys, values = zip(*[project_rows(rows, key_weight, value_weight) for rows in normed])
    heads_own = attend(query_own, keys, values, places, own_place, clip_length, clips)
    grad_inner = gather_inner(after(grad_half, normed[0]))
    heads_own, grad_inner = after((heads_own, grad_inner), heads_own)
    grad_far = join_x(jnp.concatenate(grad_far, axis=0), heads_own)
    mine, other = product_halves([heads_own], [output_weight], NN)
    other, grad_far = after((other, grad_far), other)
    grad_inner += gather_inner(grad_far)
    low, other = pair_mlp(mine, other)
    own_activated_grad = grad_activated(after(grad_own, low), down_weight)
    queries = [
        project_rows(rows, query_weight)[0] for rows in after(normed, own_activated_grad)
    ]
    other = after(other, queries)
    residual, lifted_half = lift(inputs_half, low, other, second_gain, half_kind)

    lifted_own = both(lifted_half)
    activated_own, hidden_own, mine, other = feed_own(lifted_own, up_weight, own_activated_grad)
    lifted_far = gather_outer(after(lifted_half, other))
    other, grad_inner = after((other, grad_inner), other)
    low, other = pair_mlp(mine, other)
    attended, stored = attend_all(
        after(queries, low),
        keys,
        values,
        places,
        query_place,
        groups,
        clip_length,
        clips,
    )
    other, lifted_far = after((other, lifted_far), attended)
    grad_residual, mixed_half, mixed_columns = middle(
        residual, low, other, grad_half, second_gain, half_kind, shards
    )
    heads_grad = product_back(both(mixed_half), output_weight)

    heads_first = gather_first(heads_grad)
    lifted_far = jnp.concatenate(lifted_far, axis=0)
    lifted_inner_far = gather_inner(lifted_far)
    down_mine, down_other = down_own(after(activated_own, heads_grad), down_weight)
    lifted_far = join_x(lifted_far, heads_first[1], down_other, lifted_inner_far)
    heads_grads = gather_pieces(*heads_first)
    first_lifted, first_grads = with_core([lifted_far]), with_core([grad_far])
    first_lifted = after(first_lifted, heads_grads[inner_size() + 1])
    own = (lifted_own, grad_own, activated_own, hidden_own)
    sums = feed_all(first_lifted, first_grads, up_weight, down_weight, shards, own=own)
    down_low, down_other = pair_mlp(down_mine, down_other)
    heads_grads, down_low, down_other = after((heads_grads, down_low, down_other), sums)
    lifted_inner = gather_inner(after(lifted_half, down_other))

    query_low, key_low, value_low, own_low = attend_back(
        heads_grads, queries, keys, values, attended, stored, groups
    )
    attention_weights = (query_weight, key_weight, value_weight)
    lifted_inner += [join_x(far, own_low) for far in lifted_inner_far]
    own_low, lifted_inner = after((own_low, lifted_inner), own_low)
    low, other = pair_mlp(*product_halves(own_low, attention_weights, NT))

    query_grad, key_grad, value_grad, first_gain_grad = project(
        normed,
        after((query_low, key_low, value_low), low),
        attention_weights,
        first_gain,
        kinds,
        shards,
    )
    first_gain_grad = first_gain_grad + swap(first_gain_grad, "mlp", 1)
    other, first_gain_grad = after((other, first_gain_grad), query_grad)
    input_half = last(inputs_half, low, other, grad_residual, first_gain, half_kind, shards)
    outputs_half = finish(residual, down_low, after(down_other, input_half), shards)
    mixed_part = lax.all_to_all(
        after(mixed_columns, outputs_half), "seq", split_axis=0, concat_axis=0, tiled=True
    )
    rest_lifted = with_core(after(lifted_inner, other))
    rest_grads = with_core(after(grad_inner, other))
    up_grad, down_grad = feed_all(
        after(rest_lifted, outputs_half), rest_grads, up_weight, down_weight, shards, sums
    )
    bit = 2
    while bit < lax.axis_size("mlp"):
        came = after(swap(first_gain_grad, "mlp", bit), up_grad)
        first_gain_grad = first_gain_grad + came
        bit *= 2
    placed = (input_half, outputs_half)
    input_grad, outputs = place_halves(placed, [swap(array, "mlp", 1) for array in placed])
    mixed_part = after(mixed_part, up_grad)
    output_grad, second_gain_grad = output_part(
        attended, (mixed_part, swap(mixed_part, "mlp", 1)), groups
    )

    return (
        outputs,
        input_grad,
        first_gain_grad,
        query_grad,
        key_grad,
        value_grad,
        output_grad,
        second_gain_grad,
        up_grad,
        down_grad,
    )


def solution(mesh):
    return jax.shard_map(
        body,
        mesh=mesh,
        in_specs=(
            P("seq", None),
            P(),
            P(None, "mlp"),
            P(None, "mlp"),
            P(None, "mlp"),
            P("mlp", None),
            P(),
            P(None, "mlp"),
            P("mlp", None),
            P(),
            P(),
            P(),
            P("seq", None),
        ),
        out_specs=(
            P("seq", None),
            P("seq", None),
            P(None, "seq"),
            P("seq", "mlp"),
            P("seq", "mlp"),
            P("seq", "mlp"),
            P("mlp", "seq"),
            P(None, "seq"),
            P("seq", "mlp"),
            P("mlp", "seq"),
        ),
        check_vma=False,
    )
```

```python
from functools import partial
import math

import jax
import jax.numpy as jnp
from jax import lax
from jax.experimental import pallas as pl
from jax.experimental.pallas import tpu as pltpu
from jax.sharding import PartitionSpec as P

HEAD_DIM = 128
epsilon = 1e-05
bf16 = jnp.bfloat16
f32 = jnp.float32
NEGATIVE = -1e30

WHOLE = pl.BlockSpec(memory_space=pltpu.VMEM)
NN = ((1,), (0,))
NT = ((1,), (1,))
TN = ((0,), (0,))


def dot(a, b, dims):
    return lax.dot_general(a, b, (dims, ((), ())), preferred_element_type=f32)


def params(mebibytes):
    return pltpu.CompilerParams(vmem_limit_bytes=mebibytes * 1024 * 1024)


def cost(flops, moved, transcendentals=0, share=100):
    return pl.CostEstimate(
        flops=int(flops) // share,
        bytes_accessed=int(moved) // share,
        transcendentals=int(transcendentals) // share,
    )


def swap(value, axis, bit):
    size = lax.axis_size(axis)
    return lax.ppermute(value, axis, [(i, i ^ bit) for i in range(size)])


def inner_size():
    return 1 << (int(math.log2(lax.axis_size("seq"))) // 2)


def x_size():
    return lax.axis_size("mlp") // 2


def after(values, *earlier):
    return lax.optimization_barrier((values, earlier))[0]


def in_hbm(array):
    return pltpu.with_memory_space_constraint(array, pltpu.HBM)


def own_quarter(half):
    rows = half.shape[0] // x_size()
    return lax.dynamic_slice_in_dim(half, (lax.axis_index("mlp") // 2) * rows, rows, 0)


def join_x(quarter, *earlier):
    bit = 1
    while bit < x_size():
        came = after(swap(quarter, "mlp", 2 * bit), earlier)
        quarter = jnp.concatenate([quarter, came], axis=0)
        bit *= 2
    return quarter


def gather_early(half):
    size, inner = lax.axis_size("seq"), inner_size()
    quarter = own_quarter(half)
    pieces = {0: half}
    far = {outer: swap(quarter, "seq", outer) for outer in range(inner, size, inner)}
    for bit in range(1, inner):
        pieces[bit] = swap(half, "seq", bit)
    for outer in range(inner, size, inner):
        pieces[outer] = join_x(far[outer])
        for bit in range(1, inner):
            pieces[outer | bit] = swap(pieces[outer], "seq", bit)
    return [pieces[d] for d in range(size)]


def gather_outer(half):
    size, inner = lax.axis_size("seq"), inner_size()
    quarter = own_quarter(half)
    return [swap(quarter, "seq", outer) for outer in range(inner, size, inner)]


def gather_inner(array):
    return [swap(array, "seq", bit) for bit in range(1, inner_size())]


def with_core(arrays):
    return [each for array in arrays for each in (array, swap(array, "mlp", 1))]


def gather_first(piece):
    size, inner = lax.axis_size("seq"), inner_size()
    pieces = {0: piece}
    for bit in range(1, inner):
        pieces[bit] = swap(piece, "seq", bit)
    return pieces, [swap(piece, "seq", outer) for outer in range(inner, size, inner)]


def gather_pieces(pieces, far):
    size, inner = lax.axis_size("seq"), inner_size()
    for outer, came in zip(range(inner, size, inner), far):
        pieces[outer] = came
        for bit in range(1, inner):
            pieces[outer | bit] = swap(came, "seq", bit)
    return [pieces[d] for d in range(size)]


def rounded(value):
    return lax.optimization_barrier(value.astype(bf16))


def pair_mlp(mine, other_half):
    low, other = rounded(mine + swap(other_half, "mlp", 1).astype(f32)), None
    bit = 2
    while bit < lax.axis_size("mlp"):
        if other is not None:
            low = rounded(low.astype(f32) + other.astype(f32))
        other = swap(low, "mlp", bit)
        bit *= 2
    if other is None:
        other = jnp.zeros_like(low)
    return low, other


def both(half):
    return jnp.concatenate([half, swap(half, "mlp", 1)], axis=0)


def tables_kernel(index, frames, texts, actions, *outs, shards, length, groups, clip_length):
    place_a, place_b, kind_a, kind_b, query_place, own_place, own_kind = outs
    shard_index, core = index[0], index[1]
    shape = (shards, length)
    place = lax.broadcasted_iota(jnp.int32, shape, 0) * length + lax.broadcasted_iota(
        jnp.int32, shape, 1
    )
    kinds = jnp.full(shape, 2, jnp.int32)
    for clip in range(frames.shape[0]):
        start = jnp.int32(clip * clip_length)
        within = (place >= clip * clip_length) & (place < (clip + 1) * clip_length)
        for frame in range(frames.shape[1]):
            text_end = start + texts[clip, frame]
            action_end = text_end + actions[clip, frame]
            kinds = jnp.where(within & (place >= start) & (place < text_end), 0, kinds)
            kinds = jnp.where(within & (place >= text_end) & (place < action_end), 1, kinds)
            start = action_end + frames[clip, frame]
    square = (length, length)
    down = lax.broadcasted_iota(jnp.int32, square, 0)
    across = lax.broadcasted_iota(jnp.int32, square, 1)
    earlier = (down < across).astype(f32).astype(bf16)
    rank = jnp.zeros(shape, f32)
    before = jnp.zeros((shards, 1), f32)
    for kind in range(3):
        chosen = (kinds == kind).astype(f32)
        rank += chosen * (dot(chosen.astype(bf16), earlier, NN) + before)
        before += chosen.sum(axis=1, keepdims=True)
    rank_low, kinds_low = rank.astype(bf16), kinds.astype(f32).astype(bf16)
    piece = length // shards // 2
    lane = lax.broadcasted_iota(jnp.int32, (1, length), 1).astype(f32)

    def find(shard, offset, side, row):
        wanted = (shard_index ^ offset) * (2 * piece) + (core ^ side) * piece + row
        pick = shard == lax.broadcasted_iota(jnp.int32, (length, shards), 1)
        pick = pick.astype(f32).astype(bf16)
        hit = dot(pick, rank_low, NN) == wanted.astype(f32)
        where = jnp.sum(jnp.where(hit, lane, 0.0), axis=1, keepdims=True).astype(jnp.int32)
        kind = jnp.sum(jnp.where(hit, dot(pick, kinds_low, NN), 0.0), axis=1, keepdims=True)
        return where + shard * length, kind.astype(jnp.int32)

    def as_row(column):
        return jnp.sum(jnp.where(down == across, column, 0), axis=0, keepdims=True)

    step = lax.broadcasted_iota(jnp.int32, (length, 1), 0)
    half = length // 2
    for side, (place_out, kind_out) in enumerate(((place_a, kind_a), (place_b, kind_b))):
        for block in range(shards // 2):
            token = step + block * length
            if groups > 1:
                shard, offset = token // (shards * piece), (token // piece) % shards
            else:
                offset, shard = token // half, (token % half) // piece
            where, kind = find(shard, offset, side, token % piece)
            at = pl.ds(block * length, length)
            place_out[at, :] = where
            kind_out[at, :] = kind
            query_place[:, pl.ds((2 * block + side) * length, length)] = as_row(where)
    where, kind = find((step % half) // piece, step * 0, step // half, step % piece)
    own_place[...] = as_row(where)
    own_kind[...] = kind


def tables(frames, texts, actions, shards, length, groups):
    index = jnp.stack([lax.axis_index("seq"), lax.axis_index("mlp") % 2]).astype(jnp.int32)
    total = shards * length
    column = jax.ShapeDtypeStruct((total // 2, 1), jnp.int32)
    return pl.pallas_call(
        partial(
            tables_kernel,
            shards=shards,
            length=length,
            groups=groups,
            clip_length=total // frames.shape[0],
        ),
        in_specs=[pl.BlockSpec(memory_space=pltpu.SMEM)] * 4,
        out_shape=[column] * 4
        + [
            jax.ShapeDtypeStruct((1, total), jnp.int32),
            jax.ShapeDtypeStruct((1, length), jnp.int32),
            jax.ShapeDtypeStruct((length, 1), jnp.int32),
        ],
        cost_estimate=cost(8 * total * length, 8 * 128 * total),
        name="tables",
    )(index, frames, texts, actions)


def rows_kernel(*refs, count):
    rows, weights, outs = refs[0], refs[1 : 1 + count], refs[1 + count :]
    for weight, out in zip(weights, outs):
        out[...] = dot(rows[...], weight[...], NN).astype(bf16)


def project_rows(rows, *weights):
    across = weights[0].shape[1]
    return pl.pallas_call(
        partial(rows_kernel, count=len(weights)),
        out_shape=[jax.ShapeDtypeStruct((rows.shape[0], across), bf16)] * len(weights),
        compiler_params=params(8),
        cost_estimate=cost(2 * rows.size * across * len(weights), 2 * rows.size),
        name="project_rows",
    )(rows, *weights)


def one_kernel(rows, weight, out):
    out[...] = dot(rows[...], weight[...], NT).astype(bf16)


def product_back(rows, weight):
    return pl.pallas_call(
        one_kernel,
        out_shape=jax.ShapeDtypeStruct((rows.shape[0], weight.shape[0]), bf16),
        compiler_params=params(6),
        cost_estimate=cost(2 * rows.size * weight.shape[0], 2 * weight.size),
        name="product_back",
    )(rows, weight)


def halves_kernel(*refs, count, dims):
    mine, other = refs[-2:]
    half = mine.shape[0]
    total = sum(dot(refs[k][...], refs[count + k][...], dims) for k in range(count))
    mine[...] = total[:half]
    other[...] = total[half:].astype(bf16)


def product_halves(rows, weights, dims):
    count = len(rows)
    half = rows[0].shape[0] // 2
    across = weights[0].shape[1 - dims[1][0]]
    shape = (half, across)
    return pl.pallas_call(
        partial(halves_kernel, count=count, dims=dims),
        out_shape=[jax.ShapeDtypeStruct(shape, f32), jax.ShapeDtypeStruct(shape, bf16)],
        compiler_params=params(6),
        cost_estimate=cost(2 * count * rows[0].size * across, 2 * count * weights[0].size),
        name="product_halves",
    )(*rows, *weights)


def down_own_kernel(rows, weight, mine, other, total):
    total[...] = jnp.zeros_like(total)

    def step(at):
        total[...] += dot(rows[:, at], weight[at, :], NN)

    tiles_of(weight.shape[0], math.gcd(weight.shape[0], 512), step)
    half = mine.shape[0]
    mine[...] = total[:half]
    other[...] = total[half:].astype(bf16)


def down_own(rows, weight):
    count, deep = rows.shape
    across = weight.shape[1]
    shape = (count // 2, across)
    return pl.pallas_call(
        down_own_kernel,
        in_specs=[WHOLE] * 2,
        out_specs=[WHOLE] * 2,
        out_shape=[jax.ShapeDtypeStruct(shape, f32), jax.ShapeDtypeStruct(shape, bf16)],
        scratch_shapes=[pltpu.VMEM((count, across), f32)],
        compiler_params=params(6),
        cost_estimate=cost(2 * rows.size * across, 2 * weight.size),
        name="down_own",
    )(rows, weight)


def gain_rows(gain, column):
    return jnp.where(
        column == 0, gain[0:1, :], jnp.where(column == 1, gain[1:2, :], gain[2:3, :])
    )


def normalize(values):
    mean = jnp.mean(values, axis=1, keepdims=True)
    centered = values - mean
    inverse = lax.rsqrt(jnp.mean(centered * centered, axis=1, keepdims=True) + epsilon)
    return (centered * inverse, inverse)


def norm_back(grad, normal, inverse, gains):
    scaled = grad * gains
    return inverse * (
        scaled
        - jnp.mean(scaled, axis=1, keepdims=True)
        - normal * jnp.mean(scaled * normal, axis=1, keepdims=True)
    )


def norm_kernel(*refs, groups, inner, parts):
    index, gain, kind, out = refs[0], refs[-3], refs[-2], refs[-1]
    pieces = refs[1:-3]
    rows, width = pieces[0].shape
    count = len(pieces)
    step = rows // parts
    for d, piece in enumerate(pieces):
        for part in range(parts):
            normal, _ = normalize(piece[pl.ds(part * step, step), :].astype(f32))
            place = part if d < inner else part ^ index[0]
            if groups > 1:
                each = groups // parts
                at = pl.ds(place * each, each)
                column = kind[at, d].reshape(step, 1)
                normed = (normal * gain_rows(gain, column)).astype(bf16)
                out[at, d] = normed.reshape(each, rows // groups, width)
            else:
                column = kind[d, place]
                out[d, place] = (normal * gain_rows(gain, column)).astype(bf16)


def norm_pieces(pieces, gain, kind, groups):
    rows, width = pieces[0].shape
    count = len(pieces)
    parts = x_size()
    if groups > 1:
        shape = (groups, count, rows // groups)
    else:
        shape = (count, parts, rows // parts)
    memory = [pl.BlockSpec(memory_space=pltpu.SMEM)]
    index = (lax.axis_index("mlp") // 2).astype(jnp.int32).reshape(1)
    out = pl.pallas_call(
        partial(norm_kernel, groups=groups, inner=inner_size(), parts=parts),
        in_specs=memory + [pl.BlockSpec(memory_space=pltpu.VMEM)] * (count + 2),
        out_shape=jax.ShapeDtypeStruct(shape + (width,), bf16),
        compiler_params=params(4 + count),
        cost_estimate=cost(10 * count * rows * width, 4 * count * rows * width),
        name="norm_pieces",
    )(index, *pieces, gain, kind.reshape(shape + (1,)))
    return out.reshape(count * rows, width)


def own_norm_kernel(rows, gain, kind, out):
    normal, _ = normalize(rows[...].astype(f32))
    out[...] = (normal * gain_rows(gain, kind[...])).astype(bf16)


def own_norm(rows, gain, kind):
    return pl.pallas_call(
        own_norm_kernel,
        out_shape=jax.ShapeDtypeStruct(rows.shape, bf16),
        compiler_params=params(4),
        cost_estimate=cost(10 * rows.size, 4 * rows.size),
        name="own_norm",
    )(rows, gain, kind)


def lift_kernel(rows, low, other, gain, kind, residual, lifted):
    value = rows[...].astype(f32) + (low[...].astype(f32) + other[...].astype(f32))
    residual[...] = value
    normal, _ = normalize(value)
    lifted[...] = (normal * gain_rows(gain, kind[...])).astype(bf16)


def lift(rows, low, other, gain, kind):
    return pl.pallas_call(
        lift_kernel,
        in_specs=[WHOLE] * 5,
        out_specs=[WHOLE] * 2,
        out_shape=[jax.ShapeDtypeStruct(rows.shape, f32), jax.ShapeDtypeStruct(rows.shape, bf16)],
        compiler_params=params(4),
        cost_estimate=cost(10 * rows.size, 12 * rows.size),
        name="lift",
    )(rows, low, other, gain, kind)


def kind_sums(term, kind):
    sums = [jnp.sum(jnp.where(kind == k, term, 0.0), axis=0, keepdims=True) for k in range(3)]
    high = [value.astype(bf16) for value in sums]
    low = [(value - part.astype(f32)).astype(bf16) for value, part in zip(sums, high)]
    zero = jnp.zeros((1, term.shape[1]), bf16)
    return jnp.concatenate(high + low + [zero, zero], axis=0)


def middle_kernel(index, residual, low, other, grad, gain, kind, grad_residual, mixed, parts):
    lifted_grad = low[...].astype(f32) + other[...].astype(f32)
    normal, inverse = normalize(residual[...])
    column = kind[...]
    back = norm_back(lifted_grad, normal, inverse, gain_rows(gain, column))
    value = grad[...].astype(f32) + back
    grad_residual[...] = value
    rounded_value = value.astype(bf16)
    mixed[...] = rounded_value
    sums = kind_sums(lifted_grad * normal, column)
    shards, rows, part = parts.shape
    for k in range(shards):
        at = index[0] ^ k
        parts[at, pl.ds(0, rows - 8), :] = rounded_value[:, k * part : (k + 1) * part]
        parts[at, pl.ds(rows - 8, 8), :] = sums[:, k * part : (k + 1) * part]


def middle(residual, low, other, grad, gain, kind, shards):
    rows, width = residual.shape
    index = lax.axis_index("seq").astype(jnp.int32).reshape(1)
    return pl.pallas_call(
        middle_kernel,
        in_specs=[pl.BlockSpec(memory_space=pltpu.SMEM)] + [WHOLE] * 6,
        out_specs=[WHOLE] * 3,
        out_shape=[
            jax.ShapeDtypeStruct(residual.shape, f32),
            jax.ShapeDtypeStruct(residual.shape, bf16),
            jax.ShapeDtypeStruct((shards, rows + 8, width // shards), bf16),
        ],
        compiler_params=params(6),
        cost_estimate=cost(20 * residual.size, 16 * residual.size),
        name="middle",
    )(index, residual, low, other, grad, gain, kind)


def reordered(values, shards):
    count = values.shape[0]
    piece = count // shards
    to = lax.broadcasted_iota(jnp.int32, (count, count), 0)
    source = lax.broadcasted_iota(jnp.int32, (count, count), 1)
    pick = (source == (to % shards) * piece + to // shards).astype(f32).astype(bf16)
    return dot(pick, values, NN).astype(bf16)


def finish_kernel(residual, low, other, out, *, shards):
    value = residual[...] + (low[...].astype(f32) + other[...].astype(f32))
    out[...] = reordered(value.astype(bf16), shards)


def finish(residual, low, other, shards):
    return pl.pallas_call(
        partial(finish_kernel, shards=shards),
        in_specs=[WHOLE] * 3,
        out_specs=WHOLE,
        out_shape=jax.ShapeDtypeStruct(residual.shape, bf16),
        compiler_params=params(4),
        cost_estimate=cost(2 * residual.size, 10 * residual.size),
        name="finish",
    )(residual, low, other)


def place_kernel(index, *refs):
    count = len(refs) // 3
    for mine, other, out in zip(refs[:count], refs[count : 2 * count], refs[2 * count :]):
        half = mine.shape[0]
        out[pl.ds(pl.multiple_of(index[0] * half, half), half), :] = mine[...]
        out[pl.ds(pl.multiple_of((1 - index[0]) * half, half), half), :] = other[...]


def place_halves(arrays, others):
    half, width = arrays[0].shape
    index = (lax.axis_index("mlp") % 2).astype(jnp.int32).reshape(1)
    return pl.pallas_call(
        place_kernel,
        in_specs=[pl.BlockSpec(memory_space=pltpu.SMEM)] + [WHOLE] * (2 * len(arrays)),
        out_shape=[jax.ShapeDtypeStruct((2 * half, width), bf16)] * len(arrays),
        compiler_params=params(6),
        cost_estimate=cost(half * width, 16 * half * width),
        name="place_halves",
    )(index, *arrays, *others)


def last_kernel(rows, low, other, grad_residual, gain, kind, out, *, shards):
    grad = low[...].astype(f32) + other[...].astype(f32)
    normal, inverse = normalize(rows[...].astype(f32))
    back = norm_back(grad, normal, inverse, gain_rows(gain, kind[...]))
    out[...] = reordered((grad_residual[...] + back).astype(bf16), shards)


def last(rows, low, other, grad_residual, gain, kind, shards):
    return pl.pallas_call(
        partial(last_kernel, shards=shards),
        in_specs=[WHOLE] * 6,
        out_specs=WHOLE,
        out_shape=jax.ShapeDtypeStruct(rows.shape, bf16),
        compiler_params=params(6),
        cost_estimate=cost(20 * rows.size, 12 * rows.size),
        name="last",
    )(rows, low, other, grad_residual, gain, kind)


def gelu_parts(value):
    rate = math.sqrt(2 / math.pi)
    square = value * value
    bent = jnp.tanh(value * (rate + (rate * 0.044715) * square))
    upper = 0.5 * (1 + bent)
    slope = upper + (0.5 * value) * (1 - bent * bent) * (rate + (rate * 3 * 0.044715) * square)
    return value * upper, slope


def tiles_of(extent, tile, step):
    def at(t, _):
        step(pl.ds(pl.multiple_of(t * tile, tile), tile))
        return 0

    lax.fori_loop(0, extent // tile, at, 0)


def own_kernel(lifted, up, grad_activated, activated, hidden_grads, mine, other, total):
    total[...] = jnp.zeros_like(total)

    def step(at):
        value, slope = gelu_parts(dot(lifted[...], up[:, at], NN))
        activated[:, at] = value.astype(bf16)
        hidden_grad = (grad_activated[:, at] * slope).astype(bf16)
        hidden_grads[:, at] = hidden_grad
        total[...] += dot(hidden_grad, up[:, at], NT)

    tiles_of(up.shape[1], math.gcd(up.shape[1], 512), step)
    half = mine.shape[0]
    mine[...] = total[:half]
    other[...] = total[half:].astype(bf16)


def feed_own(lifted, up, grad_activated):
    rows, width = lifted.shape
    hidden = up.shape[1]
    return pl.pallas_call(
        own_kernel,
        in_specs=[WHOLE] * 3,
        out_specs=[WHOLE] * 4,
        out_shape=[jax.ShapeDtypeStruct((rows, hidden), bf16)] * 2
        + [
            jax.ShapeDtypeStruct((rows // 2, width), f32),
            jax.ShapeDtypeStruct((rows // 2, width), bf16),
        ],
        scratch_shapes=[pltpu.VMEM((rows, width), f32)],
        compiler_params=params(8),
        cost_estimate=cost(4 * rows * width * hidden, 2 * width * hidden),
        name="feed_own",
    )(lifted, up, grad_activated)


def down_kernel(grad, down, out):
    def step(at):
        out[:, at] = dot(grad[...], down[at, :], NT)

    tiles_of(down.shape[0], math.gcd(down.shape[0], 512), step)


def grad_activated(grad, down):
    rows, width = grad.shape
    hidden = down.shape[0]
    return pl.pallas_call(
        down_kernel,
        in_specs=[WHOLE] * 2,
        out_specs=WHOLE,
        out_shape=jax.ShapeDtypeStruct((rows, hidden), f32),
        compiler_params=params(6),
        cost_estimate=cost(2 * rows * width * hidden, 2 * width * hidden),
        name="grad_activated",
    )(grad, down)


def all_kernel(index, *refs, count):
    lifted_parts, grad_parts = refs[:count], refs[count : 2 * count]
    up, down = refs[2 * count : 2 * count + 2]
    before = refs[2 * count + 2 : -5]
    up_grad, down_grad, lifted_across, hidden_kept, grad_kept = refs[-5:]
    part = up_grad.shape[0]
    mine = pl.ds(pl.multiple_of(index[0] * part, part), part)

    def rows_of(parts, at):
        return jnp.concatenate([ref[:, at] for ref in parts], axis=0)

    @pl.when(pl.program_id(0) == 0)
    def _():
        lifted_across[...] = rows_of(lifted_parts, mine).T

    first = pl.program_id(0) == 0
    last_step = pl.num_programs(0) - 1

    tile = hidden_kept.shape[1]
    at = jnp.minimum(pl.program_id(0), last_step - 1) if up.shape[1] > tile else 0
    here = pl.ds(pl.multiple_of(at * tile, tile), tile)

    def products():
        everything = slice(None)
        return (
            dot(rows_of(lifted_parts, everything), up[:, here], NN),
            dot(rows_of(grad_parts, everything), down[here, :], NT),
        )

    def finish_tile(hidden_value, activated_grad):
        value, slope = gelu_parts(hidden_value)
        hidden_grad = (activated_grad * slope).astype(bf16)
        down_term = dot(value.astype(bf16), rows_of(grad_parts, mine), TN)
        up_term = dot(lifted_across[...], hidden_grad, NN)
        if len(before) == 2:
            up_term += before[0][...].astype(f32)
            down_term += before[1][...].astype(f32)
        else:
            lifted_own, grad_own, activated, hidden_own = before
            up_term += dot(lifted_own[...], hidden_own[...], TN)
            down_term += dot(activated[...], grad_own[...], TN)
        up_grad[...] = up_term.astype(up_grad.dtype)
        down_grad[...] = down_term.astype(down_grad.dtype)

    @pl.when(first)
    def _():
        hidden_kept[...], grad_kept[...] = products()

    @pl.when((pl.program_id(0) > 0) & (pl.program_id(0) < last_step))
    def _():
        kept = hidden_kept[...], grad_kept[...]
        fresh = products()
        finish_tile(*kept)
        hidden_kept[...], grad_kept[...] = fresh

    @pl.when(pl.program_id(0) == last_step)
    def _():
        finish_tile(hidden_kept[...], grad_kept[...])


def feed_all(lifted, grad, up, down, shards, sums=(), own=()):
    counts = [array.shape[0] for array in lifted]
    rows, width = sum(counts), lifted[0].shape[1]
    count = len(counts)
    part = width // shards
    hidden = up.shape[1]
    tile = math.gcd(hidden, 256)
    steps = hidden // tile
    across = lambda t, index: (0, jnp.maximum(t - 1, 0))
    below = lambda t, index: (jnp.maximum(t - 1, 0), 0)
    mine = lambda t, index: (0, index[0])
    sum_specs = [pl.BlockSpec((part, tile), across), pl.BlockSpec((tile, part), below)]
    if own:
        own_rows = own[0].shape[0]
        more = [pl.BlockSpec((own_rows, part), mine)] * 2
        more += [pl.BlockSpec((own_rows, tile), across)] * 2
    else:
        more = sum_specs
    index = lax.axis_index("seq").astype(jnp.int32).reshape(1)
    return pl.pallas_call(
        partial(all_kernel, count=count),
        grid_spec=pltpu.PrefetchScalarGridSpec(
            num_scalar_prefetch=1,
            grid=(steps + 1,),
            in_specs=[WHOLE] * (2 * count)
            + [WHOLE] * 2
            + more,
            out_specs=sum_specs,
            scratch_shapes=[pltpu.VMEM((part, rows), bf16)]
            + [pltpu.VMEM((rows, tile), f32)] * 2,
        ),
        out_shape=[
            pltpu.HBM((part, hidden), bf16 if own else f32),
            pltpu.HBM((hidden, part), bf16 if own else f32),
        ],
        compiler_params=params((6 if own else 8) + 8 * rows // 512),
        cost_estimate=cost(
            4 * rows * hidden * (width + part),
            4 * width * hidden + 4 * rows * width,
        ),
        name="feed_all",
    )(
        index,
        *lifted,
        *grad,
        up,
        down,
        *(own or [in_hbm(array) for array in sums]),
    )


def project_kernel(index, *refs):
    normed, lows, weights = refs[0:2], refs[2:8], refs[8:11]
    gain, kinds = refs[11], refs[12:14]
    outs, gain_grad = refs[14:17], refs[17]
    for k in range(3):
        outs[k][...] = sum(dot(normed[side][...], lows[2 * k + side][...], TN) for side in range(2))
    gain_sum = [0.0, 0.0, 0.0]
    for side in range(2):
        column = kinds[side][...]
        term = sum(dot(lows[2 * k + side][...], weights[k][...], NT) for k in range(3))
        term = term * (normed[side][...].astype(f32) / gain_rows(gain, column))
        for k in range(3):
            gain_sum[k] += jnp.sum(jnp.where(column == k, term, 0.0), axis=0, keepdims=True)
    gain_grad[...] = jnp.concatenate(gain_sum, axis=0)


def project(normed, lows, weights, gain, kinds, shards):
    rows, width = normed[0].shape
    across = lows[0][0].shape[1]
    part = width // shards
    whole = lambda t, index: (0, 0)
    mine = lambda t, index: (0, index[0])
    below = lambda t, index: (index[0], 0)
    index = lax.axis_index("seq").astype(jnp.int32).reshape(1)
    return pl.pallas_call(
        project_kernel,
        grid_spec=pltpu.PrefetchScalarGridSpec(
            num_scalar_prefetch=1,
            grid=(1,),
            in_specs=[pl.BlockSpec((rows, part), mine)] * 2
            + [pl.BlockSpec((rows, across), whole)] * 6
            + [pl.BlockSpec((part, across), below)] * 3
            + [pl.BlockSpec((gain.shape[0], part), mine)]
            + [pl.BlockSpec((rows, 1), whole)] * 2,
            out_specs=[pl.BlockSpec((part, across), whole)] * 3
            + [pl.BlockSpec((gain.shape[0], part), whole)],
        ),
        out_shape=[jax.ShapeDtypeStruct((part, across), f32)] * 3
        + [jax.ShapeDtypeStruct((gain.shape[0], part), f32)],
        compiler_params=params(8),
        cost_estimate=cost(24 * rows * part * across, 12 * rows * across + 12 * part * across),
        name="project",
    )(index, *normed, *[low for pair in lows for low in pair], *weights, gain, *kinds)


def output_kernel(attended_a, attended_b, came_a, came_b, out, gain_grad, *, groups):
    total, sums = 0.0, 0.0
    shards, rows, part = came_a.shape
    half = rows - 8
    each = half // groups
    for attended, came in ((attended_a, came_a), (attended_b, came_b)):
        mixed = [
            came[d, pl.ds(group * each, each), :]
            for group in range(groups)
            for d in range(shards)
        ]
        total += dot(attended[...], jnp.concatenate(mixed, axis=0), TN)
        own_sums = 0.0
        for k in range(shards):
            own_sums += came[k, pl.ds(half, 8), :].astype(f32)
        sums += own_sums
    out[...] = total
    gain_grad[...] = sums[0:3, :] + sums[3:6, :]


def output_part(attended, came, groups):
    across, part = attended[0].shape[1], came[0].shape[2]
    return pl.pallas_call(
        partial(output_kernel, groups=groups),
        in_specs=[WHOLE] * 4,
        out_shape=[
            jax.ShapeDtypeStruct((across, part), f32),
            jax.ShapeDtypeStruct((3, part), f32),
        ],
        compiler_params=params(6),
        cost_estimate=cost(
            4 * attended[0].shape[0] * across * part, 4 * attended[0].shape[0] * (across + part)
        ),
        name="output_part",
    )(*attended, *came)


def mask_of(key_place, query_place, clip_length, clips):
    allowed = key_place <= query_place
    if clips > 1:
        allowed = allowed & (key_place // clip_length == query_place // clip_length)
    return allowed


def probabilities(scores, scale):
    top = scores[0].max(axis=0, keepdims=True)
    for block in scores[1:]:
        top = jnp.maximum(top, block.max(axis=0, keepdims=True))
    rate = scale * math.log2(math.e)
    weights = [jnp.exp2((block - top) * rate) for block in scores]
    total = weights[0].sum(axis=0, keepdims=True)
    for block in weights[1:]:
        total = total + block.sum(axis=0, keepdims=True)
    inverse = 1.0 / total
    return [block * inverse for block in weights]


def forward_kernel(query, key_a, key_b, value_a, value_b, place_a, place_b, query_place, out, **opts):
    scale = opts["scale"]
    query_place = query_place[...]
    allowed = [
        mask_of(place[...], query_place, opts["clip_length"], opts["clips"])
        for place in (place_a, place_b)
    ]
    for head in range(query.shape[1] // HEAD_DIM):
        at = pl.ds(head * HEAD_DIM, HEAD_DIM)
        scores = [
            jnp.where(mask, dot(key[:, at], query[:, at], NT), NEGATIVE)
            for mask, key in zip(allowed, (key_a, key_b))
        ]
        prob = [block.astype(bf16) for block in probabilities(scores, scale)]
        result = dot(value_a[:, at], prob[0], TN) + dot(value_b[:, at], prob[1], TN)
        out[:, at] = result.T.astype(bf16)


def attend(query, keys, values, places, query_place, clip_length, clips):
    rows, width = query.shape
    total = 2 * keys[0].shape[0]
    return pl.pallas_call(
        partial(
            forward_kernel, scale=1.0 / math.sqrt(HEAD_DIM), clip_length=clip_length, clips=clips
        ),
        out_shape=jax.ShapeDtypeStruct((rows, width), bf16),
        compiler_params=params(8),
        cost_estimate=cost(
            4 * rows * total * width, 4 * total * width, rows * total * (width // HEAD_DIM)
        ),
        name="attend",
    )(query, *keys, *values, *places, query_place)


def block_of(half):
    return min(128, half)


def reaches(half, groups):
    blocks = half // block_of(half)
    found, start = [], 0
    for index in range(blocks):
        seen, free = (index + 1, index) if groups > 1 else (blocks, 0)
        found.append((seen, free, start))
        start += seen
    return found, start


def take(first, second, low, high, at):
    block = block_of(first.shape[0])
    rows = [side[pl.ds(k * block, block), at] for k in range(low, high) for side in (first, second)]
    return jnp.concatenate(rows, axis=0)


def columns_of(head):
    return pl.ds(pl.multiple_of(head * HEAD_DIM, HEAD_DIM), HEAD_DIM)


def all_forward_kernel(*refs, groups, scale, clip_length, clips):
    query_a, query_b, key_a, key_b, value_a, value_b, place_a, place_b, query_place = refs[:9]
    attended_a, attended_b, stored, kept_probs, sems = refs[9:]
    half, width = key_a.shape
    heads = width // HEAD_DIM
    block = block_of(half)
    pair = 2 * block
    everything = slice(None)

    def copy_of(head):
        slot = head % 2
        return pltpu.make_async_copy(kept_probs.at[slot], stored.at[head], sems.at[slot])

    def one_head(head, _):
        cut = columns_of(head)
        slot = head % 2

        @pl.when(head >= 2)
        def _():
            copy_of(head - 2).wait()

        values_across = take(value_a, value_b, 0, half // block, cut).T
        for index, (seen, free, start) in enumerate(reaches(half, groups)[0]):
            mine = pl.ds(index * block, block)
            query = take(query_a, query_b, index, index + 1, cut)
            at_place = query_place[:, pl.ds(index * pair, pair)]
            place = take(place_a, place_b, free, seen, everything)
            mask = mask_of(place, at_place, clip_length, clips)
            score = dot(take(key_a, key_b, free, seen, cut), query, NT)
            scores = [jnp.where(mask, score, NEGATIVE)]
            if free:
                scores.insert(0, dot(take(key_a, key_b, 0, free, cut), query, NT))
            result, at = 0.0, 0
            for prob in probabilities(scores, scale):
                kept = prob.astype(bf16)
                rows = kept.shape[0]
                kept_probs[slot, pl.ds(start * pair + at, rows), :] = kept
                result += dot(values_across[:, at : at + rows], kept, NN)
                at += rows
            result = result.T.astype(bf16)
            attended_a[mine, cut] = result[:block]
            attended_b[mine, cut] = result[block:]
        copy_of(head).start()
        return 0

    lax.fori_loop(0, heads, one_head, 0)
    for head in range(max(0, heads - 2), heads):
        copy_of(head).wait()


def attend_all(queries, keys, values, places, query_place, groups, clip_length, clips):
    half, width = keys[0].shape
    heads = width // HEAD_DIM
    pair = 2 * block_of(half)
    deep = reaches(half, groups)[1] * pair
    outs = pl.pallas_call(
        partial(
            all_forward_kernel,
            groups=groups,
            scale=1.0 / math.sqrt(HEAD_DIM),
            clip_length=clip_length,
            clips=clips,
        ),
        in_specs=[pl.BlockSpec(memory_space=pltpu.VMEM)] * 9,
        out_specs=[pl.BlockSpec(memory_space=pltpu.VMEM)] * 2
        + [pl.BlockSpec(memory_space=pl.ANY)],
        out_shape=[jax.ShapeDtypeStruct((half, width), bf16)] * 2
        + [pltpu.HBM((heads, deep, pair), bf16)],
        scratch_shapes=[
            pltpu.VMEM((2, deep, pair), bf16),
            pltpu.SemaphoreType.DMA((2,)),
        ],
        compiler_params=params(max(10, half * half // 2**14)),
        cost_estimate=cost(16 * half * half * width, 16 * half * width, 4 * half * half * heads),
        name="attend_all",
    )(*queries, *keys, *values, *places, query_place)
    return outs[:2], outs[2]


STEP = 2


def backward_kernel(*refs, count, groups, scale):
    grad_pieces = refs[:count]
    query_a, query_b, key_a, key_b, value_a, value_b, attended_a, attended_b, stored = refs[
        count : count + 9
    ]
    outs = refs[count + 9 : count + 18]
    grad_query, grad_key, grad_value = outs[0:2], outs[2:4], outs[4:6]
    own_query, own_key, own_value = outs[6:9]
    (scores,) = refs[count + 18 :]
    half, width = key_a.shape
    rows = half // count
    group_rows = rows // groups
    block = block_of(half)
    blocks = half // block
    pair = 2 * block
    reach = reaches(half, groups)[0]

    def sources(index):
        found = []
        if groups == 1:
            for d in range(index * block // rows, (index + 1) * block // rows):
                found.append((d, 0, rows))
            return found
        each = count * group_rows
        for j in range(index * block // each, (index + 1) * block // each):
            for d in range(count):
                found.append((d, j * group_rows, group_rows))
        return found

    def one_head(head, _):
        cut = columns_of(head)

        def keep(targets, own, values, index):
            for side in range(2):
                at = side * block
                targets[side][pl.ds(index * block, block), cut] = values[at : at + block]
                for d, start, size in sources(index):
                    if d == 0:
                        own[pl.ds(side * rows + start, size), cut] = values[at : at + size]
                    at += size

        def take_grads(index):
            return jnp.concatenate(
                [
                    grad_pieces[d][pl.ds(side * rows + start, size), cut]
                    for side in range(2)
                    for d, start, size in sources(index)
                ],
                axis=0,
            )

        keys_across = take(key_a, key_b, 0, blocks, cut).T
        ones = jnp.ones((8, HEAD_DIM), bf16)
        for index, (seen, _, start) in enumerate(reach):
            result = take(attended_a, attended_b, index, index + 1, cut)
            grad = take_grads(index)
            product = grad.astype(f32) * result.astype(f32)
            high = product.astype(bf16)
            low = (product - high.astype(f32)).astype(bf16)
            delta = (dot(ones, high, NT) + dot(ones, low, NT))[0:1, :]
            back = 0.0
            for low_block in range(0, seen, STEP):
                high_block = min(low_block + STEP, seen)
                at = pl.ds((start + low_block) * pair, (high_block - low_block) * pair)
                values = take(value_a, value_b, low_block, high_block, cut)
                score = stored[head, at, :].astype(f32) * (dot(values, grad, NT) - delta)
                score = score.astype(bf16)
                scores[at, :] = score
                back += dot(keys_across[:, low_block * pair : high_block * pair], score, NN)
            keep(grad_query, own_query, (back * scale).T.astype(bf16), index)
        for index in range(blocks):
            key_sum, value_sum = 0.0, 0.0
            for other, (seen, _, start) in enumerate(reach):
                if index < seen:
                    at = pl.ds((start + index) * pair, pair)
                    query = take(query_a, query_b, other, other + 1, cut)
                    key_sum += dot(scores[at, :], query, NN)
                    value_sum += dot(stored[head, at, :], take_grads(other), NN)
            keep(grad_key, own_key, (key_sum * scale).astype(bf16), index)
            keep(grad_value, own_value, value_sum.astype(bf16), index)
        return 0

    lax.fori_loop(0, width // HEAD_DIM, one_head, 0)


def attend_back(grads, queries, keys, values, attended, stored, groups):
    half, width = keys[0].shape
    count = len(grads)
    rows = grads[0].shape[0]
    outs = pl.pallas_call(
        partial(
            backward_kernel,
            count=count,
            groups=groups,
            scale=1.0 / math.sqrt(HEAD_DIM),
        ),
        in_specs=[pl.BlockSpec(memory_space=pltpu.VMEM)] * (count + 9),
        out_specs=[pl.BlockSpec(memory_space=pltpu.VMEM)] * 9,
        out_shape=[jax.ShapeDtypeStruct((half, width), bf16)] * 6
        + [jax.ShapeDtypeStruct((rows, width), bf16)] * 3,
        scratch_shapes=[pltpu.VMEM(stored.shape[1:], bf16)],
        compiler_params=params(8 + 2 * stored.shape[1] * stored.shape[2] // 2**20),
        cost_estimate=cost(8 * 4 * half * half * width, 32 * half * width + 2 * stored.size),
        name="attend_back",
    )(*grads, *queries, *keys, *values, *attended, stored)
    return outs[0:2], outs[2:4], outs[4:6], outs[6:9]


def body(
    inputs,
    first_gain,
    query_weight,
    key_weight,
    value_weight,
    output_weight,
    second_gain,
    up_weight,
    down_weight,
    frame_sizes,
    text_counts,
    action_counts,
    cotangent,
):
    shards = lax.axis_size("seq")
    shard_index = lax.axis_index("seq")
    core = lax.axis_index("mlp") % 2
    length, width = inputs.shape
    total = length * shards
    half = length // 2
    piece = half // shards
    clips = frame_sizes.shape[0]
    clip_length = total // clips
    part = width // shards
    groups = shards if piece % 8 == 0 else 1

    def halves(rows):
        cut = rows.reshape(2, piece, shards, width)
        mine = lax.dynamic_index_in_dim(cut, core, 0, keepdims=False)
        other = lax.dynamic_index_in_dim(cut, 1 - core, 0, keepdims=False)
        return (
            mine.transpose(1, 0, 2).reshape(half, width),
            other.transpose(1, 0, 2).reshape(half, width),
        )

    inputs_half, inputs_other = halves(inputs)
    pieces = gather_early(inputs_half)
    arrived = pieces[inner_size() :: inner_size()]

    place_a, place_b, kind_a, kind_b, query_place, own_place, own_kind = tables(
        frame_sizes, text_counts, action_counts, shards, length, groups
    )
    places, kinds = (place_a, place_b), (kind_a, kind_b)
    half_kind = own_kind[:half]
    own_normed = own_norm(
        jnp.concatenate([inputs_half, inputs_other], axis=0), first_gain, own_kind
    )
    grad_half, grad_other = halves(cotangent)
    grad_own = jnp.concatenate([grad_half, grad_other], axis=0)
    (query_own,) = project_rows(after(own_normed, arrived), query_weight)
    grad_far = gather_outer(after(grad_half, arrived, pieces[inner_size() + 1]))
    pieces = after(pieces, query_own)

    normed = [norm_pieces(pieces, first_gain, kind_a, groups)]
    normed[0], grad_far = after((normed[0], grad_far), normed[0])
    normed.append(swap(normed[0], "mlp", 1))
    keys, values = zip(*[project_rows(rows, key_weight, value_weight) for rows in normed])
    heads_own = attend(query_own, keys, values, places, own_place, clip_length, clips)
    grad_inner = gather_inner(after(grad_half, normed[0]))
    heads_own, grad_inner = after((heads_own, grad_inner), heads_own)
    grad_far = join_x(jnp.concatenate(grad_far, axis=0), heads_own)
    mine, other = product_halves([heads_own], [output_weight], NN)
    other, grad_far = after((other, grad_far), other)
    grad_inner += gather_inner(grad_far)
    low, other = pair_mlp(mine, other)
    own_activated_grad = grad_activated(after(grad_own, low), down_weight)
    queries = [
        project_rows(rows, query_weight)[0] for rows in after(normed, own_activated_grad)
    ]
    other = after(other, queries)
    residual, lifted_half = lift(inputs_half, low, other, second_gain, half_kind)

    lifted_own = both(lifted_half)
    activated_own, hidden_own, mine, other = feed_own(lifted_own, up_weight, own_activated_grad)
    lifted_far = gather_outer(after(lifted_half, other))
    other, grad_inner = after((other, grad_inner), other)
    low, other = pair_mlp(mine, other)
    attended, stored = attend_all(
        after(queries, low),
        keys,
        values,
        places,
        query_place,
        groups,
        clip_length,
        clips,
    )
    other, lifted_far = after((other, lifted_far), attended)
    grad_residual, mixed_half, mixed_columns = middle(
        residual, low, other, grad_half, second_gain, half_kind, shards
    )
    heads_grad = product_back(both(mixed_half), output_weight)

    heads_first = gather_first(heads_grad)
    lifted_far = jnp.concatenate(lifted_far, axis=0)
    lifted_inner_far = gather_inner(lifted_far)
    down_mine, down_other = down_own(after(activated_own, heads_grad), down_weight)
    lifted_far = join_x(lifted_far, heads_first[1], down_other, lifted_inner_far)
    heads_grads = gather_pieces(*heads_first)
    first_lifted, first_grads = with_core([lifted_far]), with_core([grad_far])
    first_lifted = after(first_lifted, heads_grads[inner_size() + 1])
    own = (lifted_own, grad_own, activated_own, hidden_own)
    sums = feed_all(first_lifted, first_grads, up_weight, down_weight, shards, own=own)
    down_low, down_other = pair_mlp(down_mine, down_other)
    heads_grads, down_low, down_other = after((heads_grads, down_low, down_other), sums)
    inner = inner_size()
    columns_far = {
        outer: swap(after(mixed_columns[outer : outer + inner], sums), "seq", outer)
        for outer in range(inner, shards, inner)
    }
    lifted_inner = gather_inner(after(lifted_half, down_other))
    query_low, key_low, value_low, own_low = attend_back(
        heads_grads, queries, keys, values, attended, stored, groups
    )
    attention_weights = (query_weight, key_weight, value_weight)
    lifted_inner += [join_x(far, own_low) for far in lifted_inner_far]
    own_low, lifted_inner, columns_far = after((own_low, lifted_inner, columns_far), own_low)
    low, other = pair_mlp(*product_halves(own_low, attention_weights, NT))

    query_grad, key_grad, value_grad, first_gain_grad = project(
        normed,
        after((query_low, key_low, value_low), low),
        attention_weights,
        first_gain,
        kinds,
        shards,
    )
    columns_far = after(columns_far, low)
    columns_far[0] = mixed_columns[:inner]
    columns = {}
    for outer, came in columns_far.items():
        columns[outer] = came[0]
        for bit in range(1, inner):
            columns[outer | bit] = swap(came[bit], "seq", bit)
    first_gain_grad = first_gain_grad + swap(first_gain_grad, "mlp", 1)
    other, first_gain_grad, columns = after((other, first_gain_grad, columns), query_grad)
    input_half = last(inputs_half, low, other, grad_residual, first_gain, half_kind, shards)
    outputs_half = finish(residual, down_low, after(down_other, input_half), shards)
    rest_lifted = with_core(after(lifted_inner, other))
    rest_grads = with_core(after(grad_inner, other))
    up_grad, down_grad = feed_all(
        after(rest_lifted, outputs_half), rest_grads, up_weight, down_weight, shards, sums
    )
    bit = 2
    while bit < lax.axis_size("mlp"):
        came = after(swap(first_gain_grad, "mlp", bit), up_grad)
        first_gain_grad = first_gain_grad + came
        bit *= 2
    placed = (input_half, outputs_half)
    input_grad, outputs = place_halves(placed, [swap(array, "mlp", 1) for array in placed])
    mixed_part = jnp.stack([after(columns[d], up_grad) for d in range(shards)])
    output_grad, second_gain_grad = output_part(
        attended, (mixed_part, swap(mixed_part, "mlp", 1)), groups
    )

    return (
        outputs,
        input_grad,
        first_gain_grad,
        query_grad,
        key_grad,
        value_grad,
        output_grad,
        second_gain_grad,
        up_grad,
        down_grad,
    )


def solution(mesh):
    return jax.shard_map(
        body,
        mesh=mesh,
        in_specs=(
            P("seq", None),
            P(),
            P(None, "mlp"),
            P(None, "mlp"),
            P(None, "mlp"),
            P("mlp", None),
            P(),
            P(None, "mlp"),
            P("mlp", None),
            P(),
            P(),
            P(),
            P("seq", None),
        ),
        out_specs=(
            P("seq", None),
            P("seq", None),
            P(None, "seq"),
            P("seq", "mlp"),
            P("seq", "mlp"),
            P("seq", "mlp"),
            P("mlp", "seq"),
            P(None, "seq"),
            P("seq", "mlp"),
            P("mlp", "seq"),
        ),
        check_vma=False,
    )
```

```python
from functools import partial
import math

import jax
import jax.numpy as jnp
from jax import lax
from jax.experimental import pallas as pl
from jax.experimental.pallas import tpu as pltpu
from jax.sharding import PartitionSpec as P

HEAD_DIM = 128
epsilon = 1e-05
bf16 = jnp.bfloat16
f32 = jnp.float32
NEGATIVE = -1e30

WHOLE = pl.BlockSpec(memory_space=pltpu.VMEM)
NN = ((1,), (0,))
NT = ((1,), (1,))
TN = ((0,), (0,))


def dot(a, b, dims):
    return lax.dot_general(a, b, (dims, ((), ())), preferred_element_type=f32)


def params(mebibytes):
    return pltpu.CompilerParams(vmem_limit_bytes=mebibytes * 1024 * 1024)


def cost(flops, moved, transcendentals=0, share=100):
    return pl.CostEstimate(
        flops=int(flops) // share,
        bytes_accessed=int(moved) // share,
        transcendentals=int(transcendentals) // share,
    )


def swap(value, axis, bit):
    size = lax.axis_size(axis)
    return lax.ppermute(value, axis, [(i, i ^ bit) for i in range(size)])


def inner_size():
    return 1 << (int(math.log2(lax.axis_size("seq"))) // 2)


def x_size():
    return lax.axis_size("mlp") // 2


def after(values, *earlier):
    return lax.optimization_barrier((values, earlier))[0]


def in_hbm(array):
    return pltpu.with_memory_space_constraint(array, pltpu.HBM)


def own_quarter(half):
    rows = half.shape[0] // x_size()
    return lax.dynamic_slice_in_dim(half, (lax.axis_index("mlp") // 2) * rows, rows, 0)


def join_x(quarter, *earlier):
    bit = 1
    while bit < x_size():
        came = after(swap(quarter, "mlp", 2 * bit), earlier)
        quarter = jnp.concatenate([quarter, came], axis=0)
        bit *= 2
    return quarter


def gather_early(half):
    size, inner = lax.axis_size("seq"), inner_size()
    quarter = own_quarter(half)
    pieces = {0: half}
    far = {outer: swap(quarter, "seq", outer) for outer in range(inner, size, inner)}
    for bit in range(1, inner):
        pieces[bit] = swap(half, "seq", bit)
    for outer in range(inner, size, inner):
        pieces[outer] = join_x(far[outer])
        for bit in range(1, inner):
            pieces[outer | bit] = swap(pieces[outer], "seq", bit)
    return [pieces[d] for d in range(size)]


def gather_outer(half):
    size, inner = lax.axis_size("seq"), inner_size()
    quarter = own_quarter(half)
    return [swap(quarter, "seq", outer) for outer in range(inner, size, inner)]


def gather_inner(array):
    return [swap(array, "seq", bit) for bit in range(1, inner_size())]


def with_core(arrays):
    return [each for array in arrays for each in (array, swap(array, "mlp", 1))]


def gather_first(piece):
    size, inner = lax.axis_size("seq"), inner_size()
    pieces = {0: piece}
    for bit in range(1, inner):
        pieces[bit] = swap(piece, "seq", bit)
    return pieces, [swap(piece, "seq", outer) for outer in range(inner, size, inner)]


def gather_pieces(pieces, far):
    size, inner = lax.axis_size("seq"), inner_size()
    for outer, came in zip(range(inner, size, inner), far):
        pieces[outer] = came
        for bit in range(1, inner):
            pieces[outer | bit] = swap(came, "seq", bit)
    return [pieces[d] for d in range(size)]


def rounded(value):
    return lax.optimization_barrier(value.astype(bf16))


def pair_mlp(mine, other_half):
    low, other = rounded(mine + swap(other_half, "mlp", 1).astype(f32)), None
    bit = 2
    while bit < lax.axis_size("mlp"):
        if other is not None:
            low = rounded(low.astype(f32) + other.astype(f32))
        other = swap(low, "mlp", bit)
        bit *= 2
    if other is None:
        other = jnp.zeros_like(low)
    return low, other


def both(half):
    return jnp.concatenate([half, swap(half, "mlp", 1)], axis=0)


def tables_kernel(index, frames, texts, actions, *outs, shards, length, groups, clip_length):
    place_a, place_b, kind_a, kind_b, query_place, own_place, own_kind = outs
    shard_index, core = index[0], index[1]
    shape = (shards, length)
    place = lax.broadcasted_iota(jnp.int32, shape, 0) * length + lax.broadcasted_iota(
        jnp.int32, shape, 1
    )
    kinds = jnp.full(shape, 2, jnp.int32)
    for clip in range(frames.shape[0]):
        start = jnp.int32(clip * clip_length)
        within = (place >= clip * clip_length) & (place < (clip + 1) * clip_length)
        for frame in range(frames.shape[1]):
            text_end = start + texts[clip, frame]
            action_end = text_end + actions[clip, frame]
            kinds = jnp.where(within & (place >= start) & (place < text_end), 0, kinds)
            kinds = jnp.where(within & (place >= text_end) & (place < action_end), 1, kinds)
            start = action_end + frames[clip, frame]
    square = (length, length)
    down = lax.broadcasted_iota(jnp.int32, square, 0)
    across = lax.broadcasted_iota(jnp.int32, square, 1)
    earlier = (down < across).astype(f32).astype(bf16)
    rank = jnp.zeros(shape, f32)
    before = jnp.zeros((shards, 1), f32)
    for kind in range(3):
        chosen = (kinds == kind).astype(f32)
        rank += chosen * (dot(chosen.astype(bf16), earlier, NN) + before)
        before += chosen.sum(axis=1, keepdims=True)
    rank_low, kinds_low = rank.astype(bf16), kinds.astype(f32).astype(bf16)
    piece = length // shards // 2
    lane = lax.broadcasted_iota(jnp.int32, (1, length), 1).astype(f32)

    def find(shard, offset, side, row):
        wanted = (shard_index ^ offset) * (2 * piece) + (core ^ side) * piece + row
        pick = shard == lax.broadcasted_iota(jnp.int32, (length, shards), 1)
        pick = pick.astype(f32).astype(bf16)
        hit = dot(pick, rank_low, NN) == wanted.astype(f32)
        where = jnp.sum(jnp.where(hit, lane, 0.0), axis=1, keepdims=True).astype(jnp.int32)
        kind = jnp.sum(jnp.where(hit, dot(pick, kinds_low, NN), 0.0), axis=1, keepdims=True)
        return where + shard * length, kind.astype(jnp.int32)

    def as_row(column):
        return jnp.sum(jnp.where(down == across, column, 0), axis=0, keepdims=True)

    step = lax.broadcasted_iota(jnp.int32, (length, 1), 0)
    half = length // 2
    for side, (place_out, kind_out) in enumerate(((place_a, kind_a), (place_b, kind_b))):
        for block in range(shards // 2):
            token = step + block * length
            if groups > 1:
                shard, offset = token // (shards * piece), (token // piece) % shards
            else:
                offset, shard = token // half, (token % half) // piece
            where, kind = find(shard, offset, side, token % piece)
            at = pl.ds(block * length, length)
            place_out[at, :] = where
            kind_out[at, :] = kind
            query_place[:, pl.ds((2 * block + side) * length, length)] = as_row(where)
    where, kind = find((step % half) // piece, step * 0, step // half, step % piece)
    own_place[...] = as_row(where)
    own_kind[...] = kind


def tables(frames, texts, actions, shards, length, groups):
    index = jnp.stack([lax.axis_index("seq"), lax.axis_index("mlp") % 2]).astype(jnp.int32)
    total = shards * length
    column = jax.ShapeDtypeStruct((total // 2, 1), jnp.int32)
    return pl.pallas_call(
        partial(
            tables_kernel,
            shards=shards,
            length=length,
            groups=groups,
            clip_length=total // frames.shape[0],
        ),
        in_specs=[pl.BlockSpec(memory_space=pltpu.SMEM)] * 4,
        out_shape=[column] * 4
        + [
            jax.ShapeDtypeStruct((1, total), jnp.int32),
            jax.ShapeDtypeStruct((1, length), jnp.int32),
            jax.ShapeDtypeStruct((length, 1), jnp.int32),
        ],
        cost_estimate=cost(8 * total * length, 8 * 128 * total),
        name="tables",
    )(index, frames, texts, actions)


def rows_kernel(*refs, count):
    rows, weights, outs = refs[0], refs[1 : 1 + count], refs[1 + count :]
    for weight, out in zip(weights, outs):
        out[...] = dot(rows[...], weight[...], NN).astype(bf16)


def project_rows(rows, *weights):
    across = weights[0].shape[1]
    return pl.pallas_call(
        partial(rows_kernel, count=len(weights)),
        out_shape=[jax.ShapeDtypeStruct((rows.shape[0], across), bf16)] * len(weights),
        compiler_params=params(8),
        cost_estimate=cost(2 * rows.size * across * len(weights), 2 * rows.size),
        name="project_rows",
    )(rows, *weights)


def one_kernel(rows, weight, out):
    out[...] = dot(rows[...], weight[...], NT).astype(bf16)


def product_back(rows, weight):
    return pl.pallas_call(
        one_kernel,
        out_shape=jax.ShapeDtypeStruct((rows.shape[0], weight.shape[0]), bf16),
        compiler_params=params(6),
        cost_estimate=cost(2 * rows.size * weight.shape[0], 2 * weight.size),
        name="product_back",
    )(rows, weight)


def halves_kernel(*refs, count, dims):
    mine, other = refs[-2:]
    half = mine.shape[0]
    total = sum(dot(refs[k][...], refs[count + k][...], dims) for k in range(count))
    mine[...] = total[:half]
    other[...] = total[half:].astype(bf16)


def product_halves(rows, weights, dims):
    count = len(rows)
    half = rows[0].shape[0] // 2
    across = weights[0].shape[1 - dims[1][0]]
    shape = (half, across)
    return pl.pallas_call(
        partial(halves_kernel, count=count, dims=dims),
        out_shape=[jax.ShapeDtypeStruct(shape, f32), jax.ShapeDtypeStruct(shape, bf16)],
        compiler_params=params(6),
        cost_estimate=cost(2 * count * rows[0].size * across, 2 * count * weights[0].size),
        name="product_halves",
    )(*rows, *weights)


def down_own_kernel(rows, weight, mine, other, total):
    total[...] = jnp.zeros_like(total)

    def step(at):
        total[...] += dot(rows[:, at], weight[at, :], NN)

    tiles_of(weight.shape[0], math.gcd(weight.shape[0], 512), step)
    half = mine.shape[0]
    mine[...] = total[:half]
    other[...] = total[half:].astype(bf16)


def down_own(rows, weight):
    count, deep = rows.shape
    across = weight.shape[1]
    shape = (count // 2, across)
    return pl.pallas_call(
        down_own_kernel,
        in_specs=[WHOLE] * 2,
        out_specs=[WHOLE] * 2,
        out_shape=[jax.ShapeDtypeStruct(shape, f32), jax.ShapeDtypeStruct(shape, bf16)],
        scratch_shapes=[pltpu.VMEM((count, across), f32)],
        compiler_params=params(6),
        cost_estimate=cost(2 * rows.size * across, 2 * weight.size),
        name="down_own",
    )(rows, weight)


def gain_rows(gain, column):
    return jnp.where(
        column == 0, gain[0:1, :], jnp.where(column == 1, gain[1:2, :], gain[2:3, :])
    )


def normalize(values):
    mean = jnp.mean(values, axis=1, keepdims=True)
    centered = values - mean
    inverse = lax.rsqrt(jnp.mean(centered * centered, axis=1, keepdims=True) + epsilon)
    return (centered * inverse, inverse)


def norm_back(grad, normal, inverse, gains):
    scaled = grad * gains
    return inverse * (
        scaled
        - jnp.mean(scaled, axis=1, keepdims=True)
        - normal * jnp.mean(scaled * normal, axis=1, keepdims=True)
    )


def norm_kernel(*refs, groups, inner, parts):
    index, gain, kind, out = refs[0], refs[-3], refs[-2], refs[-1]
    pieces = refs[1:-3]
    rows, width = pieces[0].shape
    count = len(pieces)
    step = rows // parts
    for d, piece in enumerate(pieces):
        for part in range(parts):
            normal, _ = normalize(piece[pl.ds(part * step, step), :].astype(f32))
            place = part if d < inner else part ^ index[0]
            if groups > 1:
                each = groups // parts
                at = pl.ds(place * each, each)
                column = kind[at, d].reshape(step, 1)
                normed = (normal * gain_rows(gain, column)).astype(bf16)
                out[at, d] = normed.reshape(each, rows // groups, width)
            else:
                column = kind[d, place]
                out[d, place] = (normal * gain_rows(gain, column)).astype(bf16)


def norm_pieces(pieces, gain, kind, groups):
    rows, width = pieces[0].shape
    count = len(pieces)
    parts = x_size()
    if groups > 1:
        shape = (groups, count, rows // groups)
    else:
        shape = (count, parts, rows // parts)
    memory = [pl.BlockSpec(memory_space=pltpu.SMEM)]
    index = (lax.axis_index("mlp") // 2).astype(jnp.int32).reshape(1)
    out = pl.pallas_call(
        partial(norm_kernel, groups=groups, inner=inner_size(), parts=parts),
        in_specs=memory + [pl.BlockSpec(memory_space=pltpu.VMEM)] * (count + 2),
        out_shape=jax.ShapeDtypeStruct(shape + (width,), bf16),
        compiler_params=params(4 + count),
        cost_estimate=cost(10 * count * rows * width, 4 * count * rows * width),
        name="norm_pieces",
    )(index, *pieces, gain, kind.reshape(shape + (1,)))
    return out.reshape(count * rows, width)


def own_norm_kernel(rows, gain, kind, out):
    normal, _ = normalize(rows[...].astype(f32))
    out[...] = (normal * gain_rows(gain, kind[...])).astype(bf16)


def own_norm(rows, gain, kind):
    return pl.pallas_call(
        own_norm_kernel,
        out_shape=jax.ShapeDtypeStruct(rows.shape, bf16),
        compiler_params=params(4),
        cost_estimate=cost(10 * rows.size, 4 * rows.size),
        name="own_norm",
    )(rows, gain, kind)


def lift_kernel(rows, low, other, gain, kind, residual, lifted):
    value = rows[...].astype(f32) + (low[...].astype(f32) + other[...].astype(f32))
    residual[...] = value
    normal, _ = normalize(value)
    lifted[...] = (normal * gain_rows(gain, kind[...])).astype(bf16)


def lift(rows, low, other, gain, kind):
    return pl.pallas_call(
        lift_kernel,
        in_specs=[WHOLE] * 5,
        out_specs=[WHOLE] * 2,
        out_shape=[jax.ShapeDtypeStruct(rows.shape, f32), jax.ShapeDtypeStruct(rows.shape, bf16)],
        compiler_params=params(4),
        cost_estimate=cost(10 * rows.size, 12 * rows.size),
        name="lift",
    )(rows, low, other, gain, kind)


def kind_sums(term, kind):
    sums = [jnp.sum(jnp.where(kind == k, term, 0.0), axis=0, keepdims=True) for k in range(3)]
    high = [value.astype(bf16) for value in sums]
    low = [(value - part.astype(f32)).astype(bf16) for value, part in zip(sums, high)]
    zero = jnp.zeros((1, term.shape[1]), bf16)
    return jnp.concatenate(high + low + [zero, zero], axis=0)


def middle_kernel(index, residual, low, other, grad, gain, kind, grad_residual, mixed, parts):
    lifted_grad = low[...].astype(f32) + other[...].astype(f32)
    normal, inverse = normalize(residual[...])
    column = kind[...]
    back = norm_back(lifted_grad, normal, inverse, gain_rows(gain, column))
    value = grad[...].astype(f32) + back
    grad_residual[...] = value
    rounded_value = value.astype(bf16)
    mixed[...] = rounded_value
    sums = kind_sums(lifted_grad * normal, column)
    shards, rows, part = parts.shape
    for k in range(shards):
        at = index[0] ^ k
        parts[at, pl.ds(0, rows - 8), :] = rounded_value[:, k * part : (k + 1) * part]
        parts[at, pl.ds(rows - 8, 8), :] = sums[:, k * part : (k + 1) * part]


def middle(residual, low, other, grad, gain, kind, shards):
    rows, width = residual.shape
    index = lax.axis_index("seq").astype(jnp.int32).reshape(1)
    return pl.pallas_call(
        middle_kernel,
        in_specs=[pl.BlockSpec(memory_space=pltpu.SMEM)] + [WHOLE] * 6,
        out_specs=[WHOLE] * 3,
        out_shape=[
            jax.ShapeDtypeStruct(residual.shape, f32),
            jax.ShapeDtypeStruct(residual.shape, bf16),
            jax.ShapeDtypeStruct((shards, rows + 8, width // shards), bf16),
        ],
        compiler_params=params(6),
        cost_estimate=cost(20 * residual.size, 16 * residual.size),
        name="middle",
    )(index, residual, low, other, grad, gain, kind)


def reordered(values, shards):
    count = values.shape[0]
    piece = count // shards
    to = lax.broadcasted_iota(jnp.int32, (count, count), 0)
    source = lax.broadcasted_iota(jnp.int32, (count, count), 1)
    pick = (source == (to % shards) * piece + to // shards).astype(f32).astype(bf16)
    return dot(pick, values, NN).astype(bf16)


def finish_kernel(residual, low, other, out, *, shards):
    value = residual[...] + (low[...].astype(f32) + other[...].astype(f32))
    out[...] = reordered(value.astype(bf16), shards)


def finish(residual, low, other, shards):
    return pl.pallas_call(
        partial(finish_kernel, shards=shards),
        in_specs=[WHOLE] * 3,
        out_specs=WHOLE,
        out_shape=jax.ShapeDtypeStruct(residual.shape, bf16),
        compiler_params=params(4),
        cost_estimate=cost(2 * residual.size, 10 * residual.size),
        name="finish",
    )(residual, low, other)


def place_kernel(index, *refs):
    count = len(refs) // 3
    for mine, other, out in zip(refs[:count], refs[count : 2 * count], refs[2 * count :]):
        half = mine.shape[0]
        out[pl.ds(pl.multiple_of(index[0] * half, half), half), :] = mine[...]
        out[pl.ds(pl.multiple_of((1 - index[0]) * half, half), half), :] = other[...]


def place_halves(arrays, others):
    half, width = arrays[0].shape
    index = (lax.axis_index("mlp") % 2).astype(jnp.int32).reshape(1)
    return pl.pallas_call(
        place_kernel,
        in_specs=[pl.BlockSpec(memory_space=pltpu.SMEM)] + [WHOLE] * (2 * len(arrays)),
        out_shape=[jax.ShapeDtypeStruct((2 * half, width), bf16)] * len(arrays),
        compiler_params=params(6),
        cost_estimate=cost(half * width, 16 * half * width),
        name="place_halves",
    )(index, *arrays, *others)


def last_kernel(rows, low, other, grad_residual, gain, kind, out, *, shards):
    grad = low[...].astype(f32) + other[...].astype(f32)
    normal, inverse = normalize(rows[...].astype(f32))
    back = norm_back(grad, normal, inverse, gain_rows(gain, kind[...]))
    out[...] = reordered((grad_residual[...] + back).astype(bf16), shards)


def last(rows, low, other, grad_residual, gain, kind, shards):
    return pl.pallas_call(
        partial(last_kernel, shards=shards),
        in_specs=[WHOLE] * 6,
        out_specs=WHOLE,
        out_shape=jax.ShapeDtypeStruct(rows.shape, bf16),
        compiler_params=params(6),
        cost_estimate=cost(20 * rows.size, 12 * rows.size),
        name="last",
    )(rows, low, other, grad_residual, gain, kind)


def gelu_parts(value):
    rate = math.sqrt(2 / math.pi)
    square = value * value
    bent = jnp.tanh(value * (rate + (rate * 0.044715) * square))
    upper = 0.5 * (1 + bent)
    slope = upper + (0.5 * value) * (1 - bent * bent) * (rate + (rate * 3 * 0.044715) * square)
    return value * upper, slope


def tiles_of(extent, tile, step):
    def at(t, _):
        step(pl.ds(pl.multiple_of(t * tile, tile), tile))
        return 0

    lax.fori_loop(0, extent // tile, at, 0)


def own_kernel(lifted, up, grad_activated, activated, hidden_grads, mine, other, total):
    total[...] = jnp.zeros_like(total)

    def step(at):
        value, slope = gelu_parts(dot(lifted[...], up[:, at], NN))
        activated[:, at] = value.astype(bf16)
        hidden_grad = (grad_activated[:, at] * slope).astype(bf16)
        hidden_grads[:, at] = hidden_grad
        total[...] += dot(hidden_grad, up[:, at], NT)

    tiles_of(up.shape[1], math.gcd(up.shape[1], 512), step)
    half = mine.shape[0]
    mine[...] = total[:half]
    other[...] = total[half:].astype(bf16)


def feed_own(lifted, up, grad_activated):
    rows, width = lifted.shape
    hidden = up.shape[1]
    return pl.pallas_call(
        own_kernel,
        in_specs=[WHOLE] * 3,
        out_specs=[WHOLE] * 4,
        out_shape=[jax.ShapeDtypeStruct((rows, hidden), bf16)] * 2
        + [
            jax.ShapeDtypeStruct((rows // 2, width), f32),
            jax.ShapeDtypeStruct((rows // 2, width), bf16),
        ],
        scratch_shapes=[pltpu.VMEM((rows, width), f32)],
        compiler_params=params(8),
        cost_estimate=cost(4 * rows * width * hidden, 2 * width * hidden),
        name="feed_own",
    )(lifted, up, grad_activated)


def down_kernel(grad, down, out):
    def step(at):
        out[:, at] = dot(grad[...], down[at, :], NT)

    tiles_of(down.shape[0], math.gcd(down.shape[0], 512), step)


def grad_activated(grad, down):
    rows, width = grad.shape
    hidden = down.shape[0]
    return pl.pallas_call(
        down_kernel,
        in_specs=[WHOLE] * 2,
        out_specs=WHOLE,
        out_shape=jax.ShapeDtypeStruct((rows, hidden), f32),
        compiler_params=params(6),
        cost_estimate=cost(2 * rows * width * hidden, 2 * width * hidden),
        name="grad_activated",
    )(grad, down)


def all_kernel(index, *refs, count):
    lifted_parts, grad_parts = refs[:count], refs[count : 2 * count]
    up, down = refs[2 * count : 2 * count + 2]
    before = refs[2 * count + 2 : -5]
    up_grad, down_grad, lifted_across, hidden_kept, grad_kept = refs[-5:]
    part = up_grad.shape[0]
    mine = pl.ds(pl.multiple_of(index[0] * part, part), part)

    def rows_of(parts, at):
        return jnp.concatenate([ref[:, at] for ref in parts], axis=0)

    @pl.when(pl.program_id(0) == 0)
    def _():
        lifted_across[...] = rows_of(lifted_parts, mine).T

    first = pl.program_id(0) == 0
    last_step = pl.num_programs(0) - 1

    tile = hidden_kept.shape[1]
    at = jnp.minimum(pl.program_id(0), last_step - 1) if up.shape[1] > tile else 0
    here = pl.ds(pl.multiple_of(at * tile, tile), tile)

    def products():
        everything = slice(None)
        return (
            dot(rows_of(lifted_parts, everything), up[:, here], NN),
            dot(rows_of(grad_parts, everything), down[here, :], NT),
        )

    def finish_tile(hidden_value, activated_grad):
        value, slope = gelu_parts(hidden_value)
        hidden_grad = (activated_grad * slope).astype(bf16)
        down_term = dot(value.astype(bf16), rows_of(grad_parts, mine), TN)
        up_term = dot(lifted_across[...], hidden_grad, NN)
        if len(before) == 2:
            up_term += before[0][...].astype(f32)
            down_term += before[1][...].astype(f32)
        else:
            lifted_own, grad_own, activated, hidden_own = before
            up_term += dot(lifted_own[...], hidden_own[...], TN)
            down_term += dot(activated[...], grad_own[...], TN)
        up_grad[...] = up_term.astype(up_grad.dtype)
        down_grad[...] = down_term.astype(down_grad.dtype)

    @pl.when(first)
    def _():
        hidden_kept[...], grad_kept[...] = products()

    @pl.when((pl.program_id(0) > 0) & (pl.program_id(0) < last_step))
    def _():
        kept = hidden_kept[...], grad_kept[...]
        fresh = products()
        finish_tile(*kept)
        hidden_kept[...], grad_kept[...] = fresh

    @pl.when(pl.program_id(0) == last_step)
    def _():
        finish_tile(hidden_kept[...], grad_kept[...])


def feed_all(lifted, grad, up, down, shards, sums=(), own=()):
    counts = [array.shape[0] for array in lifted]
    rows, width = sum(counts), lifted[0].shape[1]
    count = len(counts)
    part = width // shards
    hidden = up.shape[1]
    tile = math.gcd(hidden, 256)
    steps = hidden // tile
    across = lambda t, index: (0, jnp.maximum(t - 1, 0))
    below = lambda t, index: (jnp.maximum(t - 1, 0), 0)
    mine = lambda t, index: (0, index[0])
    sum_specs = [pl.BlockSpec((part, tile), across), pl.BlockSpec((tile, part), below)]
    if own:
        own_rows = own[0].shape[0]
        more = [pl.BlockSpec((own_rows, part), mine)] * 2
        more += [pl.BlockSpec((own_rows, tile), across)] * 2
    else:
        more = sum_specs
    index = lax.axis_index("seq").astype(jnp.int32).reshape(1)
    return pl.pallas_call(
        partial(all_kernel, count=count),
        grid_spec=pltpu.PrefetchScalarGridSpec(
            num_scalar_prefetch=1,
            grid=(steps + 1,),
            in_specs=[WHOLE] * (2 * count)
            + [WHOLE] * 2
            + more,
            out_specs=sum_specs,
            scratch_shapes=[pltpu.VMEM((part, rows), bf16)]
            + [pltpu.VMEM((rows, tile), f32)] * 2,
        ),
        out_shape=[
            pltpu.HBM((part, hidden), bf16 if own else f32),
            pltpu.HBM((hidden, part), bf16 if own else f32),
        ],
        compiler_params=params((6 if own else 8) + 8 * rows // 512),
        cost_estimate=cost(
            4 * rows * hidden * (width + part),
            4 * width * hidden + 4 * rows * width,
        ),
        name="feed_all",
    )(
        index,
        *lifted,
        *grad,
        up,
        down,
        *(own or [in_hbm(array) for array in sums]),
    )


def project_kernel(index, *refs):
    normed, lows, weights = refs[0:2], refs[2:8], refs[8:11]
    gain, kinds = refs[11], refs[12:14]
    outs, gain_grad = refs[14:17], refs[17]
    for k in range(3):
        outs[k][...] = sum(dot(normed[side][...], lows[2 * k + side][...], TN) for side in range(2))
    gain_sum = [0.0, 0.0, 0.0]
    for side in range(2):
        column = kinds[side][...]
        term = sum(dot(lows[2 * k + side][...], weights[k][...], NT) for k in range(3))
        term = term * (normed[side][...].astype(f32) / gain_rows(gain, column))
        for k in range(3):
            gain_sum[k] += jnp.sum(jnp.where(column == k, term, 0.0), axis=0, keepdims=True)
    gain_grad[...] = jnp.concatenate(gain_sum, axis=0)


def project(normed, lows, weights, gain, kinds, shards):
    rows, width = normed[0].shape
    across = lows[0][0].shape[1]
    part = width // shards
    whole = lambda t, index: (0, 0)
    mine = lambda t, index: (0, index[0])
    below = lambda t, index: (index[0], 0)
    index = lax.axis_index("seq").astype(jnp.int32).reshape(1)
    return pl.pallas_call(
        project_kernel,
        grid_spec=pltpu.PrefetchScalarGridSpec(
            num_scalar_prefetch=1,
            grid=(1,),
            in_specs=[pl.BlockSpec((rows, part), mine)] * 2
            + [pl.BlockSpec((rows, across), whole)] * 6
            + [pl.BlockSpec((part, across), below)] * 3
            + [pl.BlockSpec((gain.shape[0], part), mine)]
            + [pl.BlockSpec((rows, 1), whole)] * 2,
            out_specs=[pl.BlockSpec((part, across), whole)] * 3
            + [pl.BlockSpec((gain.shape[0], part), whole)],
        ),
        out_shape=[jax.ShapeDtypeStruct((part, across), f32)] * 3
        + [jax.ShapeDtypeStruct((gain.shape[0], part), f32)],
        compiler_params=params(8),
        cost_estimate=cost(24 * rows * part * across, 12 * rows * across + 12 * part * across),
        name="project",
    )(index, *normed, *[low for pair in lows for low in pair], *weights, gain, *kinds)


def output_kernel(attended_a, attended_b, came_a, came_b, out, gain_grad, *, groups):
    total, sums = 0.0, 0.0
    shards, rows, part = came_a.shape
    half = rows - 8
    each = half // groups
    for attended, came in ((attended_a, came_a), (attended_b, came_b)):
        mixed = [
            came[d, pl.ds(group * each, each), :]
            for group in range(groups)
            for d in range(shards)
        ]
        total += dot(attended[...], jnp.concatenate(mixed, axis=0), TN)
        own_sums = 0.0
        for k in range(shards):
            own_sums += came[k, pl.ds(half, 8), :].astype(f32)
        sums += own_sums
    out[...] = total
    gain_grad[...] = sums[0:3, :] + sums[3:6, :]


def output_part(attended, came, groups):
    across, part = attended[0].shape[1], came[0].shape[2]
    return pl.pallas_call(
        partial(output_kernel, groups=groups),
        in_specs=[WHOLE] * 4,
        out_shape=[
            jax.ShapeDtypeStruct((across, part), f32),
            jax.ShapeDtypeStruct((3, part), f32),
        ],
        compiler_params=params(6),
        cost_estimate=cost(
            4 * attended[0].shape[0] * across * part, 4 * attended[0].shape[0] * (across + part)
        ),
        name="output_part",
    )(*attended, *came)


def mask_of(key_place, query_place, clip_length, clips):
    allowed = key_place <= query_place
    if clips > 1:
        allowed = allowed & (key_place // clip_length == query_place // clip_length)
    return allowed


def probabilities(scores, scale):
    top = scores[0].max(axis=0, keepdims=True)
    for block in scores[1:]:
        top = jnp.maximum(top, block.max(axis=0, keepdims=True))
    rate = scale * math.log2(math.e)
    weights = [jnp.exp2((block - top) * rate) for block in scores]
    total = weights[0].sum(axis=0, keepdims=True)
    for block in weights[1:]:
        total = total + block.sum(axis=0, keepdims=True)
    inverse = 1.0 / total
    return [block * inverse for block in weights]


def forward_kernel(query, key_a, key_b, value_a, value_b, place_a, place_b, query_place, out, **opts):
    scale = opts["scale"]
    query_place = query_place[...]
    allowed = [
        mask_of(place[...], query_place, opts["clip_length"], opts["clips"])
        for place in (place_a, place_b)
    ]
    for head in range(query.shape[1] // HEAD_DIM):
        at = pl.ds(head * HEAD_DIM, HEAD_DIM)
        scores = [
            jnp.where(mask, dot(key[:, at], query[:, at], NT), NEGATIVE)
            for mask, key in zip(allowed, (key_a, key_b))
        ]
        prob = [block.astype(bf16) for block in probabilities(scores, scale)]
        result = dot(value_a[:, at], prob[0], TN) + dot(value_b[:, at], prob[1], TN)
        out[:, at] = result.T.astype(bf16)


def attend(query, keys, values, places, query_place, clip_length, clips):
    rows, width = query.shape
    total = 2 * keys[0].shape[0]
    return pl.pallas_call(
        partial(
            forward_kernel, scale=1.0 / math.sqrt(HEAD_DIM), clip_length=clip_length, clips=clips
        ),
        out_shape=jax.ShapeDtypeStruct((rows, width), bf16),
        compiler_params=params(8),
        cost_estimate=cost(
            4 * rows * total * width, 4 * total * width, rows * total * (width // HEAD_DIM)
        ),
        name="attend",
    )(query, *keys, *values, *places, query_place)


def block_of(half):
    return min(128, half)


def reaches(half, groups):
    blocks = half // block_of(half)
    found, start = [], 0
    for index in range(blocks):
        seen, free = (index + 1, index) if groups > 1 else (blocks, 0)
        found.append((seen, free, start))
        start += seen
    return found, start


def take(first, second, low, high, at):
    block = block_of(first.shape[0])
    rows = [side[pl.ds(k * block, block), at] for k in range(low, high) for side in (first, second)]
    return jnp.concatenate(rows, axis=0)


def columns_of(head):
    return pl.ds(pl.multiple_of(head * HEAD_DIM, HEAD_DIM), HEAD_DIM)


def all_forward_kernel(*refs, groups, scale, clip_length, clips):
    query_a, query_b, key_a, key_b, value_a, value_b, place_a, place_b, query_place = refs[:9]
    attended_a, attended_b, stored, kept_probs, sems = refs[9:]
    half, width = key_a.shape
    heads = width // HEAD_DIM
    block = block_of(half)
    pair = 2 * block
    everything = slice(None)

    def copy_of(head):
        slot = head % 2
        return pltpu.make_async_copy(kept_probs.at[slot], stored.at[head], sems.at[slot])

    def one_head(head, _):
        cut = columns_of(head)
        slot = head % 2

        @pl.when(head >= 2)
        def _():
            copy_of(head - 2).wait()

        values_across = take(value_a, value_b, 0, half // block, cut).T
        for index, (seen, free, start) in enumerate(reaches(half, groups)[0]):
            mine = pl.ds(index * block, block)
            query = take(query_a, query_b, index, index + 1, cut)
            at_place = query_place[:, pl.ds(index * pair, pair)]
            place = take(place_a, place_b, free, seen, everything)
            mask = mask_of(place, at_place, clip_length, clips)
            score = dot(take(key_a, key_b, free, seen, cut), query, NT)
            scores = [jnp.where(mask, score, NEGATIVE)]
            if free:
                scores.insert(0, dot(take(key_a, key_b, 0, free, cut), query, NT))
            result, at = 0.0, 0
            for prob in probabilities(scores, scale):
                kept = prob.astype(bf16)
                rows = kept.shape[0]
                kept_probs[slot, pl.ds(start * pair + at, rows), :] = kept
                result += dot(values_across[:, at : at + rows], kept, NN)
                at += rows
            result = result.T.astype(bf16)
            attended_a[mine, cut] = result[:block]
            attended_b[mine, cut] = result[block:]
        copy_of(head).start()
        return 0

    lax.fori_loop(0, heads, one_head, 0)
    for head in range(max(0, heads - 2), heads):
        copy_of(head).wait()


def attend_all(queries, keys, values, places, query_place, groups, clip_length, clips):
    half, width = keys[0].shape
    heads = width // HEAD_DIM
    pair = 2 * block_of(half)
    deep = reaches(half, groups)[1] * pair
    outs = pl.pallas_call(
        partial(
            all_forward_kernel,
            groups=groups,
            scale=1.0 / math.sqrt(HEAD_DIM),
            clip_length=clip_length,
            clips=clips,
        ),
        in_specs=[pl.BlockSpec(memory_space=pltpu.VMEM)] * 9,
        out_specs=[pl.BlockSpec(memory_space=pltpu.VMEM)] * 2
        + [pl.BlockSpec(memory_space=pl.ANY)],
        out_shape=[jax.ShapeDtypeStruct((half, width), bf16)] * 2
        + [pltpu.HBM((heads, deep, pair), bf16)],
        scratch_shapes=[
            pltpu.VMEM((2, deep, pair), bf16),
            pltpu.SemaphoreType.DMA((2,)),
        ],
        compiler_params=params(max(10, half * half // 2**14)),
        cost_estimate=cost(16 * half * half * width, 16 * half * width, 4 * half * half * heads),
        name="attend_all",
    )(*queries, *keys, *values, *places, query_place)
    return outs[:2], outs[2]


STEP = 2


def backward_kernel(*refs, count, groups, scale):
    grad_pieces = refs[:count]
    query_a, query_b, key_a, key_b, value_a, value_b, attended_a, attended_b, stored = refs[
        count : count + 9
    ]
    outs = refs[count + 9 : count + 18]
    grad_query, grad_key, grad_value = outs[0:2], outs[2:4], outs[4:6]
    own_query, own_key, own_value = outs[6:9]
    (scores,) = refs[count + 18 :]
    half, width = key_a.shape
    rows = half // count
    group_rows = rows // groups
    block = block_of(half)
    blocks = half // block
    pair = 2 * block
    reach = reaches(half, groups)[0]

    def sources(index):
        found = []
        if groups == 1:
            for d in range(index * block // rows, (index + 1) * block // rows):
                found.append((d, 0, rows))
            return found
        each = count * group_rows
        for j in range(index * block // each, (index + 1) * block // each):
            for d in range(count):
                found.append((d, j * group_rows, group_rows))
        return found

    def one_head(head, _):
        cut = columns_of(head)

        def keep(targets, own, values, index):
            for side in range(2):
                at = side * block
                targets[side][pl.ds(index * block, block), cut] = values[at : at + block]
                for d, start, size in sources(index):
                    if d == 0:
                        own[pl.ds(side * rows + start, size), cut] = values[at : at + size]
                    at += size

        def take_grads(index):
            return jnp.concatenate(
                [
                    grad_pieces[d][pl.ds(side * rows + start, size), cut]
                    for side in range(2)
                    for d, start, size in sources(index)
                ],
                axis=0,
            )

        keys_across = take(key_a, key_b, 0, blocks, cut).T
        ones = jnp.ones((8, HEAD_DIM), bf16)
        for index, (seen, _, start) in enumerate(reach):
            result = take(attended_a, attended_b, index, index + 1, cut)
            grad = take_grads(index)
            product = grad.astype(f32) * result.astype(f32)
            high = product.astype(bf16)
            low = (product - high.astype(f32)).astype(bf16)
            delta = (dot(ones, high, NT) + dot(ones, low, NT))[0:1, :]
            back = 0.0
            for low_block in range(0, seen, STEP):
                high_block = min(low_block + STEP, seen)
                at = pl.ds((start + low_block) * pair, (high_block - low_block) * pair)
                values = take(value_a, value_b, low_block, high_block, cut)
                score = stored[head, at, :].astype(f32) * (dot(values, grad, NT) - delta)
                score = score.astype(bf16)
                scores[at, :] = score
                back += dot(keys_across[:, low_block * pair : high_block * pair], score, NN)
            keep(grad_query, own_query, (back * scale).T.astype(bf16), index)
        for index in range(blocks):
            key_sum, value_sum = 0.0, 0.0
            for other, (seen, _, start) in enumerate(reach):
                if index < seen:
                    at = pl.ds((start + index) * pair, pair)
                    query = take(query_a, query_b, other, other + 1, cut)
                    key_sum += dot(scores[at, :], query, NN)
                    value_sum += dot(stored[head, at, :], take_grads(other), NN)
            keep(grad_key, own_key, (key_sum * scale).astype(bf16), index)
            keep(grad_value, own_value, value_sum.astype(bf16), index)
        return 0

    lax.fori_loop(0, width // HEAD_DIM, one_head, 0)


def attend_back(grads, queries, keys, values, attended, stored, groups):
    half, width = keys[0].shape
    count = len(grads)
    rows = grads[0].shape[0]
    outs = pl.pallas_call(
        partial(
            backward_kernel,
            count=count,
            groups=groups,
            scale=1.0 / math.sqrt(HEAD_DIM),
        ),
        in_specs=[pl.BlockSpec(memory_space=pltpu.VMEM)] * (count + 9),
        out_specs=[pl.BlockSpec(memory_space=pltpu.VMEM)] * 9,
        out_shape=[jax.ShapeDtypeStruct((half, width), bf16)] * 6
        + [jax.ShapeDtypeStruct((rows, width), bf16)] * 3,
        scratch_shapes=[pltpu.VMEM(stored.shape[1:], bf16)],
        compiler_params=params(8 + 2 * stored.shape[1] * stored.shape[2] // 2**20),
        cost_estimate=cost(8 * 4 * half * half * width, 32 * half * width + 2 * stored.size),
        name="attend_back",
    )(*grads, *queries, *keys, *values, *attended, stored)
    return outs[0:2], outs[2:4], outs[4:6], outs[6:9]


def body(
    inputs,
    first_gain,
    query_weight,
    key_weight,
    value_weight,
    output_weight,
    second_gain,
    up_weight,
    down_weight,
    frame_sizes,
    text_counts,
    action_counts,
    cotangent,
):
    shards = lax.axis_size("seq")
    shard_index = lax.axis_index("seq")
    core = lax.axis_index("mlp") % 2
    length, width = inputs.shape
    total = length * shards
    half = length // 2
    piece = half // shards
    clips = frame_sizes.shape[0]
    clip_length = total // clips
    part = width // shards
    groups = shards if piece % 8 == 0 else 1

    def halves(rows):
        cut = rows.reshape(2, piece, shards, width)
        mine = lax.dynamic_index_in_dim(cut, core, 0, keepdims=False)
        other = lax.dynamic_index_in_dim(cut, 1 - core, 0, keepdims=False)
        return (
            mine.transpose(1, 0, 2).reshape(half, width),
            other.transpose(1, 0, 2).reshape(half, width),
        )

    inputs_half, inputs_other = halves(inputs)
    pieces = gather_early(inputs_half)
    arrived = pieces[inner_size() :: inner_size()]

    place_a, place_b, kind_a, kind_b, query_place, own_place, own_kind = tables(
        frame_sizes, text_counts, action_counts, shards, length, groups
    )
    places, kinds = (place_a, place_b), (kind_a, kind_b)
    half_kind = own_kind[:half]
    own_normed = own_norm(
        jnp.concatenate([inputs_half, inputs_other], axis=0), first_gain, own_kind
    )
    grad_half, grad_other = halves(cotangent)
    grad_own = jnp.concatenate([grad_half, grad_other], axis=0)
    (query_own,) = project_rows(after(own_normed, arrived), query_weight)
    grad_far = gather_outer(after(grad_half, arrived, pieces[inner_size() + 1]))
    pieces = after(pieces, query_own)

    normed = [norm_pieces(pieces, first_gain, kind_a, groups)]
    normed[0], grad_far = after((normed[0], grad_far), normed[0])
    normed.append(swap(normed[0], "mlp", 1))
    keys, values = zip(*[project_rows(rows, key_weight, value_weight) for rows in normed])
    heads_own = attend(query_own, keys, values, places, own_place, clip_length, clips)
    grad_inner = gather_inner(after(grad_half, normed[0]))
    heads_own, grad_inner = after((heads_own, grad_inner), heads_own)
    grad_far = join_x(jnp.concatenate(grad_far, axis=0), heads_own)
    mine, other = product_halves([heads_own], [output_weight], NN)
    other, grad_far = after((other, grad_far), other)
    grad_inner += gather_inner(grad_far)
    low, other = pair_mlp(mine, other)
    own_activated_grad = grad_activated(after(grad_own, low), down_weight)
    queries = [
        project_rows(rows, query_weight)[0] for rows in after(normed, own_activated_grad)
    ]
    other = after(other, queries)
    residual, lifted_half = lift(inputs_half, low, other, second_gain, half_kind)

    lifted_own = both(lifted_half)
    activated_own, hidden_own, mine, other = feed_own(lifted_own, up_weight, own_activated_grad)
    lifted_far = gather_outer(after(lifted_half, other))
    other, grad_inner = after((other, grad_inner), other)
    low, other = pair_mlp(mine, other)
    attended, stored = attend_all(
        after(queries, low),
        keys,
        values,
        places,
        query_place,
        groups,
        clip_length,
        clips,
    )
    other, lifted_far = after((other, lifted_far), attended)
    grad_residual, mixed_half, mixed_columns = middle(
        residual, low, other, grad_half, second_gain, half_kind, shards
    )
    heads_grad = product_back(both(mixed_half), output_weight)

    heads_first = gather_first(heads_grad)
    lifted_far = jnp.concatenate(lifted_far, axis=0)
    lifted_inner_far = gather_inner(lifted_far)
    down_mine, down_other = down_own(after(activated_own, heads_grad), down_weight)
    lifted_far = join_x(lifted_far, heads_first[1], down_other, lifted_inner_far)
    heads_grads = gather_pieces(*heads_first)
    first_lifted, first_grads = with_core([lifted_far]), with_core([grad_far])
    first_lifted = after(first_lifted, heads_grads[inner_size() + 1])
    own = (lifted_own, grad_own, activated_own, hidden_own)
    sums = feed_all(first_lifted, first_grads, up_weight, down_weight, shards, own=own)
    down_low, down_other = pair_mlp(down_mine, down_other)
    heads_grads, down_low, down_other = after((heads_grads, down_low, down_other), sums)
    inner = inner_size()
    columns_far = {
        outer: swap(after(mixed_columns[outer : outer + inner], sums), "seq", outer)
        for outer in range(inner, shards, inner)
    }
    lifted_inner = gather_inner(after(lifted_half, down_other))
    query_low, key_low, value_low, own_low = attend_back(
        heads_grads, queries, keys, values, attended, stored, groups
    )
    attention_weights = (query_weight, key_weight, value_weight)
    lifted_inner += [join_x(far, own_low) for far in lifted_inner_far]
    own_low, lifted_inner, columns_far = after((own_low, lifted_inner, columns_far), own_low)
    low, other = pair_mlp(*product_halves(own_low, attention_weights, NT))

    query_grad, key_grad, value_grad, first_gain_grad = project(
        normed,
        after((query_low, key_low, value_low), low),
        attention_weights,
        first_gain,
        kinds,
        shards,
    )
    columns_far = after(columns_far, low)
    columns_far[0] = mixed_columns[:inner]
    columns = {}
    for outer, came in columns_far.items():
        columns[outer] = came[0]
        for bit in range(1, inner):
            columns[outer | bit] = swap(came[bit], "seq", bit)
    other, columns = after((other, columns), query_grad)
    first_gain_grad = after(first_gain_grad, other)
    first_gain_grad = first_gain_grad + swap(first_gain_grad, "mlp", 1)
    input_half = last(inputs_half, low, other, grad_residual, first_gain, half_kind, shards)
    outputs_half = finish(residual, down_low, after(down_other, input_half), shards)
    rest_lifted = with_core(after(lifted_inner, other))
    rest_grads = with_core(after(grad_inner, other))
    up_grad, down_grad = feed_all(
        after(rest_lifted, outputs_half, first_gain_grad), rest_grads, up_weight, down_weight, shards, sums
    )
    bit = 2
    while bit < lax.axis_size("mlp"):
        came = after(swap(first_gain_grad, "mlp", bit), up_grad)
        first_gain_grad = first_gain_grad + came
        bit *= 2
    placed = (input_half, outputs_half)
    input_grad, outputs = place_halves(placed, [swap(array, "mlp", 1) for array in placed])
    mixed_part = jnp.stack([after(columns[d], up_grad) for d in range(shards)])
    output_grad, second_gain_grad = output_part(
        attended, (mixed_part, swap(mixed_part, "mlp", 1)), groups
    )

    return (
        outputs,
        input_grad,
        first_gain_grad,
        query_grad,
        key_grad,
        value_grad,
        output_grad,
        second_gain_grad,
        up_grad,
        down_grad,
    )


def solution(mesh):
    return jax.shard_map(
        body,
        mesh=mesh,
        in_specs=(
            P("seq", None),
            P(),
            P(None, "mlp"),
            P(None, "mlp"),
            P(None, "mlp"),
            P("mlp", None),
            P(),
            P(None, "mlp"),
            P("mlp", None),
            P(),
            P(),
            P(),
            P("seq", None),
        ),
        out_specs=(
            P("seq", None),
            P("seq", None),
            P(None, "seq"),
            P("seq", "mlp"),
            P("seq", "mlp"),
            P("seq", "mlp"),
            P("mlp", "seq"),
            P(None, "seq"),
            P("seq", "mlp"),
            P("mlp", "seq"),
        ),
        check_vma=False,
    )
```

```python
from functools import partial
import math

import jax
import jax.numpy as jnp
from jax import lax
from jax.experimental import pallas as pl
from jax.experimental.pallas import tpu as pltpu
from jax.sharding import PartitionSpec as P

HEAD_DIM = 128
epsilon = 1e-05
bf16 = jnp.bfloat16
f32 = jnp.float32
NEGATIVE = -1e30

WHOLE = pl.BlockSpec(memory_space=pltpu.VMEM)
NN = ((1,), (0,))
NT = ((1,), (1,))
TN = ((0,), (0,))


def dot(a, b, dims):
    return lax.dot_general(a, b, (dims, ((), ())), preferred_element_type=f32)


def params(mebibytes):
    return pltpu.CompilerParams(vmem_limit_bytes=mebibytes * 1024 * 1024)


def cost(flops, moved, transcendentals=0, share=100):
    return pl.CostEstimate(
        flops=int(flops) // share,
        bytes_accessed=int(moved) // share,
        transcendentals=int(transcendentals) // share,
    )


def swap(value, axis, bit):
    size = lax.axis_size(axis)
    return lax.ppermute(value, axis, [(i, i ^ bit) for i in range(size)])


def inner_size():
    return 1 << (int(math.log2(lax.axis_size("seq"))) // 2)


def x_size():
    return lax.axis_size("mlp") // 2


def after(values, *earlier):
    return lax.optimization_barrier((values, earlier))[0]


def in_hbm(array):
    return pltpu.with_memory_space_constraint(array, pltpu.HBM)


def own_quarter(half):
    rows = half.shape[0] // x_size()
    return lax.dynamic_slice_in_dim(half, (lax.axis_index("mlp") // 2) * rows, rows, 0)


def join_x(quarter, *earlier):
    bit = 1
    while bit < x_size():
        came = after(swap(quarter, "mlp", 2 * bit), earlier)
        quarter = jnp.concatenate([quarter, came], axis=0)
        bit *= 2
    return quarter


def gather_early(half):
    size, inner = lax.axis_size("seq"), inner_size()
    quarter = own_quarter(half)
    pieces = {0: half}
    far = {outer: swap(quarter, "seq", outer) for outer in range(inner, size, inner)}
    for bit in range(1, inner):
        pieces[bit] = swap(half, "seq", bit)
    for outer in range(inner, size, inner):
        pieces[outer] = join_x(far[outer])
        for bit in range(1, inner):
            pieces[outer | bit] = swap(pieces[outer], "seq", bit)
    return [pieces[d] for d in range(size)]


def gather_outer(half):
    size, inner = lax.axis_size("seq"), inner_size()
    quarter = own_quarter(half)
    return [swap(quarter, "seq", outer) for outer in range(inner, size, inner)]


def gather_inner(array):
    return [swap(array, "seq", bit) for bit in range(1, inner_size())]


def with_core(arrays):
    return [each for array in arrays for each in (array, swap(array, "mlp", 1))]


def gather_first(piece):
    size, inner = lax.axis_size("seq"), inner_size()
    pieces = {0: piece}
    for bit in range(1, inner):
        pieces[bit] = swap(piece, "seq", bit)
    return pieces, [swap(piece, "seq", outer) for outer in range(inner, size, inner)]


def gather_pieces(pieces, far):
    size, inner = lax.axis_size("seq"), inner_size()
    for outer, came in zip(range(inner, size, inner), far):
        pieces[outer] = came
        for bit in range(1, inner):
            pieces[outer | bit] = swap(came, "seq", bit)
    return [pieces[d] for d in range(size)]


def rounded(value):
    return lax.optimization_barrier(value.astype(bf16))


def pair_mlp(mine, other_half):
    low, other = rounded(mine + swap(other_half, "mlp", 1).astype(f32)), None
    bit = 2
    while bit < lax.axis_size("mlp"):
        if other is not None:
            low = rounded(low.astype(f32) + other.astype(f32))
        other = swap(low, "mlp", bit)
        bit *= 2
    if other is None:
        other = jnp.zeros_like(low)
    return low, other


def both(half):
    return jnp.concatenate([half, swap(half, "mlp", 1)], axis=0)


def tables_kernel(index, frames, texts, actions, *outs, shards, length, groups, clip_length):
    place_a, place_b, kind_a, kind_b, query_place, own_place, own_kind = outs
    shard_index, core = index[0], index[1]
    shape = (shards, length)
    place = lax.broadcasted_iota(jnp.int32, shape, 0) * length + lax.broadcasted_iota(
        jnp.int32, shape, 1
    )
    kinds = jnp.full(shape, 2, jnp.int32)
    for clip in range(frames.shape[0]):
        start = jnp.int32(clip * clip_length)
        within = (place >= clip * clip_length) & (place < (clip + 1) * clip_length)
        for frame in range(frames.shape[1]):
            text_end = start + texts[clip, frame]
            action_end = text_end + actions[clip, frame]
            kinds = jnp.where(within & (place >= start) & (place < text_end), 0, kinds)
            kinds = jnp.where(within & (place >= text_end) & (place < action_end), 1, kinds)
            start = action_end + frames[clip, frame]
    square = (length, length)
    down = lax.broadcasted_iota(jnp.int32, square, 0)
    across = lax.broadcasted_iota(jnp.int32, square, 1)
    earlier = (down < across).astype(f32).astype(bf16)
    rank = jnp.zeros(shape, f32)
    before = jnp.zeros((shards, 1), f32)
    for kind in range(3):
        chosen = (kinds == kind).astype(f32)
        rank += chosen * (dot(chosen.astype(bf16), earlier, NN) + before)
        before += chosen.sum(axis=1, keepdims=True)
    rank_low, kinds_low = rank.astype(bf16), kinds.astype(f32).astype(bf16)
    piece = length // shards // 2
    lane = lax.broadcasted_iota(jnp.int32, (1, length), 1).astype(f32)

    def find(shard, offset, side, row):
        wanted = (shard_index ^ offset) * (2 * piece) + (core ^ side) * piece + row
        pick = shard == lax.broadcasted_iota(jnp.int32, (length, shards), 1)
        pick = pick.astype(f32).astype(bf16)
        hit = dot(pick, rank_low, NN) == wanted.astype(f32)
        where = jnp.sum(jnp.where(hit, lane, 0.0), axis=1, keepdims=True).astype(jnp.int32)
        kind = jnp.sum(jnp.where(hit, dot(pick, kinds_low, NN), 0.0), axis=1, keepdims=True)
        return where + shard * length, kind.astype(jnp.int32)

    def as_row(column):
        return jnp.sum(jnp.where(down == across, column, 0), axis=0, keepdims=True)

    step = lax.broadcasted_iota(jnp.int32, (length, 1), 0)
    half = length // 2
    for side, (place_out, kind_out) in enumerate(((place_a, kind_a), (place_b, kind_b))):
        for block in range(shards // 2):
            token = step + block * length
            if groups > 1:
                shard, offset = token // (shards * piece), (token // piece) % shards
            else:
                offset, shard = token // half, (token % half) // piece
            where, kind = find(shard, offset, side, token % piece)
            at = pl.ds(block * length, length)
            place_out[at, :] = where
            kind_out[at, :] = kind
            query_place[:, pl.ds((2 * block + side) * length, length)] = as_row(where)
    where, kind = find((step % half) // piece, step * 0, step // half, step % piece)
    own_place[...] = as_row(where)
    own_kind[...] = kind


def tables(frames, texts, actions, shards, length, groups):
    index = jnp.stack([lax.axis_index("seq"), lax.axis_index("mlp") % 2]).astype(jnp.int32)
    total = shards * length
    column = jax.ShapeDtypeStruct((total // 2, 1), jnp.int32)
    return pl.pallas_call(
        partial(
            tables_kernel,
            shards=shards,
            length=length,
            groups=groups,
            clip_length=total // frames.shape[0],
        ),
        in_specs=[pl.BlockSpec(memory_space=pltpu.SMEM)] * 4,
        out_shape=[column] * 4
        + [
            jax.ShapeDtypeStruct((1, total), jnp.int32),
            jax.ShapeDtypeStruct((1, length), jnp.int32),
            jax.ShapeDtypeStruct((length, 1), jnp.int32),
        ],
        cost_estimate=cost(8 * total * length, 8 * 128 * total),
        name="tables",
    )(index, frames, texts, actions)


def rows_kernel(*refs, count):
    rows, weights, outs = refs[0], refs[1 : 1 + count], refs[1 + count :]
    for weight, out in zip(weights, outs):
        out[...] = dot(rows[...], weight[...], NN).astype(bf16)


def project_rows(rows, *weights):
    across = weights[0].shape[1]
    return pl.pallas_call(
        partial(rows_kernel, count=len(weights)),
        out_shape=[jax.ShapeDtypeStruct((rows.shape[0], across), bf16)] * len(weights),
        compiler_params=params(8),
        cost_estimate=cost(2 * rows.size * across * len(weights), 2 * rows.size),
        name="project_rows",
    )(rows, *weights)


def one_kernel(rows, weight, out):
    out[...] = dot(rows[...], weight[...], NT).astype(bf16)


def product_back(rows, weight):
    return pl.pallas_call(
        one_kernel,
        out_shape=jax.ShapeDtypeStruct((rows.shape[0], weight.shape[0]), bf16),
        compiler_params=params(6),
        cost_estimate=cost(2 * rows.size * weight.shape[0], 2 * weight.size),
        name="product_back",
    )(rows, weight)


def halves_kernel(*refs, count, dims):
    mine, other = refs[-2:]
    half = mine.shape[0]
    total = sum(dot(refs[k][...], refs[count + k][...], dims) for k in range(count))
    mine[...] = total[:half]
    other[...] = total[half:].astype(bf16)


def product_halves(rows, weights, dims):
    count = len(rows)
    half = rows[0].shape[0] // 2
    across = weights[0].shape[1 - dims[1][0]]
    shape = (half, across)
    return pl.pallas_call(
        partial(halves_kernel, count=count, dims=dims),
        out_shape=[jax.ShapeDtypeStruct(shape, f32), jax.ShapeDtypeStruct(shape, bf16)],
        compiler_params=params(6),
        cost_estimate=cost(2 * count * rows[0].size * across, 2 * count * weights[0].size),
        name="product_halves",
    )(*rows, *weights)


def down_own_kernel(rows, weight, mine, other, total):
    total[...] = jnp.zeros_like(total)

    def step(at):
        total[...] += dot(rows[:, at], weight[at, :], NN)

    tiles_of(weight.shape[0], math.gcd(weight.shape[0], 512), step)
    half = mine.shape[0]
    mine[...] = total[:half]
    other[...] = total[half:].astype(bf16)


def down_own(rows, weight):
    count, deep = rows.shape
    across = weight.shape[1]
    shape = (count // 2, across)
    return pl.pallas_call(
        down_own_kernel,
        in_specs=[WHOLE] * 2,
        out_specs=[WHOLE] * 2,
        out_shape=[jax.ShapeDtypeStruct(shape, f32), jax.ShapeDtypeStruct(shape, bf16)],
        scratch_shapes=[pltpu.VMEM((count, across), f32)],
        compiler_params=params(6),
        cost_estimate=cost(2 * rows.size * across, 2 * weight.size),
        name="down_own",
    )(rows, weight)


def gain_rows(gain, column):
    return jnp.where(
        column == 0, gain[0:1, :], jnp.where(column == 1, gain[1:2, :], gain[2:3, :])
    )


def normalize(values):
    mean = jnp.mean(values, axis=1, keepdims=True)
    centered = values - mean
    inverse = lax.rsqrt(jnp.mean(centered * centered, axis=1, keepdims=True) + epsilon)
    return (centered * inverse, inverse)


def norm_back(grad, normal, inverse, gains):
    scaled = grad * gains
    return inverse * (
        scaled
        - jnp.mean(scaled, axis=1, keepdims=True)
        - normal * jnp.mean(scaled * normal, axis=1, keepdims=True)
    )


def norm_kernel(*refs, groups, inner, parts):
    index, gain, kind, out = refs[0], refs[-3], refs[-2], refs[-1]
    pieces = refs[1:-3]
    rows, width = pieces[0].shape
    count = len(pieces)
    step = rows // parts
    for d, piece in enumerate(pieces):
        for part in range(parts):
            normal, _ = normalize(piece[pl.ds(part * step, step), :].astype(f32))
            place = part if d < inner else part ^ index[0]
            if groups > 1:
                each = groups // parts
                at = pl.ds(place * each, each)
                column = kind[at, d].reshape(step, 1)
                normed = (normal * gain_rows(gain, column)).astype(bf16)
                out[at, d] = normed.reshape(each, rows // groups, width)
            else:
                column = kind[d, place]
                out[d, place] = (normal * gain_rows(gain, column)).astype(bf16)


def norm_pieces(pieces, gain, kind, groups):
    rows, width = pieces[0].shape
    count = len(pieces)
    parts = x_size()
    if groups > 1:
        shape = (groups, count, rows // groups)
    else:
        shape = (count, parts, rows // parts)
    memory = [pl.BlockSpec(memory_space=pltpu.SMEM)]
    index = (lax.axis_index("mlp") // 2).astype(jnp.int32).reshape(1)
    out = pl.pallas_call(
        partial(norm_kernel, groups=groups, inner=inner_size(), parts=parts),
        in_specs=memory + [pl.BlockSpec(memory_space=pltpu.VMEM)] * (count + 2),
        out_shape=jax.ShapeDtypeStruct(shape + (width,), bf16),
        compiler_params=params(4 + count),
        cost_estimate=cost(10 * count * rows * width, 4 * count * rows * width),
        name="norm_pieces",
    )(index, *pieces, gain, kind.reshape(shape + (1,)))
    return out.reshape(count * rows, width)


def own_norm_kernel(rows, gain, kind, out):
    normal, _ = normalize(rows[...].astype(f32))
    out[...] = (normal * gain_rows(gain, kind[...])).astype(bf16)


def own_norm(rows, gain, kind):
    return pl.pallas_call(
        own_norm_kernel,
        out_shape=jax.ShapeDtypeStruct(rows.shape, bf16),
        compiler_params=params(4),
        cost_estimate=cost(10 * rows.size, 4 * rows.size),
        name="own_norm",
    )(rows, gain, kind)


def lift_kernel(rows, low, other, gain, kind, residual, lifted):
    value = rows[...].astype(f32) + (low[...].astype(f32) + other[...].astype(f32))
    residual[...] = value
    normal, _ = normalize(value)
    lifted[...] = (normal * gain_rows(gain, kind[...])).astype(bf16)


def lift(rows, low, other, gain, kind):
    return pl.pallas_call(
        lift_kernel,
        in_specs=[WHOLE] * 5,
        out_specs=[WHOLE] * 2,
        out_shape=[jax.ShapeDtypeStruct(rows.shape, f32), jax.ShapeDtypeStruct(rows.shape, bf16)],
        compiler_params=params(4),
        cost_estimate=cost(10 * rows.size, 12 * rows.size),
        name="lift",
    )(rows, low, other, gain, kind)


def kind_sums(term, kind):
    sums = [jnp.sum(jnp.where(kind == k, term, 0.0), axis=0, keepdims=True) for k in range(3)]
    high = [value.astype(bf16) for value in sums]
    low = [(value - part.astype(f32)).astype(bf16) for value, part in zip(sums, high)]
    zero = jnp.zeros((1, term.shape[1]), bf16)
    return jnp.concatenate(high + low + [zero, zero], axis=0)


def middle_kernel(index, residual, low, other, grad, gain, kind, grad_residual, mixed, parts):
    lifted_grad = low[...].astype(f32) + other[...].astype(f32)
    normal, inverse = normalize(residual[...])
    column = kind[...]
    back = norm_back(lifted_grad, normal, inverse, gain_rows(gain, column))
    value = grad[...].astype(f32) + back
    grad_residual[...] = value
    rounded_value = value.astype(bf16)
    mixed[...] = rounded_value
    sums = kind_sums(lifted_grad * normal, column)
    shards, rows, part = parts.shape
    for k in range(shards):
        at = index[0] ^ k
        parts[at, pl.ds(0, rows - 8), :] = rounded_value[:, k * part : (k + 1) * part]
        parts[at, pl.ds(rows - 8, 8), :] = sums[:, k * part : (k + 1) * part]


def middle(residual, low, other, grad, gain, kind, shards):
    rows, width = residual.shape
    index = lax.axis_index("seq").astype(jnp.int32).reshape(1)
    return pl.pallas_call(
        middle_kernel,
        in_specs=[pl.BlockSpec(memory_space=pltpu.SMEM)] + [WHOLE] * 6,
        out_specs=[WHOLE] * 3,
        out_shape=[
            jax.ShapeDtypeStruct(residual.shape, f32),
            jax.ShapeDtypeStruct(residual.shape, bf16),
            jax.ShapeDtypeStruct((shards, rows + 8, width // shards), bf16),
        ],
        compiler_params=params(6),
        cost_estimate=cost(20 * residual.size, 16 * residual.size),
        name="middle",
    )(index, residual, low, other, grad, gain, kind)


def reordered(values, shards):
    count = values.shape[0]
    piece = count // shards
    to = lax.broadcasted_iota(jnp.int32, (count, count), 0)
    source = lax.broadcasted_iota(jnp.int32, (count, count), 1)
    pick = (source == (to % shards) * piece + to // shards).astype(f32).astype(bf16)
    return dot(pick, values, NN).astype(bf16)


def finish_kernel(residual, low, other, out, *, shards):
    value = residual[...] + (low[...].astype(f32) + other[...].astype(f32))
    out[...] = reordered(value.astype(bf16), shards)


def finish(residual, low, other, shards):
    return pl.pallas_call(
        partial(finish_kernel, shards=shards),
        in_specs=[WHOLE] * 3,
        out_specs=WHOLE,
        out_shape=jax.ShapeDtypeStruct(residual.shape, bf16),
        compiler_params=params(4),
        cost_estimate=cost(2 * residual.size, 10 * residual.size),
        name="finish",
    )(residual, low, other)


def place_kernel(index, *refs):
    count = len(refs) // 3
    for mine, other, out in zip(refs[:count], refs[count : 2 * count], refs[2 * count :]):
        half = mine.shape[0]
        out[pl.ds(pl.multiple_of(index[0] * half, half), half), :] = mine[...]
        out[pl.ds(pl.multiple_of((1 - index[0]) * half, half), half), :] = other[...]


def place_halves(arrays, others):
    half, width = arrays[0].shape
    index = (lax.axis_index("mlp") % 2).astype(jnp.int32).reshape(1)
    return pl.pallas_call(
        place_kernel,
        in_specs=[pl.BlockSpec(memory_space=pltpu.SMEM)] + [WHOLE] * (2 * len(arrays)),
        out_shape=[jax.ShapeDtypeStruct((2 * half, width), bf16)] * len(arrays),
        compiler_params=params(6),
        cost_estimate=cost(half * width, 16 * half * width),
        name="place_halves",
    )(index, *arrays, *others)


def last_kernel(rows, low, other, grad_residual, gain, kind, out, *, shards):
    grad = low[...].astype(f32) + other[...].astype(f32)
    normal, inverse = normalize(rows[...].astype(f32))
    back = norm_back(grad, normal, inverse, gain_rows(gain, kind[...]))
    out[...] = reordered((grad_residual[...] + back).astype(bf16), shards)


def last(rows, low, other, grad_residual, gain, kind, shards):
    return pl.pallas_call(
        partial(last_kernel, shards=shards),
        in_specs=[WHOLE] * 6,
        out_specs=WHOLE,
        out_shape=jax.ShapeDtypeStruct(rows.shape, bf16),
        compiler_params=params(6),
        cost_estimate=cost(20 * rows.size, 12 * rows.size),
        name="last",
    )(rows, low, other, grad_residual, gain, kind)


def gelu_parts(value):
    rate = math.sqrt(2 / math.pi)
    square = value * value
    bent = jnp.tanh(value * (rate + (rate * 0.044715) * square))
    upper = 0.5 * (1 + bent)
    slope = upper + (0.5 * value) * (1 - bent * bent) * (rate + (rate * 3 * 0.044715) * square)
    return value * upper, slope


def tiles_of(extent, tile, step):
    def at(t, _):
        step(pl.ds(pl.multiple_of(t * tile, tile), tile))
        return 0

    lax.fori_loop(0, extent // tile, at, 0)


def own_kernel(lifted, up, grad_activated, activated, hidden_grads, mine, other, total):
    total[...] = jnp.zeros_like(total)

    def step(at):
        value, slope = gelu_parts(dot(lifted[...], up[:, at], NN))
        activated[:, at] = value.astype(bf16)
        hidden_grad = (grad_activated[:, at] * slope).astype(bf16)
        hidden_grads[:, at] = hidden_grad
        total[...] += dot(hidden_grad, up[:, at], NT)

    tiles_of(up.shape[1], math.gcd(up.shape[1], 512), step)
    half = mine.shape[0]
    mine[...] = total[:half]
    other[...] = total[half:].astype(bf16)


def feed_own(lifted, up, grad_activated):
    rows, width = lifted.shape
    hidden = up.shape[1]
    return pl.pallas_call(
        own_kernel,
        in_specs=[WHOLE] * 3,
        out_specs=[WHOLE] * 4,
        out_shape=[jax.ShapeDtypeStruct((rows, hidden), bf16)] * 2
        + [
            jax.ShapeDtypeStruct((rows // 2, width), f32),
            jax.ShapeDtypeStruct((rows // 2, width), bf16),
        ],
        scratch_shapes=[pltpu.VMEM((rows, width), f32)],
        compiler_params=params(8),
        cost_estimate=cost(4 * rows * width * hidden, 2 * width * hidden),
        name="feed_own",
    )(lifted, up, grad_activated)


def down_kernel(grad, down, out):
    def step(at):
        out[:, at] = dot(grad[...], down[at, :], NT)

    tiles_of(down.shape[0], math.gcd(down.shape[0], 512), step)


def grad_activated(grad, down):
    rows, width = grad.shape
    hidden = down.shape[0]
    return pl.pallas_call(
        down_kernel,
        in_specs=[WHOLE] * 2,
        out_specs=WHOLE,
        out_shape=jax.ShapeDtypeStruct((rows, hidden), f32),
        compiler_params=params(6),
        cost_estimate=cost(2 * rows * width * hidden, 2 * width * hidden),
        name="grad_activated",
    )(grad, down)


def all_kernel(index, *refs, count):
    lifted_parts, grad_parts = refs[:count], refs[count : 2 * count]
    up, down = refs[2 * count : 2 * count + 2]
    before = refs[2 * count + 2 : -5]
    up_grad, down_grad, lifted_across, hidden_kept, grad_kept = refs[-5:]
    part = up_grad.shape[0]
    mine = pl.ds(pl.multiple_of(index[0] * part, part), part)

    def rows_of(parts, at):
        return jnp.concatenate([ref[:, at] for ref in parts], axis=0)

    @pl.when(pl.program_id(0) == 0)
    def _():
        lifted_across[...] = rows_of(lifted_parts, mine).T

    first = pl.program_id(0) == 0
    last_step = pl.num_programs(0) - 1

    tile = hidden_kept.shape[1]
    at = jnp.minimum(pl.program_id(0), last_step - 1) if up.shape[1] > tile else 0
    here = pl.ds(pl.multiple_of(at * tile, tile), tile)

    def products():
        everything = slice(None)
        return (
            dot(rows_of(lifted_parts, everything), up[:, here], NN),
            dot(rows_of(grad_parts, everything), down[here, :], NT),
        )

    def finish_tile(hidden_value, activated_grad):
        value, slope = gelu_parts(hidden_value)
        hidden_grad = (activated_grad * slope).astype(bf16)
        down_term = dot(value.astype(bf16), rows_of(grad_parts, mine), TN)
        up_term = dot(lifted_across[...], hidden_grad, NN)
        if len(before) == 2:
            up_term += before[0][...].astype(f32)
            down_term += before[1][...].astype(f32)
        else:
            lifted_own, grad_own, activated, hidden_own = before
            up_term += dot(lifted_own[...], hidden_own[...], TN)
            down_term += dot(activated[...], grad_own[...], TN)
        up_grad[...] = up_term.astype(up_grad.dtype)
        down_grad[...] = down_term.astype(down_grad.dtype)

    @pl.when(first)
    def _():
        hidden_kept[...], grad_kept[...] = products()

    @pl.when((pl.program_id(0) > 0) & (pl.program_id(0) < last_step))
    def _():
        kept = hidden_kept[...], grad_kept[...]
        fresh = products()
        finish_tile(*kept)
        hidden_kept[...], grad_kept[...] = fresh

    @pl.when(pl.program_id(0) == last_step)
    def _():
        finish_tile(hidden_kept[...], grad_kept[...])


def feed_all(lifted, grad, up, down, shards, sums=(), own=()):
    counts = [array.shape[0] for array in lifted]
    rows, width = sum(counts), lifted[0].shape[1]
    count = len(counts)
    part = width // shards
    hidden = up.shape[1]
    tile = math.gcd(hidden, 256)
    steps = hidden // tile
    across = lambda t, index: (0, jnp.maximum(t - 1, 0))
    below = lambda t, index: (jnp.maximum(t - 1, 0), 0)
    mine = lambda t, index: (0, index[0])
    sum_specs = [pl.BlockSpec((part, tile), across), pl.BlockSpec((tile, part), below)]
    if own:
        own_rows = own[0].shape[0]
        more = [pl.BlockSpec((own_rows, part), mine)] * 2
        more += [pl.BlockSpec((own_rows, tile), across)] * 2
    else:
        more = sum_specs
    index = lax.axis_index("seq").astype(jnp.int32).reshape(1)
    return pl.pallas_call(
        partial(all_kernel, count=count),
        grid_spec=pltpu.PrefetchScalarGridSpec(
            num_scalar_prefetch=1,
            grid=(steps + 1,),
            in_specs=[WHOLE] * (2 * count)
            + [WHOLE] * 2
            + more,
            out_specs=sum_specs,
            scratch_shapes=[pltpu.VMEM((part, rows), bf16)]
            + [pltpu.VMEM((rows, tile), f32)] * 2,
        ),
        out_shape=[
            pltpu.HBM((part, hidden), bf16 if own else f32),
            pltpu.HBM((hidden, part), bf16 if own else f32),
        ],
        compiler_params=params((6 if own else 8) + 8 * rows // 512),
        cost_estimate=cost(
            4 * rows * hidden * (width + part),
            4 * width * hidden + 4 * rows * width,
        ),
        name="feed_all",
    )(
        index,
        *lifted,
        *grad,
        up,
        down,
        *(own or [in_hbm(array) for array in sums]),
    )


def project_kernel(index, *refs):
    normed, lows, weights = refs[0:2], refs[2:8], refs[8:11]
    gain, kinds = refs[11], refs[12:14]
    outs, gain_grad = refs[14:17], refs[17]
    for k in range(3):
        outs[k][...] = sum(dot(normed[side][...], lows[2 * k + side][...], TN) for side in range(2))
    gain_sum = [0.0, 0.0, 0.0]
    for side in range(2):
        column = kinds[side][...]
        term = sum(dot(lows[2 * k + side][...], weights[k][...], NT) for k in range(3))
        term = term * (normed[side][...].astype(f32) / gain_rows(gain, column))
        for k in range(3):
            gain_sum[k] += jnp.sum(jnp.where(column == k, term, 0.0), axis=0, keepdims=True)
    gain_grad[...] = jnp.concatenate(gain_sum, axis=0)


def project(normed, lows, weights, gain, kinds, shards):
    rows, width = normed[0].shape
    across = lows[0][0].shape[1]
    part = width // shards
    whole = lambda t, index: (0, 0)
    mine = lambda t, index: (0, index[0])
    below = lambda t, index: (index[0], 0)
    index = lax.axis_index("seq").astype(jnp.int32).reshape(1)
    return pl.pallas_call(
        project_kernel,
        grid_spec=pltpu.PrefetchScalarGridSpec(
            num_scalar_prefetch=1,
            grid=(1,),
            in_specs=[pl.BlockSpec((rows, part), mine)] * 2
            + [pl.BlockSpec((rows, across), whole)] * 6
            + [pl.BlockSpec((part, across), below)] * 3
            + [pl.BlockSpec((gain.shape[0], part), mine)]
            + [pl.BlockSpec((rows, 1), whole)] * 2,
            out_specs=[pl.BlockSpec((part, across), whole)] * 3
            + [pl.BlockSpec((gain.shape[0], part), whole)],
        ),
        out_shape=[jax.ShapeDtypeStruct((part, across), f32)] * 3
        + [jax.ShapeDtypeStruct((gain.shape[0], part), f32)],
        compiler_params=params(8),
        cost_estimate=cost(24 * rows * part * across, 12 * rows * across + 12 * part * across),
        name="project",
    )(index, *normed, *[low for pair in lows for low in pair], *weights, gain, *kinds)


def output_kernel(attended_a, attended_b, came_a, came_b, out, gain_grad, *, groups):
    total, sums = 0.0, 0.0
    shards, rows, part = came_a.shape
    half = rows - 8
    each = half // groups
    for attended, came in ((attended_a, came_a), (attended_b, came_b)):
        mixed = [
            came[d, pl.ds(group * each, each), :]
            for group in range(groups)
            for d in range(shards)
        ]
        total += dot(attended[...], jnp.concatenate(mixed, axis=0), TN)
        own_sums = 0.0
        for k in range(shards):
            own_sums += came[k, pl.ds(half, 8), :].astype(f32)
        sums += own_sums
    out[...] = total
    gain_grad[...] = sums[0:3, :] + sums[3:6, :]


def output_part(attended, came, groups):
    across, part = attended[0].shape[1], came[0].shape[2]
    return pl.pallas_call(
        partial(output_kernel, groups=groups),
        in_specs=[WHOLE] * 4,
        out_shape=[
            jax.ShapeDtypeStruct((across, part), f32),
            jax.ShapeDtypeStruct((3, part), f32),
        ],
        compiler_params=params(6),
        cost_estimate=cost(
            4 * attended[0].shape[0] * across * part, 4 * attended[0].shape[0] * (across + part)
        ),
        name="output_part",
    )(*attended, *came)


def mask_of(key_place, query_place, clip_length, clips):
    allowed = key_place <= query_place
    if clips > 1:
        allowed = allowed & (key_place // clip_length == query_place // clip_length)
    return allowed


def probabilities(scores, scale):
    top = scores[0].max(axis=0, keepdims=True)
    for block in scores[1:]:
        top = jnp.maximum(top, block.max(axis=0, keepdims=True))
    rate = scale * math.log2(math.e)
    weights = [jnp.exp2((block - top) * rate) for block in scores]
    total = weights[0].sum(axis=0, keepdims=True)
    for block in weights[1:]:
        total = total + block.sum(axis=0, keepdims=True)
    inverse = 1.0 / total
    return [block * inverse for block in weights]


def forward_kernel(query, key_a, key_b, value_a, value_b, place_a, place_b, query_place, out, **opts):
    scale = opts["scale"]
    query_place = query_place[...]
    allowed = [
        mask_of(place[...], query_place, opts["clip_length"], opts["clips"])
        for place in (place_a, place_b)
    ]
    for head in range(query.shape[1] // HEAD_DIM):
        at = pl.ds(head * HEAD_DIM, HEAD_DIM)
        scores = [
            jnp.where(mask, dot(key[:, at], query[:, at], NT), NEGATIVE)
            for mask, key in zip(allowed, (key_a, key_b))
        ]
        prob = [block.astype(bf16) for block in probabilities(scores, scale)]
        result = dot(value_a[:, at], prob[0], TN) + dot(value_b[:, at], prob[1], TN)
        out[:, at] = result.T.astype(bf16)


def attend(query, keys, values, places, query_place, clip_length, clips):
    rows, width = query.shape
    total = 2 * keys[0].shape[0]
    return pl.pallas_call(
        partial(
            forward_kernel, scale=1.0 / math.sqrt(HEAD_DIM), clip_length=clip_length, clips=clips
        ),
        out_shape=jax.ShapeDtypeStruct((rows, width), bf16),
        compiler_params=params(8),
        cost_estimate=cost(
            4 * rows * total * width, 4 * total * width, rows * total * (width // HEAD_DIM)
        ),
        name="attend",
    )(query, *keys, *values, *places, query_place)


def block_of(half):
    return min(128, half)


def reaches(half, groups):
    blocks = half // block_of(half)
    found, start = [], 0
    for index in range(blocks):
        seen, free = (index + 1, index) if groups > 1 else (blocks, 0)
        found.append((seen, free, start))
        start += seen
    return found, start


def take(first, second, low, high, at):
    block = block_of(first.shape[0])
    rows = [side[pl.ds(k * block, block), at] for k in range(low, high) for side in (first, second)]
    return jnp.concatenate(rows, axis=0)


def columns_of(head):
    return pl.ds(pl.multiple_of(head * HEAD_DIM, HEAD_DIM), HEAD_DIM)


def all_forward_kernel(*refs, groups, scale, clip_length, clips):
    query_a, query_b, key_a, key_b, value_a, value_b, place_a, place_b, query_place = refs[:9]
    attended_a, attended_b, stored, kept_probs, sems = refs[9:]
    half, width = key_a.shape
    heads = width // HEAD_DIM
    block = block_of(half)
    pair = 2 * block
    everything = slice(None)

    def copy_of(head):
        slot = head % 2
        return pltpu.make_async_copy(kept_probs.at[slot], stored.at[head], sems.at[slot])

    def one_head(head, _):
        cut = columns_of(head)
        slot = head % 2

        @pl.when(head >= 2)
        def _():
            copy_of(head - 2).wait()

        values_across = take(value_a, value_b, 0, half // block, cut).T
        for index, (seen, free, start) in enumerate(reaches(half, groups)[0]):
            mine = pl.ds(index * block, block)
            query = take(query_a, query_b, index, index + 1, cut)
            at_place = query_place[:, pl.ds(index * pair, pair)]
            place = take(place_a, place_b, free, seen, everything)
            mask = mask_of(place, at_place, clip_length, clips)
            score = dot(take(key_a, key_b, free, seen, cut), query, NT)
            scores = [jnp.where(mask, score, NEGATIVE)]
            if free:
                scores.insert(0, dot(take(key_a, key_b, 0, free, cut), query, NT))
            result, at = 0.0, 0
            for prob in probabilities(scores, scale):
                kept = prob.astype(bf16)
                rows = kept.shape[0]
                kept_probs[slot, pl.ds(start * pair + at, rows), :] = kept
                result += dot(values_across[:, at : at + rows], kept, NN)
                at += rows
            result = result.T.astype(bf16)
            attended_a[mine, cut] = result[:block]
            attended_b[mine, cut] = result[block:]
        copy_of(head).start()
        return 0

    lax.fori_loop(0, heads, one_head, 0)
    for head in range(max(0, heads - 2), heads):
        copy_of(head).wait()


def attend_all(queries, keys, values, places, query_place, groups, clip_length, clips):
    half, width = keys[0].shape
    heads = width // HEAD_DIM
    pair = 2 * block_of(half)
    deep = reaches(half, groups)[1] * pair
    outs = pl.pallas_call(
        partial(
            all_forward_kernel,
            groups=groups,
            scale=1.0 / math.sqrt(HEAD_DIM),
            clip_length=clip_length,
            clips=clips,
        ),
        in_specs=[pl.BlockSpec(memory_space=pltpu.VMEM)] * 9,
        out_specs=[pl.BlockSpec(memory_space=pltpu.VMEM)] * 2
        + [pl.BlockSpec(memory_space=pl.ANY)],
        out_shape=[jax.ShapeDtypeStruct((half, width), bf16)] * 2
        + [pltpu.HBM((heads, deep, pair), bf16)],
        scratch_shapes=[
            pltpu.VMEM((2, deep, pair), bf16),
            pltpu.SemaphoreType.DMA((2,)),
        ],
        compiler_params=params(max(10, half * half // 2**14)),
        cost_estimate=cost(16 * half * half * width, 16 * half * width, 4 * half * half * heads),
        name="attend_all",
    )(*queries, *keys, *values, *places, query_place)
    return outs[:2], outs[2]


STEP = 2


def backward_kernel(*refs, count, groups, scale):
    grad_pieces = refs[:count]
    query_a, query_b, key_a, key_b, value_a, value_b, attended_a, attended_b, stored = refs[
        count : count + 9
    ]
    outs = refs[count + 9 : count + 18]
    grad_query, grad_key, grad_value = outs[0:2], outs[2:4], outs[4:6]
    own_query, own_key, own_value = outs[6:9]
    (scores,) = refs[count + 18 :]
    half, width = key_a.shape
    rows = half // count
    group_rows = rows // groups
    block = block_of(half)
    blocks = half // block
    pair = 2 * block
    reach = reaches(half, groups)[0]

    def sources(index):
        found = []
        if groups == 1:
            for d in range(index * block // rows, (index + 1) * block // rows):
                found.append((d, 0, rows))
            return found
        each = count * group_rows
        for j in range(index * block // each, (index + 1) * block // each):
            for d in range(count):
                found.append((d, j * group_rows, group_rows))
        return found

    def one_head(head, _):
        cut = columns_of(head)

        def keep(targets, own, values, index):
            for side in range(2):
                at = side * block
                targets[side][pl.ds(index * block, block), cut] = values[at : at + block]
                for d, start, size in sources(index):
                    if d == 0:
                        own[pl.ds(side * rows + start, size), cut] = values[at : at + size]
                    at += size

        def take_grads(index):
            return jnp.concatenate(
                [
                    grad_pieces[d][pl.ds(side * rows + start, size), cut]
                    for side in range(2)
                    for d, start, size in sources(index)
                ],
                axis=0,
            )

        keys_across = take(key_a, key_b, 0, blocks, cut).T
        ones = jnp.ones((8, HEAD_DIM), bf16)
        for index, (seen, _, start) in enumerate(reach):
            result = take(attended_a, attended_b, index, index + 1, cut)
            grad = take_grads(index)
            product = grad.astype(f32) * result.astype(f32)
            high = product.astype(bf16)
            low = (product - high.astype(f32)).astype(bf16)
            delta = (dot(ones, high, NT) + dot(ones, low, NT))[0:1, :]
            back = 0.0
            for low_block in range(0, seen, STEP):
                high_block = min(low_block + STEP, seen)
                at = pl.ds((start + low_block) * pair, (high_block - low_block) * pair)
                values = take(value_a, value_b, low_block, high_block, cut)
                score = stored[head, at, :].astype(f32) * (dot(values, grad, NT) - delta)
                score = score.astype(bf16)
                scores[at, :] = score
                back += dot(keys_across[:, low_block * pair : high_block * pair], score, NN)
            keep(grad_query, own_query, (back * scale).T.astype(bf16), index)
        for index in range(blocks):
            key_sum, value_sum = 0.0, 0.0
            for other, (seen, _, start) in enumerate(reach):
                if index < seen:
                    at = pl.ds((start + index) * pair, pair)
                    query = take(query_a, query_b, other, other + 1, cut)
                    key_sum += dot(scores[at, :], query, NN)
                    value_sum += dot(stored[head, at, :], take_grads(other), NN)
            keep(grad_key, own_key, (key_sum * scale).astype(bf16), index)
            keep(grad_value, own_value, value_sum.astype(bf16), index)
        return 0

    lax.fori_loop(0, width // HEAD_DIM, one_head, 0)


def attend_back(grads, queries, keys, values, attended, stored, groups):
    half, width = keys[0].shape
    count = len(grads)
    rows = grads[0].shape[0]
    outs = pl.pallas_call(
        partial(
            backward_kernel,
            count=count,
            groups=groups,
            scale=1.0 / math.sqrt(HEAD_DIM),
        ),
        in_specs=[pl.BlockSpec(memory_space=pltpu.VMEM)] * (count + 9),
        out_specs=[pl.BlockSpec(memory_space=pltpu.VMEM)] * 9,
        out_shape=[jax.ShapeDtypeStruct((half, width), bf16)] * 6
        + [jax.ShapeDtypeStruct((rows, width), bf16)] * 3,
        scratch_shapes=[pltpu.VMEM(stored.shape[1:], bf16)],
        compiler_params=params(8 + 2 * stored.shape[1] * stored.shape[2] // 2**20),
        cost_estimate=cost(8 * 4 * half * half * width, 32 * half * width + 2 * stored.size),
        name="attend_back",
    )(*grads, *queries, *keys, *values, *attended, stored)
    return outs[0:2], outs[2:4], outs[4:6], outs[6:9]


def body(
    inputs,
    first_gain,
    query_weight,
    key_weight,
    value_weight,
    output_weight,
    second_gain,
    up_weight,
    down_weight,
    frame_sizes,
    text_counts,
    action_counts,
    cotangent,
):
    shards = lax.axis_size("seq")
    shard_index = lax.axis_index("seq")
    core = lax.axis_index("mlp") % 2
    length, width = inputs.shape
    total = length * shards
    half = length // 2
    piece = half // shards
    clips = frame_sizes.shape[0]
    clip_length = total // clips
    part = width // shards
    groups = shards if piece % 8 == 0 else 1

    def halves(rows):
        cut = rows.reshape(2, piece, shards, width)
        mine = lax.dynamic_index_in_dim(cut, core, 0, keepdims=False)
        other = lax.dynamic_index_in_dim(cut, 1 - core, 0, keepdims=False)
        return (
            mine.transpose(1, 0, 2).reshape(half, width),
            other.transpose(1, 0, 2).reshape(half, width),
        )

    inputs_half, inputs_other = halves(inputs)
    pieces = gather_early(inputs_half)
    arrived = pieces[inner_size() :: inner_size()]

    place_a, place_b, kind_a, kind_b, query_place, own_place, own_kind = tables(
        frame_sizes, text_counts, action_counts, shards, length, groups
    )
    places, kinds = (place_a, place_b), (kind_a, kind_b)
    half_kind = own_kind[:half]
    own_normed = own_norm(
        jnp.concatenate([inputs_half, inputs_other], axis=0), first_gain, own_kind
    )
    grad_half, grad_other = halves(cotangent)
    grad_own = jnp.concatenate([grad_half, grad_other], axis=0)
    (query_own,) = project_rows(after(own_normed, arrived), query_weight)
    grad_far = gather_outer(after(grad_half, arrived, pieces[inner_size() + 1]))
    pieces = after(pieces, query_own)

    normed = [norm_pieces(pieces, first_gain, kind_a, groups)]
    normed[0], grad_far = after((normed[0], grad_far), normed[0])
    normed.append(swap(normed[0], "mlp", 1))
    keys, values = zip(*[project_rows(rows, key_weight, value_weight) for rows in normed])
    heads_own = attend(query_own, keys, values, places, own_place, clip_length, clips)
    grad_inner = gather_inner(after(grad_half, normed[0]))
    heads_own, grad_inner = after((heads_own, grad_inner), heads_own)
    grad_far = join_x(jnp.concatenate(grad_far, axis=0), heads_own)
    mine, other = product_halves([heads_own], [output_weight], NN)
    other, grad_far = after((other, grad_far), other)
    grad_inner += gather_inner(grad_far)
    low, other = pair_mlp(mine, other)
    own_activated_grad = grad_activated(after(grad_own, low), down_weight)
    queries = [
        project_rows(rows, query_weight)[0] for rows in after(normed, own_activated_grad)
    ]
    other = after(other, queries)
    residual, lifted_half = lift(inputs_half, low, other, second_gain, half_kind)

    lifted_own = both(lifted_half)
    activated_own, hidden_own, mine, other = feed_own(lifted_own, up_weight, own_activated_grad)
    lifted_far = gather_outer(after(lifted_half, other))
    other, grad_inner = after((other, grad_inner), other)
    low, other = pair_mlp(mine, other)
    attended, stored = attend_all(
        after(queries, low),
        keys,
        values,
        places,
        query_place,
        groups,
        clip_length,
        clips,
    )
    other, lifted_far = after((other, lifted_far), attended)
    grad_residual, mixed_half, mixed_columns = middle(
        residual, low, other, grad_half, second_gain, half_kind, shards
    )
    heads_grad = product_back(both(mixed_half), output_weight)

    heads_first = gather_first(heads_grad)
    lifted_far = jnp.concatenate(lifted_far, axis=0)
    lifted_inner_far = gather_inner(lifted_far)
    down_mine, down_other = down_own(after(activated_own, heads_grad), down_weight)
    lifted_far = join_x(lifted_far, heads_first[1], down_other, lifted_inner_far)
    heads_grads = gather_pieces(*heads_first)
    first_lifted, first_grads = with_core([lifted_far]), with_core([grad_far])
    first_lifted = after(first_lifted, heads_grads[inner_size() + 1])
    own = (lifted_own, grad_own, activated_own, hidden_own)
    sums = feed_all(first_lifted, first_grads, up_weight, down_weight, shards, own=own)
    down_low, down_other = pair_mlp(down_mine, down_other)
    heads_grads, down_low, down_other = after((heads_grads, down_low, down_other), sums)
    inner = inner_size()
    columns_far = {
        outer: swap(after(mixed_columns[outer : outer + inner], sums), "seq", outer)
        for outer in range(inner, shards, inner)
    }
    lifted_inner = gather_inner(after(lifted_half, down_other))
    query_low, key_low, value_low, own_low = attend_back(
        heads_grads, queries, keys, values, attended, stored, groups
    )
    attention_weights = (query_weight, key_weight, value_weight)
    lifted_inner += [join_x(far, own_low) for far in lifted_inner_far]
    own_low, lifted_inner, columns_far = after((own_low, lifted_inner, columns_far), own_low)
    low, other = pair_mlp(*product_halves(own_low, attention_weights, NT))

    query_grad, key_grad, value_grad, first_gain_grad = project(
        normed,
        after((query_low, key_low, value_low), low),
        attention_weights,
        first_gain,
        kinds,
        shards,
    )
    columns_far = after(columns_far, low)
    columns_far[0] = after(mixed_columns[:inner], low)
    columns = {}
    for outer, came in columns_far.items():
        columns[outer] = came[0]
        for bit in range(1, inner):
            columns[outer | bit] = swap(came[bit], "seq", bit)
    other, columns = after((other, columns), query_grad)
    first_gain_grad = after(first_gain_grad, other)
    first_gain_grad = first_gain_grad + swap(first_gain_grad, "mlp", 1)
    input_half = last(inputs_half, low, other, grad_residual, first_gain, half_kind, shards)
    outputs_half = finish(residual, down_low, after(down_other, input_half), shards)
    rest_lifted = with_core(after(lifted_inner, other))
    rest_grads = with_core(after(grad_inner, other))
    up_grad, down_grad = feed_all(
        after(rest_lifted, outputs_half, first_gain_grad), rest_grads, up_weight, down_weight, shards, sums
    )
    bit = 2
    while bit < lax.axis_size("mlp"):
        came = after(swap(first_gain_grad, "mlp", bit), up_grad)
        first_gain_grad = first_gain_grad + came
        bit *= 2
    placed = (input_half, outputs_half)
    input_grad, outputs = place_halves(placed, [swap(array, "mlp", 1) for array in placed])
    mixed_part = jnp.stack([after(columns[d], up_grad) for d in range(shards)])
    output_grad, second_gain_grad = output_part(
        attended, (mixed_part, swap(mixed_part, "mlp", 1)), groups
    )

    return (
        outputs,
        input_grad,
        first_gain_grad,
        query_grad,
        key_grad,
        value_grad,
        output_grad,
        second_gain_grad,
        up_grad,
        down_grad,
    )


def solution(mesh):
    return jax.shard_map(
        body,
        mesh=mesh,
        in_specs=(
            P("seq", None),
            P(),
            P(None, "mlp"),
            P(None, "mlp"),
            P(None, "mlp"),
            P("mlp", None),
            P(),
            P(None, "mlp"),
            P("mlp", None),
            P(),
            P(),
            P(),
            P("seq", None),
        ),
        out_specs=(
            P("seq", None),
            P("seq", None),
            P(None, "seq"),
            P("seq", "mlp"),
            P("seq", "mlp"),
            P("seq", "mlp"),
            P("mlp", "seq"),
            P(None, "seq"),
            P("seq", "mlp"),
            P("mlp", "seq"),
        ),
        check_vma=False,
    )
```

```python
from functools import partial
import math

import jax
import jax.numpy as jnp
from jax import lax
from jax.experimental import pallas as pl
from jax.experimental.pallas import tpu as pltpu
from jax.sharding import PartitionSpec as P

HEAD_DIM = 128
epsilon = 1e-05
bf16 = jnp.bfloat16
f32 = jnp.float32
NEGATIVE = -1e30

WHOLE = pl.BlockSpec(memory_space=pltpu.VMEM)
NN = ((1,), (0,))
NT = ((1,), (1,))
TN = ((0,), (0,))


def dot(a, b, dims):
    return lax.dot_general(a, b, (dims, ((), ())), preferred_element_type=f32)


def params(mebibytes):
    return pltpu.CompilerParams(vmem_limit_bytes=mebibytes * 1024 * 1024)


def cost(flops, moved, transcendentals=0, share=100):
    return pl.CostEstimate(
        flops=int(flops) // share,
        bytes_accessed=int(moved) // share,
        transcendentals=int(transcendentals) // share,
    )


def swap(value, axis, bit):
    size = lax.axis_size(axis)
    return lax.ppermute(value, axis, [(i, i ^ bit) for i in range(size)])


def inner_size():
    return 1 << (int(math.log2(lax.axis_size("seq"))) // 2)


def x_size():
    return lax.axis_size("mlp") // 2


def after(values, *earlier):
    return lax.optimization_barrier((values, earlier))[0]


def in_hbm(array):
    return pltpu.with_memory_space_constraint(array, pltpu.HBM)


def own_quarter(half):
    rows = half.shape[0] // x_size()
    return lax.dynamic_slice_in_dim(half, (lax.axis_index("mlp") // 2) * rows, rows, 0)


def join_x(quarter, *earlier):
    bit = 1
    while bit < x_size():
        came = after(swap(quarter, "mlp", 2 * bit), earlier)
        quarter = jnp.concatenate([quarter, came], axis=0)
        bit *= 2
    return quarter


def gather_early(half):
    size, inner = lax.axis_size("seq"), inner_size()
    quarter = own_quarter(half)
    pieces = {0: half}
    far = {outer: swap(quarter, "seq", outer) for outer in range(inner, size, inner)}
    for bit in range(1, inner):
        pieces[bit] = swap(half, "seq", bit)
    for outer in range(inner, size, inner):
        pieces[outer] = join_x(far[outer])
        for bit in range(1, inner):
            pieces[outer | bit] = swap(pieces[outer], "seq", bit)
    return [pieces[d] for d in range(size)]


def gather_outer(half):
    size, inner = lax.axis_size("seq"), inner_size()
    quarter = own_quarter(half)
    return [swap(quarter, "seq", outer) for outer in range(inner, size, inner)]


def gather_inner(array):
    return [swap(array, "seq", bit) for bit in range(1, inner_size())]


def with_core(arrays):
    return [each for array in arrays for each in (array, swap(array, "mlp", 1))]


def gather_first(piece):
    size, inner = lax.axis_size("seq"), inner_size()
    pieces = {0: piece}
    for bit in range(1, inner):
        pieces[bit] = swap(piece, "seq", bit)
    return pieces, [swap(piece, "seq", outer) for outer in range(inner, size, inner)]


def gather_pieces(pieces, far):
    size, inner = lax.axis_size("seq"), inner_size()
    for outer, came in zip(range(inner, size, inner), far):
        pieces[outer] = came
        for bit in range(1, inner):
            pieces[outer | bit] = swap(came, "seq", bit)
    return [pieces[d] for d in range(size)]


def rounded(value):
    return lax.optimization_barrier(value.astype(bf16))


def pair_mlp(mine, other_half):
    low, other = rounded(mine + swap(other_half, "mlp", 1).astype(f32)), None
    bit = 2
    while bit < lax.axis_size("mlp"):
        if other is not None:
            low = rounded(low.astype(f32) + other.astype(f32))
        other = swap(low, "mlp", bit)
        bit *= 2
    if other is None:
        other = jnp.zeros_like(low)
    return low, other


def both(half):
    return jnp.concatenate([half, swap(half, "mlp", 1)], axis=0)


def tables_kernel(index, frames, texts, actions, *outs, shards, length, groups, clip_length):
    place_a, place_b, kind_a, kind_b, query_place, own_place, own_kind = outs
    shard_index, core = index[0], index[1]
    shape = (shards, length)
    place = lax.broadcasted_iota(jnp.int32, shape, 0) * length + lax.broadcasted_iota(
        jnp.int32, shape, 1
    )
    kinds = jnp.full(shape, 2, jnp.int32)
    for clip in range(frames.shape[0]):
        start = jnp.int32(clip * clip_length)
        within = (place >= clip * clip_length) & (place < (clip + 1) * clip_length)
        for frame in range(frames.shape[1]):
            text_end = start + texts[clip, frame]
            action_end = text_end + actions[clip, frame]
            kinds = jnp.where(within & (place >= start) & (place < text_end), 0, kinds)
            kinds = jnp.where(within & (place >= text_end) & (place < action_end), 1, kinds)
            start = action_end + frames[clip, frame]
    square = (length, length)
    down = lax.broadcasted_iota(jnp.int32, square, 0)
    across = lax.broadcasted_iota(jnp.int32, square, 1)
    earlier = (down < across).astype(f32).astype(bf16)
    rank = jnp.zeros(shape, f32)
    before = jnp.zeros((shards, 1), f32)
    for kind in range(3):
        chosen = (kinds == kind).astype(f32)
        rank += chosen * (dot(chosen.astype(bf16), earlier, NN) + before)
        before += chosen.sum(axis=1, keepdims=True)
    rank_low, kinds_low = rank.astype(bf16), kinds.astype(f32).astype(bf16)
    piece = length // shards // 2
    lane = lax.broadcasted_iota(jnp.int32, (1, length), 1).astype(f32)

    def find(shard, offset, side, row):
        wanted = (shard_index ^ offset) * (2 * piece) + (core ^ side) * piece + row
        pick = shard == lax.broadcasted_iota(jnp.int32, (length, shards), 1)
        pick = pick.astype(f32).astype(bf16)
        hit = dot(pick, rank_low, NN) == wanted.astype(f32)
        where = jnp.sum(jnp.where(hit, lane, 0.0), axis=1, keepdims=True).astype(jnp.int32)
        kind = jnp.sum(jnp.where(hit, dot(pick, kinds_low, NN), 0.0), axis=1, keepdims=True)
        return where + shard * length, kind.astype(jnp.int32)

    def as_row(column):
        return jnp.sum(jnp.where(down == across, column, 0), axis=0, keepdims=True)

    step = lax.broadcasted_iota(jnp.int32, (length, 1), 0)
    half = length // 2
    for side, (place_out, kind_out) in enumerate(((place_a, kind_a), (place_b, kind_b))):
        for block in range(shards // 2):
            token = step + block * length
            if groups > 1:
                shard, offset = token // (shards * piece), (token // piece) % shards
            else:
                offset, shard = token // half, (token % half) // piece
            where, kind = find(shard, offset, side, token % piece)
            at = pl.ds(block * length, length)
            place_out[at, :] = where
            kind_out[at, :] = kind
            query_place[:, pl.ds((2 * block + side) * length, length)] = as_row(where)
    where, kind = find((step % half) // piece, step * 0, step // half, step % piece)
    own_place[...] = as_row(where)
    own_kind[...] = kind


def tables(frames, texts, actions, shards, length, groups):
    index = jnp.stack([lax.axis_index("seq"), lax.axis_index("mlp") % 2]).astype(jnp.int32)
    total = shards * length
    column = jax.ShapeDtypeStruct((total // 2, 1), jnp.int32)
    return pl.pallas_call(
        partial(
            tables_kernel,
            shards=shards,
            length=length,
            groups=groups,
            clip_length=total // frames.shape[0],
        ),
        in_specs=[pl.BlockSpec(memory_space=pltpu.SMEM)] * 4,
        out_shape=[column] * 4
        + [
            jax.ShapeDtypeStruct((1, total), jnp.int32),
            jax.ShapeDtypeStruct((1, length), jnp.int32),
            jax.ShapeDtypeStruct((length, 1), jnp.int32),
        ],
        cost_estimate=cost(8 * total * length, 8 * 128 * total),
        name="tables",
    )(index, frames, texts, actions)


def rows_kernel(*refs, count):
    rows, weights, outs = refs[0], refs[1 : 1 + count], refs[1 + count :]
    for weight, out in zip(weights, outs):
        out[...] = dot(rows[...], weight[...], NN).astype(bf16)


def project_rows(rows, *weights):
    across = weights[0].shape[1]
    return pl.pallas_call(
        partial(rows_kernel, count=len(weights)),
        out_shape=[jax.ShapeDtypeStruct((rows.shape[0], across), bf16)] * len(weights),
        compiler_params=params(8),
        cost_estimate=cost(2 * rows.size * across * len(weights), 2 * rows.size),
        name="project_rows",
    )(rows, *weights)


def one_kernel(rows, weight, out):
    out[...] = dot(rows[...], weight[...], NT).astype(bf16)


def product_back(rows, weight):
    return pl.pallas_call(
        one_kernel,
        out_shape=jax.ShapeDtypeStruct((rows.shape[0], weight.shape[0]), bf16),
        compiler_params=params(6),
        cost_estimate=cost(2 * rows.size * weight.shape[0], 2 * weight.size),
        name="product_back",
    )(rows, weight)


def halves_kernel(*refs, count, dims):
    mine, other = refs[-2:]
    half = mine.shape[0]
    total = sum(dot(refs[k][...], refs[count + k][...], dims) for k in range(count))
    mine[...] = total[:half]
    other[...] = total[half:].astype(bf16)


def product_halves(rows, weights, dims):
    count = len(rows)
    half = rows[0].shape[0] // 2
    across = weights[0].shape[1 - dims[1][0]]
    shape = (half, across)
    return pl.pallas_call(
        partial(halves_kernel, count=count, dims=dims),
        out_shape=[jax.ShapeDtypeStruct(shape, f32), jax.ShapeDtypeStruct(shape, bf16)],
        compiler_params=params(6),
        cost_estimate=cost(2 * count * rows[0].size * across, 2 * count * weights[0].size),
        name="product_halves",
    )(*rows, *weights)


def down_own_kernel(rows, weight, mine, other, total):
    total[...] = jnp.zeros_like(total)

    def step(at):
        total[...] += dot(rows[:, at], weight[at, :], NN)

    tiles_of(weight.shape[0], math.gcd(weight.shape[0], 512), step)
    half = mine.shape[0]
    mine[...] = total[:half]
    other[...] = total[half:].astype(bf16)


def down_own(rows, weight):
    count, deep = rows.shape
    across = weight.shape[1]
    shape = (count // 2, across)
    return pl.pallas_call(
        down_own_kernel,
        in_specs=[WHOLE] * 2,
        out_specs=[WHOLE] * 2,
        out_shape=[jax.ShapeDtypeStruct(shape, f32), jax.ShapeDtypeStruct(shape, bf16)],
        scratch_shapes=[pltpu.VMEM((count, across), f32)],
        compiler_params=params(6),
        cost_estimate=cost(2 * rows.size * across, 2 * weight.size),
        name="down_own",
    )(rows, weight)


def gain_rows(gain, column):
    return jnp.where(
        column == 0, gain[0:1, :], jnp.where(column == 1, gain[1:2, :], gain[2:3, :])
    )


def normalize(values):
    mean = jnp.mean(values, axis=1, keepdims=True)
    centered = values - mean
    inverse = lax.rsqrt(jnp.mean(centered * centered, axis=1, keepdims=True) + epsilon)
    return (centered * inverse, inverse)


def norm_back(grad, normal, inverse, gains):
    scaled = grad * gains
    return inverse * (
        scaled
        - jnp.mean(scaled, axis=1, keepdims=True)
        - normal * jnp.mean(scaled * normal, axis=1, keepdims=True)
    )


def norm_kernel(*refs, groups, inner, parts):
    index, gain, kind, out = refs[0], refs[-3], refs[-2], refs[-1]
    pieces = refs[1:-3]
    rows, width = pieces[0].shape
    count = len(pieces)
    step = rows // parts
    for d, piece in enumerate(pieces):
        for part in range(parts):
            normal, _ = normalize(piece[pl.ds(part * step, step), :].astype(f32))
            place = part if d < inner else part ^ index[0]
            if groups > 1:
                each = groups // parts
                at = pl.ds(place * each, each)
                column = kind[at, d].reshape(step, 1)
                normed = (normal * gain_rows(gain, column)).astype(bf16)
                out[at, d] = normed.reshape(each, rows // groups, width)
            else:
                column = kind[d, place]
                out[d, place] = (normal * gain_rows(gain, column)).astype(bf16)


def norm_pieces(pieces, gain, kind, groups):
    rows, width = pieces[0].shape
    count = len(pieces)
    parts = x_size()
    if groups > 1:
        shape = (groups, count, rows // groups)
    else:
        shape = (count, parts, rows // parts)
    memory = [pl.BlockSpec(memory_space=pltpu.SMEM)]
    index = (lax.axis_index("mlp") // 2).astype(jnp.int32).reshape(1)
    out = pl.pallas_call(
        partial(norm_kernel, groups=groups, inner=inner_size(), parts=parts),
        in_specs=memory + [pl.BlockSpec(memory_space=pltpu.VMEM)] * (count + 2),
        out_shape=jax.ShapeDtypeStruct(shape + (width,), bf16),
        compiler_params=params(4 + count),
        cost_estimate=cost(10 * count * rows * width, 4 * count * rows * width),
        name="norm_pieces",
    )(index, *pieces, gain, kind.reshape(shape + (1,)))
    return out.reshape(count * rows, width)


def own_norm_kernel(rows, gain, kind, out):
    normal, _ = normalize(rows[...].astype(f32))
    out[...] = (normal * gain_rows(gain, kind[...])).astype(bf16)


def own_norm(rows, gain, kind):
    return pl.pallas_call(
        own_norm_kernel,
        out_shape=jax.ShapeDtypeStruct(rows.shape, bf16),
        compiler_params=params(4),
        cost_estimate=cost(10 * rows.size, 4 * rows.size),
        name="own_norm",
    )(rows, gain, kind)


def lift_kernel(rows, low, other, gain, kind, residual, lifted):
    value = rows[...].astype(f32) + (low[...].astype(f32) + other[...].astype(f32))
    residual[...] = value
    normal, _ = normalize(value)
    lifted[...] = (normal * gain_rows(gain, kind[...])).astype(bf16)


def lift(rows, low, other, gain, kind):
    return pl.pallas_call(
        lift_kernel,
        in_specs=[WHOLE] * 5,
        out_specs=[WHOLE] * 2,
        out_shape=[jax.ShapeDtypeStruct(rows.shape, f32), jax.ShapeDtypeStruct(rows.shape, bf16)],
        compiler_params=params(4),
        cost_estimate=cost(10 * rows.size, 12 * rows.size),
        name="lift",
    )(rows, low, other, gain, kind)


def kind_sums(term, kind):
    sums = [jnp.sum(jnp.where(kind == k, term, 0.0), axis=0, keepdims=True) for k in range(3)]
    high = [value.astype(bf16) for value in sums]
    low = [(value - part.astype(f32)).astype(bf16) for value, part in zip(sums, high)]
    zero = jnp.zeros((1, term.shape[1]), bf16)
    return jnp.concatenate(high + low + [zero, zero], axis=0)


def middle_kernel(index, residual, low, other, grad, gain, kind, grad_residual, mixed, parts):
    lifted_grad = low[...].astype(f32) + other[...].astype(f32)
    normal, inverse = normalize(residual[...])
    column = kind[...]
    back = norm_back(lifted_grad, normal, inverse, gain_rows(gain, column))
    value = grad[...].astype(f32) + back
    grad_residual[...] = value
    rounded_value = value.astype(bf16)
    mixed[...] = rounded_value
    sums = kind_sums(lifted_grad * normal, column)
    shards, rows, part = parts.shape
    for k in range(shards):
        at = index[0] ^ k
        parts[at, pl.ds(0, rows - 8), :] = rounded_value[:, k * part : (k + 1) * part]
        parts[at, pl.ds(rows - 8, 8), :] = sums[:, k * part : (k + 1) * part]


def middle(residual, low, other, grad, gain, kind, shards):
    rows, width = residual.shape
    index = lax.axis_index("seq").astype(jnp.int32).reshape(1)
    return pl.pallas_call(
        middle_kernel,
        in_specs=[pl.BlockSpec(memory_space=pltpu.SMEM)] + [WHOLE] * 6,
        out_specs=[WHOLE] * 3,
        out_shape=[
            jax.ShapeDtypeStruct(residual.shape, f32),
            jax.ShapeDtypeStruct(residual.shape, bf16),
            jax.ShapeDtypeStruct((shards, rows + 8, width // shards), bf16),
        ],
        compiler_params=params(6),
        cost_estimate=cost(20 * residual.size, 16 * residual.size),
        name="middle",
    )(index, residual, low, other, grad, gain, kind)


def reordered(values, shards):
    count = values.shape[0]
    piece = count // shards
    to = lax.broadcasted_iota(jnp.int32, (count, count), 0)
    source = lax.broadcasted_iota(jnp.int32, (count, count), 1)
    pick = (source == (to % shards) * piece + to // shards).astype(f32).astype(bf16)
    return dot(pick, values, NN).astype(bf16)


def finish_kernel(residual, low, other, out, *, shards):
    value = residual[...] + (low[...].astype(f32) + other[...].astype(f32))
    out[...] = reordered(value.astype(bf16), shards)


def finish(residual, low, other, shards):
    return pl.pallas_call(
        partial(finish_kernel, shards=shards),
        in_specs=[WHOLE] * 3,
        out_specs=WHOLE,
        out_shape=jax.ShapeDtypeStruct(residual.shape, bf16),
        compiler_params=params(4),
        cost_estimate=cost(2 * residual.size, 10 * residual.size),
        name="finish",
    )(residual, low, other)


def place_kernel(index, *refs):
    count = len(refs) // 3
    for mine, other, out in zip(refs[:count], refs[count : 2 * count], refs[2 * count :]):
        half = mine.shape[0]
        out[pl.ds(pl.multiple_of(index[0] * half, half), half), :] = mine[...]
        out[pl.ds(pl.multiple_of((1 - index[0]) * half, half), half), :] = other[...]


def place_halves(arrays, others):
    half, width = arrays[0].shape
    index = (lax.axis_index("mlp") % 2).astype(jnp.int32).reshape(1)
    return pl.pallas_call(
        place_kernel,
        in_specs=[pl.BlockSpec(memory_space=pltpu.SMEM)] + [WHOLE] * (2 * len(arrays)),
        out_shape=[jax.ShapeDtypeStruct((2 * half, width), bf16)] * len(arrays),
        compiler_params=params(6),
        cost_estimate=cost(half * width, 16 * half * width),
        name="place_halves",
    )(index, *arrays, *others)


def last_kernel(rows, low, other, grad_residual, gain, kind, out, *, shards):
    grad = low[...].astype(f32) + other[...].astype(f32)
    normal, inverse = normalize(rows[...].astype(f32))
    back = norm_back(grad, normal, inverse, gain_rows(gain, kind[...]))
    out[...] = reordered((grad_residual[...] + back).astype(bf16), shards)


def last(rows, low, other, grad_residual, gain, kind, shards):
    return pl.pallas_call(
        partial(last_kernel, shards=shards),
        in_specs=[WHOLE] * 6,
        out_specs=WHOLE,
        out_shape=jax.ShapeDtypeStruct(rows.shape, bf16),
        compiler_params=params(6),
        cost_estimate=cost(20 * rows.size, 12 * rows.size),
        name="last",
    )(rows, low, other, grad_residual, gain, kind)


def gelu_parts(value):
    rate = math.sqrt(2 / math.pi)
    square = value * value
    bent = jnp.tanh(value * (rate + (rate * 0.044715) * square))
    upper = 0.5 * (1 + bent)
    slope = upper + (0.5 * value) * (1 - bent * bent) * (rate + (rate * 3 * 0.044715) * square)
    return value * upper, slope


def tiles_of(extent, tile, step):
    def at(t, _):
        step(pl.ds(pl.multiple_of(t * tile, tile), tile))
        return 0

    lax.fori_loop(0, extent // tile, at, 0)


def own_kernel(lifted, up, grad_activated, activated, hidden_grads, mine, other, total):
    total[...] = jnp.zeros_like(total)

    def step(at):
        value, slope = gelu_parts(dot(lifted[...], up[:, at], NN))
        activated[:, at] = value.astype(bf16)
        hidden_grad = (grad_activated[:, at] * slope).astype(bf16)
        hidden_grads[:, at] = hidden_grad
        total[...] += dot(hidden_grad, up[:, at], NT)

    tiles_of(up.shape[1], math.gcd(up.shape[1], 512), step)
    half = mine.shape[0]
    mine[...] = total[:half]
    other[...] = total[half:].astype(bf16)


def feed_own(lifted, up, grad_activated):
    rows, width = lifted.shape
    hidden = up.shape[1]
    return pl.pallas_call(
        own_kernel,
        in_specs=[WHOLE] * 3,
        out_specs=[WHOLE] * 4,
        out_shape=[jax.ShapeDtypeStruct((rows, hidden), bf16)] * 2
        + [
            jax.ShapeDtypeStruct((rows // 2, width), f32),
            jax.ShapeDtypeStruct((rows // 2, width), bf16),
        ],
        scratch_shapes=[pltpu.VMEM((rows, width), f32)],
        compiler_params=params(8),
        cost_estimate=cost(4 * rows * width * hidden, 2 * width * hidden),
        name="feed_own",
    )(lifted, up, grad_activated)


def down_kernel(grad, down, out):
    def step(at):
        out[:, at] = dot(grad[...], down[at, :], NT)

    tiles_of(down.shape[0], math.gcd(down.shape[0], 512), step)


def grad_activated(grad, down):
    rows, width = grad.shape
    hidden = down.shape[0]
    return pl.pallas_call(
        down_kernel,
        in_specs=[WHOLE] * 2,
        out_specs=WHOLE,
        out_shape=jax.ShapeDtypeStruct((rows, hidden), f32),
        compiler_params=params(6),
        cost_estimate=cost(2 * rows * width * hidden, 2 * width * hidden),
        name="grad_activated",
    )(grad, down)


def all_kernel(index, *refs, count):
    lifted_parts, grad_parts = refs[:count], refs[count : 2 * count]
    up, down = refs[2 * count : 2 * count + 2]
    before = refs[2 * count + 2 : -5]
    up_grad, down_grad, lifted_across, hidden_kept, grad_kept = refs[-5:]
    part = up_grad.shape[0]
    mine = pl.ds(pl.multiple_of(index[0] * part, part), part)

    def rows_of(parts, at):
        return jnp.concatenate([ref[:, at] for ref in parts], axis=0)

    @pl.when(pl.program_id(0) == 0)
    def _():
        lifted_across[...] = rows_of(lifted_parts, mine).T

    first = pl.program_id(0) == 0
    last_step = pl.num_programs(0) - 1

    tile = hidden_kept.shape[1]
    at = jnp.minimum(pl.program_id(0), last_step - 1) if up.shape[1] > tile else 0
    here = pl.ds(pl.multiple_of(at * tile, tile), tile)

    def products():
        everything = slice(None)
        return (
            dot(rows_of(lifted_parts, everything), up[:, here], NN),
            dot(rows_of(grad_parts, everything), down[here, :], NT),
        )

    def finish_tile(hidden_value, activated_grad):
        value, slope = gelu_parts(hidden_value)
        hidden_grad = (activated_grad * slope).astype(bf16)
        down_term = dot(value.astype(bf16), rows_of(grad_parts, mine), TN)
        up_term = dot(lifted_across[...], hidden_grad, NN)
        if len(before) == 2:
            up_term += before[0][...].astype(f32)
            down_term += before[1][...].astype(f32)
        else:
            lifted_own, grad_own, activated, hidden_own = before
            up_term += dot(lifted_own[...], hidden_own[...], TN)
            down_term += dot(activated[...], grad_own[...], TN)
        up_grad[...] = up_term.astype(up_grad.dtype)
        down_grad[...] = down_term.astype(down_grad.dtype)

    @pl.when(first)
    def _():
        hidden_kept[...], grad_kept[...] = products()

    @pl.when((pl.program_id(0) > 0) & (pl.program_id(0) < last_step))
    def _():
        kept = hidden_kept[...], grad_kept[...]
        fresh = products()
        finish_tile(*kept)
        hidden_kept[...], grad_kept[...] = fresh

    @pl.when(pl.program_id(0) == last_step)
    def _():
        finish_tile(hidden_kept[...], grad_kept[...])


def feed_all(lifted, grad, up, down, shards, sums=(), own=()):
    counts = [array.shape[0] for array in lifted]
    rows, width = sum(counts), lifted[0].shape[1]
    count = len(counts)
    part = width // shards
    hidden = up.shape[1]
    tile = math.gcd(hidden, 256)
    steps = hidden // tile
    across = lambda t, index: (0, jnp.maximum(t - 1, 0))
    below = lambda t, index: (jnp.maximum(t - 1, 0), 0)
    mine = lambda t, index: (0, index[0])
    sum_specs = [pl.BlockSpec((part, tile), across), pl.BlockSpec((tile, part), below)]
    if own:
        own_rows = own[0].shape[0]
        more = [pl.BlockSpec((own_rows, part), mine)] * 2
        more += [pl.BlockSpec((own_rows, tile), across)] * 2
    else:
        more = sum_specs
    index = lax.axis_index("seq").astype(jnp.int32).reshape(1)
    return pl.pallas_call(
        partial(all_kernel, count=count),
        grid_spec=pltpu.PrefetchScalarGridSpec(
            num_scalar_prefetch=1,
            grid=(steps + 1,),
            in_specs=[WHOLE] * (2 * count)
            + [WHOLE] * 2
            + more,
            out_specs=sum_specs,
            scratch_shapes=[pltpu.VMEM((part, rows), bf16)]
            + [pltpu.VMEM((rows, tile), f32)] * 2,
        ),
        out_shape=[
            pltpu.HBM((part, hidden), bf16 if own else f32),
            pltpu.HBM((hidden, part), bf16 if own else f32),
        ],
        compiler_params=params((6 if own else 8) + 8 * rows // 512),
        cost_estimate=cost(
            4 * rows * hidden * (width + part),
            4 * width * hidden + 4 * rows * width,
        ),
        name="feed_all",
    )(
        index,
        *lifted,
        *grad,
        up,
        down,
        *(own or [in_hbm(array) for array in sums]),
    )


def project_kernel(index, *refs):
    normed, lows, weights = refs[0:2], refs[2:8], refs[8:11]
    gain, kinds = refs[11], refs[12:14]
    outs, gain_grad = refs[14:17], refs[17]
    for k in range(3):
        outs[k][...] = sum(dot(normed[side][...], lows[2 * k + side][...], TN) for side in range(2))
    gain_sum = [0.0, 0.0, 0.0]
    for side in range(2):
        column = kinds[side][...]
        term = sum(dot(lows[2 * k + side][...], weights[k][...], NT) for k in range(3))
        term = term * (normed[side][...].astype(f32) / gain_rows(gain, column))
        for k in range(3):
            gain_sum[k] += jnp.sum(jnp.where(column == k, term, 0.0), axis=0, keepdims=True)
    gain_grad[...] = jnp.concatenate(gain_sum, axis=0)


def project(normed, lows, weights, gain, kinds, shards):
    rows, width = normed[0].shape
    across = lows[0][0].shape[1]
    part = width // shards
    whole = lambda t, index: (0, 0)
    mine = lambda t, index: (0, index[0])
    below = lambda t, index: (index[0], 0)
    index = lax.axis_index("seq").astype(jnp.int32).reshape(1)
    return pl.pallas_call(
        project_kernel,
        grid_spec=pltpu.PrefetchScalarGridSpec(
            num_scalar_prefetch=1,
            grid=(1,),
            in_specs=[pl.BlockSpec((rows, part), mine)] * 2
            + [pl.BlockSpec((rows, across), whole)] * 6
            + [pl.BlockSpec((part, across), below)] * 3
            + [pl.BlockSpec((gain.shape[0], part), mine)]
            + [pl.BlockSpec((rows, 1), whole)] * 2,
            out_specs=[pl.BlockSpec((part, across), whole)] * 3
            + [pl.BlockSpec((gain.shape[0], part), whole)],
        ),
        out_shape=[jax.ShapeDtypeStruct((part, across), f32)] * 3
        + [jax.ShapeDtypeStruct((gain.shape[0], part), f32)],
        compiler_params=params(8),
        cost_estimate=cost(24 * rows * part * across, 12 * rows * across + 12 * part * across),
        name="project",
    )(index, *normed, *[low for pair in lows for low in pair], *weights, gain, *kinds)


def output_kernel(
    attended_a, attended_b, came_a, came_b, first_mine, first_came, out, gain_grad, first, *, groups
):
    total, sums = 0.0, 0.0
    shards, rows, part = came_a.shape
    half = rows - 8
    each = half // groups
    for attended, came in ((attended_a, came_a), (attended_b, came_b)):
        mixed = [
            came[d, pl.ds(group * each, each), :]
            for group in range(groups)
            for d in range(shards)
        ]
        total += dot(attended[...], jnp.concatenate(mixed, axis=0), TN)
        own_sums = 0.0
        for k in range(shards):
            own_sums += came[k, pl.ds(half, 8), :].astype(f32)
        sums += own_sums
    out[...] = total
    gain_grad[...] = sums[0:3, :] + sums[3:6, :]
    first[...] = first_mine[...] + first_came[...]


def output_part(attended, came, first, groups):
    across, part = attended[0].shape[1], came[0].shape[2]
    return pl.pallas_call(
        partial(output_kernel, groups=groups),
        in_specs=[WHOLE] * 6,
        out_shape=[
            jax.ShapeDtypeStruct((across, part), f32),
        ]
        + [jax.ShapeDtypeStruct((3, part), f32)] * 2,
        compiler_params=params(6),
        cost_estimate=cost(
            4 * attended[0].shape[0] * across * part, 4 * attended[0].shape[0] * (across + part)
        ),
        name="output_part",
    )(*attended, *came, *first)


def mask_of(key_place, query_place, clip_length, clips):
    allowed = key_place <= query_place
    if clips > 1:
        allowed = allowed & (key_place // clip_length == query_place // clip_length)
    return allowed


def probabilities(scores, scale):
    top = scores[0].max(axis=0, keepdims=True)
    for block in scores[1:]:
        top = jnp.maximum(top, block.max(axis=0, keepdims=True))
    rate = scale * math.log2(math.e)
    weights = [jnp.exp2((block - top) * rate) for block in scores]
    total = weights[0].sum(axis=0, keepdims=True)
    for block in weights[1:]:
        total = total + block.sum(axis=0, keepdims=True)
    inverse = 1.0 / total
    return [block * inverse for block in weights]


def forward_kernel(query, key_a, key_b, value_a, value_b, place_a, place_b, query_place, out, **opts):
    scale = opts["scale"]
    query_place = query_place[...]
    allowed = [
        mask_of(place[...], query_place, opts["clip_length"], opts["clips"])
        for place in (place_a, place_b)
    ]
    for head in range(query.shape[1] // HEAD_DIM):
        at = pl.ds(head * HEAD_DIM, HEAD_DIM)
        scores = [
            jnp.where(mask, dot(key[:, at], query[:, at], NT), NEGATIVE)
            for mask, key in zip(allowed, (key_a, key_b))
        ]
        prob = [block.astype(bf16) for block in probabilities(scores, scale)]
        result = dot(value_a[:, at], prob[0], TN) + dot(value_b[:, at], prob[1], TN)
        out[:, at] = result.T.astype(bf16)


def attend(query, keys, values, places, query_place, clip_length, clips):
    rows, width = query.shape
    total = 2 * keys[0].shape[0]
    return pl.pallas_call(
        partial(
            forward_kernel, scale=1.0 / math.sqrt(HEAD_DIM), clip_length=clip_length, clips=clips
        ),
        out_shape=jax.ShapeDtypeStruct((rows, width), bf16),
        compiler_params=params(8),
        cost_estimate=cost(
            4 * rows * total * width, 4 * total * width, rows * total * (width // HEAD_DIM)
        ),
        name="attend",
    )(query, *keys, *values, *places, query_place)


def block_of(half):
    return min(128, half)


def reaches(half, groups):
    blocks = half // block_of(half)
    found, start = [], 0
    for index in range(blocks):
        seen, free = (index + 1, index) if groups > 1 else (blocks, 0)
        found.append((seen, free, start))
        start += seen
    return found, start


def take(first, second, low, high, at):
    block = block_of(first.shape[0])
    rows = [side[pl.ds(k * block, block), at] for k in range(low, high) for side in (first, second)]
    return jnp.concatenate(rows, axis=0)


def columns_of(head):
    return pl.ds(pl.multiple_of(head * HEAD_DIM, HEAD_DIM), HEAD_DIM)


def all_forward_kernel(*refs, groups, scale, clip_length, clips):
    query_a, query_b, key_a, key_b, value_a, value_b, place_a, place_b, query_place = refs[:9]
    attended_a, attended_b, stored, kept_probs, sems = refs[9:]
    half, width = key_a.shape
    heads = width // HEAD_DIM
    block = block_of(half)
    pair = 2 * block
    everything = slice(None)

    def copy_of(head):
        slot = head % 2
        return pltpu.make_async_copy(kept_probs.at[slot], stored.at[head], sems.at[slot])

    def one_head(head, _):
        cut = columns_of(head)
        slot = head % 2

        @pl.when(head >= 2)
        def _():
            copy_of(head - 2).wait()

        values_across = take(value_a, value_b, 0, half // block, cut).T
        for index, (seen, free, start) in enumerate(reaches(half, groups)[0]):
            mine = pl.ds(index * block, block)
            query = take(query_a, query_b, index, index + 1, cut)
            at_place = query_place[:, pl.ds(index * pair, pair)]
            place = take(place_a, place_b, free, seen, everything)
            mask = mask_of(place, at_place, clip_length, clips)
            score = dot(take(key_a, key_b, free, seen, cut), query, NT)
            scores = [jnp.where(mask, score, NEGATIVE)]
            if free:
                scores.insert(0, dot(take(key_a, key_b, 0, free, cut), query, NT))
            result, at = 0.0, 0
            for prob in probabilities(scores, scale):
                kept = prob.astype(bf16)
                rows = kept.shape[0]
                kept_probs[slot, pl.ds(start * pair + at, rows), :] = kept
                result += dot(values_across[:, at : at + rows], kept, NN)
                at += rows
            result = result.T.astype(bf16)
            attended_a[mine, cut] = result[:block]
            attended_b[mine, cut] = result[block:]
        copy_of(head).start()
        return 0

    lax.fori_loop(0, heads, one_head, 0)
    for head in range(max(0, heads - 2), heads):
        copy_of(head).wait()


def attend_all(queries, keys, values, places, query_place, groups, clip_length, clips):
    half, width = keys[0].shape
    heads = width // HEAD_DIM
    pair = 2 * block_of(half)
    deep = reaches(half, groups)[1] * pair
    outs = pl.pallas_call(
        partial(
            all_forward_kernel,
            groups=groups,
            scale=1.0 / math.sqrt(HEAD_DIM),
            clip_length=clip_length,
            clips=clips,
        ),
        in_specs=[pl.BlockSpec(memory_space=pltpu.VMEM)] * 9,
        out_specs=[pl.BlockSpec(memory_space=pltpu.VMEM)] * 2
        + [pl.BlockSpec(memory_space=pl.ANY)],
        out_shape=[jax.ShapeDtypeStruct((half, width), bf16)] * 2
        + [pltpu.HBM((heads, deep, pair), bf16)],
        scratch_shapes=[
            pltpu.VMEM((2, deep, pair), bf16),
            pltpu.SemaphoreType.DMA((2,)),
        ],
        compiler_params=params(max(10, half * half // 2**14)),
        cost_estimate=cost(16 * half * half * width, 16 * half * width, 4 * half * half * heads),
        name="attend_all",
    )(*queries, *keys, *values, *places, query_place)
    return outs[:2], outs[2]


STEP = 2


def backward_kernel(*refs, count, groups, scale):
    grad_pieces = refs[:count]
    query_a, query_b, key_a, key_b, value_a, value_b, attended_a, attended_b, stored = refs[
        count : count + 9
    ]
    outs = refs[count + 9 : count + 18]
    grad_query, grad_key, grad_value = outs[0:2], outs[2:4], outs[4:6]
    own_query, own_key, own_value = outs[6:9]
    (scores,) = refs[count + 18 :]
    half, width = key_a.shape
    rows = half // count
    group_rows = rows // groups
    block = block_of(half)
    blocks = half // block
    pair = 2 * block
    reach = reaches(half, groups)[0]

    def sources(index):
        found = []
        if groups == 1:
            for d in range(index * block // rows, (index + 1) * block // rows):
                found.append((d, 0, rows))
            return found
        each = count * group_rows
        for j in range(index * block // each, (index + 1) * block // each):
            for d in range(count):
                found.append((d, j * group_rows, group_rows))
        return found

    def one_head(head, _):
        cut = columns_of(head)

        def keep(targets, own, values, index):
            for side in range(2):
                at = side * block
                targets[side][pl.ds(index * block, block), cut] = values[at : at + block]
                for d, start, size in sources(index):
                    if d == 0:
                        own[pl.ds(side * rows + start, size), cut] = values[at : at + size]
                    at += size

        def take_grads(index):
            return jnp.concatenate(
                [
                    grad_pieces[d][pl.ds(side * rows + start, size), cut]
                    for side in range(2)
                    for d, start, size in sources(index)
                ],
                axis=0,
            )

        keys_across = take(key_a, key_b, 0, blocks, cut).T
        ones = jnp.ones((8, HEAD_DIM), bf16)
        for index, (seen, _, start) in enumerate(reach):
            result = take(attended_a, attended_b, index, index + 1, cut)
            grad = take_grads(index)
            product = grad.astype(f32) * result.astype(f32)
            high = product.astype(bf16)
            low = (product - high.astype(f32)).astype(bf16)
            delta = (dot(ones, high, NT) + dot(ones, low, NT))[0:1, :]
            back = 0.0
            for low_block in range(0, seen, STEP):
                high_block = min(low_block + STEP, seen)
                at = pl.ds((start + low_block) * pair, (high_block - low_block) * pair)
                values = take(value_a, value_b, low_block, high_block, cut)
                score = stored[head, at, :].astype(f32) * (dot(values, grad, NT) - delta)
                score = score.astype(bf16)
                scores[at, :] = score
                back += dot(keys_across[:, low_block * pair : high_block * pair], score, NN)
            keep(grad_query, own_query, (back * scale).T.astype(bf16), index)
        for index in range(blocks):
            key_sum, value_sum = 0.0, 0.0
            for other, (seen, _, start) in enumerate(reach):
                if index < seen:
                    at = pl.ds((start + index) * pair, pair)
                    query = take(query_a, query_b, other, other + 1, cut)
                    key_sum += dot(scores[at, :], query, NN)
                    value_sum += dot(stored[head, at, :], take_grads(other), NN)
            keep(grad_key, own_key, (key_sum * scale).astype(bf16), index)
            keep(grad_value, own_value, value_sum.astype(bf16), index)
        return 0

    lax.fori_loop(0, width // HEAD_DIM, one_head, 0)


def attend_back(grads, queries, keys, values, attended, stored, groups):
    half, width = keys[0].shape
    count = len(grads)
    rows = grads[0].shape[0]
    outs = pl.pallas_call(
        partial(
            backward_kernel,
            count=count,
            groups=groups,
            scale=1.0 / math.sqrt(HEAD_DIM),
        ),
        in_specs=[pl.BlockSpec(memory_space=pltpu.VMEM)] * (count + 9),
        out_specs=[pl.BlockSpec(memory_space=pltpu.VMEM)] * 9,
        out_shape=[jax.ShapeDtypeStruct((half, width), bf16)] * 6
        + [jax.ShapeDtypeStruct((rows, width), bf16)] * 3,
        scratch_shapes=[pltpu.VMEM(stored.shape[1:], bf16)],
        compiler_params=params(8 + 2 * stored.shape[1] * stored.shape[2] // 2**20),
        cost_estimate=cost(8 * 4 * half * half * width, 32 * half * width + 2 * stored.size),
        name="attend_back",
    )(*grads, *queries, *keys, *values, *attended, stored)
    return outs[0:2], outs[2:4], outs[4:6], outs[6:9]


def body(
    inputs,
    first_gain,
    query_weight,
    key_weight,
    value_weight,
    output_weight,
    second_gain,
    up_weight,
    down_weight,
    frame_sizes,
    text_counts,
    action_counts,
    cotangent,
):
    shards = lax.axis_size("seq")
    shard_index = lax.axis_index("seq")
    core = lax.axis_index("mlp") % 2
    length, width = inputs.shape
    total = length * shards
    half = length // 2
    piece = half // shards
    clips = frame_sizes.shape[0]
    clip_length = total // clips
    part = width // shards
    groups = shards if piece % 8 == 0 else 1

    def halves(rows):
        cut = rows.reshape(2, piece, shards, width)
        mine = lax.dynamic_index_in_dim(cut, core, 0, keepdims=False)
        other = lax.dynamic_index_in_dim(cut, 1 - core, 0, keepdims=False)
        return (
            mine.transpose(1, 0, 2).reshape(half, width),
            other.transpose(1, 0, 2).reshape(half, width),
        )

    inputs_half, inputs_other = halves(inputs)
    pieces = gather_early(inputs_half)
    arrived = pieces[inner_size() :: inner_size()]

    place_a, place_b, kind_a, kind_b, query_place, own_place, own_kind = tables(
        frame_sizes, text_counts, action_counts, shards, length, groups
    )
    places, kinds = (place_a, place_b), (kind_a, kind_b)
    half_kind = own_kind[:half]
    own_normed = own_norm(
        jnp.concatenate([inputs_half, inputs_other], axis=0), first_gain, own_kind
    )
    grad_half, grad_other = halves(cotangent)
    grad_own = jnp.concatenate([grad_half, grad_other], axis=0)
    (query_own,) = project_rows(after(own_normed, arrived), query_weight)
    grad_far = gather_outer(after(grad_half, arrived, pieces[inner_size() + 1]))
    pieces = after(pieces, query_own)

    normed = [norm_pieces(pieces, first_gain, kind_a, groups)]
    normed[0], grad_far = after((normed[0], grad_far), normed[0])
    normed.append(swap(normed[0], "mlp", 1))
    keys, values = zip(*[project_rows(rows, key_weight, value_weight) for rows in normed])
    heads_own = attend(query_own, keys, values, places, own_place, clip_length, clips)
    grad_inner = gather_inner(after(grad_half, normed[0]))
    heads_own, grad_inner = after((heads_own, grad_inner), heads_own)
    grad_far = join_x(jnp.concatenate(grad_far, axis=0), heads_own)
    mine, other = product_halves([heads_own], [output_weight], NN)
    other, grad_far = after((other, grad_far), other)
    grad_inner += gather_inner(grad_far)
    low, other = pair_mlp(mine, other)
    own_activated_grad = grad_activated(after(grad_own, low), down_weight)
    queries = [
        project_rows(rows, query_weight)[0] for rows in after(normed, own_activated_grad)
    ]
    other = after(other, queries)
    residual, lifted_half = lift(inputs_half, low, other, second_gain, half_kind)

    lifted_own = both(lifted_half)
    activated_own, hidden_own, mine, other = feed_own(lifted_own, up_weight, own_activated_grad)
    lifted_far = gather_outer(after(lifted_half, other))
    other, grad_inner = after((other, grad_inner), other)
    low, other = pair_mlp(mine, other)
    attended, stored = attend_all(
        after(queries, low),
        keys,
        values,
        places,
        query_place,
        groups,
        clip_length,
        clips,
    )
    other, lifted_far = after((other, lifted_far), attended)
    grad_residual, mixed_half, mixed_columns = middle(
        residual, low, other, grad_half, second_gain, half_kind, shards
    )
    heads_grad = product_back(both(mixed_half), output_weight)

    heads_first = gather_first(heads_grad)
    lifted_far = jnp.concatenate(lifted_far, axis=0)
    lifted_inner_far = gather_inner(lifted_far)
    down_mine, down_other = down_own(after(activated_own, heads_grad), down_weight)
    lifted_far = join_x(lifted_far, heads_first[1], down_other, lifted_inner_far)
    heads_grads = gather_pieces(*heads_first)
    first_lifted, first_grads = with_core([lifted_far]), with_core([grad_far])
    first_lifted = after(first_lifted, heads_grads[inner_size() + 1])
    own = (lifted_own, grad_own, activated_own, hidden_own)
    sums = feed_all(first_lifted, first_grads, up_weight, down_weight, shards, own=own)
    down_low, down_other = pair_mlp(down_mine, down_other)
    heads_grads, down_low, down_other = after((heads_grads, down_low, down_other), sums)
    inner = inner_size()
    columns_far = {
        outer: swap(after(mixed_columns[outer : outer + inner], sums), "seq", outer)
        for outer in range(inner, shards, inner)
    }
    lifted_inner = gather_inner(after(lifted_half, down_other))
    query_low, key_low, value_low, own_low = attend_back(
        heads_grads, queries, keys, values, attended, stored, groups
    )
    attention_weights = (query_weight, key_weight, value_weight)
    lifted_inner += [join_x(far, own_low) for far in lifted_inner_far]
    own_low, lifted_inner, columns_far = after((own_low, lifted_inner, columns_far), own_low)
    low, other = pair_mlp(*product_halves(own_low, attention_weights, NT))

    query_grad, key_grad, value_grad, first_gain_grad = project(
        normed,
        after((query_low, key_low, value_low), low),
        attention_weights,
        first_gain,
        kinds,
        shards,
    )
    columns_far = after(columns_far, low)
    columns_far[0] = after(mixed_columns[:inner], low)
    columns = {}
    for outer, came in columns_far.items():
        columns[outer] = came[0]
        for bit in range(1, inner):
            columns[outer | bit] = swap(came[bit], "seq", bit)
    other, columns = after((other, columns), query_grad)
    first_gain_grad = after(first_gain_grad, other)
    first_gain_grad = first_gain_grad + swap(first_gain_grad, "mlp", 1)
    input_half = last(inputs_half, low, other, grad_residual, first_gain, half_kind, shards)
    outputs_half = finish(residual, down_low, after(down_other, input_half), shards)
    rest_lifted = with_core(after(lifted_inner, other))
    rest_grads = with_core(after(grad_inner, other))
    up_grad, down_grad = feed_all(
        after(rest_lifted, outputs_half, first_gain_grad), rest_grads, up_weight, down_weight, shards, sums
    )
    first_came = jnp.zeros_like(first_gain_grad)
    bit = 2
    while bit < lax.axis_size("mlp"):
        if bit > 2:
            first_gain_grad = first_gain_grad + first_came
        first_came = after(swap(first_gain_grad, "mlp", bit), up_grad)
        bit *= 2
    placed = (input_half, outputs_half)
    input_grad, outputs = place_halves(placed, [swap(array, "mlp", 1) for array in placed])
    mixed_part = jnp.stack([after(columns[d], up_grad) for d in range(shards)])
    output_grad, second_gain_grad, first_gain_grad = output_part(
        attended,
        (mixed_part, swap(mixed_part, "mlp", 1)),
        (first_gain_grad, first_came),
        groups,
    )

    return (
        outputs,
        input_grad,
        first_gain_grad,
        query_grad,
        key_grad,
        value_grad,
        output_grad,
        second_gain_grad,
        up_grad,
        down_grad,
    )


def solution(mesh):
    return jax.shard_map(
        body,
        mesh=mesh,
        in_specs=(
            P("seq", None),
            P(),
            P(None, "mlp"),
            P(None, "mlp"),
            P(None, "mlp"),
            P("mlp", None),
            P(),
            P(None, "mlp"),
            P("mlp", None),
            P(),
            P(),
            P(),
            P("seq", None),
        ),
        out_specs=(
            P("seq", None),
            P("seq", None),
            P(None, "seq"),
            P("seq", "mlp"),
            P("seq", "mlp"),
            P("seq", "mlp"),
            P("mlp", "seq"),
            P(None, "seq"),
            P("seq", "mlp"),
            P("mlp", "seq"),
        ),
        check_vma=False,
    )
```

```python
from functools import partial
import math

import jax
import jax.numpy as jnp
from jax import lax
from jax.experimental import pallas as pl
from jax.experimental.pallas import tpu as pltpu
from jax.sharding import PartitionSpec as P

HEAD_DIM = 128
epsilon = 1e-05
bf16 = jnp.bfloat16
f32 = jnp.float32
NEGATIVE = -1e30

WHOLE = pl.BlockSpec(memory_space=pltpu.VMEM)
NN = ((1,), (0,))
NT = ((1,), (1,))
TN = ((0,), (0,))


def dot(a, b, dims):
    return lax.dot_general(a, b, (dims, ((), ())), preferred_element_type=f32)


def params(mebibytes):
    return pltpu.CompilerParams(vmem_limit_bytes=mebibytes * 1024 * 1024)


def cost(flops, moved, transcendentals=0, share=100):
    return pl.CostEstimate(
        flops=int(flops) // share,
        bytes_accessed=int(moved) // share,
        transcendentals=int(transcendentals) // share,
    )


def swap(value, axis, bit):
    size = lax.axis_size(axis)
    return lax.ppermute(value, axis, [(i, i ^ bit) for i in range(size)])


def inner_size():
    return 1 << (int(math.log2(lax.axis_size("seq"))) // 2)


def x_size():
    return lax.axis_size("mlp") // 2


def after(values, *earlier):
    return lax.optimization_barrier((values, earlier))[0]


def in_hbm(array):
    return pltpu.with_memory_space_constraint(array, pltpu.HBM)


def own_quarter(half):
    rows = half.shape[0] // x_size()
    return lax.dynamic_slice_in_dim(half, (lax.axis_index("mlp") // 2) * rows, rows, 0)


def join_x(quarter, *earlier):
    bit = 1
    while bit < x_size():
        came = after(swap(quarter, "mlp", 2 * bit), earlier)
        quarter = jnp.concatenate([quarter, came], axis=0)
        bit *= 2
    return quarter


def gather_early(half):
    size, inner = lax.axis_size("seq"), inner_size()
    quarter = own_quarter(half)
    pieces = {0: half}
    far = {outer: swap(quarter, "seq", outer) for outer in range(inner, size, inner)}
    for bit in range(1, inner):
        pieces[bit] = swap(half, "seq", bit)
    for outer in range(inner, size, inner):
        pieces[outer] = join_x(far[outer])
        for bit in range(1, inner):
            pieces[outer | bit] = swap(pieces[outer], "seq", bit)
    return [pieces[d] for d in range(size)]


def gather_outer(half):
    size, inner = lax.axis_size("seq"), inner_size()
    quarter = own_quarter(half)
    return [swap(quarter, "seq", outer) for outer in range(inner, size, inner)]


def gather_inner(array):
    return [swap(array, "seq", bit) for bit in range(1, inner_size())]


def with_core(arrays):
    return [each for array in arrays for each in (array, swap(array, "mlp", 1))]


def gather_first(piece):
    size, inner = lax.axis_size("seq"), inner_size()
    pieces = {0: piece}
    for bit in range(1, inner):
        pieces[bit] = swap(piece, "seq", bit)
    return pieces, [swap(piece, "seq", outer) for outer in range(inner, size, inner)]


def gather_pieces(pieces, far):
    size, inner = lax.axis_size("seq"), inner_size()
    for outer, came in zip(range(inner, size, inner), far):
        pieces[outer] = came
        for bit in range(1, inner):
            pieces[outer | bit] = swap(came, "seq", bit)
    return [pieces[d] for d in range(size)]


def rounded(value):
    return lax.optimization_barrier(value.astype(bf16))


def pair_mlp(mine, other_half):
    low, other = rounded(mine + swap(other_half, "mlp", 1).astype(f32)), None
    bit = 2
    while bit < lax.axis_size("mlp"):
        if other is not None:
            low = rounded(low.astype(f32) + other.astype(f32))
        other = swap(low, "mlp", bit)
        bit *= 2
    if other is None:
        other = jnp.zeros_like(low)
    return low, other


def both(half):
    return jnp.concatenate([half, swap(half, "mlp", 1)], axis=0)


def tables_kernel(index, frames, texts, actions, *outs, shards, length, groups, clip_length):
    place_a, place_b, kind_a, kind_b, query_place, own_place, own_kind = outs
    shard_index, core = index[0], index[1]
    shape = (shards, length)
    place = lax.broadcasted_iota(jnp.int32, shape, 0) * length + lax.broadcasted_iota(
        jnp.int32, shape, 1
    )
    kinds = jnp.full(shape, 2, jnp.int32)
    for clip in range(frames.shape[0]):
        start = jnp.int32(clip * clip_length)
        within = (place >= clip * clip_length) & (place < (clip + 1) * clip_length)
        for frame in range(frames.shape[1]):
            text_end = start + texts[clip, frame]
            action_end = text_end + actions[clip, frame]
            kinds = jnp.where(within & (place >= start) & (place < text_end), 0, kinds)
            kinds = jnp.where(within & (place >= text_end) & (place < action_end), 1, kinds)
            start = action_end + frames[clip, frame]
    square = (length, length)
    down = lax.broadcasted_iota(jnp.int32, square, 0)
    across = lax.broadcasted_iota(jnp.int32, square, 1)
    earlier = (down < across).astype(f32).astype(bf16)
    rank = jnp.zeros(shape, f32)
    before = jnp.zeros((shards, 1), f32)
    for kind in range(3):
        chosen = (kinds == kind).astype(f32)
        rank += chosen * (dot(chosen.astype(bf16), earlier, NN) + before)
        before += chosen.sum(axis=1, keepdims=True)
    rank_low, kinds_low = rank.astype(bf16), kinds.astype(f32).astype(bf16)
    piece = length // shards // 2
    lane = lax.broadcasted_iota(jnp.int32, (1, length), 1).astype(f32)

    def find(shard, offset, side, row):
        wanted = (shard_index ^ offset) * (2 * piece) + (core ^ side) * piece + row
        pick = shard == lax.broadcasted_iota(jnp.int32, (length, shards), 1)
        pick = pick.astype(f32).astype(bf16)
        hit = dot(pick, rank_low, NN) == wanted.astype(f32)
        where = jnp.sum(jnp.where(hit, lane, 0.0), axis=1, keepdims=True).astype(jnp.int32)
        kind = jnp.sum(jnp.where(hit, dot(pick, kinds_low, NN), 0.0), axis=1, keepdims=True)
        return where + shard * length, kind.astype(jnp.int32)

    def as_row(column):
        return jnp.sum(jnp.where(down == across, column, 0), axis=0, keepdims=True)

    step = lax.broadcasted_iota(jnp.int32, (length, 1), 0)
    half = length // 2
    for side, (place_out, kind_out) in enumerate(((place_a, kind_a), (place_b, kind_b))):
        for block in range(shards // 2):
            token = step + block * length
            if groups > 1:
                shard, offset = token // (shards * piece), (token // piece) % shards
            else:
                offset, shard = token // half, (token % half) // piece
            where, kind = find(shard, offset, side, token % piece)
            at = pl.ds(block * length, length)
            place_out[at, :] = where
            kind_out[at, :] = kind
            query_place[:, pl.ds((2 * block + side) * length, length)] = as_row(where)
    where, kind = find((step % half) // piece, step * 0, step // half, step % piece)
    own_place[...] = as_row(where)
    own_kind[...] = kind


def tables(frames, texts, actions, shards, length, groups):
    index = jnp.stack([lax.axis_index("seq"), lax.axis_index("mlp") % 2]).astype(jnp.int32)
    total = shards * length
    column = jax.ShapeDtypeStruct((total // 2, 1), jnp.int32)
    return pl.pallas_call(
        partial(
            tables_kernel,
            shards=shards,
            length=length,
            groups=groups,
            clip_length=total // frames.shape[0],
        ),
        in_specs=[pl.BlockSpec(memory_space=pltpu.SMEM)] * 4,
        out_shape=[column] * 4
        + [
            jax.ShapeDtypeStruct((1, total), jnp.int32),
            jax.ShapeDtypeStruct((1, length), jnp.int32),
            jax.ShapeDtypeStruct((length, 1), jnp.int32),
        ],
        cost_estimate=cost(8 * total * length, 8 * 128 * total),
        name="tables",
    )(index, frames, texts, actions)


def rows_kernel(*refs, count):
    rows, weights, outs = refs[0], refs[1 : 1 + count], refs[1 + count :]
    for weight, out in zip(weights, outs):
        out[...] = dot(rows[...], weight[...], NN).astype(bf16)


def project_rows(rows, *weights):
    across = weights[0].shape[1]
    return pl.pallas_call(
        partial(rows_kernel, count=len(weights)),
        out_shape=[jax.ShapeDtypeStruct((rows.shape[0], across), bf16)] * len(weights),
        compiler_params=params(8),
        cost_estimate=cost(2 * rows.size * across * len(weights), 2 * rows.size),
        name="project_rows",
    )(rows, *weights)


def one_kernel(rows, weight, out):
    out[...] = dot(rows[...], weight[...], NT).astype(bf16)


def product_back(rows, weight):
    return pl.pallas_call(
        one_kernel,
        out_shape=jax.ShapeDtypeStruct((rows.shape[0], weight.shape[0]), bf16),
        compiler_params=params(6),
        cost_estimate=cost(2 * rows.size * weight.shape[0], 2 * weight.size),
        name="product_back",
    )(rows, weight)


def halves_kernel(*refs, count, dims):
    mine, other = refs[-2:]
    half = mine.shape[0]
    total = sum(dot(refs[k][...], refs[count + k][...], dims) for k in range(count))
    mine[...] = total[:half]
    other[...] = total[half:].astype(bf16)


def product_halves(rows, weights, dims):
    count = len(rows)
    half = rows[0].shape[0] // 2
    across = weights[0].shape[1 - dims[1][0]]
    shape = (half, across)
    return pl.pallas_call(
        partial(halves_kernel, count=count, dims=dims),
        out_shape=[jax.ShapeDtypeStruct(shape, f32), jax.ShapeDtypeStruct(shape, bf16)],
        compiler_params=params(6),
        cost_estimate=cost(2 * count * rows[0].size * across, 2 * count * weights[0].size),
        name="product_halves",
    )(*rows, *weights)


def down_own_kernel(rows, weight, mine, other, total):
    total[...] = jnp.zeros_like(total)

    def step(at):
        total[...] += dot(rows[:, at], weight[at, :], NN)

    tiles_of(weight.shape[0], math.gcd(weight.shape[0], 512), step)
    half = mine.shape[0]
    mine[...] = total[:half]
    other[...] = total[half:].astype(bf16)


def down_own(rows, weight):
    count, deep = rows.shape
    across = weight.shape[1]
    shape = (count // 2, across)
    return pl.pallas_call(
        down_own_kernel,
        in_specs=[WHOLE] * 2,
        out_specs=[WHOLE] * 2,
        out_shape=[jax.ShapeDtypeStruct(shape, f32), jax.ShapeDtypeStruct(shape, bf16)],
        scratch_shapes=[pltpu.VMEM((count, across), f32)],
        compiler_params=params(6),
        cost_estimate=cost(2 * rows.size * across, 2 * weight.size),
        name="down_own",
    )(rows, weight)


def gain_rows(gain, column):
    return jnp.where(
        column == 0, gain[0:1, :], jnp.where(column == 1, gain[1:2, :], gain[2:3, :])
    )


def normalize(values):
    mean = jnp.mean(values, axis=1, keepdims=True)
    centered = values - mean
    inverse = lax.rsqrt(jnp.mean(centered * centered, axis=1, keepdims=True) + epsilon)
    return (centered * inverse, inverse)


def norm_back(grad, normal, inverse, gains):
    scaled = grad * gains
    return inverse * (
        scaled
        - jnp.mean(scaled, axis=1, keepdims=True)
        - normal * jnp.mean(scaled * normal, axis=1, keepdims=True)
    )


def norm_kernel(*refs, groups, inner, parts):
    index, gain, kind, out = refs[0], refs[-3], refs[-2], refs[-1]
    pieces = refs[1:-3]
    rows, width = pieces[0].shape
    count = len(pieces)
    step = rows // parts
    for d, piece in enumerate(pieces):
        for part in range(parts):
            normal, _ = normalize(piece[pl.ds(part * step, step), :].astype(f32))
            place = part if d < inner else part ^ index[0]
            if groups > 1:
                each = groups // parts
                at = pl.ds(place * each, each)
                column = kind[at, d].reshape(step, 1)
                normed = (normal * gain_rows(gain, column)).astype(bf16)
                out[at, d] = normed.reshape(each, rows // groups, width)
            else:
                column = kind[d, place]
                out[d, place] = (normal * gain_rows(gain, column)).astype(bf16)


def norm_pieces(pieces, gain, kind, groups):
    rows, width = pieces[0].shape
    count = len(pieces)
    parts = x_size()
    if groups > 1:
        shape = (groups, count, rows // groups)
    else:
        shape = (count, parts, rows // parts)
    memory = [pl.BlockSpec(memory_space=pltpu.SMEM)]
    index = (lax.axis_index("mlp") // 2).astype(jnp.int32).reshape(1)
    out = pl.pallas_call(
        partial(norm_kernel, groups=groups, inner=inner_size(), parts=parts),
        in_specs=memory + [pl.BlockSpec(memory_space=pltpu.VMEM)] * (count + 2),
        out_shape=jax.ShapeDtypeStruct(shape + (width,), bf16),
        compiler_params=params(4 + count),
        cost_estimate=cost(10 * count * rows * width, 4 * count * rows * width),
        name="norm_pieces",
    )(index, *pieces, gain, kind.reshape(shape + (1,)))
    return out.reshape(count * rows, width)


def own_norm_kernel(rows, gain, kind, out):
    normal, _ = normalize(rows[...].astype(f32))
    out[...] = (normal * gain_rows(gain, kind[...])).astype(bf16)


def own_norm(rows, gain, kind):
    return pl.pallas_call(
        own_norm_kernel,
        out_shape=jax.ShapeDtypeStruct(rows.shape, bf16),
        compiler_params=params(4),
        cost_estimate=cost(10 * rows.size, 4 * rows.size),
        name="own_norm",
    )(rows, gain, kind)


def lift_kernel(rows, low, other, gain, kind, residual, lifted):
    value = rows[...].astype(f32) + (low[...].astype(f32) + other[...].astype(f32))
    residual[...] = value
    normal, _ = normalize(value)
    lifted[...] = (normal * gain_rows(gain, kind[...])).astype(bf16)


def lift(rows, low, other, gain, kind):
    return pl.pallas_call(
        lift_kernel,
        in_specs=[WHOLE] * 5,
        out_specs=[WHOLE] * 2,
        out_shape=[jax.ShapeDtypeStruct(rows.shape, f32), jax.ShapeDtypeStruct(rows.shape, bf16)],
        compiler_params=params(4),
        cost_estimate=cost(10 * rows.size, 12 * rows.size),
        name="lift",
    )(rows, low, other, gain, kind)


def kind_sums(term, kind):
    sums = [jnp.sum(jnp.where(kind == k, term, 0.0), axis=0, keepdims=True) for k in range(3)]
    high = [value.astype(bf16) for value in sums]
    low = [(value - part.astype(f32)).astype(bf16) for value, part in zip(sums, high)]
    zero = jnp.zeros((1, term.shape[1]), bf16)
    return jnp.concatenate(high + low + [zero, zero], axis=0)


def middle_kernel(index, residual, low, other, grad, gain, kind, grad_residual, mixed, parts):
    lifted_grad = low[...].astype(f32) + other[...].astype(f32)
    normal, inverse = normalize(residual[...])
    column = kind[...]
    back = norm_back(lifted_grad, normal, inverse, gain_rows(gain, column))
    value = grad[...].astype(f32) + back
    grad_residual[...] = value
    rounded_value = value.astype(bf16)
    mixed[...] = rounded_value
    sums = kind_sums(lifted_grad * normal, column)
    shards, rows, part = parts.shape
    for k in range(shards):
        at = index[0] ^ k
        parts[at, pl.ds(0, rows - 8), :] = rounded_value[:, k * part : (k + 1) * part]
        parts[at, pl.ds(rows - 8, 8), :] = sums[:, k * part : (k + 1) * part]


def middle(residual, low, other, grad, gain, kind, shards):
    rows, width = residual.shape
    index = lax.axis_index("seq").astype(jnp.int32).reshape(1)
    return pl.pallas_call(
        middle_kernel,
        in_specs=[pl.BlockSpec(memory_space=pltpu.SMEM)] + [WHOLE] * 6,
        out_specs=[WHOLE] * 3,
        out_shape=[
            jax.ShapeDtypeStruct(residual.shape, f32),
            jax.ShapeDtypeStruct(residual.shape, bf16),
            jax.ShapeDtypeStruct((shards, rows + 8, width // shards), bf16),
        ],
        compiler_params=params(6),
        cost_estimate=cost(20 * residual.size, 16 * residual.size),
        name="middle",
    )(index, residual, low, other, grad, gain, kind)


def reordered(values, shards):
    count = values.shape[0]
    piece = count // shards
    to = lax.broadcasted_iota(jnp.int32, (count, count), 0)
    source = lax.broadcasted_iota(jnp.int32, (count, count), 1)
    pick = (source == (to % shards) * piece + to // shards).astype(f32).astype(bf16)
    return dot(pick, values, NN).astype(bf16)


def finish_kernel(residual, low, other, out, *, shards):
    value = residual[...] + (low[...].astype(f32) + other[...].astype(f32))
    out[...] = reordered(value.astype(bf16), shards)


def finish(residual, low, other, shards):
    return pl.pallas_call(
        partial(finish_kernel, shards=shards),
        in_specs=[WHOLE] * 3,
        out_specs=WHOLE,
        out_shape=jax.ShapeDtypeStruct(residual.shape, bf16),
        compiler_params=params(4),
        cost_estimate=cost(2 * residual.size, 10 * residual.size),
        name="finish",
    )(residual, low, other)


def place_kernel(index, *refs):
    count = len(refs) // 3
    for mine, other, out in zip(refs[:count], refs[count : 2 * count], refs[2 * count :]):
        half = mine.shape[0]
        out[pl.ds(pl.multiple_of(index[0] * half, half), half), :] = mine[...]
        out[pl.ds(pl.multiple_of((1 - index[0]) * half, half), half), :] = other[...]


def place_halves(arrays, others):
    half, width = arrays[0].shape
    index = (lax.axis_index("mlp") % 2).astype(jnp.int32).reshape(1)
    return pl.pallas_call(
        place_kernel,
        in_specs=[pl.BlockSpec(memory_space=pltpu.SMEM)] + [WHOLE] * (2 * len(arrays)),
        out_shape=[jax.ShapeDtypeStruct((2 * half, width), bf16)] * len(arrays),
        compiler_params=params(6),
        cost_estimate=cost(half * width, 16 * half * width),
        name="place_halves",
    )(index, *arrays, *others)


def last_kernel(rows, low, other, grad_residual, gain, kind, out, *, shards):
    grad = low[...].astype(f32) + other[...].astype(f32)
    normal, inverse = normalize(rows[...].astype(f32))
    back = norm_back(grad, normal, inverse, gain_rows(gain, kind[...]))
    out[...] = reordered((grad_residual[...] + back).astype(bf16), shards)


def last(rows, low, other, grad_residual, gain, kind, shards):
    return pl.pallas_call(
        partial(last_kernel, shards=shards),
        in_specs=[WHOLE] * 6,
        out_specs=WHOLE,
        out_shape=jax.ShapeDtypeStruct(rows.shape, bf16),
        compiler_params=params(6),
        cost_estimate=cost(20 * rows.size, 12 * rows.size),
        name="last",
    )(rows, low, other, grad_residual, gain, kind)


def gelu_parts(value):
    rate = math.sqrt(2 / math.pi)
    bend = value * (rate + (rate * 0.044715) * (value * value))
    upper = 0.5 + 0.5 * jnp.tanh(bend)
    slope = upper + (upper * (1 - upper)) * (6 * bend - (4 * rate) * value)
    return value * upper, slope


def tiles_of(extent, tile, step):
    def at(t, _):
        step(pl.ds(pl.multiple_of(t * tile, tile), tile))
        return 0

    lax.fori_loop(0, extent // tile, at, 0)


def own_kernel(lifted, up, grad_activated, activated, hidden_grads, mine, other, total):
    total[...] = jnp.zeros_like(total)

    def step(at):
        value, slope = gelu_parts(dot(lifted[...], up[:, at], NN))
        activated[:, at] = value.astype(bf16)
        hidden_grad = (grad_activated[:, at] * slope).astype(bf16)
        hidden_grads[:, at] = hidden_grad
        total[...] += dot(hidden_grad, up[:, at], NT)

    tiles_of(up.shape[1], math.gcd(up.shape[1], 512), step)
    half = mine.shape[0]
    mine[...] = total[:half]
    other[...] = total[half:].astype(bf16)


def feed_own(lifted, up, grad_activated):
    rows, width = lifted.shape
    hidden = up.shape[1]
    return pl.pallas_call(
        own_kernel,
        in_specs=[WHOLE] * 3,
        out_specs=[WHOLE] * 4,
        out_shape=[jax.ShapeDtypeStruct((rows, hidden), bf16)] * 2
        + [
            jax.ShapeDtypeStruct((rows // 2, width), f32),
            jax.ShapeDtypeStruct((rows // 2, width), bf16),
        ],
        scratch_shapes=[pltpu.VMEM((rows, width), f32)],
        compiler_params=params(8),
        cost_estimate=cost(4 * rows * width * hidden, 2 * width * hidden),
        name="feed_own",
    )(lifted, up, grad_activated)


def down_kernel(grad, down, out):
    def step(at):
        out[:, at] = dot(grad[...], down[at, :], NT)

    tiles_of(down.shape[0], math.gcd(down.shape[0], 512), step)


def grad_activated(grad, down):
    rows, width = grad.shape
    hidden = down.shape[0]
    return pl.pallas_call(
        down_kernel,
        in_specs=[WHOLE] * 2,
        out_specs=WHOLE,
        out_shape=jax.ShapeDtypeStruct((rows, hidden), f32),
        compiler_params=params(6),
        cost_estimate=cost(2 * rows * width * hidden, 2 * width * hidden),
        name="grad_activated",
    )(grad, down)


def all_kernel(index, *refs, count):
    lifted_parts, grad_parts = refs[:count], refs[count : 2 * count]
    up, down = refs[2 * count : 2 * count + 2]
    before = refs[2 * count + 2 : -5]
    up_grad, down_grad, lifted_across, hidden_kept, grad_kept = refs[-5:]
    part = up_grad.shape[0]
    mine = pl.ds(pl.multiple_of(index[0] * part, part), part)

    def rows_of(parts, at):
        return jnp.concatenate([ref[:, at] for ref in parts], axis=0)

    @pl.when(pl.program_id(0) == 0)
    def _():
        lifted_across[...] = rows_of(lifted_parts, mine).T

    first = pl.program_id(0) == 0
    last_step = pl.num_programs(0) - 1

    tile = hidden_kept.shape[1]
    at = jnp.minimum(pl.program_id(0), last_step - 1) if up.shape[1] > tile else 0
    here = pl.ds(pl.multiple_of(at * tile, tile), tile)

    def products():
        everything = slice(None)
        return (
            dot(rows_of(lifted_parts, everything), up[:, here], NN),
            dot(rows_of(grad_parts, everything), down[here, :], NT),
        )

    def finish_tile(hidden_value, activated_grad):
        value, slope = gelu_parts(hidden_value)
        hidden_grad = (activated_grad * slope).astype(bf16)
        down_term = dot(value.astype(bf16), rows_of(grad_parts, mine), TN)
        up_term = dot(lifted_across[...], hidden_grad, NN)
        if len(before) == 2:
            up_term += before[0][...].astype(f32)
            down_term += before[1][...].astype(f32)
        else:
            lifted_own, grad_own, activated, hidden_own = before
            up_term += dot(lifted_own[...], hidden_own[...], TN)
            down_term += dot(activated[...], grad_own[...], TN)
        up_grad[...] = up_term.astype(up_grad.dtype)
        down_grad[...] = down_term.astype(down_grad.dtype)

    @pl.when(first)
    def _():
        hidden_kept[...], grad_kept[...] = products()

    @pl.when((pl.program_id(0) > 0) & (pl.program_id(0) < last_step))
    def _():
        kept = hidden_kept[...], grad_kept[...]
        fresh = products()
        finish_tile(*kept)
        hidden_kept[...], grad_kept[...] = fresh

    @pl.when(pl.program_id(0) == last_step)
    def _():
        finish_tile(hidden_kept[...], grad_kept[...])


def feed_all(lifted, grad, up, down, shards, sums=(), own=()):
    counts = [array.shape[0] for array in lifted]
    rows, width = sum(counts), lifted[0].shape[1]
    count = len(counts)
    part = width // shards
    hidden = up.shape[1]
    tile = math.gcd(hidden, 256)
    steps = hidden // tile
    across = lambda t, index: (0, jnp.maximum(t - 1, 0))
    below = lambda t, index: (jnp.maximum(t - 1, 0), 0)
    mine = lambda t, index: (0, index[0])
    sum_specs = [pl.BlockSpec((part, tile), across), pl.BlockSpec((tile, part), below)]
    if own:
        own_rows = own[0].shape[0]
        more = [pl.BlockSpec((own_rows, part), mine)] * 2
        more += [pl.BlockSpec((own_rows, tile), across)] * 2
    else:
        more = sum_specs
    index = lax.axis_index("seq").astype(jnp.int32).reshape(1)
    return pl.pallas_call(
        partial(all_kernel, count=count),
        grid_spec=pltpu.PrefetchScalarGridSpec(
            num_scalar_prefetch=1,
            grid=(steps + 1,),
            in_specs=[WHOLE] * (2 * count)
            + [WHOLE] * 2
            + more,
            out_specs=sum_specs,
            scratch_shapes=[pltpu.VMEM((part, rows), bf16)]
            + [pltpu.VMEM((rows, tile), f32)] * 2,
        ),
        out_shape=[
            pltpu.HBM((part, hidden), bf16 if own else f32),
            pltpu.HBM((hidden, part), bf16 if own else f32),
        ],
        compiler_params=params((6 if own else 8) + 8 * rows // 512),
        cost_estimate=cost(
            4 * rows * hidden * (width + part),
            4 * width * hidden + 4 * rows * width,
        ),
        name="feed_all",
    )(
        index,
        *lifted,
        *grad,
        up,
        down,
        *(own or [in_hbm(array) for array in sums]),
    )


def project_kernel(index, *refs):
    normed, lows, weights = refs[0:2], refs[2:8], refs[8:11]
    gain, kinds = refs[11], refs[12:14]
    outs, gain_grad = refs[14:17], refs[17]
    for k in range(3):
        outs[k][...] = sum(dot(normed[side][...], lows[2 * k + side][...], TN) for side in range(2))
    gain_sum = [0.0, 0.0, 0.0]
    for side in range(2):
        column = kinds[side][...]
        term = sum(dot(lows[2 * k + side][...], weights[k][...], NT) for k in range(3))
        term = term * (normed[side][...].astype(f32) / gain_rows(gain, column))
        for k in range(3):
            gain_sum[k] += jnp.sum(jnp.where(column == k, term, 0.0), axis=0, keepdims=True)
    gain_grad[...] = jnp.concatenate(gain_sum, axis=0)


def project(normed, lows, weights, gain, kinds, shards):
    rows, width = normed[0].shape
    across = lows[0][0].shape[1]
    part = width // shards
    whole = lambda t, index: (0, 0)
    mine = lambda t, index: (0, index[0])
    below = lambda t, index: (index[0], 0)
    index = lax.axis_index("seq").astype(jnp.int32).reshape(1)
    return pl.pallas_call(
        project_kernel,
        grid_spec=pltpu.PrefetchScalarGridSpec(
            num_scalar_prefetch=1,
            grid=(1,),
            in_specs=[pl.BlockSpec((rows, part), mine)] * 2
            + [pl.BlockSpec((rows, across), whole)] * 6
            + [pl.BlockSpec((part, across), below)] * 3
            + [pl.BlockSpec((gain.shape[0], part), mine)]
            + [pl.BlockSpec((rows, 1), whole)] * 2,
            out_specs=[pl.BlockSpec((part, across), whole)] * 3
            + [pl.BlockSpec((gain.shape[0], part), whole)],
        ),
        out_shape=[jax.ShapeDtypeStruct((part, across), f32)] * 3
        + [jax.ShapeDtypeStruct((gain.shape[0], part), f32)],
        compiler_params=params(8),
        cost_estimate=cost(24 * rows * part * across, 12 * rows * across + 12 * part * across),
        name="project",
    )(index, *normed, *[low for pair in lows for low in pair], *weights, gain, *kinds)


def output_kernel(
    attended_a, attended_b, came_a, came_b, first_mine, first_came, out, gain_grad, first, *, groups
):
    total, sums = 0.0, 0.0
    shards, rows, part = came_a.shape
    half = rows - 8
    each = half // groups
    for attended, came in ((attended_a, came_a), (attended_b, came_b)):
        mixed = [
            came[d, pl.ds(group * each, each), :]
            for group in range(groups)
            for d in range(shards)
        ]
        total += dot(attended[...], jnp.concatenate(mixed, axis=0), TN)
        own_sums = 0.0
        for k in range(shards):
            own_sums += came[k, pl.ds(half, 8), :].astype(f32)
        sums += own_sums
    out[...] = total
    gain_grad[...] = sums[0:3, :] + sums[3:6, :]
    first[...] = first_mine[...] + first_came[...]


def output_part(attended, came, first, groups):
    across, part = attended[0].shape[1], came[0].shape[2]
    return pl.pallas_call(
        partial(output_kernel, groups=groups),
        in_specs=[WHOLE] * 6,
        out_shape=[
            jax.ShapeDtypeStruct((across, part), f32),
        ]
        + [jax.ShapeDtypeStruct((3, part), f32)] * 2,
        compiler_params=params(6),
        cost_estimate=cost(
            4 * attended[0].shape[0] * across * part, 4 * attended[0].shape[0] * (across + part)
        ),
        name="output_part",
    )(*attended, *came, *first)


def mask_of(key_place, query_place, clip_length, clips):
    allowed = key_place <= query_place
    if clips > 1:
        allowed = allowed & (key_place // clip_length == query_place // clip_length)
    return allowed


def probabilities(scores, scale):
    top = scores[0].max(axis=0, keepdims=True)
    for block in scores[1:]:
        top = jnp.maximum(top, block.max(axis=0, keepdims=True))
    rate = scale * math.log2(math.e)
    weights = [jnp.exp2((block - top) * rate) for block in scores]
    total = weights[0].sum(axis=0, keepdims=True)
    for block in weights[1:]:
        total = total + block.sum(axis=0, keepdims=True)
    inverse = 1.0 / total
    return [block * inverse for block in weights]


def forward_kernel(query, key_a, key_b, value_a, value_b, place_a, place_b, query_place, out, **opts):
    scale = opts["scale"]
    query_place = query_place[...]
    allowed = [
        mask_of(place[...], query_place, opts["clip_length"], opts["clips"])
        for place in (place_a, place_b)
    ]
    for head in range(query.shape[1] // HEAD_DIM):
        at = pl.ds(head * HEAD_DIM, HEAD_DIM)
        scores = [
            jnp.where(mask, dot(key[:, at], query[:, at], NT), NEGATIVE)
            for mask, key in zip(allowed, (key_a, key_b))
        ]
        prob = [block.astype(bf16) for block in probabilities(scores, scale)]
        result = dot(value_a[:, at], prob[0], TN) + dot(value_b[:, at], prob[1], TN)
        out[:, at] = result.T.astype(bf16)


def attend(query, keys, values, places, query_place, clip_length, clips):
    rows, width = query.shape
    total = 2 * keys[0].shape[0]
    return pl.pallas_call(
        partial(
            forward_kernel, scale=1.0 / math.sqrt(HEAD_DIM), clip_length=clip_length, clips=clips
        ),
        out_shape=jax.ShapeDtypeStruct((rows, width), bf16),
        compiler_params=params(8),
        cost_estimate=cost(
            4 * rows * total * width, 4 * total * width, rows * total * (width // HEAD_DIM)
        ),
        name="attend",
    )(query, *keys, *values, *places, query_place)


def block_of(half):
    return min(128, half)


def reaches(half, groups):
    blocks = half // block_of(half)
    found, start = [], 0
    for index in range(blocks):
        seen, free = (index + 1, index) if groups > 1 else (blocks, 0)
        found.append((seen, free, start))
        start += seen
    return found, start


def take(first, second, low, high, at):
    block = block_of(first.shape[0])
    rows = [side[pl.ds(k * block, block), at] for k in range(low, high) for side in (first, second)]
    return jnp.concatenate(rows, axis=0)


def columns_of(head):
    return pl.ds(pl.multiple_of(head * HEAD_DIM, HEAD_DIM), HEAD_DIM)


def all_forward_kernel(*refs, groups, scale, clip_length, clips):
    query_a, query_b, key_a, key_b, value_a, value_b, place_a, place_b, query_place = refs[:9]
    attended_a, attended_b, stored, kept_probs, sems = refs[9:]
    half, width = key_a.shape
    heads = width // HEAD_DIM
    block = block_of(half)
    pair = 2 * block
    everything = slice(None)

    def copy_of(head):
        slot = head % 2
        return pltpu.make_async_copy(kept_probs.at[slot], stored.at[head], sems.at[slot])

    def one_head(head, _):
        cut = columns_of(head)
        slot = head % 2

        @pl.when(head >= 2)
        def _():
            copy_of(head - 2).wait()

        values_across = take(value_a, value_b, 0, half // block, cut).T
        for index, (seen, free, start) in enumerate(reaches(half, groups)[0]):
            mine = pl.ds(index * block, block)
            query = take(query_a, query_b, index, index + 1, cut)
            at_place = query_place[:, pl.ds(index * pair, pair)]
            place = take(place_a, place_b, free, seen, everything)
            mask = mask_of(place, at_place, clip_length, clips)
            score = dot(take(key_a, key_b, free, seen, cut), query, NT)
            scores = [jnp.where(mask, score, NEGATIVE)]
            if free:
                scores.insert(0, dot(take(key_a, key_b, 0, free, cut), query, NT))
            result, at = 0.0, 0
            for prob in probabilities(scores, scale):
                kept = prob.astype(bf16)
                rows = kept.shape[0]
                kept_probs[slot, pl.ds(start * pair + at, rows), :] = kept
                result += dot(values_across[:, at : at + rows], kept, NN)
                at += rows
            result = result.T.astype(bf16)
            attended_a[mine, cut] = result[:block]
            attended_b[mine, cut] = result[block:]
        copy_of(head).start()
        return 0

    lax.fori_loop(0, heads, one_head, 0)
    for head in range(max(0, heads - 2), heads):
        copy_of(head).wait()


def attend_all(queries, keys, values, places, query_place, groups, clip_length, clips):
    half, width = keys[0].shape
    heads = width // HEAD_DIM
    pair = 2 * block_of(half)
    deep = reaches(half, groups)[1] * pair
    outs = pl.pallas_call(
        partial(
            all_forward_kernel,
            groups=groups,
            scale=1.0 / math.sqrt(HEAD_DIM),
            clip_length=clip_length,
            clips=clips,
        ),
        in_specs=[pl.BlockSpec(memory_space=pltpu.VMEM)] * 9,
        out_specs=[pl.BlockSpec(memory_space=pltpu.VMEM)] * 2
        + [pl.BlockSpec(memory_space=pl.ANY)],
        out_shape=[jax.ShapeDtypeStruct((half, width), bf16)] * 2
        + [pltpu.HBM((heads, deep, pair), bf16)],
        scratch_shapes=[
            pltpu.VMEM((2, deep, pair), bf16),
            pltpu.SemaphoreType.DMA((2,)),
        ],
        compiler_params=params(max(10, half * half // 2**14)),
        cost_estimate=cost(16 * half * half * width, 16 * half * width, 4 * half * half * heads),
        name="attend_all",
    )(*queries, *keys, *values, *places, query_place)
    return outs[:2], outs[2]


STEP = 2


def backward_kernel(*refs, count, groups, scale):
    grad_pieces = refs[:count]
    query_a, query_b, key_a, key_b, value_a, value_b, attended_a, attended_b, stored = refs[
        count : count + 9
    ]
    outs = refs[count + 9 : count + 18]
    grad_query, grad_key, grad_value = outs[0:2], outs[2:4], outs[4:6]
    own_query, own_key, own_value = outs[6:9]
    (scores,) = refs[count + 18 :]
    half, width = key_a.shape
    rows = half // count
    group_rows = rows // groups
    block = block_of(half)
    blocks = half // block
    pair = 2 * block
    reach = reaches(half, groups)[0]

    def sources(index):
        found = []
        if groups == 1:
            for d in range(index * block // rows, (index + 1) * block // rows):
                found.append((d, 0, rows))
            return found
        each = count * group_rows
        for j in range(index * block // each, (index + 1) * block // each):
            for d in range(count):
                found.append((d, j * group_rows, group_rows))
        return found

    def one_head(head, _):
        cut = columns_of(head)

        def keep(targets, own, values, index):
            for side in range(2):
                at = side * block
                targets[side][pl.ds(index * block, block), cut] = values[at : at + block]
                for d, start, size in sources(index):
                    if d == 0:
                        own[pl.ds(side * rows + start, size), cut] = values[at : at + size]
                    at += size

        def take_grads(index):
            return jnp.concatenate(
                [
                    grad_pieces[d][pl.ds(side * rows + start, size), cut]
                    for side in range(2)
                    for d, start, size in sources(index)
                ],
                axis=0,
            )

        keys_across = take(key_a, key_b, 0, blocks, cut).T
        ones = jnp.ones((8, HEAD_DIM), bf16)
        for index, (seen, _, start) in enumerate(reach):
            result = take(attended_a, attended_b, index, index + 1, cut)
            grad = take_grads(index)
            product = grad.astype(f32) * result.astype(f32)
            high = product.astype(bf16)
            low = (product - high.astype(f32)).astype(bf16)
            delta = (dot(ones, high, NT) + dot(ones, low, NT))[0:1, :]
            back = 0.0
            for low_block in range(0, seen, STEP):
                high_block = min(low_block + STEP, seen)
                at = pl.ds((start + low_block) * pair, (high_block - low_block) * pair)
                values = take(value_a, value_b, low_block, high_block, cut)
                score = stored[head, at, :].astype(f32) * (dot(values, grad, NT) - delta)
                score = score.astype(bf16)
                scores[at, :] = score
                back += dot(keys_across[:, low_block * pair : high_block * pair], score, NN)
            keep(grad_query, own_query, (back * scale).T.astype(bf16), index)
        for index in range(blocks):
            key_sum, value_sum = 0.0, 0.0
            for other, (seen, _, start) in enumerate(reach):
                if index < seen:
                    at = pl.ds((start + index) * pair, pair)
                    query = take(query_a, query_b, other, other + 1, cut)
                    key_sum += dot(scores[at, :], query, NN)
                    value_sum += dot(stored[head, at, :], take_grads(other), NN)
            keep(grad_key, own_key, (key_sum * scale).astype(bf16), index)
            keep(grad_value, own_value, value_sum.astype(bf16), index)
        return 0

    lax.fori_loop(0, width // HEAD_DIM, one_head, 0)


def attend_back(grads, queries, keys, values, attended, stored, groups):
    half, width = keys[0].shape
    count = len(grads)
    rows = grads[0].shape[0]
    outs = pl.pallas_call(
        partial(
            backward_kernel,
            count=count,
            groups=groups,
            scale=1.0 / math.sqrt(HEAD_DIM),
        ),
        in_specs=[pl.BlockSpec(memory_space=pltpu.VMEM)] * (count + 9),
        out_specs=[pl.BlockSpec(memory_space=pltpu.VMEM)] * 9,
        out_shape=[jax.ShapeDtypeStruct((half, width), bf16)] * 6
        + [jax.ShapeDtypeStruct((rows, width), bf16)] * 3,
        scratch_shapes=[pltpu.VMEM(stored.shape[1:], bf16)],
        compiler_params=params(8 + 2 * stored.shape[1] * stored.shape[2] // 2**20),
        cost_estimate=cost(8 * 4 * half * half * width, 32 * half * width + 2 * stored.size),
        name="attend_back",
    )(*grads, *queries, *keys, *values, *attended, stored)
    return outs[0:2], outs[2:4], outs[4:6], outs[6:9]


def body(
    inputs,
    first_gain,
    query_weight,
    key_weight,
    value_weight,
    output_weight,
    second_gain,
    up_weight,
    down_weight,
    frame_sizes,
    text_counts,
    action_counts,
    cotangent,
):
    shards = lax.axis_size("seq")
    shard_index = lax.axis_index("seq")
    core = lax.axis_index("mlp") % 2
    length, width = inputs.shape
    total = length * shards
    half = length // 2
    piece = half // shards
    clips = frame_sizes.shape[0]
    clip_length = total // clips
    part = width // shards
    groups = shards if piece % 8 == 0 else 1

    def halves(rows):
        cut = rows.reshape(2, piece, shards, width)
        mine = lax.dynamic_index_in_dim(cut, core, 0, keepdims=False)
        other = lax.dynamic_index_in_dim(cut, 1 - core, 0, keepdims=False)
        return (
            mine.transpose(1, 0, 2).reshape(half, width),
            other.transpose(1, 0, 2).reshape(half, width),
        )

    inputs_half, inputs_other = halves(inputs)
    pieces = gather_early(inputs_half)
    arrived = pieces[inner_size() :: inner_size()]

    place_a, place_b, kind_a, kind_b, query_place, own_place, own_kind = tables(
        frame_sizes, text_counts, action_counts, shards, length, groups
    )
    places, kinds = (place_a, place_b), (kind_a, kind_b)
    half_kind = own_kind[:half]
    own_normed = own_norm(
        jnp.concatenate([inputs_half, inputs_other], axis=0), first_gain, own_kind
    )
    grad_half, grad_other = halves(cotangent)
    grad_own = jnp.concatenate([grad_half, grad_other], axis=0)
    (query_own,) = project_rows(after(own_normed, arrived), query_weight)
    grad_far = gather_outer(after(grad_half, arrived, pieces[inner_size() + 1]))
    pieces = after(pieces, query_own)

    normed = [norm_pieces(pieces, first_gain, kind_a, groups)]
    normed[0], grad_far = after((normed[0], grad_far), normed[0])
    normed.append(swap(normed[0], "mlp", 1))
    keys, values = zip(*[project_rows(rows, key_weight, value_weight) for rows in normed])
    heads_own = attend(query_own, keys, values, places, own_place, clip_length, clips)
    grad_inner = gather_inner(after(grad_half, normed[0]))
    heads_own, grad_inner = after((heads_own, grad_inner), heads_own)
    grad_far = join_x(jnp.concatenate(grad_far, axis=0), heads_own)
    mine, other = product_halves([heads_own], [output_weight], NN)
    other, grad_far = after((other, grad_far), other)
    grad_inner += gather_inner(grad_far)
    low, other = pair_mlp(mine, other)
    own_activated_grad = grad_activated(after(grad_own, low), down_weight)
    queries = [
        project_rows(rows, query_weight)[0] for rows in after(normed, own_activated_grad)
    ]
    other = after(other, queries)
    residual, lifted_half = lift(inputs_half, low, other, second_gain, half_kind)

    lifted_own = both(lifted_half)
    activated_own, hidden_own, mine, other = feed_own(lifted_own, up_weight, own_activated_grad)
    lifted_far = gather_outer(after(lifted_half, other))
    other, grad_inner = after((other, grad_inner), other)
    low, other = pair_mlp(mine, other)
    attended, stored = attend_all(
        after(queries, low),
        keys,
        values,
        places,
        query_place,
        groups,
        clip_length,
        clips,
    )
    other, lifted_far = after((other, lifted_far), attended)
    grad_residual, mixed_half, mixed_columns = middle(
        residual, low, other, grad_half, second_gain, half_kind, shards
    )
    heads_grad = product_back(both(mixed_half), output_weight)

    heads_first = gather_first(heads_grad)
    lifted_far = jnp.concatenate(lifted_far, axis=0)
    lifted_inner_far = gather_inner(lifted_far)
    down_mine, down_other = down_own(after(activated_own, heads_grad), down_weight)
    lifted_far = join_x(lifted_far, heads_first[1], down_other, lifted_inner_far)
    heads_grads = gather_pieces(*heads_first)
    first_lifted, first_grads = with_core([lifted_far]), with_core([grad_far])
    first_lifted = after(first_lifted, heads_grads[inner_size() + 1])
    own = (lifted_own, grad_own, activated_own, hidden_own)
    sums = feed_all(first_lifted, first_grads, up_weight, down_weight, shards, own=own)
    down_low, down_other = pair_mlp(down_mine, down_other)
    heads_grads, down_low, down_other = after((heads_grads, down_low, down_other), sums)
    inner = inner_size()
    columns_far = {
        outer: swap(after(mixed_columns[outer : outer + inner], sums), "seq", outer)
        for outer in range(inner, shards, inner)
    }
    lifted_inner = gather_inner(after(lifted_half, down_other))
    query_low, key_low, value_low, own_low = attend_back(
        heads_grads, queries, keys, values, attended, stored, groups
    )
    attention_weights = (query_weight, key_weight, value_weight)
    lifted_inner += [join_x(far, own_low) for far in lifted_inner_far]
    own_low, lifted_inner, columns_far = after((own_low, lifted_inner, columns_far), own_low)
    low, other = pair_mlp(*product_halves(own_low, attention_weights, NT))

    query_grad, key_grad, value_grad, first_gain_grad = project(
        normed,
        after((query_low, key_low, value_low), low),
        attention_weights,
        first_gain,
        kinds,
        shards,
    )
    columns_far = after(columns_far, low)
    columns_far[0] = after(mixed_columns[:inner], low)
    columns = {}
    for outer, came in columns_far.items():
        columns[outer] = came[0]
        for bit in range(1, inner):
            columns[outer | bit] = swap(came[bit], "seq", bit)
    other, columns = after((other, columns), query_grad)
    first_gain_grad = after(first_gain_grad, other)
    first_gain_grad = first_gain_grad + swap(first_gain_grad, "mlp", 1)
    input_half = last(inputs_half, low, other, grad_residual, first_gain, half_kind, shards)
    outputs_half = finish(residual, down_low, after(down_other, input_half), shards)
    rest_lifted = with_core(after(lifted_inner, other))
    rest_grads = with_core(after(grad_inner, other))
    up_grad, down_grad = feed_all(
        after(rest_lifted, outputs_half, first_gain_grad), rest_grads, up_weight, down_weight, shards, sums
    )
    first_came = jnp.zeros_like(first_gain_grad)
    bit = 2
    while bit < lax.axis_size("mlp"):
        if bit > 2:
            first_gain_grad = first_gain_grad + first_came
        first_came = after(swap(first_gain_grad, "mlp", bit), up_grad)
        bit *= 2
    placed = (input_half, outputs_half)
    input_grad, outputs = place_halves(placed, [swap(array, "mlp", 1) for array in placed])
    mixed_part = jnp.stack([after(columns[d], up_grad) for d in range(shards)])
    output_grad, second_gain_grad, first_gain_grad = output_part(
        attended,
        (mixed_part, swap(mixed_part, "mlp", 1)),
        (first_gain_grad, first_came),
        groups,
    )

    return (
        outputs,
        input_grad,
        first_gain_grad,
        query_grad,
        key_grad,
        value_grad,
        output_grad,
        second_gain_grad,
        up_grad,
        down_grad,
    )


def solution(mesh):
    return jax.shard_map(
        body,
        mesh=mesh,
        in_specs=(
            P("seq", None),
            P(),
            P(None, "mlp"),
            P(None, "mlp"),
            P(None, "mlp"),
            P("mlp", None),
            P(),
            P(None, "mlp"),
            P("mlp", None),
            P(),
            P(),
            P(),
            P("seq", None),
        ),
        out_specs=(
            P("seq", None),
            P("seq", None),
            P(None, "seq"),
            P("seq", "mlp"),
            P("seq", "mlp"),
            P("seq", "mlp"),
            P("mlp", "seq"),
            P(None, "seq"),
            P("seq", "mlp"),
            P("mlp", "seq"),
        ),
        check_vma=False,
    )
```
